32 devices in a mesh: tok: 8 (over y, x, core), tab: 4 (over z).
Axes of the slice: x: 2, y: 2, z: 4, core: 2. Of those that a mesh axis runs over, the one named last changes fastest.
Arguments:
- embedded: bfloat16 [32768, 1024], P(('tok', 'tab')), may hold values from -6 to 6
- cell_index: int32 [64, 512], P(('tok', 'tab')), may hold values from 0 to 127, never falling along the last dimension, each value on 1 to 60 neighbouring positions
- cell_boxes: int32 [64, 4, 512], P(('tok', 'tab')), may hold values from 0 to 1000
- box_tables: bfloat16 [4, 1001, 1024], P('tab'), may hold values from -2.390625 to 2.390625
- joined_weight: bfloat16 [1024, 3072], replicated, may hold values from -0.25 to 0.25
- output_weight: bfloat16 [1024, 1024], replicated, may hold values from -0.75 to 0.75
- expand_weight: bfloat16 [1024, 4096], replicated, may hold values from -0.1875 to 0.1875
- reduce_weight: bfloat16 [4096, 1024], replicated, may hold values from -0.09375 to 0.09375
- hidden_bias: float32 [4096], replicated, may hold values from -3 to 3
- bias_rows: float32 [4, 1024], replicated, may hold values from -3 to 3
- norm_gains: float32 [3, 1024], replicated, may hold values from 0.5 to 1.5
- norm_shifts: float32 [3, 1024], replicated, may hold values from -1.8 to 1.8
- cotangent: bfloat16 [32768, 1024], P(('tok', 'tab')), may hold values from -6 to 6
Outputs:
- layer_out: bfloat16 [32768, 1024], P(('tok', 'tab'))
- embedded_grad: float32 [32768, 1024], P(('tok', 'tab'))
- tables_grad: float32 [4, 1001, 1024], P('tab')
- joined_grad: float32 [1024, 3072], P('tok', 'tab')
- output_grad: float32 [1024, 1024], P('tok', 'tab')
- expand_grad: float32 [1024, 4096], P('tok', 'tab')
- reduce_grad: float32 [4096, 1024], P('tok', 'tab')
- hidden_bias_grad: float32 [4096], replicated
- biases_grad: float32 [4, 1024], replicated
- gains_grad: float32 [3, 1024], replicated
- shifts_grad: float32 [3, 1024], replicated
The draws below stay inside these ranges and needn't reach their ends.
Inputs may be any that keep to these rules, and one draw needn't show every extreme that they name: `cell_index`: within a page the cell slot never falls from token to token, and each cell holds 1 to 60 tokens.
All inputs are finite; a program needn't handle non-finite values.
Results may differ from the reference program's by a relative error of at most 0.035.
Values may be sent and summed in bfloat16 or wider, within the bound.
A program may use at most 256 MiB of HBM per device.

```python
import math
import jax
import jax.numpy as jnp
import numpy as np
from jax import lax

D = 1024
FF = 4096
HEADS = 16
HEAD_DIM = 64
TABLE_ROWS = 1001
PAGE_LEN = 512
CELL_MOST = 60
PAGES = 64
TOKENS = 32768


def set_ends(array, own_key, low, largest):
    longest = array.shape.index(max(array.shape))
    spots = []
    for shift in (0, 1):
        where = [jax.random.randint(jax.random.fold_in(own_key, axis), (), 0, length) for axis, length in enumerate(array.shape)]
        where[longest] = (where[longest] + shift) % array.shape[longest]
        spots.append(tuple(where))
    return array.at[spots[0]].set(low).at[spots[1]].set(largest)


def level_of(rng, extent, pieces, smallest, largest):
    level, own = 1.0, jax.random.fold_in(rng, 6)
    for axis_at, blocks in pieces:
        draws = jnp.exp(jax.random.uniform(jax.random.fold_in(own, axis_at), (blocks,), jnp.float32, smallest / len(pieces), largest / len(pieces)))
        level = level * jnp.repeat(draws, extent[axis_at] // blocks).reshape([-1 if axis == axis_at else 1 for axis in range(len(extent))])
    return level


def profile(number_of, total, reach, skew):
    portions = [(1 << 20) // math.isqrt(standing ** skew) + 1 for standing in range(2, number_of + 1)]
    spare, given = total - reach - (number_of - 1), [1] * (number_of - 1)
    while spare > 0:
        movable = [i for i in range(number_of - 1) if given[i] < reach]
        mass, budget = sum([portions[i] for i in movable]), spare
        for i in movable:
            extra = min(reach - given[i], max(1, budget * portions[i] // mass), spare)
            given[i] = given[i] + extra
            spare = spare - extra
    return np.array([reach] + given)


def ragged(own_key, number_of, total, bound, skew):
    if number_of == 2:
        one = jax.random.randint(own_key, (), max(1, total - bound), min(bound, total - 1) + 1)
        return jnp.stack([one, total - one])
    tallies = jnp.asarray(profile(number_of, total, bound, skew), jnp.int32)
    twos = (number_of - 1) // 2
    giver, sink = tallies[1:1 + 2 * twos:2], tallies[2:2 + 2 * twos:2]
    margin = jnp.minimum(giver - 1, bound - sink)
    moved = jax.random.randint(jax.random.fold_in(own_key, 1), (twos,), 0, 1 << 20) % (margin + 1)
    tallies = tallies.at[1:1 + 2 * twos:2].set(giver - moved).at[2:2 + 2 * twos:2].set(sink + moved)
    return tallies[jax.random.permutation(jax.random.fold_in(own_key, 2), number_of)]


def scatter_about(rng, extent, scale, most, cuts=(), kind=jnp.bfloat16):
    factor_of = level_of(rng, extent, cuts, -0.22, 0.18) if cuts else 1.0
    values = jax.random.normal(rng, extent, jnp.float32) * scale * factor_of
    return jnp.minimum(jnp.maximum(values, -most), most).astype(kind)


def setup_inputs(seed: int = 0) -> dict:
    streams_of = jax.random.split(jax.random.key(seed), 14)
    return {
        "embedded": scatter_about(streams_of[0], (TOKENS, D), 1.0, 6.0, ((0, 32),)),
        "cell_index": jax.vmap(lambda own: jnp.searchsorted(jnp.cumsum(ragged(own, PAGE_LEN // 4, PAGE_LEN, CELL_MOST, 2)), jnp.arange(PAGE_LEN), side="right"))(jax.random.split(streams_of[1], PAGES)).reshape((PAGES, PAGE_LEN)).astype(jnp.int32),
        "cell_boxes": set_ends(jax.random.randint(streams_of[2], (PAGES, 4, PAGE_LEN), 0, TABLE_ROWS), jax.random.fold_in(streams_of[2], 1), 0, TABLE_ROWS - 1).astype(jnp.int32),
        "box_tables": scatter_about(streams_of[3], (4, TABLE_ROWS, D), 0.4, 2.390625, ((0, 4),)),
        "joined_weight": scatter_about(streams_of[4], (D, 3 * D), (D // 2) ** -0.5, 0.25),
        "output_weight": scatter_about(streams_of[5], (D, D), (D // 16) ** -0.5, 0.75),
        "expand_weight": scatter_about(streams_of[6], (D, FF), D ** -0.5, 0.1875),
        "reduce_weight": scatter_about(streams_of[7], (FF, D), FF ** -0.5, 0.09375),
        "hidden_bias": scatter_about(streams_of[8], (FF,), 0.5, 3.0, (), jnp.float32),
        "bias_rows": scatter_about(streams_of[9], (4, D), 0.5, 3.0, (), jnp.float32),
        "norm_gains": jnp.clip(1.0 + 0.1 * jax.random.normal(streams_of[10], (3, D), jnp.float32), 0.5, 1.5),
        "norm_shifts": scatter_about(streams_of[11], (3, D), 0.3, 1.8, (), jnp.float32),
        "cotangent": scatter_about(streams_of[12], (TOKENS, D), 1.0, 6.0, ((0, 32),)),
    }


@jax.custom_vjp
def low(v):
    return lax.optimization_barrier(v.astype(jnp.bfloat16)).astype(jnp.float32)

@jax.custom_vjp
def low_back(v):
    return v

def low_keep(v):
    return (low(v), None)

def low_pass(kept, grad):
    return (grad,)

def back_keep(v):
    return (v, None)

def back_low(kept, grad):
    return (low(grad),)
low.defvjp(low_keep, low_pass)
low_back.defvjp(back_keep, back_low)
EPSILON = 1e-05
HIGHEST = lax.Precision.HIGHEST

def layer_norm(values, gain_row, shift_row):
    average = lax.optimization_barrier(jnp.mean(values, axis=-1, keepdims=True))
    centred = values - average
    variance = lax.optimization_barrier(jnp.mean(centred * centred, axis=-1, keepdims=True))
    return centred * lax.rsqrt(variance + EPSILON) * gain_row + shift_row

def gelu_exact(values):
    return jax.nn.gelu(values, approximate=False)

def box_indices(cell_index, cell_boxes):
    chosen = jnp.take_along_axis(cell_boxes, jnp.broadcast_to(cell_index[:, None, :], cell_boxes.shape), axis=2)
    left_edge = jnp.minimum(chosen[:, 0], chosen[:, 2]).reshape(-1)
    right_edge = jnp.maximum(chosen[:, 0], chosen[:, 2]).reshape(-1)
    top_edge = jnp.minimum(chosen[:, 1], chosen[:, 3]).reshape(-1)
    bottom_edge = jnp.maximum(chosen[:, 1], chosen[:, 3]).reshape(-1)
    return (left_edge, right_edge, top_edge, bottom_edge, right_edge - left_edge, bottom_edge - top_edge)

def attend_page(operands):
    queries, keys_page, values_page = operands
    length = queries.shape[0]
    split_query = queries.reshape(length, HEADS, HEAD_DIM)
    split_key = keys_page.reshape(length, HEADS, HEAD_DIM)
    split_value = values_page.reshape(length, HEADS, HEAD_DIM)
    scores = low_back(jnp.einsum('qhd,khd->hqk', split_query, split_key, precision=HIGHEST))
    weights_soft = low(jax.nn.softmax(scores, axis=-1))
    mixed = jnp.einsum('hqk,khd->qhd', weights_soft, split_value, precision=HIGHEST)
    return mixed.reshape(length, HEADS * HEAD_DIM)

def forward(embedded, box_tables, joined_weight, output_weight, expand_weight, reduce_weight, hidden_bias, bias_rows, norm_gains, norm_shifts, indices):
    left_edge, right_edge, top_edge, bottom_edge, across, upward = indices
    term_across = box_tables[0][left_edge] + box_tables[0][right_edge]
    term_down = box_tables[1][top_edge] + box_tables[1][bottom_edge]
    box_embed = low_back(low(term_across) + low(term_down) + low(box_tables[2][across]) + low(box_tables[3][upward]))
    normed = layer_norm(embedded + box_embed, norm_gains[0], norm_shifts[0])
    joined = jnp.dot(low(normed), joined_weight, precision=HIGHEST)
    score_scale = HEAD_DIM ** (-0.5)
    queries = low_back(low((joined[:, :D] + bias_rows[0]) * score_scale))
    keys_all = low_back(low(joined[:, D:2 * D]))
    values_all = low_back(low(joined[:, 2 * D:] + bias_rows[1]))
    paged = (PAGES, PAGE_LEN, D)
    mixed = lax.map(jax.checkpoint(attend_page), (queries.reshape(paged), keys_all.reshape(paged), values_all.reshape(paged)))
    mixed = low_back(low(mixed.reshape(TOKENS, D)))
    attn_branch = low_back(jnp.dot(mixed, output_weight, precision=HIGHEST) + bias_rows[2])
    after_attn = layer_norm(normed + attn_branch, norm_gains[1], norm_shifts[1])
    hidden = low_back(jnp.dot(low(after_attn), expand_weight, precision=HIGHEST) + hidden_bias)
    activated = low(gelu_exact(hidden))
    ffn_branch = low_back(jnp.dot(activated, reduce_weight, precision=HIGHEST) + bias_rows[3])
    return layer_norm(after_attn + ffn_branch, norm_gains[2], norm_shifts[2])

def reference(embedded, cell_index, cell_boxes, box_tables, joined_weight, output_weight, expand_weight, reduce_weight, hidden_bias, bias_rows, norm_gains, norm_shifts, cotangent):
    indices = box_indices(cell_index, cell_boxes)
    params = (embedded.astype(jnp.float32), box_tables.astype(jnp.float32), joined_weight.astype(jnp.float32), output_weight.astype(jnp.float32), expand_weight.astype(jnp.float32), reduce_weight.astype(jnp.float32), hidden_bias.astype(jnp.float32), bias_rows.astype(jnp.float32), norm_gains.astype(jnp.float32), norm_shifts.astype(jnp.float32))

    def apply_layer(*inputs):
        return forward(*inputs, indices)
    output, pullback = jax.vjp(apply_layer, *params)
    grads = pullback(cotangent.astype(jnp.float32))
    return (output.astype(jnp.bfloat16), grads[0], grads[1], grads[2], grads[3], grads[4], grads[5], grads[6], grads[7], grads[8], grads[9])
```

```python
import functools

import jax
import jax.numpy as jnp
from jax import lax
from jax.experimental import pallas as pl
from jax.experimental.pallas import tpu as pltpu
from jax.sharding import PartitionSpec as P

HEADS = 16
HEAD_DIM = 64
CELLS = 128
EPSILON = 1e-05
SCALE = HEAD_DIM ** (-0.5)
LOG2E = 1.4426950408889634
F32 = jnp.float32
BF = jnp.bfloat16
NN = ((1,), (0,))
NT = ((1,), (1,))
TN = ((0,), (0,))
ANY = pl.ANY

TAIL_P = 0.305
TAIL_C = (
    0.12164194255155772,
    0.12243138164026345,
    0.10365178645525906,
    0.12022714029486306,
    -0.03641303195181058,
    0.1839499605096701,
    -0.15192310059752684,
    0.03643391798251271,
)


def dot(a, b, dims):
    return lax.dot_general(a, b, (dims, ((), ())), preferred_element_type=F32)


def params(**kw):
    return pltpu.CompilerParams(vmem_limit_bytes=60 << 20, **kw)


def cost(flops, nbytes, trans=0):
    return pl.CostEstimate(
        flops=int(flops), bytes_accessed=int(nbytes), transcendentals=int(trans)
    )


def full(shape):
    zeros = (0,) * len(shape)
    return pl.BlockSpec(shape, lambda *_: zeros, pipeline_mode=pl.Buffered(1))


def gelu_parts(h):
    a = jnp.abs(h)
    t = 1.0 / (1.0 + TAIL_P * a)
    poly = jnp.full_like(t, TAIL_C[-1])
    for c in TAIL_C[-2::-1]:
        poly = poly * t + c
    e = jnp.exp2(h * h * (-0.5 * LOG2E))
    tail = poly * t * e
    phi_cdf = jnp.where(h > 0, 1.0 - tail, tail)
    act = h * phi_cdf
    slope = phi_cdf + h * e * 0.3989422804014327
    return act, slope


def norm_stats(v):
    mean = jnp.mean(v, axis=-1, keepdims=True)
    centred = v - mean
    var = jnp.mean(centred * centred, axis=-1, keepdims=True)
    rstd = lax.rsqrt(var + EPSILON)
    return centred * rstd, rstd


def norm_back(y, xh, rstd, gain):
    u = y * gain
    return (
        u - jnp.mean(u, axis=-1, keepdims=True) - xh * jnp.mean(u * xh, axis=-1, keepdims=True)
    ) * rstd


def colsum(v):
    return jnp.sum(v, axis=0, keepdims=True)


def lookup_kernel(idx, table, out):
    rows = table.shape[0]
    count = idx.shape[2]
    number = lax.broadcasted_iota(jnp.int32, (rows, count), 0)
    first = (number == idx[0, 0:1, :]).astype(F32)
    second = (number == idx[0, 1:2, :]).astype(F32)
    out[0] = dot((first + second).astype(BF), table[...], TN).astype(BF)


def lookup(idx, table):
    groups, _, count = idx.shape
    rows, width = table.shape
    return pl.pallas_call(
        lookup_kernel,
        grid=(groups,),
        in_specs=[
            pl.BlockSpec((1, 2, count), lambda i: (i, 0, 0)),
            full((rows, width)),
        ],
        out_specs=pl.BlockSpec((1, count, width), lambda i: (i, 0, 0)),
        out_shape=jax.ShapeDtypeStruct((groups, count, width), BF),
        compiler_params=params(),
        cost_estimate=cost(2 * groups * count * rows * width, 2 * groups * count * width),
        name="lookup",
    )(idx, table)


def embed_kernel(
    emb, ci, t0, t1, t2, t3, w, gains, shifts, bias, q, k, v, normed, low, rstd_out
):
    width = emb.shape[1]
    tokens = emb.shape[0]
    cells = jnp.concatenate([t0[...], t1[...], t2[...], t3[...]], axis=0)
    number = lax.broadcasted_iota(jnp.int32, (CELLS, tokens), 0)
    pick = (number == ci[0]).astype(F32).astype(BF)
    pick = jnp.concatenate([pick] * 4, axis=0)
    box = dot(pick, cells, TN)
    xh, rstd = norm_stats(emb[...].astype(F32) + box)
    y = xh * gains[0:1] + shifts[0:1]
    normed[...] = y
    rstd_out[...] = rstd
    y_low = y.astype(BF)
    low[...] = y_low
    q[...] = ((dot(y_low, w[:, :width], NN) + bias[0:1]) * SCALE).astype(BF)
    k[...] = dot(y_low, w[:, width : 2 * width], NN).astype(BF)
    v[...] = (dot(y_low, w[:, 2 * width :], NN) + bias[1:2]).astype(BF)


def embed(emb, ci, terms, w, gains, shifts, bias):
    tokens, width = emb.shape
    pages, length = ci.shape
    rows = pl.BlockSpec((length, width), lambda i: (i, 0))
    cell_rows = pl.BlockSpec((CELLS, width), lambda i: (i, 0))
    shape = lambda dt, n=width: jax.ShapeDtypeStruct((tokens, n), dt)
    return pl.pallas_call(
        embed_kernel,
        grid=(pages,),
        in_specs=[rows, pl.BlockSpec((1, 1, length), lambda i: (i, 0, 0))]
        + [cell_rows] * 4
        + [full(w.shape), full(gains.shape), full(shifts.shape), full(bias.shape)],
        out_specs=[rows] * 5 + [pl.BlockSpec((length, 1), lambda i: (i, 0))],
        out_shape=[shape(BF), shape(BF), shape(BF), shape(F32), shape(BF), shape(F32, 1)],
        compiler_params=params(),
        cost_estimate=cost(2 * tokens * width * 3 * width, 26 << 20),
        name="embed_joined",
    )(emb, ci.reshape(pages, 1, length), *terms, w, gains, shifts, bias)


HP = 4


def head_masks(length, pair):
    lane = lax.broadcasted_iota(jnp.int32, (length, pair), 1)
    return lane < HEAD_DIM


def attn_fwd_kernel(q, k, v, mixed, lse):
    length = q.shape[0]
    pair = 2 * HEAD_DIM
    low_half = head_masks(length, pair)
    zero = jnp.zeros((length, pair), BF)
    for p in range(HP // 2):
        cols = slice(p * pair, (p + 1) * pair)
        qp, kp, vp = q[:, cols], k[:, cols], v[:, cols]
        vt = vp.T
        outs = []
        for h in range(2):
            km = jnp.where(low_half, kp, zero) if h == 0 else jnp.where(low_half, zero, kp)
            st = dot(km, qp, NT)
            top = jnp.max(st, axis=0, keepdims=True)
            raised = jnp.exp2((st - top) * LOG2E)
            total = jnp.sum(raised, axis=0, keepdims=True)
            lse[0, 0, 2 * p + h : 2 * p + h + 1, :] = top + jnp.log(total)
            ot = dot(vt[h * HEAD_DIM : (h + 1) * HEAD_DIM], raised.astype(BF), NN)
            outs.append(ot * (1.0 / total))
        mixed[:, cols] = jnp.concatenate(outs, axis=0).T.astype(BF)


def attn_fwd(q, k, v, pages):
    tokens, width = q.shape
    length = tokens // pages
    steps = HEADS // HP
    blk = pl.BlockSpec((length, HP * HEAD_DIM), lambda i, j: (i, j))
    return pl.pallas_call(
        attn_fwd_kernel,
        grid=(pages, steps),
        in_specs=[blk] * 3,
        out_specs=[blk, pl.BlockSpec((1, 1, HP, length), lambda i, j: (i, j, 0, 0))],
        out_shape=[
            jax.ShapeDtypeStruct((tokens, width), BF),
            jax.ShapeDtypeStruct((pages, steps, HP, length), F32),
        ],
        compiler_params=params(),
        cost_estimate=cost(14e9, 8 << 20, pages * HEADS * length * length),
        name="attention",
    )(q, k, v)


def attn_bwd_kernel(q, k, v, mixed, go, lse, gj, sums):
    length = q.shape[0]
    pair = 2 * HEAD_DIM
    low_half = head_masks(length, pair)
    zero = jnp.zeros((length, pair), BF)
    page = pl.program_id(1)

    def pick(x, h):
        return jnp.where(low_half, x, zero) if h == 0 else jnp.where(low_half, zero, x)

    for p in range(HP // 2):
        cols = slice(p * pair, (p + 1) * pair)
        qp, kp, vp, op, gp = q[:, cols], k[:, cols], v[:, cols], mixed[:, cols], go[:, cols]
        kt = kp.T
        prod_t = (op.astype(F32) * gp.astype(F32)).T
        dq_t, dk, dv = [], None, None
        for h in range(2):
            st = dot(pick(kp, h), qp, NT)
            probs = jnp.exp2((st - lse[0, 0, 2 * p + h : 2 * p + h + 1, :]) * LOG2E)
            dv_h = dot(probs.astype(BF), pick(gp, h), NN)
            dpt = dot(pick(vp, h), gp, NT)
            delta = colsum(prod_t[h * HEAD_DIM : (h + 1) * HEAD_DIM])
            ds = (probs * (dpt - delta)).astype(BF)
            dk_h = dot(ds, pick(qp, h), NN)
            dq_t.append(dot(kt[h * HEAD_DIM : (h + 1) * HEAD_DIM], ds, NN))
            dv = dv_h if dv is None else dv + dv_h
            dk = dk_h if dk is None else dk + dk_h
        dq = (jnp.concatenate(dq_t, axis=0).T.astype(BF).astype(F32) * SCALE).astype(BF)
        dv = dv.astype(BF)
        gj[0, :, cols] = dq
        gj[1, :, cols] = dk.astype(BF)
        gj[2, :, cols] = dv
        part = jnp.concatenate([colsum(dq.astype(F32)), colsum(dv.astype(F32))], axis=0)

        @pl.when(page == 0)
        def _():
            sums[:, cols] = part

        @pl.when(page != 0)
        def _():
            sums[:, cols] = sums[:, cols] + part


def attn_bwd(q, k, v, mixed, go, lse, pages):
    tokens, width = q.shape
    length = tokens // pages
    steps = HEADS // HP
    wide = HP * HEAD_DIM
    blk = pl.BlockSpec((length, wide), lambda j, i: (i, j))
    return pl.pallas_call(
        attn_bwd_kernel,
        grid=(steps, pages),
        in_specs=[blk] * 5 + [pl.BlockSpec((1, 1, HP, length), lambda j, i: (i, j, 0, 0))],
        out_specs=[
            pl.BlockSpec((3, length, wide), lambda j, i: (0, i, j)),
            pl.BlockSpec((2, wide), lambda j, i: (0, j)),
        ],
        out_shape=[
            jax.ShapeDtypeStruct((3, tokens, width), BF),
            jax.ShapeDtypeStruct((2, width), F32),
        ],
        compiler_params=params(),
        cost_estimate=cost(35e9, 16 << 20, pages * HEADS * length * length),
        name="attention_back",
    )(q, k, v, mixed, go, lse)


FC = 1024


def ffn_fwd_kernel(
    mixed, normed, wo, we, wr, hb, bias, gains, shifts, cot,
    out, after_out, low_out, rstd_out, act_out, slope_out, gs2_out, gffn_out, sums,
):
    ff = we.shape[1]
    attn_sum = normed[...] + (dot(mixed[...], wo[...], NN) + bias[2:3])
    xh, rstd = norm_stats(attn_sum)
    after = xh * gains[1:2] + shifts[1:2]
    after_out[...] = after
    rstd_out[...] = rstd
    low = after.astype(BF)
    low_out[...] = low
    total = after + bias[3:4]
    for j in range(ff // FC):
        cols = slice(j * FC, (j + 1) * FC)
        act, slope = gelu_parts(dot(low, we[:, cols], NN) + hb[:, cols])
        act = act.astype(BF)
        act_out[:, cols] = act
        slope_out[:, cols] = slope.astype(BF)
        total = total + dot(act, wr[cols, :], NN)
    xh, rstd = norm_stats(total)
    out[...] = (xh * gains[2:3] + shifts[2:3]).astype(BF)
    y = cot[...].astype(F32)
    gs2 = norm_back(y, xh, rstd, gains[2:3])
    gs2_out[...] = gs2
    gffn = gs2.astype(BF)
    gffn_out[...] = gffn
    part = jnp.concatenate([colsum(y * xh), colsum(y), colsum(gffn.astype(F32))], axis=0)

    @pl.when(pl.program_id(0) == 0)
    def _():
        sums[...] = part

    @pl.when(pl.program_id(0) != 0)
    def _():
        sums[...] = sums[...] + part


def ffn_fwd(mixed, normed, wo, we, wr, hb, bias, gains, shifts, cot, tile):
    tokens, width = mixed.shape
    ff = we.shape[1]
    rows = pl.BlockSpec((tile, width), lambda i: (i, 0))
    long = pl.BlockSpec((tile, ff), lambda i: (i, 0))
    shape = lambda dt, n=width: jax.ShapeDtypeStruct((tokens, n), dt)
    hb = hb.reshape(1, ff)
    return pl.pallas_call(
        ffn_fwd_kernel,
        grid=(tokens // tile,),
        in_specs=[rows, rows]
        + [full(a.shape) for a in (wo, we, wr, hb, bias, gains, shifts)]
        + [rows],
        out_specs=[rows, rows, rows, pl.BlockSpec((tile, 1), lambda i: (i, 0)), long, long, rows, rows]
        + [pl.BlockSpec((3, width), lambda i: (0, 0))],
        out_shape=[
            shape(BF), shape(F32), shape(BF), shape(F32, 1), shape(BF, ff), shape(BF, ff),
            shape(F32), shape(BF), jax.ShapeDtypeStruct((3, width), F32),
        ],
        compiler_params=params(),
        cost_estimate=cost(2 * tokens * width * (width + 2 * ff), 60 << 20, tokens * ff * 2),
        name="ffn_forward",
    )(mixed, normed, wo, we, wr, hb, bias, gains, shifts, cot)


def ffn_bwd_kernel(
    gffn, slope, gs2, after, rstd, wr, we, wo, gains, shifts,
    gh_out, gs1_out, gattn_out, gmixed_out, hsum, sums,
):
    ff = we.shape[1]
    first = pl.program_id(0) == 0
    g = gffn[...]
    total = gs2[...]
    hparts = []
    for j in range(ff // FC):
        cols = slice(j * FC, (j + 1) * FC)
        gh = (dot(g, wr[cols, :], NT) * slope[:, cols].astype(F32)).astype(BF)
        gh_out[:, cols] = gh
        hparts.append(colsum(gh.astype(F32)))
        total = total + dot(gh, we[:, cols], NT)
    hpart = jnp.concatenate(hparts, axis=1)
    xh = (after[...] - shifts[1:2]) * (1.0 / gains[1:2])
    gs1 = norm_back(total, xh, rstd[...], gains[1:2])
    gs1_out[...] = gs1
    gattn = gs1.astype(BF)
    gattn_out[...] = gattn
    gmixed_out[...] = dot(gattn, wo[...], NT).astype(BF)
    part = jnp.concatenate(
        [colsum(total * xh), colsum(total), colsum(gattn.astype(F32))], axis=0
    )

    @pl.when(first)
    def _():
        sums[...] = part
        hsum[...] = hpart

    @pl.when(jnp.logical_not(first))
    def _():
        sums[...] = sums[...] + part
        hsum[...] = hsum[...] + hpart


def ffn_bwd(gffn, slope, gs2, after, rstd, wr, we, wo, gains, shifts, tile):
    tokens, width = gffn.shape
    ff = we.shape[1]
    rows = pl.BlockSpec((tile, width), lambda i: (i, 0))
    long = pl.BlockSpec((tile, ff), lambda i: (i, 0))
    shape = lambda dt, n=width: jax.ShapeDtypeStruct((tokens, n), dt)
    return pl.pallas_call(
        ffn_bwd_kernel,
        grid=(tokens // tile,),
        in_specs=[rows, long, rows, rows, pl.BlockSpec((tile, 1), lambda i: (i, 0))]
        + [full(a.shape) for a in (wr, we, wo, gains, shifts)],
        out_specs=[long, rows, rows, rows]
        + [pl.BlockSpec((1, ff), lambda i: (0, 0)), pl.BlockSpec((3, width), lambda i: (0, 0))],
        out_shape=[
            shape(BF, ff), shape(F32), shape(BF), shape(BF),
            jax.ShapeDtypeStruct((1, ff), F32), jax.ShapeDtypeStruct((3, width), F32),
        ],
        compiler_params=params(),
        cost_estimate=cost(2 * tokens * width * (width + 2 * ff), 60 << 20),
        name="ffn_backward",
    )(gffn, slope, gs2, after, rstd, wr, we, wo, gains, shifts)


def embed_bwd_kernel(gs1, gj, w, normed, rstd, ci, gains, shifts, out, cells, sums):
    width = gs1.shape[1]
    tokens = gs1.shape[0]
    total = gs1[...]
    for n in range(3):
        total = total + dot(gj[n], w[:, n * width : (n + 1) * width], NT)
    xh = (normed[...] - shifts[0:1]) * (1.0 / gains[0:1])
    grad = norm_back(total, xh, rstd[...], gains[0:1])
    out[...] = grad
    number = lax.broadcasted_iota(jnp.int32, (CELLS, tokens), 0)
    pick = (number == ci[0]).astype(F32).astype(BF)
    cells[...] = dot(pick, grad.astype(BF), NN).astype(BF)
    part = jnp.concatenate([colsum(total * xh), colsum(total)], axis=0)

    @pl.when(pl.program_id(0) == 0)
    def _():
        sums[...] = part

    @pl.when(pl.program_id(0) != 0)
    def _():
        sums[...] = sums[...] + part


def embed_bwd(gs1, gj, w, normed, rstd, ci, gains, shifts):
    tokens, width = gs1.shape
    pages, length = ci.shape
    rows = pl.BlockSpec((length, width), lambda i: (i, 0))
    return pl.pallas_call(
        embed_bwd_kernel,
        grid=(pages,),
        in_specs=[
            rows,
            pl.BlockSpec((3, length, width), lambda i: (0, i, 0)),
            full(w.shape),
            rows,
            pl.BlockSpec((length, 1), lambda i: (i, 0)),
            pl.BlockSpec((1, 1, length), lambda i: (i, 0, 0)),
            full(gains.shape),
            full(shifts.shape),
        ],
        out_specs=[
            rows,
            pl.BlockSpec((CELLS, width), lambda i: (i, 0)),
            pl.BlockSpec((2, width), lambda i: (0, 0)),
        ],
        out_shape=[
            jax.ShapeDtypeStruct((tokens, width), F32),
            jax.ShapeDtypeStruct((pages * CELLS, width), BF),
            jax.ShapeDtypeStruct((2, width), F32),
        ],
        compiler_params=params(),
        cost_estimate=cost(2 * tokens * width * 3 * width, 26 << 20),
        name="embed_backward",
    )(gs1, gj, w, normed, rstd, ci.reshape(pages, 1, length), gains, shifts)


def table_kernel(tok, idx, g0, g1, g2, g3, out_a, out_b):
    rows = out_a.shape[1]
    count = idx.shape[2]
    half = out_a.shape[2]
    base = (pl.program_id(0) ^ tok[0]) * rows
    number = lax.broadcasted_iota(jnp.int32, (rows, count), 0) + base
    picks = []
    for s in range(4):
        first = (number == idx[s, 0:1, :]).astype(F32)
        second = (number == idx[s, 1:2, :]).astype(F32)
        picks.append((first + second).astype(BF))
    pick = jnp.concatenate(picks, axis=1)
    grads = jnp.concatenate([g0[...], g1[...], g2[...], g3[...]], axis=0)
    total = dot(pick, grads, NN).astype(BF)
    out_a[0] = total[:, :half]
    out_b[0] = total[:, half:]


def table_part(tok, idx, grads, blocks):
    groups, _, count = idx.shape
    width = grads[0].shape[1]
    rows = 1024 // blocks
    half = width // 2
    out = pl.BlockSpec((1, rows, half), lambda i, t: (i, 0, 0))
    return pl.pallas_call(
        table_kernel,
        grid_spec=pltpu.PrefetchScalarGridSpec(
            num_scalar_prefetch=1,
            grid=(blocks,),
            in_specs=[full(idx.shape)] + [full((count, width))] * groups,
            out_specs=[out, out],
        ),
        out_shape=[jax.ShapeDtypeStruct((blocks, rows, half), BF)] * 2,
        compiler_params=params(),
        cost_estimate=cost(2 * 1024 * groups * count * width, 4 << 20),
        name="table_grad",
    )(tok, idx, *grads)


def table_out_kernel(tok, a, b, out):
    half = a.shape[2]
    out[0, :, :half] = a[0].astype(F32)
    out[0, :, half:] = b[0].astype(F32)


def table_out(tok, a, b, table_rows):
    blocks, rows, half = a.shape
    src = pl.BlockSpec((1, rows, half), lambda i, t: (i ^ t[0], 0, 0))
    return pl.pallas_call(
        table_out_kernel,
        grid_spec=pltpu.PrefetchScalarGridSpec(
            num_scalar_prefetch=1,
            grid=(blocks,),
            in_specs=[src, src],
            out_specs=pl.BlockSpec((1, rows, 2 * half), lambda i, t: (0, i, 0)),
        ),
        out_shape=jax.ShapeDtypeStruct((1, table_rows, 2 * half), F32),
        compiler_params=params(),
        cost_estimate=cost(0, 6 << 20),
        name="table_write",
    )(tok, a, b)


def block_of(tok, j, core):
    return (tok ^ (((j & 1) << 2) | (j & 2))) & 6 | core


def rows_partner_kernel(tok, lhs, *refs, count):
    rhs, (pa, pb, turned) = refs[:count], refs[count:]
    core = (tok[0] & 1) ^ 1
    turn_rows(tok, lhs, turned, core)
    g = dot(turned[...], jnp.concatenate([r[...].reshape(r.shape[-2:]) for r in rhs], axis=1), NN)
    rows = lhs.shape[1] // 8
    half = pa.shape[3]
    for j in range(4):
        pa[j, 0] = g[j * rows : (j + 1) * rows, :half].astype(BF)
        pb[j, 0] = g[j * rows : (j + 1) * rows, half:].astype(BF)


def turn_rows(tok, lhs, turned, core):
    rows = lhs.shape[1] // 8

    @pl.when(pl.program_id(0) == 0)
    def _():
        for j in range(4):
            start = pl.multiple_of(block_of(tok[0], j, core) * rows, rows)
            turned[j * rows : (j + 1) * rows, :] = lhs[:, pl.ds(start, rows)].T


def rows_own_kernel(tok, lhs, *refs, count):
    rhs = refs[:count]
    ra, rb, sa, ka, sb, kb, turned = refs[count:]
    turn_rows(tok, lhs, turned, tok[0] & 1)
    g = dot(turned[...], jnp.concatenate([r[...].reshape(r.shape[-2:]) for r in rhs], axis=1), NN)
    rows = lhs.shape[1] // 8
    half = ra.shape[3]
    for j in range(4):
        rx, ry = j >> 1, j & 1
        a = (g[j * rows : (j + 1) * rows, :half] + ra[j, 0].astype(F32)).astype(BF)
        b = (g[j * rows : (j + 1) * rows, half:] + rb[j, 0].astype(F32)).astype(BF)
        (sa if rx else ka)[ry, 0] = a
        (sb if ry else kb)[rx, 0] = b


def rows_call(tok, lhs, rhs_list, rhs_specs, width, received):
    tokens, d = lhs.shape
    rows = d // 8
    half = width // 2
    count = len(rhs_list)
    spec = lambda n: pl.BlockSpec((n, 1, rows, half), lambda z, t: (0, z, 0, 0))
    shape = lambda n: jax.ShapeDtypeStruct((n, 4, rows, half), BF)
    own = received is not None
    kernel = rows_own_kernel if own else rows_partner_kernel
    outs = [2, 2, 2, 2] if own else [4, 4]
    return pl.pallas_call(
        functools.partial(kernel, count=count),
        grid_spec=pltpu.PrefetchScalarGridSpec(
            num_scalar_prefetch=1,
            grid=(4,),
            in_specs=[full(lhs.shape)] + rhs_specs + ([spec(4)] * 2 if own else []),
            out_specs=[spec(n) for n in outs],
            scratch_shapes=[pltpu.VMEM((d // 2, tokens), BF)],
        ),
        out_shape=[shape(n) for n in outs],
        compiler_params=params(),
        cost_estimate=cost(4 * tokens * d * width, 6 * d * width + 2 * tokens * d),
        name="weight_grad_own" if own else "weight_grad_partner",
    )(tok, lhs, *rhs_list, *(received or ()))


def cols_partner_kernel(tok, lhs, rhs, pa, pb, turned):
    @pl.when(pl.program_id(0) == 0)
    def _():
        turned[...] = lhs[...].T

    g = dot(turned[...], rhs[...], NN)
    half = pa.shape[3]
    pa[0] = g[:, :half].astype(BF).reshape(pa.shape[1:])
    pb[0] = g[:, half:].astype(BF).reshape(pb.shape[1:])


def cols_own_kernel(tok, lhs, rhs, ra, rb, sa, ka, sb, kb, turned):
    step = pl.program_id(0)

    @pl.when(step == 0)
    def _():
        turned[...] = lhs[...].T

    g = dot(turned[...], rhs[...], NN)
    half = ra.shape[3]
    a = (g[:, :half].reshape(ra.shape[1:]) + ra[0].astype(F32)).astype(BF)
    b = (g[:, half:].reshape(rb.shape[1:]) + rb[0].astype(F32)).astype(BF)
    rx = step < 2
    ry = step % 2 == 0

    @pl.when(rx)
    def _():
        sa[0] = a

    @pl.when(jnp.logical_not(rx))
    def _():
        ka[0] = a

    @pl.when(ry)
    def _():
        sb[0] = b

    @pl.when(jnp.logical_not(ry))
    def _():
        kb[0] = b


def cols_call(tok, lhs, rhs, received):
    tokens, d = lhs.shape
    f = rhs.shape[1] // 8
    half = f // 2
    rows = d // 4
    own = received is not None
    flip = 0 if own else 1
    rhs_spec = pl.BlockSpec(
        (tokens, f), lambda s, t: (0, block_of(t[0], 3 - s, (t[0] & 1) ^ flip))
    )
    blk = lambda index: pl.BlockSpec((1, 4, rows, half), lambda s, t: (index(s), 0, 0, 0))
    whole = blk(lambda s: 3 - s)
    shape = lambda n: jax.ShapeDtypeStruct((n, 4, rows, half), BF)
    late = lambda s: 1 - s // 3
    if own:
        out_specs = [
            blk(lambda s: 1 - jnp.minimum(s, 1)),
            blk(late),
            blk(lambda s: 1 - s // 2),
            blk(late),
        ]
    else:
        out_specs = [whole, whole]
    return pl.pallas_call(
        cols_own_kernel if own else cols_partner_kernel,
        grid_spec=pltpu.PrefetchScalarGridSpec(
            num_scalar_prefetch=1,
            grid=(4,),
            in_specs=[full(lhs.shape), rhs_spec] + ([whole, whole] if own else []),
            out_specs=out_specs,
            scratch_shapes=[pltpu.VMEM((d, tokens), BF)],
        ),
        out_shape=[shape(2)] * 4 if own else [shape(4)] * 2,
        compiler_params=params(),
        cost_estimate=cost(8 * tokens * d * f, 24 * d * f + 2 * tokens * d),
        name="weight_grad_own" if own else "weight_grad_partner",
    )(tok, lhs, rhs, *(received or ()))


def flip_tok(value, bit, size):
    return lax.ppermute(value, "tok", [(i, i ^ bit) for i in range(size)])


def shift_tab(value, shift, size):
    return lax.ppermute(value, "tab", [(i, (i + shift) % size) for i in range(size)])


def plus(a, b):
    return (a.astype(F32) + b.astype(F32)).astype(BF)


def scatter_sum(send, keep, bits, n_tok, n_tab):
    got = flip_tok(send, bits[0], n_tok)
    send = plus(keep[1], got[1])
    keep = plus(keep[0], got[0])
    got = flip_tok(send, bits[1], n_tok)
    part = plus(keep, got)
    z = lax.axis_index("tab")
    take = lambda i: lax.dynamic_index_in_dim(part, i, 0, keepdims=False)
    total = take(z).astype(F32)
    for shift in range(1, n_tab):
        total = total + shift_tab(take((z + shift) % n_tab), shift, n_tab).astype(F32)
    return total


def weight_grad(call, n_tok, n_tab):
    pa, pb = call(None)
    received = (flip_tok(pa, 1, n_tok), flip_tok(pb, 1, n_tok))
    sa, ka, sb, kb = call(received)
    return (
        scatter_sum(sa, ka, (2, 4), n_tok, n_tab),
        scatter_sum(sb, kb, (4, 2), n_tok, n_tab),
    )


def table_sum(part, bits, n_tok):
    rows, cols = part.shape[1:]
    block = {i: part[i] for i in range(8)}
    order = list(bits)
    for bit in order:
        sent = [i for i in sorted(block) if i & bit]
        got = flip_tok(jnp.stack([block[i] for i in sent]), bit, n_tok)
        for n, i in enumerate(sent):
            block[i ^ bit] = plus(block[i ^ bit], got[n])
            del block[i]
    for bit in reversed(order):
        held = sorted(block)
        got = flip_tok(jnp.stack([block[i] for i in held]), bit, n_tok)
        for n, i in enumerate(held):
            block[i ^ bit] = got[n]
    return jnp.stack([block[i] for i in range(8)])


def small_sum(value, n_tok, n_tab):
    bit = 1
    while bit < n_tok:
        value = value + flip_tok(value, bit, n_tok)
        bit *= 2
    total = value
    for shift in range(1, n_tab):
        total = total + shift_tab(value, shift, n_tab)
    return total


def body(
    n_tok, n_tab,
    embedded, cell_index, cell_boxes, box_tables, joined_weight, output_weight,
    expand_weight, reduce_weight, hidden_bias, bias_rows, norm_gains, norm_shifts, cotangent,
):
    tokens, width = embedded.shape
    pages, length = cell_index.shape
    table_rows = box_tables.shape[1]
    ff = expand_weight.shape[1]
    tok = lax.axis_index("tok").astype(jnp.int32).reshape(1)
    z = lax.axis_index("tab")
    cubic = n_tok == 8

    corners = cell_boxes[:, :, :CELLS]
    lo = lambda n: jnp.minimum(corners[:, n], corners[:, n + 2]).reshape(-1)
    hi = lambda n: jnp.maximum(corners[:, n], corners[:, n + 2]).reshape(-1)
    left, right, top, bottom = lo(0), hi(0), lo(1), hi(1)
    none = jnp.full_like(left, -1)
    index_table = jnp.stack(
        [
            jnp.stack([left, right]),
            jnp.stack([top, bottom]),
            jnp.stack([right - left, none]),
            jnp.stack([bottom - top, none]),
        ]
    )
    pick_table = lambda i: lax.dynamic_index_in_dim(index_table, i, 0, keepdims=False)
    group_index = jnp.stack(
        [pick_table(z)]
        + [shift_tab(pick_table((z + s) % n_tab), s, n_tab) for s in range(1, n_tab)]
    )
    padded = jnp.pad(box_tables[0], ((0, 1024 - table_rows), (0, 0)))
    found = lookup(group_index, padded)
    terms = [found[0]] + [shift_tab(found[s], n_tab - s, n_tab) for s in range(1, n_tab)]

    q, k, v, normed, normed_low, rstd0 = embed(
        embedded, cell_index, terms, joined_weight, norm_gains, norm_shifts, bias_rows
    )
    mixed, lse = attn_fwd(q, k, v, pages)
    layer_out, after, after_low, rstd1, act, slope, gs2, gffn, sums2 = ffn_fwd(
        mixed, normed, output_weight, expand_weight, reduce_weight, hidden_bias,
        bias_rows, norm_gains, norm_shifts, cotangent, 256,
    )
    gh, gs1, gattn, gmixed, hidden_sum, sums1 = ffn_bwd(
        gffn, slope, gs2, after, rstd1, reduce_weight, expand_weight, output_weight,
        norm_gains, norm_shifts, 256,
    )
    gj, sums_qv = attn_bwd(q, k, v, mixed, gmixed, lse, pages)
    embedded_grad, cell_grad, sums0 = embed_bwd(
        gs1, gj, joined_weight, normed, rstd0, cell_index, norm_gains, norm_shifts
    )

    cell_grads = [cell_grad] + [shift_tab(cell_grad, s, n_tab) for s in range(1, n_tab)]
    part_a, part_b = table_part(tok if cubic else jnp.zeros_like(tok), group_index, cell_grads, 8)
    if cubic:
        whole_a = table_sum(part_a, (1, 2, 4), n_tok)
        whole_b = table_sum(part_b, (1, 4, 2), n_tok)
        tables_grad = table_out(tok, whole_a, whole_b, table_rows)
    else:
        both = jnp.concatenate([part_a, part_b], axis=2).astype(F32)
        tables_grad = lax.psum(both.reshape(1, -1, width)[:, :table_rows], "tok")

    small = jnp.concatenate(
        [
            sums0.reshape(-1), sums1.reshape(-1), sums2.reshape(-1),
            sums_qv.reshape(-1), hidden_sum.reshape(-1),
        ]
    ).reshape(-1, 128)
    small = small_sum(small, n_tok, n_tab).reshape(-1)
    row = small.reshape(-1, width)
    gains_grad = jnp.stack([row[0], row[2], row[5]])
    shifts_grad = jnp.stack([row[1], row[3], row[6]])
    biases_grad = jnp.stack([row[8], row[9], row[4], row[7]])
    hidden_bias_grad = small[10 * width :]

    if cubic:
        wide_spec = pl.BlockSpec((tokens, ff // 4), lambda s, t: (0, s))
        out_spec = pl.BlockSpec((tokens, width // 4), lambda s, t: (0, s))
        quarter = width // 4
        third = lambda n: pl.BlockSpec(
            (1, tokens, quarter), lambda s, t: ((3 * s + n) // 4, 0, (3 * s + n) % 4)
        )
        ra, rb = weight_grad(lambda r: cols_call(tok, gffn, act, r), n_tok, n_tab)
        ea, eb = weight_grad(
            lambda r: rows_call(tok, after_low, [gh], [wide_spec], ff // 4, r), n_tok, n_tab
        )
        oa, ob = weight_grad(
            lambda r: rows_call(tok, mixed, [gattn], [out_spec], width // 4, r), n_tok, n_tab
        )
        ja, jb = weight_grad(
            lambda r: rows_call(
                tok, normed_low, [gj, gj, gj], [third(0), third(1), third(2)], 3 * quarter, r
            ),
            n_tok, n_tab,
        )
        reduce_grad = jnp.concatenate([ra, rb], axis=1).T
        expand_grad = jnp.concatenate([ea, eb], axis=1)
        output_grad = jnp.concatenate([oa, ob], axis=1)
        joined_grad = jnp.concatenate([ja, jb], axis=1)
    else:
        both = lambda a, b: jnp.einsum("ta,tb->ab", a, b, preferred_element_type=F32).astype(BF)

        def scattered(part):
            part = lax.psum_scatter(part, "tok", scatter_dimension=0, tiled=True)
            return lax.psum_scatter(part, "tab", scatter_dimension=1, tiled=True).astype(F32)

        reduce_grad = scattered(both(act, gffn))
        expand_grad = scattered(both(after_low, gh))
        output_grad = scattered(both(mixed, gattn))
        joined_grad = scattered(both(normed_low, jnp.concatenate([gj[0], gj[1], gj[2]], axis=1)))

    return (
        layer_out, embedded_grad, tables_grad, joined_grad, output_grad, expand_grad,
        reduce_grad, hidden_bias_grad, biases_grad, gains_grad, shifts_grad,
    )


def solution(mesh):
    rows = P(("tok", "tab"), None)
    return jax.shard_map(
        functools.partial(body, mesh.shape["tok"], mesh.shape["tab"]),
        mesh=mesh,
        in_specs=(
            rows, rows, P(("tok", "tab"), None, None), P("tab", None, None),
            P(), P(), P(), P(), P(), P(), P(), P(), rows,
        ),
        out_specs=(
            rows, rows, P("tab", None, None), P("tok", "tab"), P("tok", "tab"),
            P("tok", "tab"), P("tok", "tab"), P(), P(), P(), P(),
        ),
        check_vma=False,
    )
```

```python
import functools

import jax
import jax.numpy as jnp
from jax import lax
from jax.experimental import pallas as pl
from jax.experimental.pallas import tpu as pltpu
from jax.sharding import PartitionSpec as P

HEADS = 16
HEAD_DIM = 64
CELLS = 128
EPSILON = 1e-05
SCALE = HEAD_DIM ** (-0.5)
LOG2E = 1.4426950408889634
F32 = jnp.float32
BF = jnp.bfloat16
NN = ((1,), (0,))
NT = ((1,), (1,))
TN = ((0,), (0,))
ANY = pl.ANY

TAIL_P = 0.305
TAIL_C = (
    0.12164194255155772,
    0.12243138164026345,
    0.10365178645525906,
    0.12022714029486306,
    -0.03641303195181058,
    0.1839499605096701,
    -0.15192310059752684,
    0.03643391798251271,
)


def dot(a, b, dims):
    return lax.dot_general(a, b, (dims, ((), ())), preferred_element_type=F32)


def params(**kw):
    return pltpu.CompilerParams(vmem_limit_bytes=60 << 20, **kw)


def cost(flops, nbytes, trans=0):
    return pl.CostEstimate(
        flops=int(flops), bytes_accessed=int(nbytes), transcendentals=int(trans)
    )


def full(shape):
    zeros = (0,) * len(shape)
    return pl.BlockSpec(shape, lambda *_: zeros, pipeline_mode=pl.Buffered(1))


def gelu_parts(h):
    a = jnp.abs(h)
    t = 1.0 / (1.0 + TAIL_P * a)
    poly = jnp.full_like(t, TAIL_C[-1])
    for c in TAIL_C[-2::-1]:
        poly = poly * t + c
    e = jnp.exp2(h * h * (-0.5 * LOG2E))
    tail = poly * t * e
    phi_cdf = jnp.where(h > 0, 1.0 - tail, tail)
    act = h * phi_cdf
    slope = phi_cdf + h * e * 0.3989422804014327
    return act, slope


def norm_stats(v):
    mean = jnp.mean(v, axis=-1, keepdims=True)
    centred = v - mean
    var = jnp.mean(centred * centred, axis=-1, keepdims=True)
    rstd = lax.rsqrt(var + EPSILON)
    return centred * rstd, rstd


def norm_back(y, xh, rstd, gain):
    u = y * gain
    return (
        u - jnp.mean(u, axis=-1, keepdims=True) - xh * jnp.mean(u * xh, axis=-1, keepdims=True)
    ) * rstd


def colsum(v):
    return jnp.sum(v, axis=0, keepdims=True)


def lookup_kernel(idx, table, out):
    rows = table.shape[0]
    count = idx.shape[2]
    number = lax.broadcasted_iota(jnp.int32, (rows, count), 0)
    first = (number == idx[0, 0:1, :]).astype(F32)
    second = (number == idx[0, 1:2, :]).astype(F32)
    out[0] = dot((first + second).astype(BF), table[...], TN).astype(BF)


def lookup(idx, table):
    groups, _, count = idx.shape
    rows, width = table.shape
    return pl.pallas_call(
        lookup_kernel,
        grid=(groups,),
        in_specs=[
            pl.BlockSpec((1, 2, count), lambda i: (i, 0, 0)),
            full((rows, width)),
        ],
        out_specs=pl.BlockSpec((1, count, width), lambda i: (i, 0, 0)),
        out_shape=jax.ShapeDtypeStruct((groups, count, width), BF),
        compiler_params=params(),
        cost_estimate=cost(2 * groups * count * rows * width, 2 * groups * count * width),
        name="lookup",
    )(idx, table)


def embed_kernel(
    emb, ci, t0, t1, t2, t3, w, gains, shifts, bias, q, k, v, normed, low, rstd_out
):
    width = emb.shape[1]
    tokens = emb.shape[0]
    cells = jnp.concatenate([t0[...], t1[...], t2[...], t3[...]], axis=0)
    number = lax.broadcasted_iota(jnp.int32, (CELLS, tokens), 0)
    pick = (number == ci[0]).astype(F32).astype(BF)
    pick = jnp.concatenate([pick] * 4, axis=0)
    box = dot(pick, cells, TN)
    xh, rstd = norm_stats(emb[...].astype(F32) + box)
    y = xh * gains[0:1] + shifts[0:1]
    normed[...] = y
    rstd_out[...] = rstd
    y_low = y.astype(BF)
    low[...] = y_low
    q[...] = ((dot(y_low, w[:, :width], NN) + bias[0:1]) * SCALE).astype(BF)
    k[...] = dot(y_low, w[:, width : 2 * width], NN).astype(BF)
    v[...] = (dot(y_low, w[:, 2 * width :], NN) + bias[1:2]).astype(BF)


def embed(emb, ci, terms, w, gains, shifts, bias):
    tokens, width = emb.shape
    pages, length = ci.shape
    rows = pl.BlockSpec((length, width), lambda i: (i, 0))
    cell_rows = pl.BlockSpec((CELLS, width), lambda i: (i, 0))
    shape = lambda dt, n=width: jax.ShapeDtypeStruct((tokens, n), dt)
    return pl.pallas_call(
        embed_kernel,
        grid=(pages,),
        in_specs=[rows, pl.BlockSpec((1, 1, length), lambda i: (i, 0, 0))]
        + [cell_rows] * 4
        + [full(w.shape), full(gains.shape), full(shifts.shape), full(bias.shape)],
        out_specs=[rows] * 5 + [pl.BlockSpec((length, 1), lambda i: (i, 0))],
        out_shape=[shape(BF), shape(BF), shape(BF), shape(F32), shape(BF), shape(F32, 1)],
        compiler_params=params(),
        cost_estimate=cost(2 * tokens * width * 3 * width, 26 << 20),
        name="embed_joined",
    )(emb, ci.reshape(pages, 1, length), *terms, w, gains, shifts, bias)


STAGES = 4


def neighbours():
    tok, z = lax.axis_index("tok"), lax.axis_index("tab")
    core = {"tok": tok + 1 - 2 * (tok % 2)}
    x = {"tok": tok + 2 - 4 * ((tok // 2) % 2)}
    y = {"tok": tok + 4 - 8 * (tok // 4)}
    peers = [{"tab": (z + s) % 4} for s in range(1, 4)]
    return core, x, y, peers


def meet(devices):
    barrier = pltpu.get_barrier_semaphore()
    for d in devices:
        pl.semaphore_signal(barrier, inc=1, device_id=d, device_id_type=pl.DeviceIdType.MESH)
    pl.semaphore_wait(barrier, len(devices))


def sum_scratch(rows, cols):
    part = lambda *n: pltpu.VMEM((*n, rows, cols), BF)
    return [
        part(2, 4, 4), part(2, 4, 4), part(2, 4, 2), part(2, 4), part(2, 3),
        pltpu.SemaphoreType.DMA((2, 4)),
        pltpu.SemaphoreType.DMA((STAGES, 2, 4)),
        pltpu.SemaphoreType.DMA((STAGES, 2, 4)),
    ]


class Summing:
    def __init__(self, grads, out, scratch):
        self.grads, self.out = grads, out
        self.own, self.r0, self.r1, self.r2, self.r3, self.local, self.sent, self.got = scratch
        core, x, y, peers = neighbours()
        self.core, self.first, self.second, self.peers = core, (x, y), (y, x), peers
        self.z = lax.axis_index("tab")

    def devices(self):
        return [self.core, self.first[0], self.first[1], *self.peers]

    def copy(self, stage, ch, i):
        zc = (self.z + (i + 1)) % 4
        src, dst, to = (
            (lambda: self.grads[ch].at[1, zc], self.r0.at[ch, i], self.core),
            (lambda: self.own.at[ch, i, pl.ds(2, 2)], self.r1.at[ch, i], self.first[ch]),
            (lambda: self.own.at[ch, i, 1], self.r2.at[ch, i], self.second[ch]),
            (lambda: self.own.at[ch, i, 0], self.r3.at[ch, min(i, 2)], self.peers[min(i, 2)]),
        )[stage]
        return pltpu.make_async_remote_copy(
            src_ref=src(), dst_ref=dst,
            send_sem=self.sent.at[stage, ch, i], recv_sem=self.got.at[stage, ch, i],
            device_id=to, device_id_type=pl.DeviceIdType.MESH,
        )

    def load(self, ch, i):
        zc = (self.z + (i + 1)) % 4
        return pltpu.make_async_copy(
            self.grads[ch].at[0, zc], self.own.at[ch, i], self.local.at[ch, i]
        )

    def start(self):
        for i in range(4):
            for ch in range(2):
                self.copy(0, ch, i).start()
                self.load(ch, i).start()

    def step(self, stage, i):
        for ch in range(2):
            self.copy(stage - 1, ch, i).wait_recv()
            if stage == 1:
                self.load(ch, i).wait()

                def add(j, _, ch=ch):
                    self.own[ch, i, j] = self.own[ch, i, j] + self.r0[ch, i, j]
                    return 0

                lax.fori_loop(0, 4, add, 0)
            elif stage == 2:

                def add(j, _, ch=ch):
                    self.own[ch, i, j] = self.own[ch, i, j] + self.r1[ch, i, j]
                    return 0

                lax.fori_loop(0, 2, add, 0)
            elif i < 3:
                self.own[ch, i, 0] = self.own[ch, i, 0] + self.r2[ch, i]
            if stage < 3 or i < 3:
                self.copy(stage, ch, i).start()

    def finish(self):
        for ch in range(2):
            total = self.own[ch, 3, 0].astype(F32) + self.r2[ch, 3].astype(F32)
            for i in range(3):
                self.copy(3, ch, i).wait_recv()
                total = total + self.r3[ch, i].astype(F32)
            self.out[ch] = total
        for stage in range(STAGES):
            for ch in range(2):
                for i in range(4 if stage < 3 else 3):
                    self.copy(stage, ch, i).wait_send()

    def run(self, step, plan):
        for at, events in plan.items():

            @pl.when(step == at)
            def _(events=events):
                for stage, i in events:
                    if stage == 0:
                        self.start()
                    elif stage == 4:
                        self.finish()
                    else:
                        self.step(stage, i)


def sum_specs(grads, number):
    if grads is None:
        return [], [], [], [], {}
    rows, cols = grads[0].shape[3:]
    return (
        [pl.BlockSpec(memory_space=pl.ANY)] * 2,
        [full((2, rows, cols))],
        [jax.ShapeDtypeStruct((2, rows, cols), F32)],
        sum_scratch(rows, cols),
        {"has_side_effects": True, "collective_id": number},
    )


HP = 4


def head_masks(length, pair):
    lane = lax.broadcasted_iota(jnp.int32, (length, pair), 1)
    return lane < HEAD_DIM


def attn_fwd_kernel(q, k, v, mixed, lse):
    length = q.shape[0]
    pair = 2 * HEAD_DIM
    low_half = head_masks(length, pair)
    zero = jnp.zeros((length, pair), BF)
    for p in range(HP // 2):
        cols = slice(p * pair, (p + 1) * pair)
        qp, kp, vp = q[:, cols], k[:, cols], v[:, cols]
        vt = vp.T
        outs = []
        for h in range(2):
            km = jnp.where(low_half, kp, zero) if h == 0 else jnp.where(low_half, zero, kp)
            st = dot(km, qp, NT)
            top = jnp.max(st, axis=0, keepdims=True)
            raised = jnp.exp2((st - top) * LOG2E)
            total = jnp.sum(raised, axis=0, keepdims=True)
            lse[0, 0, 2 * p + h : 2 * p + h + 1, :] = top + jnp.log(total)
            ot = dot(vt[h * HEAD_DIM : (h + 1) * HEAD_DIM], raised.astype(BF), NN)
            outs.append(ot * (1.0 / total))
        mixed[:, cols] = jnp.concatenate(outs, axis=0).T.astype(BF)


def attn_fwd(q, k, v, pages):
    tokens, width = q.shape
    length = tokens // pages
    steps = HEADS // HP
    blk = pl.BlockSpec((length, HP * HEAD_DIM), lambda i, j: (i, j))
    return pl.pallas_call(
        attn_fwd_kernel,
        grid=(pages, steps),
        in_specs=[blk] * 3,
        out_specs=[blk, pl.BlockSpec((1, 1, HP, length), lambda i, j: (i, j, 0, 0))],
        out_shape=[
            jax.ShapeDtypeStruct((tokens, width), BF),
            jax.ShapeDtypeStruct((pages, steps, HP, length), F32),
        ],
        compiler_params=params(),
        cost_estimate=cost(14e9, 8 << 20, pages * HEADS * length * length),
        name="attention",
    )(q, k, v)


ATTN_PLAN = {
    0: [(0, 0)],
    1: [(1, 0)],
    2: [(1, 1)],
    3: [(2, 0), (1, 2)],
    5: [(2, 1), (1, 3)],
    6: [(3, 0)],
}
ATTN_TAIL = [(2, 2), (3, 1), (2, 3), (3, 2), (3, 3), (4, 0)]


def attn_bwd_kernel(*refs, summed):
    q, k, v, mixed, go, lse = refs[:6]
    refs = refs[6:]
    grads, refs = refs[: 2 * summed], refs[2 * summed :]
    gj, sums = refs[:2]
    refs = refs[2:]
    step = pl.program_id(0) * pl.num_programs(1) + pl.program_id(1)
    last = pl.num_programs(0) * pl.num_programs(1) - 1
    if summed:
        summing = Summing(grads, refs[0], refs[1:])

        @pl.when(step == 0)
        def _():
            meet(summing.devices())

        summing.run(step, ATTN_PLAN)
    length = q.shape[0]
    pair = 2 * HEAD_DIM
    low_half = head_masks(length, pair)
    zero = jnp.zeros((length, pair), BF)
    page = pl.program_id(1)

    def pick(x, h):
        return jnp.where(low_half, x, zero) if h == 0 else jnp.where(low_half, zero, x)

    for p in range(HP // 2):
        cols = slice(p * pair, (p + 1) * pair)
        qp, kp, vp, op, gp = q[:, cols], k[:, cols], v[:, cols], mixed[:, cols], go[:, cols]
        kt = kp.T
        prod_t = (op.astype(F32) * gp.astype(F32)).T
        dq_t, dk, dv = [], None, None
        for h in range(2):
            st = dot(pick(kp, h), qp, NT)
            probs = jnp.exp2((st - lse[0, 0, 2 * p + h : 2 * p + h + 1, :]) * LOG2E)
            dv_h = dot(probs.astype(BF), pick(gp, h), NN)
            dpt = dot(pick(vp, h), gp, NT)
            delta = colsum(prod_t[h * HEAD_DIM : (h + 1) * HEAD_DIM])
            ds = (probs * (dpt - delta)).astype(BF)
            dk_h = dot(ds, pick(qp, h), NN)
            dq_t.append(dot(kt[h * HEAD_DIM : (h + 1) * HEAD_DIM], ds, NN))
            dv = dv_h if dv is None else dv + dv_h
            dk = dk_h if dk is None else dk + dk_h
        dq = (jnp.concatenate(dq_t, axis=0).T.astype(BF).astype(F32) * SCALE).astype(BF)
        dv = dv.astype(BF)
        gj[0, :, cols] = dq
        gj[1, :, cols] = dk.astype(BF)
        gj[2, :, cols] = dv
        part = jnp.concatenate([colsum(dq.astype(F32)), colsum(dv.astype(F32))], axis=0)

        @pl.when(page == 0)
        def _():
            sums[:, cols] = part

        @pl.when(page != 0)
        def _():
            sums[:, cols] = sums[:, cols] + part

    if summed:
        summing.run(step, {last: ATTN_TAIL})


def attn_bwd(q, k, v, mixed, go, lse, pages, grads):
    tokens, width = q.shape
    more_in, more_out, more_shape, more_scratch, more = sum_specs(grads, 2)
    length = tokens // pages
    steps = HEADS // HP
    wide = HP * HEAD_DIM
    blk = pl.BlockSpec((length, wide), lambda j, i: (i, j))
    return pl.pallas_call(
        functools.partial(attn_bwd_kernel, summed=grads is not None),
        grid=(steps, pages),
        in_specs=[blk] * 5
        + [pl.BlockSpec((1, 1, HP, length), lambda j, i: (i, j, 0, 0))]
        + more_in,
        out_specs=[
            pl.BlockSpec((3, length, wide), lambda j, i: (0, i, j)),
            pl.BlockSpec((2, wide), lambda j, i: (0, j)),
        ]
        + more_out,
        out_shape=[
            jax.ShapeDtypeStruct((3, tokens, width), BF),
            jax.ShapeDtypeStruct((2, width), F32),
        ]
        + more_shape,
        scratch_shapes=more_scratch,
        compiler_params=params(**more),
        cost_estimate=cost(35e9, 16 << 20, pages * HEADS * length * length),
        name="attention_back",
    )(q, k, v, mixed, go, lse, *(grads or ()))


FC = 512
FWD = 1024
RC = 128
MC = 512


def ffn_fwd_kernel(
    mixed, normed, wo, we, wr, hb, bias, gains, shifts, cot,
    out, after_out, low_out, rstd_out, act_out, slope_out, gs2_out, gffn_out, sums,
):
    ff = we.shape[1]
    attn_sum = normed[...] + (dot(mixed[...], wo[...], NN) + bias[2:3])
    xh, rstd = norm_stats(attn_sum)
    after = xh * gains[1:2] + shifts[1:2]
    after_out[...] = after
    rstd_out[...] = rstd
    low = after.astype(BF)
    low_out[...] = low
    total = after + bias[3:4]
    for j in range(ff // FWD):
        cols = slice(j * FWD, (j + 1) * FWD)
        act, slope = gelu_parts(dot(low, we[:, cols], NN) + hb[:, cols])
        act = act.astype(BF)
        act_out[:, cols] = act
        slope_out[:, cols] = slope.astype(BF)
        total = total + dot(act, wr[cols, :], NN)
    xh, rstd = norm_stats(total)
    out[...] = (xh * gains[2:3] + shifts[2:3]).astype(BF)
    y = cot[...].astype(F32)
    gs2 = norm_back(y, xh, rstd, gains[2:3])
    gs2_out[...] = gs2
    gffn = gs2.astype(BF)
    gffn_out[...] = gffn
    part = jnp.concatenate([colsum(y * xh), colsum(y), colsum(gffn.astype(F32))], axis=0)

    @pl.when(pl.program_id(0) == 0)
    def _():
        sums[...] = part

    @pl.when(pl.program_id(0) != 0)
    def _():
        sums[...] = sums[...] + part


def ffn_fwd(mixed, normed, wo, we, wr, hb, bias, gains, shifts, cot, tile):
    tokens, width = mixed.shape
    ff = we.shape[1]
    rows = pl.BlockSpec((tile, width), lambda i: (i, 0))
    long = pl.BlockSpec((tile, ff), lambda i: (i, 0))
    shape = lambda dt, n=width: jax.ShapeDtypeStruct((tokens, n), dt)
    hb = hb.reshape(1, ff)
    return pl.pallas_call(
        ffn_fwd_kernel,
        grid=(tokens // tile,),
        in_specs=[rows, rows]
        + [full(a.shape) for a in (wo, we, wr, hb, bias, gains, shifts)]
        + [rows],
        out_specs=[rows, rows, rows, pl.BlockSpec((tile, 1), lambda i: (i, 0)), long, long, rows, rows]
        + [pl.BlockSpec((3, width), lambda i: (0, 0))],
        out_shape=[
            shape(BF), shape(F32), shape(BF), shape(F32, 1), shape(BF, ff), shape(BF, ff),
            shape(F32), shape(BF), jax.ShapeDtypeStruct((3, width), F32),
        ],
        compiler_params=params(),
        cost_estimate=cost(2 * tokens * width * (width + 2 * ff), 60 << 20, tokens * ff * 2),
        name="ffn_forward",
    )(mixed, normed, wo, we, wr, hb, bias, gains, shifts, cot)


FFN_PLAN = {
    0: [(0, 0)],
    1: [(1, 0)],
    2: [(1, 1)],
    3: [(2, 0), (1, 2)],
    4: [(2, 1), (1, 3)],
    5: [(3, 0)],
    7: [(2, 2), (3, 1)],
}
FFN_TAIL = [(2, 3), (3, 2), (3, 3), (4, 0)]


def ffn_bwd_kernel(*refs, summed):
    gffn, gs2, after, rstd, wo, gains, shifts, slope, wr, we = refs[:10]
    refs = refs[10:]
    grads, refs = refs[: 2 * summed], refs[2 * summed :]
    gh_out, gs1_out, gattn_out, gmixed_out, hsum, sums = refs[:6]
    refs = refs[6:]
    step, last = pl.program_id(0), pl.num_programs(0) - 1
    tokens, width = gffn.shape
    if summed:
        summing = Summing(grads, refs[0], refs[1:])

        @pl.when(step == 0)
        def _():
            meet(summing.devices())

        summing.run(step, FFN_PLAN)

    @pl.when(step == 0)
    def _():
        gs1_out[...] = gs2[...]

    part = jnp.zeros((1, slope.shape[1]), F32)
    for m in range(0, tokens, MC):
        rows = slice(m, m + MC)
        gh = (dot(gffn[rows, :], wr[...], NT) * slope[rows, :].astype(F32)).astype(BF)
        gh_out[rows, :] = gh
        part = part + colsum(gh.astype(F32))
        gs1_out[rows, :] = gs1_out[rows, :] + dot(gh, we[...], NT)
    hsum[...] = part

    @pl.when(step == last)
    def _():
        def norm(i, carry):
            rows = pl.ds(pl.multiple_of(i * RC, RC), RC)
            total = gs1_out[rows, :]
            xh = (after[rows, :] - shifts[1:2]) * (1.0 / gains[1:2])
            gs1 = norm_back(total, xh, rstd[rows, :], gains[1:2])
            gs1_out[rows, :] = gs1
            gattn = gs1.astype(BF)
            gattn_out[rows, :] = gattn
            g, s, b = carry
            return g + colsum(total * xh), s + colsum(total), b + colsum(gattn.astype(F32))

        zero = jnp.zeros((1, width), F32)
        sums[...] = jnp.concatenate(
            lax.fori_loop(0, tokens // RC, norm, (zero, zero, zero)), axis=0
        )
        for m in range(0, tokens, MC):
            rows = slice(m, m + MC)
            gmixed_out[rows, :] = dot(gattn_out[rows, :], wo[...], NT).astype(BF)

    if summed:
        summing.run(step, {last: FFN_TAIL})


def ffn_bwd(gffn, slope, gs2, after, rstd, wr, we, wo, gains, shifts, grads):
    tokens, width = gffn.shape
    ff = we.shape[1]
    whole = full((tokens, width))
    long = pl.BlockSpec((tokens, FC), lambda s: (0, s))
    shape = lambda dt, n=width: jax.ShapeDtypeStruct((tokens, n), dt)
    more_in, more_out, more_shape, more_scratch, more = sum_specs(grads, 1)
    return pl.pallas_call(
        functools.partial(ffn_bwd_kernel, summed=grads is not None),
        grid=(ff // FC,),
        in_specs=[whole, whole, whole, full((tokens, 1))]
        + [full(a.shape) for a in (wo, gains, shifts)]
        + [
            long,
            pl.BlockSpec((FC, width), lambda s: (s, 0)),
            pl.BlockSpec((width, FC), lambda s: (0, s)),
        ]
        + more_in,
        out_specs=[long, whole, whole, whole]
        + [pl.BlockSpec((1, FC), lambda s: (0, s)), full((3, width))]
        + more_out,
        out_shape=[
            shape(BF, ff), shape(F32), shape(BF), shape(BF),
            jax.ShapeDtypeStruct((1, ff), F32), jax.ShapeDtypeStruct((3, width), F32),
        ]
        + more_shape,
        scratch_shapes=more_scratch,
        compiler_params=params(**more),
        cost_estimate=cost(2 * tokens * width * (width + 2 * ff), 60 << 20),
        name="ffn_backward",
    )(gffn, gs2, after, rstd, wo, gains, shifts, slope, wr, we, *(grads or ()))


EMBED_PLAN = {0: [(0, 0)], 1: [(1, 0), (1, 1)]}
EMBED_TAIL = [
    (2, 0), (1, 2), (2, 1), (3, 0), (1, 3), (2, 2), (3, 1), (2, 3), (3, 2), (3, 3), (4, 0),
]


def embed_bwd_kernel(*refs, summed):
    gs1, gj, w, normed, rstd, ci, gains, shifts = refs[:8]
    refs = refs[8:]
    grads, refs = refs[: 2 * summed], refs[2 * summed :]
    out, cells, sums = refs[:3]
    refs = refs[3:]
    step, last = pl.program_id(0), pl.num_programs(0) - 1
    if summed:
        summing = Summing(grads, refs[0], refs[1:])

        @pl.when(step == 0)
        def _():
            meet(summing.devices())

        summing.run(step, EMBED_PLAN)
    width = gs1.shape[1]
    tokens = gs1.shape[0]
    total = gs1[...]
    for n in range(3):
        total = total + dot(gj[n], w[:, n * width : (n + 1) * width], NT)
    xh = (normed[...] - shifts[0:1]) * (1.0 / gains[0:1])
    grad = norm_back(total, xh, rstd[...], gains[0:1])
    out[...] = grad
    number = lax.broadcasted_iota(jnp.int32, (CELLS, tokens), 0)
    pick = (number == ci[0]).astype(F32).astype(BF)
    cells[...] = dot(pick, grad.astype(BF), NN).astype(BF)
    part = jnp.concatenate([colsum(total * xh), colsum(total)], axis=0)

    @pl.when(pl.program_id(0) == 0)
    def _():
        sums[...] = part

    @pl.when(pl.program_id(0) != 0)
    def _():
        sums[...] = sums[...] + part

    if summed:
        summing.run(step, {last: EMBED_TAIL})


def embed_bwd(gs1, gj, w, normed, rstd, ci, gains, shifts, grads):
    tokens, width = gs1.shape
    more_in, more_out, more_shape, more_scratch, more = sum_specs(grads, 3)
    pages, length = ci.shape
    rows = pl.BlockSpec((length, width), lambda i: (i, 0))
    return pl.pallas_call(
        functools.partial(embed_bwd_kernel, summed=grads is not None),
        grid=(pages,),
        in_specs=[
            rows,
            pl.BlockSpec((3, length, width), lambda i: (0, i, 0)),
            full(w.shape),
            rows,
            pl.BlockSpec((length, 1), lambda i: (i, 0)),
            pl.BlockSpec((1, 1, length), lambda i: (i, 0, 0)),
            full(gains.shape),
            full(shifts.shape),
        ]
        + more_in,
        out_specs=[
            rows,
            pl.BlockSpec((CELLS, width), lambda i: (i, 0)),
            pl.BlockSpec((2, width), lambda i: (0, 0)),
        ]
        + more_out,
        out_shape=[
            jax.ShapeDtypeStruct((tokens, width), F32),
            jax.ShapeDtypeStruct((pages * CELLS, width), BF),
            jax.ShapeDtypeStruct((2, width), F32),
        ]
        + more_shape,
        scratch_shapes=more_scratch,
        compiler_params=params(**more),
        cost_estimate=cost(2 * tokens * width * 3 * width, 26 << 20),
        name="embed_backward",
    )(
        gs1, gj, w, normed, rstd, ci.reshape(pages, 1, length), gains, shifts, *(grads or ())
    )


def table_kernel(tok, idx, g0, g1, g2, g3, out_a, out_b):
    rows = out_a.shape[1]
    count = idx.shape[2]
    half = out_a.shape[2]
    base = (pl.program_id(0) ^ tok[0]) * rows
    number = lax.broadcasted_iota(jnp.int32, (rows, count), 0) + base
    picks = []
    for s in range(4):
        first = (number == idx[s, 0:1, :]).astype(F32)
        second = (number == idx[s, 1:2, :]).astype(F32)
        picks.append((first + second).astype(BF))
    pick = jnp.concatenate(picks, axis=1)
    grads = jnp.concatenate([g0[...], g1[...], g2[...], g3[...]], axis=0)
    total = dot(pick, grads, NN).astype(BF)
    out_a[0] = total[:, :half]
    out_b[0] = total[:, half:]


def table_part(tok, idx, grads, blocks):
    groups, _, count = idx.shape
    width = grads[0].shape[1]
    rows = 1024 // blocks
    half = width // 2
    out = pl.BlockSpec((1, rows, half), lambda i, t: (i, 0, 0))
    return pl.pallas_call(
        table_kernel,
        grid_spec=pltpu.PrefetchScalarGridSpec(
            num_scalar_prefetch=1,
            grid=(blocks,),
            in_specs=[full(idx.shape)] + [full((count, width))] * groups,
            out_specs=[out, out],
        ),
        out_shape=[jax.ShapeDtypeStruct((blocks, rows, half), BF)] * 2,
        compiler_params=params(),
        cost_estimate=cost(2 * 1024 * groups * count * width, 4 << 20),
        name="table_grad",
    )(tok, idx, *grads)


def table_out_kernel(tok, a, b, out):
    half = a.shape[2]
    out[0, :, :half] = a[0].astype(F32)
    out[0, :, half:] = b[0].astype(F32)


def table_out(tok, a, b, table_rows):
    blocks, rows, half = a.shape
    src = pl.BlockSpec((1, rows, half), lambda i, t: (i ^ t[0], 0, 0))
    return pl.pallas_call(
        table_out_kernel,
        grid_spec=pltpu.PrefetchScalarGridSpec(
            num_scalar_prefetch=1,
            grid=(blocks,),
            in_specs=[src, src],
            out_specs=pl.BlockSpec((1, rows, 2 * half), lambda i, t: (0, i, 0)),
        ),
        out_shape=jax.ShapeDtypeStruct((1, table_rows, 2 * half), F32),
        compiler_params=params(),
        cost_estimate=cost(0, 6 << 20),
        name="table_write",
    )(tok, a, b)


def split_rel(r):
    return r & 1, (r >> 1) & 1, r >> 2


def reduce_kernel(tok, gffn, act, ga, gb):
    g = dot(gffn[...], act[...], TN)
    half = ga.shape[4]
    ga[0, :, 0] = g[:, :half].astype(BF).reshape(ga.shape[1], *ga.shape[3:])
    gb[0, :, 0] = g[:, half:].astype(BF).reshape(gb.shape[1], *gb.shape[3:])


def reduce_part(tok, gffn, act):
    tokens, d = gffn.shape
    f = act.shape[1] // 8
    rows, half = d // 4, f // 2

    def index(ch):
        def at(s, t):
            core, x, y = split_rel(7 - s)
            return (core, 0, 2 * y + x if ch else 2 * x + y, 0, 0)

        return at

    shape = jax.ShapeDtypeStruct((2, 4, 4, rows, half), BF)
    return pl.pallas_call(
        reduce_kernel,
        grid_spec=pltpu.PrefetchScalarGridSpec(
            num_scalar_prefetch=1,
            grid=(8,),
            in_specs=[
                full(gffn.shape),
                pl.BlockSpec((tokens, f), lambda s, t: (0, t[0] ^ (7 - s))),
            ],
            out_specs=[pl.BlockSpec((1, 4, 1, rows, half), index(ch)) for ch in range(2)],
        ),
        out_shape=[shape, shape],
        compiler_params=params(),
        cost_estimate=cost(16 * tokens * d * f, 20 << 20),
        name="reduce_grad",
    )(tok, gffn, act)


def rows_kernel(tok, *refs, groups):
    count = len(groups)
    lhs, refs = refs[:count], refs[count:]
    rhs = []
    for n in groups:
        rhs.append(refs[:n])
        refs = refs[n:]
    ga, gb = refs[:2]
    turned = refs[2:]
    rows = lhs[0].shape[1] // 8
    half = rows // 2

    @pl.when(pl.program_id(0) == 0)
    def _():
        for a, b in zip(lhs, turned):
            for r in range(8):
                start = pl.multiple_of((tok[0] ^ r) * rows, rows)
                b[:, r * rows : (r + 1) * rows] = a[:, pl.ds(start, rows)]

    at = 0
    for a, blocks in zip(turned, rhs):
        for block in blocks:
            block = block[...].reshape(block.shape[-2:])
            for n in range(0, block.shape[1], 512):
                piece = block[:, n : n + 512]
                g = dot(a[...], piece, TN).astype(BF)
                cols = slice(at, at + piece.shape[1])
                at += piece.shape[1]
                for r in range(8):
                    core, x, y = split_rel(r)
                    ga[core, 0, 2 * x + y, :, cols] = g[r * rows : r * rows + half]
                    gb[core, 0, 2 * y + x, :, cols] = g[r * rows + half : (r + 1) * rows]


def rows_part(tok, pairs, name):
    tokens, d = pairs[0][0].shape
    half = d // 16
    width = sum(spec.block_shape[-1] for _, _, specs in pairs for spec in specs)
    shape = jax.ShapeDtypeStruct((2, 4, 4, half, width), BF)
    out = pl.BlockSpec((2, 1, 4, half, width), lambda s, t: (0, s, 0, 0, 0))
    return pl.pallas_call(
        functools.partial(rows_kernel, groups=[len(p[1]) for p in pairs]),
        grid_spec=pltpu.PrefetchScalarGridSpec(
            num_scalar_prefetch=1,
            grid=(4,),
            in_specs=[full(p[0].shape) for p in pairs] + [s for p in pairs for s in p[2]],
            out_specs=[out, out],
            scratch_shapes=[pltpu.VMEM((tokens, d), BF) for _ in pairs],
        ),
        out_shape=[shape, shape],
        compiler_params=params(),
        cost_estimate=cost(8 * tokens * d * width, 24 << 20),
        name=name,
    )(tok, *[p[0] for p in pairs], *[r for p in pairs for r in p[1]])


def flip_tok(value, bit, size):
    return lax.ppermute(value, "tok", [(i, i ^ bit) for i in range(size)])


def shift_tab(value, shift, size):
    return lax.ppermute(value, "tab", [(i, (i + shift) % size) for i in range(size)])


def plus(a, b):
    return (a.astype(F32) + b.astype(F32)).astype(BF)


def table_sum(part, bits, n_tok):
    rows, cols = part.shape[1:]
    block = {i: part[i] for i in range(8)}
    order = list(bits)
    for bit in order:
        sent = [i for i in sorted(block) if i & bit]
        got = flip_tok(jnp.stack([block[i] for i in sent]), bit, n_tok)
        for n, i in enumerate(sent):
            block[i ^ bit] = plus(block[i ^ bit], got[n])
            del block[i]
    for bit in reversed(order):
        held = sorted(block)
        got = flip_tok(jnp.stack([block[i] for i in held]), bit, n_tok)
        for n, i in enumerate(held):
            block[i ^ bit] = got[n]
    return jnp.stack([block[i] for i in range(8)])


def small_sum(value, n_tok, n_tab):
    bit = 1
    while bit < n_tok:
        value = value + flip_tok(value, bit, n_tok)
        bit *= 2
    total = value
    for shift in range(1, n_tab):
        total = total + shift_tab(value, shift, n_tab)
    return total


def body(
    n_tok, n_tab,
    embedded, cell_index, cell_boxes, box_tables, joined_weight, output_weight,
    expand_weight, reduce_weight, hidden_bias, bias_rows, norm_gains, norm_shifts, cotangent,
):
    tokens, width = embedded.shape
    pages, length = cell_index.shape
    table_rows = box_tables.shape[1]
    ff = expand_weight.shape[1]
    tok = lax.axis_index("tok").astype(jnp.int32).reshape(1)
    z = lax.axis_index("tab")
    cubic = n_tok == 8

    corners = cell_boxes[:, :, :CELLS]
    lo = lambda n: jnp.minimum(corners[:, n], corners[:, n + 2]).reshape(-1)
    hi = lambda n: jnp.maximum(corners[:, n], corners[:, n + 2]).reshape(-1)
    left, right, top, bottom = lo(0), hi(0), lo(1), hi(1)
    none = jnp.full_like(left, -1)
    index_table = jnp.stack(
        [
            jnp.stack([left, right]),
            jnp.stack([top, bottom]),
            jnp.stack([right - left, none]),
            jnp.stack([bottom - top, none]),
        ]
    )
    pick_table = lambda i: lax.dynamic_index_in_dim(index_table, i, 0, keepdims=False)
    group_index = jnp.stack(
        [pick_table(z)]
        + [shift_tab(pick_table((z + s) % n_tab), s, n_tab) for s in range(1, n_tab)]
    )
    padded = jnp.pad(box_tables[0], ((0, 1024 - table_rows), (0, 0)))
    found = lookup(group_index, padded)
    terms = [found[0]] + [shift_tab(found[s], n_tab - s, n_tab) for s in range(1, n_tab)]

    q, k, v, normed, normed_low, rstd0 = embed(
        embedded, cell_index, terms, joined_weight, norm_gains, norm_shifts, bias_rows
    )
    mixed, lse = attn_fwd(q, k, v, pages)
    layer_out, after, after_low, rstd1, act, slope, gs2, gffn, sums2 = ffn_fwd(
        mixed, normed, output_weight, expand_weight, reduce_weight, hidden_bias,
        bias_rows, norm_gains, norm_shifts, cotangent, min(256, tokens),
    )
    quarter = width // 4
    parts = reduce_part(tok, gffn, act) if cubic else None
    gh, gs1, gattn, gmixed, hidden_sum, sums1, *reduce_sum = ffn_bwd(
        gffn, slope, gs2, after, rstd1, reduce_weight, expand_weight, output_weight,
        norm_gains, norm_shifts, parts,
    )
    if cubic:
        columns = lambda n: pl.BlockSpec((tokens, n), lambda s, t: (0, s))
        parts = rows_part(
            tok,
            [(after_low, [gh], [columns(ff // 4)]), (mixed, [gattn], [columns(quarter)])],
            "expand_output_grad",
        )
    gj, sums_qv, *expand_sum = attn_bwd(q, k, v, mixed, gmixed, lse, pages, parts)
    if cubic:
        third = lambda n: pl.BlockSpec(
            (1, tokens, quarter), lambda s, t: ((3 * s + n) // 4, 0, (3 * s + n) % 4)
        )
        parts = rows_part(
            tok, [(normed_low, [gj, gj, gj], [third(0), third(1), third(2)])], "joined_grad"
        )
    embedded_grad, cell_grad, sums0, *joined_sum = embed_bwd(
        gs1, gj, joined_weight, normed, rstd0, cell_index, norm_gains, norm_shifts, parts
    )

    cell_grads = [cell_grad] + [shift_tab(cell_grad, s, n_tab) for s in range(1, n_tab)]
    part_a, part_b = table_part(tok if cubic else jnp.zeros_like(tok), group_index, cell_grads, 8)
    if cubic:
        whole_a = table_sum(part_a, (1, 2, 4), n_tok)
        whole_b = table_sum(part_b, (1, 4, 2), n_tok)
        tables_grad = table_out(tok, whole_a, whole_b, table_rows)
    else:
        both = jnp.concatenate([part_a, part_b], axis=2).astype(F32)
        tables_grad = lax.psum(both.reshape(1, -1, width)[:, :table_rows], "tok")

    small = jnp.concatenate(
        [
            sums0.reshape(-1), sums1.reshape(-1), sums2.reshape(-1),
            sums_qv.reshape(-1), hidden_sum.reshape(-1),
        ]
    ).reshape(-1, 128)
    small = small_sum(small, n_tok, n_tab).reshape(-1)
    row = small.reshape(-1, width)
    gains_grad = jnp.stack([row[0], row[2], row[5]])
    shifts_grad = jnp.stack([row[1], row[3], row[6]])
    biases_grad = jnp.stack([row[8], row[9], row[4], row[7]])
    hidden_bias_grad = small[10 * width :]

    if cubic:
        reduce_grad = jnp.concatenate([reduce_sum[0][0], reduce_sum[0][1]], axis=1).T
        expand_sum = expand_sum[0].reshape(-1, expand_sum[0].shape[2])
        expand_grad = expand_sum[:, : ff // 4]
        output_grad = expand_sum[:, ff // 4 :]
        joined_grad = joined_sum[0].reshape(-1, joined_sum[0].shape[2])
    else:
        both = lambda a, b: jnp.einsum("ta,tb->ab", a, b, preferred_element_type=F32).astype(BF)

        def scattered(part):
            part = lax.psum_scatter(part, "tok", scatter_dimension=0, tiled=True)
            return lax.psum_scatter(part, "tab", scatter_dimension=1, tiled=True).astype(F32)

        reduce_grad = scattered(both(act, gffn))
        expand_grad = scattered(both(after_low, gh))
        output_grad = scattered(both(mixed, gattn))
        joined_grad = scattered(both(normed_low, jnp.concatenate([gj[0], gj[1], gj[2]], axis=1)))

    return (
        layer_out, embedded_grad, tables_grad, joined_grad, output_grad, expand_grad,
        reduce_grad, hidden_bias_grad, biases_grad, gains_grad, shifts_grad,
    )


def solution(mesh):
    rows = P(("tok", "tab"), None)
    return jax.shard_map(
        functools.partial(body, mesh.shape["tok"], mesh.shape["tab"]),
        mesh=mesh,
        in_specs=(
            rows, rows, P(("tok", "tab"), None, None), P("tab", None, None),
            P(), P(), P(), P(), P(), P(), P(), P(), rows,
        ),
        out_specs=(
            rows, rows, P("tab", None, None), P("tok", "tab"), P("tok", "tab"),
            P("tok", "tab"), P("tok", "tab"), P(), P(), P(), P(),
        ),
        check_vma=False,
    )
```

```python
import functools

import jax
import jax.numpy as jnp
from jax import lax
from jax.experimental import pallas as pl
from jax.experimental.pallas import tpu as pltpu
from jax.sharding import PartitionSpec as P

HEADS = 16
HEAD_DIM = 64
CELLS = 128
EPSILON = 1e-05
SCALE = HEAD_DIM ** (-0.5)
LOG2E = 1.4426950408889634
F32 = jnp.float32
BF = jnp.bfloat16
NN = ((1,), (0,))
NT = ((1,), (1,))
TN = ((0,), (0,))
ANY = pl.ANY

TAIL_P = 0.305
TAIL_C = (
    0.12164194255155772,
    0.12243138164026345,
    0.10365178645525906,
    0.12022714029486306,
    -0.03641303195181058,
    0.1839499605096701,
    -0.15192310059752684,
    0.03643391798251271,
)


def dot(a, b, dims):
    return lax.dot_general(a, b, (dims, ((), ())), preferred_element_type=F32)


def params(**kw):
    return pltpu.CompilerParams(vmem_limit_bytes=60 << 20, **kw)


def cost(flops, nbytes, trans=0):
    return pl.CostEstimate(
        flops=int(flops), bytes_accessed=int(nbytes), transcendentals=int(trans)
    )


def full(shape):
    zeros = (0,) * len(shape)
    return pl.BlockSpec(shape, lambda *_: zeros, pipeline_mode=pl.Buffered(1))


def gelu_parts(h):
    a = jnp.abs(h)
    t = 1.0 / (1.0 + TAIL_P * a)
    poly = jnp.full_like(t, TAIL_C[-1])
    for c in TAIL_C[-2::-1]:
        poly = poly * t + c
    e = jnp.exp2(h * h * (-0.5 * LOG2E))
    tail = poly * t * e
    phi_cdf = jnp.where(h > 0, 1.0 - tail, tail)
    act = h * phi_cdf
    slope = phi_cdf + h * e * 0.3989422804014327
    return act, slope


def norm_stats(v):
    mean = jnp.mean(v, axis=-1, keepdims=True)
    centred = v - mean
    var = jnp.mean(centred * centred, axis=-1, keepdims=True)
    rstd = lax.rsqrt(var + EPSILON)
    return centred * rstd, rstd


def norm_back(y, xh, rstd, gain):
    u = y * gain
    return (
        u - jnp.mean(u, axis=-1, keepdims=True) - xh * jnp.mean(u * xh, axis=-1, keepdims=True)
    ) * rstd


def colsum(v):
    return jnp.sum(v, axis=0, keepdims=True)


def lookup_kernel(idx, table, out):
    rows = table.shape[0]
    count = idx.shape[2]
    number = lax.broadcasted_iota(jnp.int32, (rows, count), 0)
    first = (number == idx[0, 0:1, :]).astype(F32)
    second = (number == idx[0, 1:2, :]).astype(F32)
    out[0] = dot((first + second).astype(BF), table[...], TN).astype(BF)


def lookup(idx, table):
    groups, _, count = idx.shape
    rows, width = table.shape
    return pl.pallas_call(
        lookup_kernel,
        grid=(groups,),
        in_specs=[
            pl.BlockSpec((1, 2, count), lambda i: (i, 0, 0)),
            full((rows, width)),
        ],
        out_specs=pl.BlockSpec((1, count, width), lambda i: (i, 0, 0)),
        out_shape=jax.ShapeDtypeStruct((groups, count, width), BF),
        compiler_params=params(),
        cost_estimate=cost(2 * groups * count * rows * width, 2 * groups * count * width),
        name="lookup",
    )(idx, table)


def embed_kernel(
    emb, ci, t0, t1, t2, t3, w, gains, shifts, bias, q, k, v, normed, low, rstd_out
):
    width = emb.shape[1]
    tokens = emb.shape[0]
    cells = jnp.concatenate([t0[...], t1[...], t2[...], t3[...]], axis=0)
    number = lax.broadcasted_iota(jnp.int32, (CELLS, tokens), 0)
    pick = (number == ci[0]).astype(F32).astype(BF)
    pick = jnp.concatenate([pick] * 4, axis=0)
    box = dot(pick, cells, TN)
    xh, rstd = norm_stats(emb[...].astype(F32) + box)
    y = xh * gains[0:1] + shifts[0:1]
    normed[...] = y
    rstd_out[...] = rstd
    y_low = y.astype(BF)
    low[...] = y_low
    q[...] = ((dot(y_low, w[:, :width], NN) + bias[0:1]) * SCALE).astype(BF)
    k[...] = dot(y_low, w[:, width : 2 * width], NN).astype(BF)
    v[...] = (dot(y_low, w[:, 2 * width :], NN) + bias[1:2]).astype(BF)


def embed(emb, ci, terms, w, gains, shifts, bias):
    tokens, width = emb.shape
    pages, length = ci.shape
    rows = pl.BlockSpec((length, width), lambda i: (i, 0))
    cell_rows = pl.BlockSpec((CELLS, width), lambda i: (i, 0))
    shape = lambda dt, n=width: jax.ShapeDtypeStruct((tokens, n), dt)
    return pl.pallas_call(
        embed_kernel,
        grid=(pages,),
        in_specs=[rows, pl.BlockSpec((1, 1, length), lambda i: (i, 0, 0))]
        + [cell_rows] * 4
        + [full(w.shape), full(gains.shape), full(shifts.shape), full(bias.shape)],
        out_specs=[rows] * 5 + [pl.BlockSpec((length, 1), lambda i: (i, 0))],
        out_shape=[shape(BF), shape(BF), shape(BF), shape(F32), shape(BF), shape(F32, 1)],
        compiler_params=params(),
        cost_estimate=cost(2 * tokens * width * 3 * width, 26 << 20),
        name="embed_joined",
    )(emb, ci.reshape(pages, 1, length), *terms, w, gains, shifts, bias)


STAGES = 4


def neighbours():
    tok, z = lax.axis_index("tok"), lax.axis_index("tab")
    core = {"tok": tok + 1 - 2 * (tok % 2)}
    x = {"tok": tok + 2 - 4 * ((tok // 2) % 2)}
    y = {"tok": tok + 4 - 8 * (tok // 4)}
    peers = [{"tab": (z + s) % 4} for s in range(1, 4)]
    return core, x, y, peers


def meet(devices):
    barrier = pltpu.get_barrier_semaphore()
    for d in devices:
        pl.semaphore_signal(barrier, inc=1, device_id=d, device_id_type=pl.DeviceIdType.MESH)
    pl.semaphore_wait(barrier, len(devices))


def sum_scratch(rows, cols):
    part = lambda *n: pltpu.VMEM((*n, rows, cols), BF)
    return [
        part(2, 4, 4), part(2, 4, 4), part(2, 4, 2), part(2, 4), part(2, 3),
        pltpu.SemaphoreType.DMA((2, 4)),
        pltpu.SemaphoreType.DMA((STAGES, 2, 4)),
        pltpu.SemaphoreType.DMA((STAGES, 2, 4)),
    ]


class Summing:
    def __init__(self, grads, out, scratch):
        self.grads, self.out = grads, out
        self.own, self.r0, self.r1, self.r2, self.r3, self.local, self.sent, self.got = scratch
        core, x, y, peers = neighbours()
        self.core, self.first, self.second, self.peers = core, (x, y), (y, x), peers
        self.z = lax.axis_index("tab")

    def devices(self):
        return [self.core, self.first[0], self.first[1], *self.peers]

    def copy(self, stage, ch, i):
        zc = (self.z + (i + 1)) % 4
        src, dst, to = (
            (lambda: self.grads[ch].at[1, zc], self.r0.at[ch, i], self.core),
            (lambda: self.own.at[ch, i, pl.ds(2, 2)], self.r1.at[ch, i], self.first[ch]),
            (lambda: self.own.at[ch, i, 1], self.r2.at[ch, i], self.second[ch]),
            (lambda: self.own.at[ch, i, 0], self.r3.at[ch, min(i, 2)], self.peers[min(i, 2)]),
        )[stage]
        return pltpu.make_async_remote_copy(
            src_ref=src(), dst_ref=dst,
            send_sem=self.sent.at[stage, ch, i], recv_sem=self.got.at[stage, ch, i],
            device_id=to, device_id_type=pl.DeviceIdType.MESH,
        )

    def load(self, ch, i):
        zc = (self.z + (i + 1)) % 4
        return pltpu.make_async_copy(
            self.grads[ch].at[0, zc], self.own.at[ch, i], self.local.at[ch, i]
        )

    def start(self):
        for i in range(4):
            for ch in range(2):
                self.copy(0, ch, i).start()
                self.load(ch, i).start()

    def step(self, stage, i):
        for ch in range(2):
            self.copy(stage - 1, ch, i).wait_recv()
            if stage == 1:
                self.load(ch, i).wait()

                def add(j, _, ch=ch):
                    self.own[ch, i, j] = self.own[ch, i, j] + self.r0[ch, i, j]
                    return 0

                lax.fori_loop(0, 4, add, 0)
            elif stage == 2:

                def add(j, _, ch=ch):
                    self.own[ch, i, j] = self.own[ch, i, j] + self.r1[ch, i, j]
                    return 0

                lax.fori_loop(0, 2, add, 0)
            elif i < 3:
                self.own[ch, i, 0] = self.own[ch, i, 0] + self.r2[ch, i]
            if stage < 3 or i < 3:
                self.copy(stage, ch, i).start()

    def finish(self):
        for ch in range(2):
            total = self.own[ch, 3, 0].astype(F32) + self.r2[ch, 3].astype(F32)
            for i in range(3):
                self.copy(3, ch, i).wait_recv()
                total = total + self.r3[ch, i].astype(F32)
            self.out[ch] = total
        for stage in range(STAGES):
            for ch in range(2):
                for i in range(4 if stage < 3 else 3):
                    self.copy(stage, ch, i).wait_send()

    def run(self, step, plan):
        for at, events in plan.items():

            @pl.when(step == at)
            def _(events=events):
                for stage, i in events:
                    if stage == 0:
                        self.start()
                    elif stage == 4:
                        self.finish()
                    else:
                        self.step(stage, i)


def sum_specs(grads, number):
    if grads is None:
        return [], [], [], [], {}
    rows, cols = grads[0].shape[3:]
    return (
        [pl.BlockSpec(memory_space=pl.ANY)] * 2,
        [full((2, rows, cols))],
        [jax.ShapeDtypeStruct((2, rows, cols), F32)],
        sum_scratch(rows, cols),
        {"has_side_effects": True, "collective_id": number},
    )


HP = 4


def head_masks(length, pair):
    lane = lax.broadcasted_iota(jnp.int32, (length, pair), 1)
    return lane < HEAD_DIM


def attn_fwd_kernel(q, k, v, mixed, lse):
    length = q.shape[0]
    pair = 2 * HEAD_DIM
    low_half = head_masks(length, pair)
    zero = jnp.zeros((length, pair), BF)
    for p in range(HP // 2):
        cols = slice(p * pair, (p + 1) * pair)
        qp, kp, vp = q[:, cols], k[:, cols], v[:, cols]
        vt = vp.T
        outs = []
        for h in range(2):
            km = jnp.where(low_half, kp, zero) if h == 0 else jnp.where(low_half, zero, kp)
            st = dot(km, qp, NT)
            top = jnp.max(st, axis=0, keepdims=True)
            raised = jnp.exp2((st - top) * LOG2E)
            total = jnp.sum(raised, axis=0, keepdims=True)
            lse[0, 0, 2 * p + h : 2 * p + h + 1, :] = top + jnp.log(total)
            ot = dot(vt[h * HEAD_DIM : (h + 1) * HEAD_DIM], raised.astype(BF), NN)
            outs.append(ot * (1.0 / total))
        mixed[:, cols] = jnp.concatenate(outs, axis=0).T.astype(BF)


def attn_fwd(q, k, v, pages):
    tokens, width = q.shape
    length = tokens // pages
    steps = HEADS // HP
    blk = pl.BlockSpec((length, HP * HEAD_DIM), lambda i, j: (i, j))
    return pl.pallas_call(
        attn_fwd_kernel,
        grid=(pages, steps),
        in_specs=[blk] * 3,
        out_specs=[blk, pl.BlockSpec((1, 1, HP, length), lambda i, j: (i, j, 0, 0))],
        out_shape=[
            jax.ShapeDtypeStruct((tokens, width), BF),
            jax.ShapeDtypeStruct((pages, steps, HP, length), F32),
        ],
        compiler_params=params(),
        cost_estimate=cost(14e9, 8 << 20, pages * HEADS * length * length),
        name="attention",
    )(q, k, v)


ATTN_PLAN = {
    0: [(0, 0)],
    1: [(1, 0)],
    2: [(1, 1)],
    3: [(2, 0), (1, 2)],
    5: [(2, 1), (1, 3)],
    6: [(3, 0)],
}
ATTN_TAIL = [(2, 2), (3, 1), (2, 3), (3, 2), (3, 3), (4, 0)]


def attn_bwd_kernel(*refs, summed):
    q, k, v, mixed, go, lse = refs[:6]
    refs = refs[6:]
    grads, refs = refs[: 2 * summed], refs[2 * summed :]
    gj, sums = refs[:2]
    refs = refs[2:]
    step = pl.program_id(0) * pl.num_programs(1) + pl.program_id(1)
    last = pl.num_programs(0) * pl.num_programs(1) - 1
    if summed:
        summing = Summing(grads, refs[0], refs[1:])

        @pl.when(step == 0)
        def _():
            meet(summing.devices())

        summing.run(step, ATTN_PLAN)
    length = q.shape[0]
    pair = 2 * HEAD_DIM
    low_half = head_masks(length, pair)
    zero = jnp.zeros((length, pair), BF)
    page = pl.program_id(1)

    def pick(x, h):
        return jnp.where(low_half, x, zero) if h == 0 else jnp.where(low_half, zero, x)

    for p in range(HP // 2):
        cols = slice(p * pair, (p + 1) * pair)
        qp, kp, vp, op, gp = q[:, cols], k[:, cols], v[:, cols], mixed[:, cols], go[:, cols]
        kt = kp.T
        prod_t = (op.astype(F32) * gp.astype(F32)).T
        dq_t, dk, dv = [], None, None
        for h in range(2):
            st = dot(pick(kp, h), qp, NT)
            probs = jnp.exp2((st - lse[0, 0, 2 * p + h : 2 * p + h + 1, :]) * LOG2E)
            dv_h = dot(probs.astype(BF), pick(gp, h), NN)
            dpt = dot(pick(vp, h), gp, NT)
            delta = colsum(prod_t[h * HEAD_DIM : (h + 1) * HEAD_DIM])
            ds = (probs * (dpt - delta)).astype(BF)
            dk_h = dot(ds, pick(qp, h), NN)
            dq_t.append(dot(kt[h * HEAD_DIM : (h + 1) * HEAD_DIM], ds, NN))
            dv = dv_h if dv is None else dv + dv_h
            dk = dk_h if dk is None else dk + dk_h
        dq = (jnp.concatenate(dq_t, axis=0).T.astype(BF).astype(F32) * SCALE).astype(BF)
        dv = dv.astype(BF)
        gj[0, :, cols] = dq
        gj[1, :, cols] = dk.astype(BF)
        gj[2, :, cols] = dv
        part = jnp.concatenate([colsum(dq.astype(F32)), colsum(dv.astype(F32))], axis=0)

        @pl.when(page == 0)
        def _():
            sums[:, cols] = part

        @pl.when(page != 0)
        def _():
            sums[:, cols] = sums[:, cols] + part

    if summed:
        summing.run(step, {last: ATTN_TAIL})


def attn_bwd(q, k, v, mixed, go, lse, pages, grads):
    tokens, width = q.shape
    more_in, more_out, more_shape, more_scratch, more = sum_specs(grads, 2)
    length = tokens // pages
    steps = HEADS // HP
    wide = HP * HEAD_DIM
    blk = pl.BlockSpec((length, wide), lambda j, i: (i, j))
    return pl.pallas_call(
        functools.partial(attn_bwd_kernel, summed=grads is not None),
        grid=(steps, pages),
        in_specs=[blk] * 5
        + [pl.BlockSpec((1, 1, HP, length), lambda j, i: (i, j, 0, 0))]
        + more_in,
        out_specs=[
            pl.BlockSpec((3, length, wide), lambda j, i: (0, i, j)),
            pl.BlockSpec((2, wide), lambda j, i: (0, j)),
        ]
        + more_out,
        out_shape=[
            jax.ShapeDtypeStruct((3, tokens, width), BF),
            jax.ShapeDtypeStruct((2, width), F32),
        ]
        + more_shape,
        scratch_shapes=more_scratch,
        compiler_params=params(**more),
        cost_estimate=cost(35e9, 16 << 20, pages * HEADS * length * length),
        name="attention_back",
    )(q, k, v, mixed, go, lse, *(grads or ()))


FC = 512
FWD = 1024
RC = 128
MC = 512


def ffn_fwd_kernel(
    mixed, normed, wo, we, wr, hb, bias, gains, shifts, cot,
    out, after_out, low_out, rstd_out, act_out, slope_out, gs2_out, gffn_out, sums,
):
    ff = we.shape[1]
    attn_sum = normed[...] + (dot(mixed[...], wo[...], NN) + bias[2:3])
    xh, rstd = norm_stats(attn_sum)
    after = xh * gains[1:2] + shifts[1:2]
    after_out[...] = after
    rstd_out[...] = rstd
    low = after.astype(BF)
    low_out[...] = low
    total = after + bias[3:4]
    for j in range(ff // FWD):
        cols = slice(j * FWD, (j + 1) * FWD)
        act, slope = gelu_parts(dot(low, we[:, cols], NN) + hb[:, cols])
        act = act.astype(BF)
        act_out[:, cols] = act
        slope_out[:, cols] = slope.astype(BF)
        total = total + dot(act, wr[cols, :], NN)
    xh, rstd = norm_stats(total)
    out[...] = (xh * gains[2:3] + shifts[2:3]).astype(BF)
    y = cot[...].astype(F32)
    gs2 = norm_back(y, xh, rstd, gains[2:3])
    gs2_out[...] = gs2
    gffn = gs2.astype(BF)
    gffn_out[...] = gffn
    part = jnp.concatenate([colsum(y * xh), colsum(y), colsum(gffn.astype(F32))], axis=0)

    @pl.when(pl.program_id(0) == 0)
    def _():
        sums[...] = part

    @pl.when(pl.program_id(0) != 0)
    def _():
        sums[...] = sums[...] + part


def ffn_fwd(mixed, normed, wo, we, wr, hb, bias, gains, shifts, cot, tile):
    tokens, width = mixed.shape
    ff = we.shape[1]
    rows = pl.BlockSpec((tile, width), lambda i: (i, 0))
    long = pl.BlockSpec((tile, ff), lambda i: (i, 0))
    shape = lambda dt, n=width: jax.ShapeDtypeStruct((tokens, n), dt)
    hb = hb.reshape(1, ff)
    return pl.pallas_call(
        ffn_fwd_kernel,
        grid=(tokens // tile,),
        in_specs=[rows, rows]
        + [full(a.shape) for a in (wo, we, wr, hb, bias, gains, shifts)]
        + [rows],
        out_specs=[rows, rows, rows, pl.BlockSpec((tile, 1), lambda i: (i, 0)), long, long, rows, rows]
        + [pl.BlockSpec((3, width), lambda i: (0, 0))],
        out_shape=[
            shape(BF), shape(F32), shape(BF), shape(F32, 1), shape(BF, ff), shape(BF, ff),
            shape(F32), shape(BF), jax.ShapeDtypeStruct((3, width), F32),
        ],
        compiler_params=params(),
        cost_estimate=cost(2 * tokens * width * (width + 2 * ff), 60 << 20, tokens * ff * 2),
        name="ffn_forward",
    )(mixed, normed, wo, we, wr, hb, bias, gains, shifts, cot)


FFN_PLAN = {
    0: [(0, 0)],
    1: [(1, 0)],
    2: [(1, 1)],
    3: [(2, 0), (1, 2)],
    4: [(2, 1), (1, 3)],
    5: [(3, 0)],
    7: [(2, 2), (3, 1)],
}
FFN_TAIL = [(2, 3), (3, 2), (3, 3), (4, 0)]


def ffn_bwd_kernel(*refs, summed):
    gffn, gs2, after, rstd, wo, gains, shifts, slope, wr, we = refs[:10]
    refs = refs[10:]
    grads, refs = refs[: 2 * summed], refs[2 * summed :]
    gh_out, gs1_out, gattn_out, gmixed_out, hsum, sums = refs[:6]
    refs = refs[6:]
    step, last = pl.program_id(0), pl.num_programs(0) - 1
    tokens, width = gffn.shape
    if summed:
        summing = Summing(grads, refs[0], refs[1:])

        @pl.when(step == 0)
        def _():
            meet(summing.devices())

        summing.run(step, FFN_PLAN)

    @pl.when(step == 0)
    def _():
        gs1_out[...] = gs2[...]

    part = jnp.zeros((1, slope.shape[1]), F32)
    for m in range(0, tokens, MC):
        rows = slice(m, m + MC)
        gh = (dot(gffn[rows, :], wr[...], NT) * slope[rows, :].astype(F32)).astype(BF)
        gh_out[rows, :] = gh
        part = part + colsum(gh.astype(F32))
        gs1_out[rows, :] = gs1_out[rows, :] + dot(gh, we[...], NT)
    hsum[...] = part

    @pl.when(step == last)
    def _():
        def norm(i, carry):
            rows = pl.ds(pl.multiple_of(i * RC, RC), RC)
            total = gs1_out[rows, :]
            xh = (after[rows, :] - shifts[1:2]) * (1.0 / gains[1:2])
            gs1 = norm_back(total, xh, rstd[rows, :], gains[1:2])
            gs1_out[rows, :] = gs1
            gattn = gs1.astype(BF)
            gattn_out[rows, :] = gattn
            g, s, b = carry
            return g + colsum(total * xh), s + colsum(total), b + colsum(gattn.astype(F32))

        zero = jnp.zeros((1, width), F32)
        sums[...] = jnp.concatenate(
            lax.fori_loop(0, tokens // RC, norm, (zero, zero, zero)), axis=0
        )
        for m in range(0, tokens, MC):
            rows = slice(m, m + MC)
            gmixed_out[rows, :] = dot(gattn_out[rows, :], wo[...], NT).astype(BF)

    if summed:
        summing.run(step, {last: FFN_TAIL})


def ffn_bwd(gffn, slope, gs2, after, rstd, wr, we, wo, gains, shifts, grads):
    tokens, width = gffn.shape
    ff = we.shape[1]
    whole = full((tokens, width))
    long = pl.BlockSpec((tokens, FC), lambda s: (0, s))
    shape = lambda dt, n=width: jax.ShapeDtypeStruct((tokens, n), dt)
    more_in, more_out, more_shape, more_scratch, more = sum_specs(grads, 1)
    return pl.pallas_call(
        functools.partial(ffn_bwd_kernel, summed=grads is not None),
        grid=(ff // FC,),
        in_specs=[whole, whole, whole, full((tokens, 1))]
        + [full(a.shape) for a in (wo, gains, shifts)]
        + [
            long,
            pl.BlockSpec((FC, width), lambda s: (s, 0)),
            pl.BlockSpec((width, FC), lambda s: (0, s)),
        ]
        + more_in,
        out_specs=[long, whole, whole, whole]
        + [pl.BlockSpec((1, FC), lambda s: (0, s)), full((3, width))]
        + more_out,
        out_shape=[
            shape(BF, ff), shape(F32), shape(BF), shape(BF),
            jax.ShapeDtypeStruct((1, ff), F32), jax.ShapeDtypeStruct((3, width), F32),
        ]
        + more_shape,
        scratch_shapes=more_scratch,
        compiler_params=params(**more),
        cost_estimate=cost(2 * tokens * width * (width + 2 * ff), 60 << 20),
        name="ffn_backward",
    )(gffn, gs2, after, rstd, wo, gains, shifts, slope, wr, we, *(grads or ()))


def embed_bwd_kernel(gs1, gj, w, normed, rstd, ci, gains, shifts, out, cells, sums):
    width = gs1.shape[1]
    tokens = gs1.shape[0]
    total = gs1[...]
    for n in range(3):
        total = total + dot(gj[n], w[:, n * width : (n + 1) * width], NT)
    xh = (normed[...] - shifts[0:1]) * (1.0 / gains[0:1])
    grad = norm_back(total, xh, rstd[...], gains[0:1])
    out[...] = grad
    number = lax.broadcasted_iota(jnp.int32, (CELLS, tokens), 0)
    pick = (number == ci[0]).astype(F32).astype(BF)
    cells[...] = dot(pick, grad.astype(BF), NN).astype(BF)
    part = jnp.concatenate([colsum(total * xh), colsum(total)], axis=0)

    @pl.when(pl.program_id(0) == 0)
    def _():
        sums[...] = part

    @pl.when(pl.program_id(0) != 0)
    def _():
        sums[...] = sums[...] + part


def embed_bwd(gs1, gj, w, normed, rstd, ci, gains, shifts):
    tokens, width = gs1.shape
    pages, length = ci.shape
    rows = pl.BlockSpec((length, width), lambda i: (i, 0))
    return pl.pallas_call(
        embed_bwd_kernel,
        grid=(pages,),
        in_specs=[
            rows,
            pl.BlockSpec((3, length, width), lambda i: (0, i, 0)),
            full(w.shape),
            rows,
            pl.BlockSpec((length, 1), lambda i: (i, 0)),
            pl.BlockSpec((1, 1, length), lambda i: (i, 0, 0)),
            full(gains.shape),
            full(shifts.shape),
        ],
        out_specs=[
            rows,
            pl.BlockSpec((CELLS, width), lambda i: (i, 0)),
            pl.BlockSpec((2, width), lambda i: (0, 0)),
        ],
        out_shape=[
            jax.ShapeDtypeStruct((tokens, width), F32),
            jax.ShapeDtypeStruct((pages * CELLS, width), BF),
            jax.ShapeDtypeStruct((2, width), F32),
        ],
        compiler_params=params(),
        cost_estimate=cost(2 * tokens * width * 3 * width, 26 << 20),
        name="embed_backward",
    )(gs1, gj, w, normed, rstd, ci.reshape(pages, 1, length), gains, shifts)


def table_kernel(tok, idx, g0, g1, g2, g3, out_a, out_b):
    rows = out_a.shape[1]
    count = idx.shape[2]
    half = out_a.shape[2]
    base = (pl.program_id(0) ^ tok[0]) * rows
    number = lax.broadcasted_iota(jnp.int32, (rows, count), 0) + base
    picks = []
    for s in range(4):
        first = (number == idx[s, 0:1, :]).astype(F32)
        second = (number == idx[s, 1:2, :]).astype(F32)
        picks.append((first + second).astype(BF))
    pick = jnp.concatenate(picks, axis=1)
    grads = jnp.concatenate([g0[...], g1[...], g2[...], g3[...]], axis=0)
    total = dot(pick, grads, NN).astype(BF)
    out_a[0] = total[:, :half]
    out_b[0] = total[:, half:]


def table_part(tok, idx, grads, blocks):
    groups, _, count = idx.shape
    width = grads[0].shape[1]
    rows = 1024 // blocks
    half = width // 2
    out = pl.BlockSpec((1, rows, half), lambda i, t: (i, 0, 0))
    return pl.pallas_call(
        table_kernel,
        grid_spec=pltpu.PrefetchScalarGridSpec(
            num_scalar_prefetch=1,
            grid=(blocks,),
            in_specs=[full(idx.shape)] + [full((count, width))] * groups,
            out_specs=[out, out],
        ),
        out_shape=[jax.ShapeDtypeStruct((blocks, rows, half), BF)] * 2,
        compiler_params=params(),
        cost_estimate=cost(2 * 1024 * groups * count * width, 4 << 20),
        name="table_grad",
    )(tok, idx, *grads)


BLOCK = 128


class TableSum:
    def __init__(self, scratch, done):
        self.part, self.r0, self.r1, self.r2, self.sent, self.got = scratch
        self.done = done
        tok = lax.axis_index("tok")
        core, x, y, _ = neighbours()
        self.c, cx, cy = tok % 2, (tok // 2) % 2, tok // 4
        self.core, self.first, self.second = core, (x, y), (y, x)
        self.f, self.g = (cx, cy), (cy, cx)

    def copy(self, stage, ch, u):
        c, f, g = self.c, self.f[ch], self.g[ch]
        part, done = self.part.at[ch, u], self.done.at[ch, u]
        src, dst, to = (
            (lambda: part.at[1 - c], self.r0.at[ch, u], self.core),
            (lambda: part.at[c, 1 - f], self.r1.at[ch, u], self.first[ch]),
            (lambda: part.at[c, f, 1 - g], self.r2.at[ch, u], self.second[ch]),
            (lambda: done.at[c, f, g], None, self.second[ch]),
            (lambda: done.at[c, f], None, self.first[ch]),
            (lambda: done.at[c], None, self.core),
        )[stage]
        src = src()
        return pltpu.make_async_remote_copy(
            src_ref=src, dst_ref=src if dst is None else dst,
            send_sem=self.sent.at[stage, ch, u], recv_sem=self.got.at[stage, ch, u],
            device_id=to, device_id_type=pl.DeviceIdType.MESH,
        )

    def store(self, u, ch, value):
        for b in range(8):
            c, x, y = split_rel(b)
            f, g = (x, y) if ch == 0 else (y, x)
            self.part[ch, u, c, f, g] = value[b * BLOCK : (b + 1) * BLOCK]
        self.copy(0, ch, u).start()

    def step(self, stage, u):
        for ch in range(2):
            c, f, g = self.c, self.f[ch], self.g[ch]
            self.copy(stage - 1, ch, u).wait_recv()
            if stage == 1:
                self.part[ch, u, c] = self.part[ch, u, c] + self.r0[ch, u]
            elif stage == 2:
                self.part[ch, u, c, f] = self.part[ch, u, c, f] + self.r1[ch, u]
            elif stage == 3:
                self.done[ch, u, c, f, g] = self.part[ch, u, c, f, g] + self.r2[ch, u]
            if stage < 6:
                self.copy(stage, ch, u).start()

    def finish(self):
        for stage in range(6):
            for ch in range(2):
                for u in range(2):
                    self.copy(stage, ch, u).wait_send()


def closing_kernel(
    cells, idx, small, ga, gb, done, joined, small_out,
    ring, total, ring_sent, ring_got, held, arrived, small_sent, small_got, *scratch,
):
    summing = Summing((ga, gb), joined, scratch[:8])
    table = TableSum(scratch[8:], done)
    core, x, y, peers = neighbours()
    z = lax.axis_index("tab")
    hops = [core, x, y, {"tab": z + 1 - 2 * (z % 2)}, {"tab": z + 2 - 4 * (z // 2)}]
    meet([core, x, y, *peers])
    count = cells.shape[0]
    half = count // 2

    def pass_on(k, h):
        rows = pl.ds(h * half, half)
        src = cells.at[rows] if k == 0 else ring.at[k - 1, rows]
        return pltpu.make_async_remote_copy(
            src_ref=src, dst_ref=ring.at[k, rows],
            send_sem=ring_sent.at[k, h], recv_sem=ring_got.at[k, h],
            device_id=peers[0], device_id_type=pl.DeviceIdType.MESH,
        )

    def small_copy(n):
        return pltpu.make_async_remote_copy(
            src_ref=held.at[n], dst_ref=arrived.at[n],
            send_sem=small_sent.at[n], recv_sem=small_got.at[n],
            device_id=hops[n], device_id_type=pl.DeviceIdType.MESH,
        )

    def small_step(n):
        small_copy(n - 1).wait_recv()
        value = held[n - 1] + arrived[n - 1]
        if n < 5:
            held[n] = value
            small_copy(n).start()
        else:
            small_out[...] = value

    def relay(k, h):
        pass_on(k - 1, h).wait_recv()
        pass_on(k, h).start()

    def pick(s):
        number = lax.broadcasted_iota(jnp.int32, (total.shape[0], count), 0)
        first = (number == idx[s, 0:1, :]).astype(F32)
        second = (number == idx[s, 1:2, :]).astype(F32)
        return (first + second).astype(BF)

    pass_on(0, 0).start()
    pass_on(0, 1).start()
    held[0] = small[...]
    small_copy(0).start()
    summing.start()
    total[...] = dot(pick(0), cells[...], NN)
    small_step(1)
    summing.step(1, 0)
    small_step(2)
    summing.step(1, 1)
    small_step(3)
    relay(1, 0)
    summing.step(2, 0)
    summing.step(1, 2)
    relay(1, 1)
    total[...] = total[...] + dot(pick(1), ring[0], NN)
    summing.step(2, 1)
    summing.step(1, 3)
    relay(2, 0)
    small_step(4)
    summing.step(2, 2)
    relay(2, 1)
    summing.step(3, 0)
    summing.step(3, 1)
    total[...] = total[...] + dot(pick(2), ring[1], NN)
    summing.step(2, 3)
    summing.step(3, 2)
    small_step(5)
    last = pick(3)
    pass_on(2, 0).wait_recv()
    pass_on(2, 1).wait_recv()
    wide = total.shape[1] // 4
    for u in range(2):
        for ch in range(2):
            cols = slice((2 * ch + u) * wide, (2 * ch + u + 1) * wide)
            value = total[:, cols] + dot(last, ring[2, :, cols], NN)
            table.store(u, ch, value.astype(BF))
    summing.step(3, 3)
    table.step(1, 0)
    table.step(1, 1)
    table.step(2, 0)
    table.step(2, 1)
    table.step(3, 0)
    table.step(3, 1)
    table.step(4, 0)
    table.step(4, 1)
    summing.finish()
    table.step(5, 0)
    table.step(5, 1)
    table.step(6, 0)
    table.step(6, 1)
    table.finish()
    for k in range(3):
        for h in range(2):
            pass_on(k, h).wait_send()
    for n in range(5):
        small_copy(n).wait_send()


def closing(cells, idx, small, grads):
    count, width = cells.shape
    rows, cols = grads[0].shape[3:]
    wide = width // 4
    part = lambda *n: pltpu.VMEM((2, 2, *n, BLOCK, wide), BF)
    done = (2, 2, 2, 2, 2, BLOCK, wide)
    dma = pltpu.SemaphoreType.DMA
    return pl.pallas_call(
        closing_kernel,
        grid=(1,),
        in_specs=[full(cells.shape), full(idx.shape), full(small.shape)]
        + [pl.BlockSpec(memory_space=pl.ANY)] * 2,
        out_specs=[full(done), full((2, rows, cols)), full(small.shape)],
        out_shape=[
            jax.ShapeDtypeStruct(done, BF),
            jax.ShapeDtypeStruct((2, rows, cols), F32),
            jax.ShapeDtypeStruct(small.shape, F32),
        ],
        scratch_shapes=[
            pltpu.VMEM((3, count, width), BF), pltpu.VMEM((8 * BLOCK, width), F32),
            dma((3, 2)), dma((3, 2)),
            pltpu.VMEM((5, *small.shape), F32), pltpu.VMEM((5, *small.shape), F32), dma((5,)), dma((5,)),
        ]
        + sum_scratch(rows, cols)
        + [part(2, 2, 2), part(2, 2), part(2), part(), dma((6, 2, 2)), dma((6, 2, 2))],
        compiler_params=params(has_side_effects=True, collective_id=3),
        cost_estimate=cost(8 * count * width * 1024, 24 << 20),
        name="closing",
    )(cells, idx, small, *grads)


def table_out_kernel(a, b, out):
    wide = a.shape[6]
    for n, piece in enumerate((a, b)):
        for u in range(2):
            at = (2 * n + u) * wide
            out[:, 0, at : at + wide] = piece[0, u, 0, 0, 0].astype(F32)


def table_out(done, table_rows):
    wide = done.shape[6]
    block = (1, 2, 1, 1, 1, BLOCK, wide)
    first = lambda i: (0, 0, i % 2, (i // 2) % 2, i // 4, 0, 0)
    second = lambda i: (1, 0, i % 2, i // 4, (i // 2) % 2, 0, 0)
    out = pl.pallas_call(
        table_out_kernel,
        grid=(8,),
        in_specs=[pl.BlockSpec(block, first), pl.BlockSpec(block, second)],
        out_specs=pl.BlockSpec((BLOCK, 1, 4 * wide), lambda i: (i, 0, 0)),
        out_shape=jax.ShapeDtypeStruct((table_rows, 1, 4 * wide), F32),
        compiler_params=params(),
        cost_estimate=cost(0, 6 << 20),
        name="table_write",
    )(done, done)
    return out.transpose(1, 0, 2)


def split_rel(r):
    return r & 1, (r >> 1) & 1, r >> 2


def reduce_kernel(tok, gffn, act, ga, gb):
    g = dot(gffn[...], act[...], TN)
    half = ga.shape[4]
    ga[0, :, 0] = g[:, :half].astype(BF).reshape(ga.shape[1], *ga.shape[3:])
    gb[0, :, 0] = g[:, half:].astype(BF).reshape(gb.shape[1], *gb.shape[3:])


def reduce_part(tok, gffn, act):
    tokens, d = gffn.shape
    f = act.shape[1] // 8
    rows, half = d // 4, f // 2

    def index(ch):
        def at(s, t):
            core, x, y = split_rel(7 - s)
            return (core, 0, 2 * y + x if ch else 2 * x + y, 0, 0)

        return at

    shape = jax.ShapeDtypeStruct((2, 4, 4, rows, half), BF)
    return pl.pallas_call(
        reduce_kernel,
        grid_spec=pltpu.PrefetchScalarGridSpec(
            num_scalar_prefetch=1,
            grid=(8,),
            in_specs=[
                full(gffn.shape),
                pl.BlockSpec((tokens, f), lambda s, t: (0, t[0] ^ (7 - s))),
            ],
            out_specs=[pl.BlockSpec((1, 4, 1, rows, half), index(ch)) for ch in range(2)],
        ),
        out_shape=[shape, shape],
        compiler_params=params(),
        cost_estimate=cost(16 * tokens * d * f, 20 << 20),
        name="reduce_grad",
    )(tok, gffn, act)


def rows_kernel(tok, *refs, groups):
    count = len(groups)
    lhs, refs = refs[:count], refs[count:]
    rhs = []
    for n in groups:
        rhs.append(refs[:n])
        refs = refs[n:]
    ga, gb = refs[:2]
    turned = refs[2:]
    rows = lhs[0].shape[1] // 8
    half = rows // 2

    @pl.when(pl.program_id(0) == 0)
    def _():
        for a, b in zip(lhs, turned):
            for r in range(8):
                start = pl.multiple_of((tok[0] ^ r) * rows, rows)
                b[:, r * rows : (r + 1) * rows] = a[:, pl.ds(start, rows)]

    at = 0
    for a, blocks in zip(turned, rhs):
        for block in blocks:
            block = block[...].reshape(block.shape[-2:])
            for n in range(0, block.shape[1], 512):
                piece = block[:, n : n + 512]
                g = dot(a[...], piece, TN).astype(BF)
                cols = slice(at, at + piece.shape[1])
                at += piece.shape[1]
                for r in range(8):
                    core, x, y = split_rel(r)
                    ga[core, 0, 2 * x + y, :, cols] = g[r * rows : r * rows + half]
                    gb[core, 0, 2 * y + x, :, cols] = g[r * rows + half : (r + 1) * rows]


def rows_part(tok, pairs, name):
    tokens, d = pairs[0][0].shape
    half = d // 16
    width = sum(spec.block_shape[-1] for _, _, specs in pairs for spec in specs)
    shape = jax.ShapeDtypeStruct((2, 4, 4, half, width), BF)
    out = pl.BlockSpec((2, 1, 4, half, width), lambda s, t: (0, s, 0, 0, 0))
    return pl.pallas_call(
        functools.partial(rows_kernel, groups=[len(p[1]) for p in pairs]),
        grid_spec=pltpu.PrefetchScalarGridSpec(
            num_scalar_prefetch=1,
            grid=(4,),
            in_specs=[full(p[0].shape) for p in pairs] + [s for p in pairs for s in p[2]],
            out_specs=[out, out],
            scratch_shapes=[pltpu.VMEM((tokens, d), BF) for _ in pairs],
        ),
        out_shape=[shape, shape],
        compiler_params=params(),
        cost_estimate=cost(8 * tokens * d * width, 24 << 20),
        name=name,
    )(tok, *[p[0] for p in pairs], *[r for p in pairs for r in p[1]])


def flip_tok(value, bit, size):
    return lax.ppermute(value, "tok", [(i, i ^ bit) for i in range(size)])


def shift_tab(value, shift, size):
    return lax.ppermute(value, "tab", [(i, (i + shift) % size) for i in range(size)])


def small_sum(value, n_tok, n_tab):
    bit = 1
    while bit < n_tok:
        value = value + flip_tok(value, bit, n_tok)
        bit *= 2
    total = value
    for shift in range(1, n_tab):
        total = total + shift_tab(value, shift, n_tab)
    return total


def body(
    n_tok, n_tab,
    embedded, cell_index, cell_boxes, box_tables, joined_weight, output_weight,
    expand_weight, reduce_weight, hidden_bias, bias_rows, norm_gains, norm_shifts, cotangent,
):
    tokens, width = embedded.shape
    pages, length = cell_index.shape
    table_rows = box_tables.shape[1]
    ff = expand_weight.shape[1]
    tok = lax.axis_index("tok").astype(jnp.int32).reshape(1)
    z = lax.axis_index("tab")
    cubic = n_tok == 8 and n_tab == 4

    corners = cell_boxes[:, :, :CELLS]
    lo = lambda n: jnp.minimum(corners[:, n], corners[:, n + 2]).reshape(-1)
    hi = lambda n: jnp.maximum(corners[:, n], corners[:, n + 2]).reshape(-1)
    left, right, top, bottom = lo(0), hi(0), lo(1), hi(1)
    none = jnp.full_like(left, -1)
    index_table = jnp.stack(
        [
            jnp.stack([left, right]),
            jnp.stack([top, bottom]),
            jnp.stack([right - left, none]),
            jnp.stack([bottom - top, none]),
        ]
    )
    pick_table = lambda i: lax.dynamic_index_in_dim(index_table, i, 0, keepdims=False)
    group_index = jnp.stack(
        [pick_table(z)]
        + [shift_tab(pick_table((z + s) % n_tab), s, n_tab) for s in range(1, n_tab)]
    )
    padded = jnp.pad(box_tables[0], ((0, 1024 - table_rows), (0, 0)))
    found = lookup(group_index, padded)
    terms = [found[0]] + [shift_tab(found[s], n_tab - s, n_tab) for s in range(1, n_tab)]

    q, k, v, normed, normed_low, rstd0 = embed(
        embedded, cell_index, terms, joined_weight, norm_gains, norm_shifts, bias_rows
    )
    mixed, lse = attn_fwd(q, k, v, pages)
    layer_out, after, after_low, rstd1, act, slope, gs2, gffn, sums2 = ffn_fwd(
        mixed, normed, output_weight, expand_weight, reduce_weight, hidden_bias,
        bias_rows, norm_gains, norm_shifts, cotangent, min(256, tokens),
    )
    quarter = width // 4
    parts = reduce_part(tok, gffn, act) if cubic else None
    gh, gs1, gattn, gmixed, hidden_sum, sums1, *reduce_sum = ffn_bwd(
        gffn, slope, gs2, after, rstd1, reduce_weight, expand_weight, output_weight,
        norm_gains, norm_shifts, parts,
    )
    if cubic:
        columns = lambda n: pl.BlockSpec((tokens, n), lambda s, t: (0, s))
        parts = rows_part(
            tok,
            [(after_low, [gh], [columns(ff // 4)]), (mixed, [gattn], [columns(quarter)])],
            "expand_output_grad",
        )
    gj, sums_qv, *expand_sum = attn_bwd(q, k, v, mixed, gmixed, lse, pages, parts)
    if cubic:
        third = lambda n: pl.BlockSpec(
            (1, tokens, quarter), lambda s, t: ((3 * s + n) // 4, 0, (3 * s + n) % 4)
        )
        parts = rows_part(
            tok, [(normed_low, [gj, gj, gj], [third(0), third(1), third(2)])], "joined_grad"
        )
    embedded_grad, cell_grad, sums0 = embed_bwd(
        gs1, gj, joined_weight, normed, rstd0, cell_index, norm_gains, norm_shifts
    )

    small = jnp.concatenate(
        [
            sums0.reshape(-1), sums1.reshape(-1), sums2.reshape(-1),
            sums_qv.reshape(-1), hidden_sum.reshape(-1),
        ]
    ).reshape(-1, 128)
    if cubic:
        done, joined_sum, small = closing(cell_grad, group_index, small, parts)
        tables_grad = table_out(done, table_rows)
    else:
        cell_grads = [cell_grad] + [shift_tab(cell_grad, s, n_tab) for s in range(1, n_tab)]
        part_a, part_b = table_part(jnp.zeros_like(tok), group_index, cell_grads, 8)
        both = jnp.concatenate([part_a, part_b], axis=2).astype(F32)
        tables_grad = lax.psum(both.reshape(1, -1, width)[:, :table_rows], "tok")
        small = small_sum(small, n_tok, n_tab)
    small = small.reshape(-1)
    row = small.reshape(-1, width)
    gains_grad = jnp.stack([row[0], row[2], row[5]])
    shifts_grad = jnp.stack([row[1], row[3], row[6]])
    biases_grad = jnp.stack([row[8], row[9], row[4], row[7]])
    hidden_bias_grad = small[10 * width :]

    if cubic:
        reduce_grad = jnp.concatenate([reduce_sum[0][0], reduce_sum[0][1]], axis=1).T
        expand_sum = expand_sum[0].reshape(-1, expand_sum[0].shape[2])
        expand_grad = expand_sum[:, : ff // 4]
        output_grad = expand_sum[:, ff // 4 :]
        joined_grad = joined_sum.reshape(-1, joined_sum.shape[2])
    else:
        both = lambda a, b: jnp.einsum("ta,tb->ab", a, b, preferred_element_type=F32).astype(BF)

        def scattered(part):
            part = lax.psum_scatter(part, "tok", scatter_dimension=0, tiled=True)
            return lax.psum_scatter(part, "tab", scatter_dimension=1, tiled=True).astype(F32)

        reduce_grad = scattered(both(act, gffn))
        expand_grad = scattered(both(after_low, gh))
        output_grad = scattered(both(mixed, gattn))
        joined_grad = scattered(both(normed_low, jnp.concatenate([gj[0], gj[1], gj[2]], axis=1)))

    return (
        layer_out, embedded_grad, tables_grad, joined_grad, output_grad, expand_grad,
        reduce_grad, hidden_bias_grad, biases_grad, gains_grad, shifts_grad,
    )


def solution(mesh):
    rows = P(("tok", "tab"), None)
    return jax.shard_map(
        functools.partial(body, mesh.shape["tok"], mesh.shape["tab"]),
        mesh=mesh,
        in_specs=(
            rows, rows, P(("tok", "tab"), None, None), P("tab", None, None),
            P(), P(), P(), P(), P(), P(), P(), P(), rows,
        ),
        out_specs=(
            rows, rows, P("tab", None, None), P("tok", "tab"), P("tok", "tab"),
            P("tok", "tab"), P("tok", "tab"), P(), P(), P(), P(),
        ),
        check_vma=False,
    )
```

```python
import functools

import jax
import jax.numpy as jnp
from jax import lax
from jax.experimental import pallas as pl
from jax.experimental.pallas import tpu as pltpu
from jax.sharding import PartitionSpec as P

HEADS = 16
HEAD_DIM = 64
CELLS = 128
EPSILON = 1e-05
SCALE = HEAD_DIM ** (-0.5)
LOG2E = 1.4426950408889634
F32 = jnp.float32
BF = jnp.bfloat16
NN = ((1,), (0,))
NT = ((1,), (1,))
TN = ((0,), (0,))
ANY = pl.ANY

TAIL_P = 0.305
TAIL_C = (
    0.12164194255155772,
    0.12243138164026345,
    0.10365178645525906,
    0.12022714029486306,
    -0.03641303195181058,
    0.1839499605096701,
    -0.15192310059752684,
    0.03643391798251271,
)


def dot(a, b, dims):
    return lax.dot_general(a, b, (dims, ((), ())), preferred_element_type=F32)


def params(**kw):
    return pltpu.CompilerParams(vmem_limit_bytes=60 << 20, **kw)


def cost(flops, nbytes, trans=0):
    return pl.CostEstimate(
        flops=int(flops), bytes_accessed=int(nbytes), transcendentals=int(trans)
    )


def full(shape):
    zeros = (0,) * len(shape)
    return pl.BlockSpec(shape, lambda *_: zeros, pipeline_mode=pl.Buffered(1))


def gelu_parts(h):
    a = jnp.abs(h)
    t = 1.0 / (1.0 + TAIL_P * a)
    poly = jnp.full_like(t, TAIL_C[-1])
    for c in TAIL_C[-2::-1]:
        poly = poly * t + c
    e = jnp.exp2(h * h * (-0.5 * LOG2E))
    tail = poly * t * e
    phi_cdf = jnp.where(h > 0, 1.0 - tail, tail)
    act = h * phi_cdf
    slope = phi_cdf + h * e * 0.3989422804014327
    return act, slope


def norm_stats(v):
    mean = jnp.mean(v, axis=-1, keepdims=True)
    centred = v - mean
    var = jnp.mean(centred * centred, axis=-1, keepdims=True)
    rstd = lax.rsqrt(var + EPSILON)
    return centred * rstd, rstd


def norm_back(y, xh, rstd, gain):
    u = y * gain
    return (
        u - jnp.mean(u, axis=-1, keepdims=True) - xh * jnp.mean(u * xh, axis=-1, keepdims=True)
    ) * rstd


def colsum(v):
    return jnp.sum(v, axis=0, keepdims=True)


def lookup_kernel(idx, table, out):
    rows = table.shape[0]
    count = idx.shape[2]
    number = lax.broadcasted_iota(jnp.int32, (rows, count), 0)
    first = (number == idx[0, 0:1, :]).astype(F32)
    second = (number == idx[0, 1:2, :]).astype(F32)
    out[0] = dot((first + second).astype(BF), table[...], TN).astype(BF)


def lookup(idx, table):
    groups, _, count = idx.shape
    rows, width = table.shape
    return pl.pallas_call(
        lookup_kernel,
        grid=(groups,),
        in_specs=[
            pl.BlockSpec((1, 2, count), lambda i: (i, 0, 0)),
            full((rows, width)),
        ],
        out_specs=pl.BlockSpec((1, count, width), lambda i: (i, 0, 0)),
        out_shape=jax.ShapeDtypeStruct((groups, count, width), BF),
        compiler_params=params(),
        cost_estimate=cost(2 * groups * count * rows * width, 2 * groups * count * width),
        name="lookup",
    )(idx, table)


def embed_kernel(
    emb, ci, t0, t1, t2, t3, w, gains, shifts, bias, q, k, v, normed, low, rstd_out
):
    width = emb.shape[1]
    tokens = emb.shape[0]
    cells = jnp.concatenate([t0[...], t1[...], t2[...], t3[...]], axis=0)
    number = lax.broadcasted_iota(jnp.int32, (CELLS, tokens), 0)
    pick = (number == ci[0]).astype(F32).astype(BF)
    pick = jnp.concatenate([pick] * 4, axis=0)
    box = dot(pick, cells, TN)
    xh, rstd = norm_stats(emb[...].astype(F32) + box)
    y = xh * gains[0:1] + shifts[0:1]
    normed[...] = y
    rstd_out[...] = rstd
    y_low = y.astype(BF)
    low[...] = y_low
    q[...] = ((dot(y_low, w[:, :width], NN) + bias[0:1]) * SCALE).astype(BF)
    k[...] = dot(y_low, w[:, width : 2 * width], NN).astype(BF)
    v[...] = (dot(y_low, w[:, 2 * width :], NN) + bias[1:2]).astype(BF)


def embed(emb, ci, terms, w, gains, shifts, bias):
    tokens, width = emb.shape
    pages, length = ci.shape
    rows = pl.BlockSpec((length, width), lambda i: (i, 0))
    cell_rows = pl.BlockSpec((CELLS, width), lambda i: (i, 0))
    shape = lambda dt, n=width: jax.ShapeDtypeStruct((tokens, n), dt)
    return pl.pallas_call(
        embed_kernel,
        grid=(pages,),
        in_specs=[rows, pl.BlockSpec((1, 1, length), lambda i: (i, 0, 0))]
        + [cell_rows] * 4
        + [full(w.shape), full(gains.shape), full(shifts.shape), full(bias.shape)],
        out_specs=[rows] * 5 + [pl.BlockSpec((length, 1), lambda i: (i, 0))],
        out_shape=[shape(BF), shape(BF), shape(BF), shape(F32), shape(BF), shape(F32, 1)],
        compiler_params=params(),
        cost_estimate=cost(2 * tokens * width * 3 * width, 26 << 20),
        name="embed_joined",
    )(emb, ci.reshape(pages, 1, length), *terms, w, gains, shifts, bias)


STAGES = 4


def neighbours():
    tok, z = lax.axis_index("tok"), lax.axis_index("tab")
    core = {"tok": tok + 1 - 2 * (tok % 2)}
    x = {"tok": tok + 2 - 4 * ((tok // 2) % 2)}
    y = {"tok": tok + 4 - 8 * (tok // 4)}
    peers = [{"tab": (z + s) % 4} for s in range(1, 4)]
    return core, x, y, peers


def meet(devices):
    barrier = pltpu.get_barrier_semaphore()
    for d in devices:
        pl.semaphore_signal(barrier, inc=1, device_id=d, device_id_type=pl.DeviceIdType.MESH)
    pl.semaphore_wait(barrier, len(devices))


def sum_scratch(rows, cols):
    part = lambda *n: pltpu.VMEM((*n, rows, cols), BF)
    return [
        part(2, 4, 4), part(2, 4, 4), part(2, 4, 2), part(2, 4), part(2, 3),
        pltpu.SemaphoreType.DMA((2, 4)),
        pltpu.SemaphoreType.DMA((STAGES, 2, 4)),
        pltpu.SemaphoreType.DMA((STAGES, 2, 4)),
    ]


class Summing:
    def __init__(self, grads, out, scratch):
        self.grads, self.out = grads, out
        self.own, self.r0, self.r1, self.r2, self.r3, self.local, self.sent, self.got = scratch
        core, x, y, peers = neighbours()
        self.core, self.first, self.second, self.peers = core, (x, y), (y, x), peers
        self.z = lax.axis_index("tab")

    def devices(self):
        return [self.core, self.first[0], self.first[1], *self.peers]

    def copy(self, stage, ch, i):
        zc = (self.z + (i + 1)) % 4
        src, dst, to = (
            (lambda: self.grads[ch].at[1, zc], self.r0.at[ch, i], self.core),
            (lambda: self.own.at[ch, i, pl.ds(2, 2)], self.r1.at[ch, i], self.first[ch]),
            (lambda: self.own.at[ch, i, 1], self.r2.at[ch, i], self.second[ch]),
            (lambda: self.own.at[ch, i, 0], self.r3.at[ch, min(i, 2)], self.peers[min(i, 2)]),
        )[stage]
        return pltpu.make_async_remote_copy(
            src_ref=src(), dst_ref=dst,
            send_sem=self.sent.at[stage, ch, i], recv_sem=self.got.at[stage, ch, i],
            device_id=to, device_id_type=pl.DeviceIdType.MESH,
        )

    def load(self, ch, i):
        zc = (self.z + (i + 1)) % 4
        return pltpu.make_async_copy(
            self.grads[ch].at[0, zc], self.own.at[ch, i], self.local.at[ch, i]
        )

    def start(self):
        for i in range(4):
            for ch in range(2):
                self.copy(0, ch, i).start()
                self.load(ch, i).start()

    def step(self, stage, i):
        for ch in range(2):
            self.copy(stage - 1, ch, i).wait_recv()
            if stage == 1:
                self.load(ch, i).wait()

                def add(j, _, ch=ch):
                    self.own[ch, i, j] = self.own[ch, i, j] + self.r0[ch, i, j]
                    return 0

                lax.fori_loop(0, 4, add, 0)
            elif stage == 2:

                def add(j, _, ch=ch):
                    self.own[ch, i, j] = self.own[ch, i, j] + self.r1[ch, i, j]
                    return 0

                lax.fori_loop(0, 2, add, 0)
            elif i < 3:
                self.own[ch, i, 0] = self.own[ch, i, 0] + self.r2[ch, i]
            if stage < 3 or i < 3:
                self.copy(stage, ch, i).start()

    def finish(self):
        for ch in range(2):
            total = self.own[ch, 3, 0].astype(F32) + self.r2[ch, 3].astype(F32)
            for i in range(3):
                self.copy(3, ch, i).wait_recv()
                total = total + self.r3[ch, i].astype(F32)
            self.out[ch] = total
        for stage in range(STAGES):
            for ch in range(2):
                for i in range(4 if stage < 3 else 3):
                    self.copy(stage, ch, i).wait_send()

    def run(self, step, plan):
        for at, events in plan.items():

            @pl.when(step == at)
            def _(events=events):
                for stage, i in events:
                    if stage == 0:
                        self.start()
                    elif stage == 4:
                        self.finish()
                    else:
                        self.step(stage, i)


def sum_specs(grads, number):
    if grads is None:
        return [], [], [], [], {}
    rows, cols = grads[0].shape[3:]
    return (
        [pl.BlockSpec(memory_space=pl.ANY)] * 2,
        [full((2, rows, cols))],
        [jax.ShapeDtypeStruct((2, rows, cols), F32)],
        sum_scratch(rows, cols),
        {"has_side_effects": True, "collective_id": number},
    )


HP = 4


def head_masks(length, pair):
    lane = lax.broadcasted_iota(jnp.int32, (length, pair), 1)
    return lane < HEAD_DIM


def attn_fwd_kernel(q, k, v, mixed, lse):
    length = q.shape[0]
    pair = 2 * HEAD_DIM
    low_half = head_masks(length, pair)
    zero = jnp.zeros((length, pair), BF)
    for p in range(HP // 2):
        cols = slice(p * pair, (p + 1) * pair)
        qp, kp, vp = q[:, cols], k[:, cols], v[:, cols]
        vt = vp.T
        outs = []
        for h in range(2):
            km = jnp.where(low_half, kp, zero) if h == 0 else jnp.where(low_half, zero, kp)
            st = dot(km, qp, NT)
            top = jnp.max(st, axis=0, keepdims=True)
            raised = jnp.exp2((st - top) * LOG2E)
            total = jnp.sum(raised, axis=0, keepdims=True)
            lse[0, 0, 2 * p + h : 2 * p + h + 1, :] = top + jnp.log(total)
            ot = dot(vt[h * HEAD_DIM : (h + 1) * HEAD_DIM], raised.astype(BF), NN)
            outs.append(ot * (1.0 / total))
        mixed[:, cols] = jnp.concatenate(outs, axis=0).T.astype(BF)


def attn_fwd(q, k, v, pages):
    tokens, width = q.shape
    length = tokens // pages
    steps = HEADS // HP
    blk = pl.BlockSpec((length, HP * HEAD_DIM), lambda i, j: (i, j))
    return pl.pallas_call(
        attn_fwd_kernel,
        grid=(pages, steps),
        in_specs=[blk] * 3,
        out_specs=[blk, pl.BlockSpec((1, 1, HP, length), lambda i, j: (i, j, 0, 0))],
        out_shape=[
            jax.ShapeDtypeStruct((tokens, width), BF),
            jax.ShapeDtypeStruct((pages, steps, HP, length), F32),
        ],
        compiler_params=params(),
        cost_estimate=cost(14e9, 8 << 20, pages * HEADS * length * length),
        name="attention",
    )(q, k, v)


def attn_back(q, k, v, mixed, go, lse, put):
    length = q.shape[0]
    pair = 2 * HEAD_DIM
    low_half = head_masks(length, pair)
    zero = jnp.zeros((length, pair), BF)

    def pick(x, h):
        return jnp.where(low_half, x, zero) if h == 0 else jnp.where(low_half, zero, x)

    for p in range(HP // 2):
        cols = slice(p * pair, (p + 1) * pair)
        qp, kp, vp, op, gp = q[:, cols], k[:, cols], v[:, cols], mixed[:, cols], go[:, cols]
        kt = kp.T
        prod_t = (op.astype(F32) * gp.astype(F32)).T
        dq_t, dk, dv = [], None, None
        for h in range(2):
            st = dot(pick(kp, h), qp, NT)
            probs = jnp.exp2((st - lse[0, 0, 2 * p + h : 2 * p + h + 1, :]) * LOG2E)
            dv_h = dot(probs.astype(BF), pick(gp, h), NN)
            dpt = dot(pick(vp, h), gp, NT)
            delta = colsum(prod_t[h * HEAD_DIM : (h + 1) * HEAD_DIM])
            ds = (probs * (dpt - delta)).astype(BF)
            dk_h = dot(ds, pick(qp, h), NN)
            dq_t.append(dot(kt[h * HEAD_DIM : (h + 1) * HEAD_DIM], ds, NN))
            dv = dv_h if dv is None else dv + dv_h
            dk = dk_h if dk is None else dk + dk_h
        dq = (jnp.concatenate(dq_t, axis=0).T.astype(BF).astype(F32) * SCALE).astype(BF)
        put(p * pair, pair, dq, dk.astype(BF), dv.astype(BF))


FC = 512
FWD = 1024
RC = 128
MC = 512


def ffn_fwd_kernel(
    mixed, normed, wo, we, wr, hb, bias, gains, shifts, cot,
    out, after_out, low_out, rstd_out, act_out, slope_out, gs2_out, gffn_out, sums,
):
    ff = we.shape[1]
    attn_sum = normed[...] + (dot(mixed[...], wo[...], NN) + bias[2:3])
    xh, rstd = norm_stats(attn_sum)
    after = xh * gains[1:2] + shifts[1:2]
    after_out[...] = after
    rstd_out[...] = rstd
    low = after.astype(BF)
    low_out[...] = low
    total = after + bias[3:4]
    for j in range(ff // FWD):
        cols = slice(j * FWD, (j + 1) * FWD)
        act, slope = gelu_parts(dot(low, we[:, cols], NN) + hb[:, cols])
        act = act.astype(BF)
        act_out[:, cols] = act
        slope_out[:, cols] = slope.astype(BF)
        total = total + dot(act, wr[cols, :], NN)
    xh, rstd = norm_stats(total)
    out[...] = (xh * gains[2:3] + shifts[2:3]).astype(BF)
    y = cot[...].astype(F32)
    gs2 = norm_back(y, xh, rstd, gains[2:3])
    gs2_out[...] = gs2
    gffn = gs2.astype(BF)
    gffn_out[...] = gffn
    part = jnp.concatenate([colsum(y * xh), colsum(y), colsum(gffn.astype(F32))], axis=0)

    @pl.when(pl.program_id(0) == 0)
    def _():
        sums[...] = part

    @pl.when(pl.program_id(0) != 0)
    def _():
        sums[...] = sums[...] + part


def ffn_fwd(mixed, normed, wo, we, wr, hb, bias, gains, shifts, cot, tile):
    tokens, width = mixed.shape
    ff = we.shape[1]
    rows = pl.BlockSpec((tile, width), lambda i: (i, 0))
    long = pl.BlockSpec((tile, ff), lambda i: (i, 0))
    shape = lambda dt, n=width: jax.ShapeDtypeStruct((tokens, n), dt)
    hb = hb.reshape(1, ff)
    return pl.pallas_call(
        ffn_fwd_kernel,
        grid=(tokens // tile,),
        in_specs=[rows, rows]
        + [full(a.shape) for a in (wo, we, wr, hb, bias, gains, shifts)]
        + [rows],
        out_specs=[rows, rows, rows, pl.BlockSpec((tile, 1), lambda i: (i, 0)), long, long, rows, rows]
        + [pl.BlockSpec((3, width), lambda i: (0, 0))],
        out_shape=[
            shape(BF), shape(F32), shape(BF), shape(F32, 1), shape(BF, ff), shape(BF, ff),
            shape(F32), shape(BF), jax.ShapeDtypeStruct((3, width), F32),
        ],
        compiler_params=params(),
        cost_estimate=cost(2 * tokens * width * (width + 2 * ff), 60 << 20, tokens * ff * 2),
        name="ffn_forward",
    )(mixed, normed, wo, we, wr, hb, bias, gains, shifts, cot)


FFN_PLAN = {
    0: [(0, 0)],
    1: [(1, 0)],
    2: [(1, 1)],
    3: [(2, 0), (1, 2)],
    4: [(2, 1), (1, 3)],
    5: [(3, 0)],
    7: [(2, 2), (3, 1)],
}
FFN_TAIL = [(2, 3), (3, 2), (3, 3), (4, 0)]


def ffn_bwd_kernel(*refs, summed):
    gffn, gs2, after, rstd, wo, gains, shifts, slope, wr, we = refs[:10]
    refs = refs[10:]
    grads, refs = refs[: 2 * summed], refs[2 * summed :]
    gh_out, gs1_out, gattn_out, gmixed_out, hsum, sums = refs[:6]
    refs = refs[6:]
    step, last = pl.program_id(0), pl.num_programs(0) - 1
    tokens, width = gffn.shape
    if summed:
        summing = Summing(grads, refs[0], refs[1:])

        @pl.when(step == 0)
        def _():
            meet(summing.devices())

        summing.run(step, FFN_PLAN)

    @pl.when(step == 0)
    def _():
        gs1_out[...] = gs2[...]

    part = jnp.zeros((1, slope.shape[1]), F32)
    for m in range(0, tokens, MC):
        rows = slice(m, m + MC)
        gh = (dot(gffn[rows, :], wr[...], NT) * slope[rows, :].astype(F32)).astype(BF)
        gh_out[rows, :] = gh
        part = part + colsum(gh.astype(F32))
        gs1_out[rows, :] = gs1_out[rows, :] + dot(gh, we[...], NT)
    hsum[...] = part

    @pl.when(step == last)
    def _():
        def norm(i, carry):
            rows = pl.ds(pl.multiple_of(i * RC, RC), RC)
            total = gs1_out[rows, :]
            xh = (after[rows, :] - shifts[1:2]) * (1.0 / gains[1:2])
            gs1 = norm_back(total, xh, rstd[rows, :], gains[1:2])
            gs1_out[rows, :] = gs1
            gattn = gs1.astype(BF)
            gattn_out[rows, :] = gattn
            g, s, b = carry
            return g + colsum(total * xh), s + colsum(total), b + colsum(gattn.astype(F32))

        zero = jnp.zeros((1, width), F32)
        sums[...] = jnp.concatenate(
            lax.fori_loop(0, tokens // RC, norm, (zero, zero, zero)), axis=0
        )
        for m in range(0, tokens, MC):
            rows = slice(m, m + MC)
            gmixed_out[rows, :] = dot(gattn_out[rows, :], wo[...], NT).astype(BF)

    if summed:
        summing.run(step, {last: FFN_TAIL})


def ffn_bwd(gffn, slope, gs2, after, rstd, wr, we, wo, gains, shifts, grads):
    tokens, width = gffn.shape
    ff = we.shape[1]
    whole = full((tokens, width))
    long = pl.BlockSpec((tokens, FC), lambda s: (0, s))
    shape = lambda dt, n=width: jax.ShapeDtypeStruct((tokens, n), dt)
    more_in, more_out, more_shape, more_scratch, more = sum_specs(grads, 1)
    return pl.pallas_call(
        functools.partial(ffn_bwd_kernel, summed=grads is not None),
        grid=(ff // FC,),
        in_specs=[whole, whole, whole, full((tokens, 1))]
        + [full(a.shape) for a in (wo, gains, shifts)]
        + [
            long,
            pl.BlockSpec((FC, width), lambda s: (s, 0)),
            pl.BlockSpec((width, FC), lambda s: (0, s)),
        ]
        + more_in,
        out_specs=[long, whole, whole, whole]
        + [pl.BlockSpec((1, FC), lambda s: (0, s)), full((3, width))]
        + more_out,
        out_shape=[
            shape(BF, ff), shape(F32), shape(BF), shape(BF),
            jax.ShapeDtypeStruct((1, ff), F32), jax.ShapeDtypeStruct((3, width), F32),
        ]
        + more_shape,
        scratch_shapes=more_scratch,
        compiler_params=params(**more),
        cost_estimate=cost(2 * tokens * width * (width + 2 * ff), 60 << 20),
        name="ffn_backward",
    )(gffn, gs2, after, rstd, wo, gains, shifts, slope, wr, we, *(grads or ()))


BACK_PLAN = {
    0: [(0, 0)],
    1: [(1, 0)],
    2: [(1, 1)],
    3: [(2, 0), (1, 2)],
    5: [(2, 1), (1, 3)],
    6: [(3, 0)],
    8: [(2, 2)],
    9: [(3, 1)],
    11: [(2, 3)],
    12: [(3, 2)],
    13: [(3, 3)],
}


def rel_of(b):
    tok = lax.axis_index("tok")
    core, x, y = split_rel(b)
    flip = lambda static, mine: 1 - mine if static else mine
    return flip(core, tok % 2), flip(x, (tok // 2) % 2), flip(y, tok // 4)


def put_rows(g, ga, gb, cols, rows):
    half = rows // 2
    for b in range(8):
        core, x, y = rel_of(b)
        ga[core, 0, 2 * x + y, :, cols] = g[b * rows : b * rows + half]
        gb[core, 0, 2 * y + x, :, cols] = g[b * rows + half : (b + 1) * rows]


def back_kernel(*refs, pages, summed):
    q, k, v, mixed, go, lse, low, gs1, w, normed, rstd, ci, gains, shifts = refs[:14]
    refs = refs[14:]
    grads, refs = refs[: 2 * summed], refs[2 * summed :]
    out, cells, sums0, sums_qv = refs[:4]
    refs = refs[4:]
    if summed:
        ga, gb, summed_out, gj = refs[:4]
        summing = Summing(grads, summed_out, refs[4:])
    else:
        gj_out, gj = refs
    step = pl.program_id(0)
    width = gs1.shape[1]
    length = q.shape[0]
    groups = HEADS // HP
    wide = HP * HEAD_DIM
    n_attn = groups * pages
    n_joined = 4 if summed else 0

    if summed:

        @pl.when(step == 0)
        def _():
            meet(summing.devices())

        summing.run(step, BACK_PLAN)

    @pl.when(step < n_attn)
    def _():
        group, page = step // pages, step % pages
        rows = pl.ds(pl.multiple_of(page * length, length), length)

        def put(at, size, dq, dk, dv):
            cols = pl.ds(pl.multiple_of(group * wide + at, size), size)
            gj[0, rows, cols] = dq
            gj[1, rows, cols] = dk
            gj[2, rows, cols] = dv
            part = jnp.concatenate([colsum(dq.astype(F32)), colsum(dv.astype(F32))], axis=0)

            @pl.when(page == 0)
            def _():
                sums_qv[:, cols] = part

            @pl.when(page != 0)
            def _():
                sums_qv[:, cols] = sums_qv[:, cols] + part

        attn_back(q, k, v, mixed, go, lse, put)

    if summed:
        quarter = width // 4
        for n in range(n_joined):

            @pl.when(step == n_attn + n)
            def _(n=n):
                for m in range(3):
                    third, at = (3 * n + m) // 4, (3 * n + m) % 4
                    piece = gj[third, :, at * quarter : (at + 1) * quarter]
                    g = dot(low[...], piece, TN).astype(BF)
                    put_rows(g, ga, gb, slice(m * quarter, (m + 1) * quarter), width // 8)

    @pl.when(step >= n_attn + n_joined)
    def _():
        page = step - (n_attn + n_joined)
        rows = pl.ds(pl.multiple_of(page * length, length), length)
        total = gs1[...]
        for n in range(3):
            total = total + dot(gj[n, rows, :], w[:, n * width : (n + 1) * width], NT)
        xh = (normed[...] - shifts[0:1]) * (1.0 / gains[0:1])
        grad = norm_back(total, xh, rstd[...], gains[0:1])
        out[...] = grad
        number = lax.broadcasted_iota(jnp.int32, (CELLS, length), 0)
        pick = (number == ci[0]).astype(F32).astype(BF)
        cells[...] = dot(pick, grad.astype(BF), NN).astype(BF)
        part = jnp.concatenate([colsum(total * xh), colsum(total)], axis=0)

        @pl.when(page == 0)
        def _():
            sums0[...] = part

        @pl.when(page != 0)
        def _():
            sums0[...] = sums0[...] + part

    if summed:

        @pl.when(step == pl.num_programs(0) - 1)
        def _():
            summing.finish()
    else:
        gj_out[...] = gj[...]


def back(q, k, v, mixed, go, lse, low, gs1, w, normed, rstd, ci, gains, shifts, grads):
    tokens, width = q.shape
    pages, length = ci.shape
    groups = HEADS // HP
    wide = HP * HEAD_DIM
    summed = grads is not None
    n_attn = groups * pages
    before = n_attn + (4 if summed else 0)
    at = lambda s: jnp.minimum(s, n_attn - 1)
    page = lambda s: jnp.maximum(s - before, 0)
    block = lambda s: jnp.clip(s - n_attn, 0, 3)
    blk = pl.BlockSpec((length, wide), lambda s: (at(s) % pages, at(s) // pages))
    rows = pl.BlockSpec((length, width), lambda s: (page(s), 0))
    out_specs = [
        rows,
        pl.BlockSpec((CELLS, width), lambda s: (page(s), 0)),
        full((2, width)),
        full((2, width)),
    ]
    out_shape = [
        jax.ShapeDtypeStruct((tokens, width), F32),
        jax.ShapeDtypeStruct((pages * CELLS, width), BF),
        jax.ShapeDtypeStruct((2, width), F32),
        jax.ShapeDtypeStruct((2, width), F32),
    ]
    whole_gj = (3, tokens, width)
    more_in, more_out, more_shape, more_scratch, more = sum_specs(grads, 2)
    if summed:
        half = width // 16
        piece = pl.BlockSpec((2, 1, 4, half, 3 * width // 4), lambda s: (0, block(s), 0, 0, 0))
        out_specs += [piece, piece]
        out_shape += [jax.ShapeDtypeStruct((2, 4, 4, half, 3 * width // 4), BF)] * 2
    else:
        out_specs += [full(whole_gj)]
        out_shape += [jax.ShapeDtypeStruct(whole_gj, BF)]
    return pl.pallas_call(
        functools.partial(back_kernel, pages=pages, summed=summed),
        grid=(before + pages,),
        in_specs=[blk] * 5
        + [
            pl.BlockSpec((1, 1, HP, length), lambda s: (at(s) % pages, at(s) // pages, 0, 0)),
            full(low.shape),
            rows,
            full(w.shape),
            rows,
            pl.BlockSpec((length, 1), lambda s: (page(s), 0)),
            pl.BlockSpec((1, 1, length), lambda s: (page(s), 0, 0)),
            full(gains.shape),
            full(shifts.shape),
        ]
        + more_in,
        out_specs=out_specs + more_out,
        out_shape=out_shape + more_shape,
        scratch_shapes=[pltpu.VMEM(whole_gj, BF)] + more_scratch,
        compiler_params=params(**more),
        cost_estimate=cost(70e9, 40 << 20, pages * HEADS * length * length),
        name="attention_joined_embed_back",
    )(
        q, k, v, mixed, go, lse, low, gs1, w, normed, rstd, ci.reshape(pages, 1, length),
        gains, shifts, *(grads or ()),
    )


def table_kernel(tok, idx, g0, g1, g2, g3, out_a, out_b):
    rows = out_a.shape[1]
    count = idx.shape[2]
    half = out_a.shape[2]
    base = (pl.program_id(0) ^ tok[0]) * rows
    number = lax.broadcasted_iota(jnp.int32, (rows, count), 0) + base
    picks = []
    for s in range(4):
        first = (number == idx[s, 0:1, :]).astype(F32)
        second = (number == idx[s, 1:2, :]).astype(F32)
        picks.append((first + second).astype(BF))
    pick = jnp.concatenate(picks, axis=1)
    grads = jnp.concatenate([g0[...], g1[...], g2[...], g3[...]], axis=0)
    total = dot(pick, grads, NN).astype(BF)
    out_a[0] = total[:, :half]
    out_b[0] = total[:, half:]


def table_part(tok, idx, grads, blocks):
    groups, _, count = idx.shape
    width = grads[0].shape[1]
    rows = 1024 // blocks
    half = width // 2
    out = pl.BlockSpec((1, rows, half), lambda i, t: (i, 0, 0))
    return pl.pallas_call(
        table_kernel,
        grid_spec=pltpu.PrefetchScalarGridSpec(
            num_scalar_prefetch=1,
            grid=(blocks,),
            in_specs=[full(idx.shape)] + [full((count, width))] * groups,
            out_specs=[out, out],
        ),
        out_shape=[jax.ShapeDtypeStruct((blocks, rows, half), BF)] * 2,
        compiler_params=params(),
        cost_estimate=cost(2 * 1024 * groups * count * width, 4 << 20),
        name="table_grad",
    )(tok, idx, *grads)


BLOCK = 128


class TableSum:
    def __init__(self, scratch, done):
        self.part, self.r0, self.r1, self.r2, self.sent, self.got = scratch
        self.done = done
        tok = lax.axis_index("tok")
        core, x, y, _ = neighbours()
        self.c, cx, cy = tok % 2, (tok // 2) % 2, tok // 4
        self.core, self.first, self.second = core, (x, y), (y, x)
        self.f, self.g = (cx, cy), (cy, cx)

    def copy(self, stage, ch, u):
        c, f, g = self.c, self.f[ch], self.g[ch]
        part, done = self.part.at[ch, u], self.done.at[ch, u]
        src, dst, to = (
            (lambda: part.at[1 - c], self.r0.at[ch, u], self.core),
            (lambda: part.at[c, 1 - f], self.r1.at[ch, u], self.first[ch]),
            (lambda: part.at[c, f, 1 - g], self.r2.at[ch, u], self.second[ch]),
            (lambda: done.at[c, f, g], None, self.second[ch]),
            (lambda: done.at[c, f], None, self.first[ch]),
            (lambda: done.at[c], None, self.core),
        )[stage]
        src = src()
        return pltpu.make_async_remote_copy(
            src_ref=src, dst_ref=src if dst is None else dst,
            send_sem=self.sent.at[stage, ch, u], recv_sem=self.got.at[stage, ch, u],
            device_id=to, device_id_type=pl.DeviceIdType.MESH,
        )

    def store(self, u, ch, value):
        for b in range(8):
            c, x, y = split_rel(b)
            f, g = (x, y) if ch == 0 else (y, x)
            self.part[ch, u, c, f, g] = value[b * BLOCK : (b + 1) * BLOCK]
        self.copy(0, ch, u).start()

    def step(self, stage, u):
        for ch in range(2):
            c, f, g = self.c, self.f[ch], self.g[ch]
            self.copy(stage - 1, ch, u).wait_recv()
            if stage == 1:
                self.part[ch, u, c] = self.part[ch, u, c] + self.r0[ch, u]
            elif stage == 2:
                self.part[ch, u, c, f] = self.part[ch, u, c, f] + self.r1[ch, u]
            elif stage == 3:
                self.done[ch, u, c, f, g] = self.part[ch, u, c, f, g] + self.r2[ch, u]
            if stage < 6:
                self.copy(stage, ch, u).start()

    def finish(self):
        for stage in range(6):
            for ch in range(2):
                for u in range(2):
                    self.copy(stage, ch, u).wait_send()


def closing_kernel(
    cells, idx, small, ga, gb, done, joined, small_out,
    ring, total, ring_sent, ring_got, held, arrived, small_sent, small_got, *scratch,
):
    summing = Summing((ga, gb), joined, scratch[:8])
    table = TableSum(scratch[8:], done)
    core, x, y, peers = neighbours()
    z = lax.axis_index("tab")
    hops = [core, x, y, {"tab": z + 1 - 2 * (z % 2)}, {"tab": z + 2 - 4 * (z // 2)}]
    meet([core, x, y, *peers])
    count = cells.shape[0]
    half = count // 2

    def pass_on(k, h):
        rows = pl.ds(h * half, half)
        src = cells.at[rows] if k == 0 else ring.at[k - 1, rows]
        return pltpu.make_async_remote_copy(
            src_ref=src, dst_ref=ring.at[k, rows],
            send_sem=ring_sent.at[k, h], recv_sem=ring_got.at[k, h],
            device_id=peers[0], device_id_type=pl.DeviceIdType.MESH,
        )

    def small_copy(n):
        return pltpu.make_async_remote_copy(
            src_ref=held.at[n], dst_ref=arrived.at[n],
            send_sem=small_sent.at[n], recv_sem=small_got.at[n],
            device_id=hops[n], device_id_type=pl.DeviceIdType.MESH,
        )

    def small_step(n):
        small_copy(n - 1).wait_recv()
        value = held[n - 1] + arrived[n - 1]
        if n < 5:
            held[n] = value
            small_copy(n).start()
        else:
            small_out[...] = value

    def relay(k, h):
        pass_on(k - 1, h).wait_recv()
        pass_on(k, h).start()

    def pick(s):
        number = lax.broadcasted_iota(jnp.int32, (total.shape[0], count), 0)
        first = (number == idx[s, 0:1, :]).astype(F32)
        second = (number == idx[s, 1:2, :]).astype(F32)
        return (first + second).astype(BF)

    pass_on(0, 0).start()
    pass_on(0, 1).start()
    held[0] = small[...]
    small_copy(0).start()
    summing.start()
    total[...] = dot(pick(0), cells[...], NN)
    small_step(1)
    summing.step(1, 0)
    small_step(2)
    summing.step(1, 1)
    small_step(3)
    relay(1, 0)
    summing.step(2, 0)
    summing.step(1, 2)
    relay(1, 1)
    total[...] = total[...] + dot(pick(1), ring[0], NN)
    summing.step(2, 1)
    summing.step(1, 3)
    relay(2, 0)
    small_step(4)
    summing.step(2, 2)
    relay(2, 1)
    summing.step(3, 0)
    summing.step(3, 1)
    total[...] = total[...] + dot(pick(2), ring[1], NN)
    summing.step(2, 3)
    summing.step(3, 2)
    small_step(5)
    last = pick(3)
    pass_on(2, 0).wait_recv()
    pass_on(2, 1).wait_recv()
    wide = total.shape[1] // 4
    for u in range(2):
        for ch in range(2):
            cols = slice((2 * ch + u) * wide, (2 * ch + u + 1) * wide)
            value = total[:, cols] + dot(last, ring[2, :, cols], NN)
            table.store(u, ch, value.astype(BF))
    summing.step(3, 3)
    table.step(1, 0)
    table.step(1, 1)
    table.step(2, 0)
    table.step(2, 1)
    table.step(3, 0)
    table.step(3, 1)
    table.step(4, 0)
    table.step(4, 1)
    summing.finish()
    table.step(5, 0)
    table.step(5, 1)
    table.step(6, 0)
    table.step(6, 1)
    table.finish()
    for k in range(3):
        for h in range(2):
            pass_on(k, h).wait_send()
    for n in range(5):
        small_copy(n).wait_send()


def closing(cells, idx, small, grads):
    count, width = cells.shape
    rows, cols = grads[0].shape[3:]
    wide = width // 4
    part = lambda *n: pltpu.VMEM((2, 2, *n, BLOCK, wide), BF)
    done = (2, 2, 2, 2, 2, BLOCK, wide)
    dma = pltpu.SemaphoreType.DMA
    return pl.pallas_call(
        closing_kernel,
        grid=(1,),
        in_specs=[full(cells.shape), full(idx.shape), full(small.shape)]
        + [pl.BlockSpec(memory_space=pl.ANY)] * 2,
        out_specs=[full(done), full((2, rows, cols)), full(small.shape)],
        out_shape=[
            jax.ShapeDtypeStruct(done, BF),
            jax.ShapeDtypeStruct((2, rows, cols), F32),
            jax.ShapeDtypeStruct(small.shape, F32),
        ],
        scratch_shapes=[
            pltpu.VMEM((3, count, width), BF), pltpu.VMEM((8 * BLOCK, width), F32),
            dma((3, 2)), dma((3, 2)),
            pltpu.VMEM((5, *small.shape), F32), pltpu.VMEM((5, *small.shape), F32), dma((5,)), dma((5,)),
        ]
        + sum_scratch(rows, cols)
        + [part(2, 2, 2), part(2, 2), part(2), part(), dma((6, 2, 2)), dma((6, 2, 2))],
        compiler_params=params(has_side_effects=True, collective_id=3),
        cost_estimate=cost(8 * count * width * 1024, 24 << 20),
        name="closing",
    )(cells, idx, small, *grads)


def table_out_kernel(a, b, out):
    wide = a.shape[6]
    for n, piece in enumerate((a, b)):
        for u in range(2):
            at = (2 * n + u) * wide
            out[:, 0, at : at + wide] = piece[0, u, 0, 0, 0].astype(F32)


def table_out(done, table_rows):
    wide = done.shape[6]
    block = (1, 2, 1, 1, 1, BLOCK, wide)
    first = lambda i: (0, 0, i % 2, (i // 2) % 2, i // 4, 0, 0)
    second = lambda i: (1, 0, i % 2, i // 4, (i // 2) % 2, 0, 0)
    out = pl.pallas_call(
        table_out_kernel,
        grid=(8,),
        in_specs=[pl.BlockSpec(block, first), pl.BlockSpec(block, second)],
        out_specs=pl.BlockSpec((BLOCK, 1, 4 * wide), lambda i: (i, 0, 0)),
        out_shape=jax.ShapeDtypeStruct((table_rows, 1, 4 * wide), F32),
        compiler_params=params(),
        cost_estimate=cost(0, 6 << 20),
        name="table_write",
    )(done, done)
    return out.transpose(1, 0, 2)


def split_rel(r):
    return r & 1, (r >> 1) & 1, r >> 2


def reduce_kernel(tok, gffn, act, ga, gb):
    g = dot(gffn[...], act[...], TN)
    half = ga.shape[4]
    ga[0, :, 0] = g[:, :half].astype(BF).reshape(ga.shape[1], *ga.shape[3:])
    gb[0, :, 0] = g[:, half:].astype(BF).reshape(gb.shape[1], *gb.shape[3:])


def reduce_part(tok, gffn, act):
    tokens, d = gffn.shape
    f = act.shape[1] // 8
    rows, half = d // 4, f // 2

    def index(ch):
        def at(s, t):
            core, x, y = split_rel(7 - s)
            return (core, 0, 2 * y + x if ch else 2 * x + y, 0, 0)

        return at

    shape = jax.ShapeDtypeStruct((2, 4, 4, rows, half), BF)
    return pl.pallas_call(
        reduce_kernel,
        grid_spec=pltpu.PrefetchScalarGridSpec(
            num_scalar_prefetch=1,
            grid=(8,),
            in_specs=[
                full(gffn.shape),
                pl.BlockSpec((tokens, f), lambda s, t: (0, t[0] ^ (7 - s))),
            ],
            out_specs=[pl.BlockSpec((1, 4, 1, rows, half), index(ch)) for ch in range(2)],
        ),
        out_shape=[shape, shape],
        compiler_params=params(),
        cost_estimate=cost(16 * tokens * d * f, 20 << 20),
        name="reduce_grad",
    )(tok, gffn, act)


def rows_kernel(tok, *refs, groups):
    count = len(groups)
    lhs, refs = refs[:count], refs[count:]
    rhs = []
    for n in groups:
        rhs.append(refs[:n])
        refs = refs[n:]
    ga, gb = refs[:2]
    turned = refs[2:]
    rows = lhs[0].shape[1] // 8
    half = rows // 2

    @pl.when(pl.program_id(0) == 0)
    def _():
        for a, b in zip(lhs, turned):
            for r in range(8):
                start = pl.multiple_of((tok[0] ^ r) * rows, rows)
                b[:, r * rows : (r + 1) * rows] = a[:, pl.ds(start, rows)]

    at = 0
    for a, blocks in zip(turned, rhs):
        for block in blocks:
            block = block[...].reshape(block.shape[-2:])
            for n in range(0, block.shape[1], 512):
                piece = block[:, n : n + 512]
                g = dot(a[...], piece, TN).astype(BF)
                cols = slice(at, at + piece.shape[1])
                at += piece.shape[1]
                for r in range(8):
                    core, x, y = split_rel(r)
                    ga[core, 0, 2 * x + y, :, cols] = g[r * rows : r * rows + half]
                    gb[core, 0, 2 * y + x, :, cols] = g[r * rows + half : (r + 1) * rows]


def rows_part(tok, pairs, name):
    tokens, d = pairs[0][0].shape
    half = d // 16
    width = sum(spec.block_shape[-1] for _, _, specs in pairs for spec in specs)
    shape = jax.ShapeDtypeStruct((2, 4, 4, half, width), BF)
    out = pl.BlockSpec((2, 1, 4, half, width), lambda s, t: (0, s, 0, 0, 0))
    return pl.pallas_call(
        functools.partial(rows_kernel, groups=[len(p[1]) for p in pairs]),
        grid_spec=pltpu.PrefetchScalarGridSpec(
            num_scalar_prefetch=1,
            grid=(4,),
            in_specs=[full(p[0].shape) for p in pairs] + [s for p in pairs for s in p[2]],
            out_specs=[out, out],
            scratch_shapes=[pltpu.VMEM((tokens, d), BF) for _ in pairs],
        ),
        out_shape=[shape, shape],
        compiler_params=params(),
        cost_estimate=cost(8 * tokens * d * width, 24 << 20),
        name=name,
    )(tok, *[p[0] for p in pairs], *[r for p in pairs for r in p[1]])


def flip_tok(value, bit, size):
    return lax.ppermute(value, "tok", [(i, i ^ bit) for i in range(size)])


def shift_tab(value, shift, size):
    return lax.ppermute(value, "tab", [(i, (i + shift) % size) for i in range(size)])


def small_sum(value, n_tok, n_tab):
    bit = 1
    while bit < n_tok:
        value = value + flip_tok(value, bit, n_tok)
        bit *= 2
    total = value
    for shift in range(1, n_tab):
        total = total + shift_tab(value, shift, n_tab)
    return total


def body(
    n_tok, n_tab,
    embedded, cell_index, cell_boxes, box_tables, joined_weight, output_weight,
    expand_weight, reduce_weight, hidden_bias, bias_rows, norm_gains, norm_shifts, cotangent,
):
    tokens, width = embedded.shape
    pages, length = cell_index.shape
    table_rows = box_tables.shape[1]
    ff = expand_weight.shape[1]
    tok = lax.axis_index("tok").astype(jnp.int32).reshape(1)
    z = lax.axis_index("tab")
    cubic = n_tok == 8 and n_tab == 4

    corners = cell_boxes[:, :, :CELLS]
    lo = lambda n: jnp.minimum(corners[:, n], corners[:, n + 2]).reshape(-1)
    hi = lambda n: jnp.maximum(corners[:, n], corners[:, n + 2]).reshape(-1)
    left, right, top, bottom = lo(0), hi(0), lo(1), hi(1)
    none = jnp.full_like(left, -1)
    index_table = jnp.stack(
        [
            jnp.stack([left, right]),
            jnp.stack([top, bottom]),
            jnp.stack([right - left, none]),
            jnp.stack([bottom - top, none]),
        ]
    )
    pick_table = lambda i: lax.dynamic_index_in_dim(index_table, i, 0, keepdims=False)
    group_index = jnp.stack(
        [pick_table(z)]
        + [shift_tab(pick_table((z + s) % n_tab), s, n_tab) for s in range(1, n_tab)]
    )
    padded = jnp.pad(box_tables[0], ((0, 1024 - table_rows), (0, 0)))
    found = lookup(group_index, padded)
    terms = [found[0]] + [shift_tab(found[s], n_tab - s, n_tab) for s in range(1, n_tab)]

    q, k, v, normed, normed_low, rstd0 = embed(
        embedded, cell_index, terms, joined_weight, norm_gains, norm_shifts, bias_rows
    )
    mixed, lse = attn_fwd(q, k, v, pages)
    layer_out, after, after_low, rstd1, act, slope, gs2, gffn, sums2 = ffn_fwd(
        mixed, normed, output_weight, expand_weight, reduce_weight, hidden_bias,
        bias_rows, norm_gains, norm_shifts, cotangent, min(256, tokens),
    )
    quarter = width // 4
    parts = reduce_part(tok, gffn, act) if cubic else None
    gh, gs1, gattn, gmixed, hidden_sum, sums1, *reduce_sum = ffn_bwd(
        gffn, slope, gs2, after, rstd1, reduce_weight, expand_weight, output_weight,
        norm_gains, norm_shifts, parts,
    )
    if cubic:
        columns = lambda n: pl.BlockSpec((tokens, n), lambda s, t: (0, s))
        parts = rows_part(
            tok,
            [(after_low, [gh], [columns(ff // 4)]), (mixed, [gattn], [columns(quarter)])],
            "expand_output_grad",
        )
    embedded_grad, cell_grad, sums0, sums_qv, *more = back(
        q, k, v, mixed, gmixed, lse, normed_low, gs1, joined_weight, normed, rstd0, cell_index,
        norm_gains, norm_shifts, parts,
    )
    if cubic:
        parts, expand_sum = more[:2], more[2:]
    else:
        gj = more[0]

    small = jnp.concatenate(
        [
            sums0.reshape(-1), sums1.reshape(-1), sums2.reshape(-1),
            sums_qv.reshape(-1), hidden_sum.reshape(-1),
        ]
    ).reshape(-1, 128)
    if cubic:
        done, joined_sum, small = closing(cell_grad, group_index, small, parts)
        tables_grad = table_out(done, table_rows)
    else:
        cell_grads = [cell_grad] + [shift_tab(cell_grad, s, n_tab) for s in range(1, n_tab)]
        part_a, part_b = table_part(jnp.zeros_like(tok), group_index, cell_grads, 8)
        both = jnp.concatenate([part_a, part_b], axis=2).astype(F32)
        tables_grad = lax.psum(both.reshape(1, -1, width)[:, :table_rows], "tok")
        small = small_sum(small, n_tok, n_tab)
    small = small.reshape(-1)
    row = small.reshape(-1, width)
    gains_grad = jnp.stack([row[0], row[2], row[5]])
    shifts_grad = jnp.stack([row[1], row[3], row[6]])
    biases_grad = jnp.stack([row[8], row[9], row[4], row[7]])
    hidden_bias_grad = small[10 * width :]

    if cubic:
        reduce_grad = jnp.concatenate([reduce_sum[0][0], reduce_sum[0][1]], axis=1).T
        expand_sum = expand_sum[0].reshape(-1, expand_sum[0].shape[2])
        expand_grad = expand_sum[:, : ff // 4]
        output_grad = expand_sum[:, ff // 4 :]
        joined_grad = joined_sum.reshape(-1, joined_sum.shape[2])
    else:
        both = lambda a, b: jnp.einsum("ta,tb->ab", a, b, preferred_element_type=F32).astype(BF)

        def scattered(part):
            part = lax.psum_scatter(part, "tok", scatter_dimension=0, tiled=True)
            return lax.psum_scatter(part, "tab", scatter_dimension=1, tiled=True).astype(F32)

        reduce_grad = scattered(both(act, gffn))
        expand_grad = scattered(both(after_low, gh))
        output_grad = scattered(both(mixed, gattn))
        joined_grad = scattered(both(normed_low, jnp.concatenate([gj[0], gj[1], gj[2]], axis=1)))

    return (
        layer_out, embedded_grad, tables_grad, joined_grad, output_grad, expand_grad,
        reduce_grad, hidden_bias_grad, biases_grad, gains_grad, shifts_grad,
    )


def solution(mesh):
    rows = P(("tok", "tab"), None)
    return jax.shard_map(
        functools.partial(body, mesh.shape["tok"], mesh.shape["tab"]),
        mesh=mesh,
        in_specs=(
            rows, rows, P(("tok", "tab"), None, None), P("tab", None, None),
            P(), P(), P(), P(), P(), P(), P(), P(), rows,
        ),
        out_specs=(
            rows, rows, P("tab", None, None), P("tok", "tab"), P("tok", "tab"),
            P("tok", "tab"), P("tok", "tab"), P(), P(), P(), P(),
        ),
        check_vma=False,
    )
```

```python
import functools

import jax
import jax.numpy as jnp
from jax import lax
from jax.experimental import pallas as pl
from jax.experimental.pallas import tpu as pltpu
from jax.sharding import PartitionSpec as P

HEADS = 16
HEAD_DIM = 64
CELLS = 128
EPSILON = 1e-05
SCALE = HEAD_DIM ** (-0.5)
LOG2E = 1.4426950408889634
F32 = jnp.float32
BF = jnp.bfloat16
NN = ((1,), (0,))
NT = ((1,), (1,))
TN = ((0,), (0,))
ANY = pl.ANY

TAIL_P = 0.305
TAIL_C = (
    0.12164194255155772,
    0.12243138164026345,
    0.10365178645525906,
    0.12022714029486306,
    -0.03641303195181058,
    0.1839499605096701,
    -0.15192310059752684,
    0.03643391798251271,
)


def dot(a, b, dims):
    return lax.dot_general(a, b, (dims, ((), ())), preferred_element_type=F32)


def params(**kw):
    return pltpu.CompilerParams(vmem_limit_bytes=60 << 20, **kw)


def cost(flops, nbytes, trans=0):
    return pl.CostEstimate(
        flops=int(flops), bytes_accessed=int(nbytes), transcendentals=int(trans)
    )


def full(shape):
    zeros = (0,) * len(shape)
    return pl.BlockSpec(shape, lambda *_: zeros, pipeline_mode=pl.Buffered(1))


def gelu_parts(h):
    a = jnp.abs(h)
    t = 1.0 / (1.0 + TAIL_P * a)
    poly = jnp.full_like(t, TAIL_C[-1])
    for c in TAIL_C[-2::-1]:
        poly = poly * t + c
    e = jnp.exp2(h * h * (-0.5 * LOG2E))
    tail = poly * t * e
    phi_cdf = jnp.where(h > 0, 1.0 - tail, tail)
    act = h * phi_cdf
    slope = phi_cdf + h * e * 0.3989422804014327
    return act, slope


def norm_stats(v):
    mean = jnp.mean(v, axis=-1, keepdims=True)
    centred = v - mean
    var = jnp.mean(centred * centred, axis=-1, keepdims=True)
    rstd = lax.rsqrt(var + EPSILON)
    return centred * rstd, rstd


def norm_back(y, xh, rstd, gain):
    u = y * gain
    return (
        u - jnp.mean(u, axis=-1, keepdims=True) - xh * jnp.mean(u * xh, axis=-1, keepdims=True)
    ) * rstd


def colsum(v):
    return jnp.sum(v, axis=0, keepdims=True)


def lookup_kernel(idx, table, out):
    rows = table.shape[0]
    count = idx.shape[2]
    number = lax.broadcasted_iota(jnp.int32, (rows, count), 0)
    first = (number == idx[0, 0:1, :]).astype(F32)
    second = (number == idx[0, 1:2, :]).astype(F32)
    out[0] = dot((first + second).astype(BF), table[...], TN).astype(BF)


def lookup(idx, table):
    groups, _, count = idx.shape
    rows, width = table.shape
    return pl.pallas_call(
        lookup_kernel,
        grid=(groups,),
        in_specs=[
            pl.BlockSpec((1, 2, count), lambda i: (i, 0, 0)),
            full((rows, width)),
        ],
        out_specs=pl.BlockSpec((1, count, width), lambda i: (i, 0, 0)),
        out_shape=jax.ShapeDtypeStruct((groups, count, width), BF),
        compiler_params=params(),
        cost_estimate=cost(2 * groups * count * rows * width, 2 * groups * count * width),
        name="lookup",
    )(idx, table)


def embed_kernel(
    emb, ci, t0, t1, t2, t3, w, gains, shifts, bias, q, k, v, normed, low, rstd_out
):
    width = emb.shape[1]
    tokens = emb.shape[0]
    cells = jnp.concatenate([t0[...], t1[...], t2[...], t3[...]], axis=0)
    number = lax.broadcasted_iota(jnp.int32, (CELLS, tokens), 0)
    pick = (number == ci[0]).astype(F32).astype(BF)
    pick = jnp.concatenate([pick] * 4, axis=0)
    box = dot(pick, cells, TN)
    xh, rstd = norm_stats(emb[...].astype(F32) + box)
    y = xh * gains[0:1] + shifts[0:1]
    normed[...] = y
    rstd_out[...] = rstd
    y_low = y.astype(BF)
    low[...] = y_low
    q[...] = ((dot(y_low, w[:, :width], NN) + bias[0:1]) * SCALE).astype(BF)
    k[...] = dot(y_low, w[:, width : 2 * width], NN).astype(BF)
    v[...] = (dot(y_low, w[:, 2 * width :], NN) + bias[1:2]).astype(BF)


def embed(emb, ci, terms, w, gains, shifts, bias):
    tokens, width = emb.shape
    pages, length = ci.shape
    rows = pl.BlockSpec((length, width), lambda i: (i, 0))
    cell_rows = pl.BlockSpec((CELLS, width), lambda i: (i, 0))
    shape = lambda dt, n=width: jax.ShapeDtypeStruct((tokens, n), dt)
    return pl.pallas_call(
        embed_kernel,
        grid=(pages,),
        in_specs=[rows, pl.BlockSpec((1, 1, length), lambda i: (i, 0, 0))]
        + [cell_rows] * 4
        + [full(w.shape), full(gains.shape), full(shifts.shape), full(bias.shape)],
        out_specs=[rows] * 5 + [pl.BlockSpec((length, 1), lambda i: (i, 0))],
        out_shape=[shape(BF), shape(BF), shape(BF), shape(F32), shape(BF), shape(F32, 1)],
        compiler_params=params(),
        cost_estimate=cost(2 * tokens * width * 3 * width, 26 << 20),
        name="embed_joined",
    )(emb, ci.reshape(pages, 1, length), *terms, w, gains, shifts, bias)


STAGES = 4


def neighbours():
    tok, z = lax.axis_index("tok"), lax.axis_index("tab")
    core = {"tok": tok + 1 - 2 * (tok % 2)}
    x = {"tok": tok + 2 - 4 * ((tok // 2) % 2)}
    y = {"tok": tok + 4 - 8 * (tok // 4)}
    peers = [{"tab": (z + s) % 4} for s in range(1, 4)]
    return core, x, y, peers


def meet(devices):
    barrier = pltpu.get_barrier_semaphore()
    for d in devices:
        pl.semaphore_signal(barrier, inc=1, device_id=d, device_id_type=pl.DeviceIdType.MESH)
    pl.semaphore_wait(barrier, len(devices))


def sum_scratch(rows, cols):
    part = lambda *n: pltpu.VMEM((*n, rows, cols), BF)
    return [
        part(2, 4, 4), part(2, 4, 4), part(2, 4, 2), part(2, 4), part(2, 3),
        pltpu.SemaphoreType.DMA((2, 4)),
        pltpu.SemaphoreType.DMA((STAGES, 2, 4)),
        pltpu.SemaphoreType.DMA((STAGES, 2, 4)),
    ]


class Summing:
    def __init__(self, grads, out, scratch):
        self.grads, self.out = grads, out
        if grads is None:
            both, scratch = scratch[0], (scratch[0].at[0], *scratch[1:5], None, *scratch[5:])
            self.part = both.at[1]
        self.own, self.r0, self.r1, self.r2, self.r3, self.local, self.sent, self.got = scratch
        core, x, y, peers = neighbours()
        self.core, self.first, self.second, self.peers = core, (x, y), (y, x), peers
        self.z = lax.axis_index("tab")

    def devices(self):
        return [self.core, self.first[0], self.first[1], *self.peers]

    def copy(self, stage, ch, i):
        zc = (self.z + (i + 1)) % 4
        src, dst, to = (
            (
                lambda: self.part.at[ch, i] if self.grads is None else self.grads[ch].at[1, zc],
                self.r0.at[ch, i],
                self.core,
            ),
            (lambda: self.own.at[ch, i, pl.ds(2, 2)], self.r1.at[ch, i], self.first[ch]),
            (lambda: self.own.at[ch, i, 1], self.r2.at[ch, i], self.second[ch]),
            (lambda: self.own.at[ch, i, 0], self.r3.at[ch, min(i, 2)], self.peers[min(i, 2)]),
        )[stage]
        return pltpu.make_async_remote_copy(
            src_ref=src(), dst_ref=dst,
            send_sem=self.sent.at[stage, ch, i], recv_sem=self.got.at[stage, ch, i],
            device_id=to, device_id_type=pl.DeviceIdType.MESH,
        )

    def load(self, ch, i):
        zc = (self.z + (i + 1)) % 4
        return pltpu.make_async_copy(
            self.grads[ch].at[0, zc], self.own.at[ch, i], self.local.at[ch, i]
        )

    def start(self):
        for i in range(4):
            for ch in range(2):
                self.copy(0, ch, i).start()
                if self.grads is not None:
                    self.load(ch, i).start()

    def step(self, stage, i):
        for ch in range(2):
            self.copy(stage - 1, ch, i).wait_recv()
            if stage == 1:
                if self.grads is not None:
                    self.load(ch, i).wait()

                def add(j, _, ch=ch):
                    self.own[ch, i, j] = self.own[ch, i, j] + self.r0[ch, i, j]
                    return 0

                lax.fori_loop(0, 4, add, 0)
            elif stage == 2:

                def add(j, _, ch=ch):
                    self.own[ch, i, j] = self.own[ch, i, j] + self.r1[ch, i, j]
                    return 0

                lax.fori_loop(0, 2, add, 0)
            elif i < 3:
                self.own[ch, i, 0] = self.own[ch, i, 0] + self.r2[ch, i]
            if stage < 3 or i < 3:
                self.copy(stage, ch, i).start()

    def finish(self):
        for ch in range(2):
            total = self.own[ch, 3, 0].astype(F32) + self.r2[ch, 3].astype(F32)
            for i in range(3):
                self.copy(3, ch, i).wait_recv()
                total = total + self.r3[ch, i].astype(F32)
            self.out[ch] = total
        for stage in range(STAGES):
            for ch in range(2):
                for i in range(4 if stage < 3 else 3):
                    self.copy(stage, ch, i).wait_send()

    def run(self, step, plan):
        for at, events in plan.items():

            @pl.when(step == at)
            def _(events=events):
                for stage, i in events:
                    if stage == 0:
                        self.start()
                    elif stage == 4:
                        self.finish()
                    else:
                        self.step(stage, i)


def split_rel(r):
    return r & 1, (r >> 1) & 1, r >> 2


def rel_of(b):
    tok = lax.axis_index("tok")
    core, x, y = split_rel(b)
    flip = lambda static, mine: 1 - mine if static else mine
    return flip(core, tok % 2), flip(x, (tok // 2) % 2), flip(y, tok // 4)


def put_rows(g, ga, gb, cols, rows):
    half = rows // 2
    for b in range(8):
        core, x, y = rel_of(b)
        ga[core, 0, 2 * x + y, :, cols] = g[b * rows : b * rows + half]
        gb[core, 0, 2 * y + x, :, cols] = g[b * rows + half : (b + 1) * rows]


def sum_specs(grads, number):
    if grads is None:
        return [], [], [], [], {}
    rows, cols = grads[0].shape[3:]
    return (
        [pl.BlockSpec(memory_space=pl.ANY)] * 2,
        [full((2, rows, cols))],
        [jax.ShapeDtypeStruct((2, rows, cols), F32)],
        sum_scratch(rows, cols),
        {"has_side_effects": True, "collective_id": number},
    )


HP = 4


def head_masks(length, pair):
    lane = lax.broadcasted_iota(jnp.int32, (length, pair), 1)
    return lane < HEAD_DIM


def attn_fwd_kernel(q, k, v, mixed, lse):
    length = q.shape[0]
    pair = 2 * HEAD_DIM
    low_half = head_masks(length, pair)
    zero = jnp.zeros((length, pair), BF)
    for p in range(HP // 2):
        cols = slice(p * pair, (p + 1) * pair)
        qp, kp, vp = q[:, cols], k[:, cols], v[:, cols]
        vt = vp.T
        outs = []
        for h in range(2):
            km = jnp.where(low_half, kp, zero) if h == 0 else jnp.where(low_half, zero, kp)
            st = dot(km, qp, NT)
            top = jnp.max(st, axis=0, keepdims=True)
            raised = jnp.exp2((st - top) * LOG2E)
            total = jnp.sum(raised, axis=0, keepdims=True)
            lse[0, 0, 2 * p + h : 2 * p + h + 1, :] = top + jnp.log(total)
            ot = dot(vt[h * HEAD_DIM : (h + 1) * HEAD_DIM], raised.astype(BF), NN)
            outs.append(ot * (1.0 / total))
        mixed[:, cols] = jnp.concatenate(outs, axis=0).T.astype(BF)


def attn_fwd(q, k, v, pages):
    tokens, width = q.shape
    length = tokens // pages
    steps = HEADS // HP
    blk = pl.BlockSpec((length, HP * HEAD_DIM), lambda i, j: (i, j))
    return pl.pallas_call(
        attn_fwd_kernel,
        grid=(pages, steps),
        in_specs=[blk] * 3,
        out_specs=[blk, pl.BlockSpec((1, 1, HP, length), lambda i, j: (i, j, 0, 0))],
        out_shape=[
            jax.ShapeDtypeStruct((tokens, width), BF),
            jax.ShapeDtypeStruct((pages, steps, HP, length), F32),
        ],
        compiler_params=params(),
        cost_estimate=cost(14e9, 8 << 20, pages * HEADS * length * length),
        name="attention",
    )(q, k, v)


def attn_back(q, k, v, mixed, go, lse, put):
    length = q.shape[0]
    pair = 2 * HEAD_DIM
    low_half = head_masks(length, pair)
    zero = jnp.zeros((length, pair), BF)

    def pick(x, h):
        return jnp.where(low_half, x, zero) if h == 0 else jnp.where(low_half, zero, x)

    for p in range(HP // 2):
        cols = slice(p * pair, (p + 1) * pair)
        qp, kp, vp, op, gp = q[:, cols], k[:, cols], v[:, cols], mixed[:, cols], go[:, cols]
        kt = kp.T
        prod_t = (op.astype(F32) * gp.astype(F32)).T
        dq_t, dk, dv = [], None, None
        for h in range(2):
            st = dot(pick(kp, h), qp, NT)
            probs = jnp.exp2((st - lse[0, 0, 2 * p + h : 2 * p + h + 1, :]) * LOG2E)
            dv_h = dot(probs.astype(BF), pick(gp, h), NN)
            dpt = dot(pick(vp, h), gp, NT)
            delta = colsum(prod_t[h * HEAD_DIM : (h + 1) * HEAD_DIM])
            ds = (probs * (dpt - delta)).astype(BF)
            dk_h = dot(ds, pick(qp, h), NN)
            dq_t.append(dot(kt[h * HEAD_DIM : (h + 1) * HEAD_DIM], ds, NN))
            dv = dv_h if dv is None else dv + dv_h
            dk = dk_h if dk is None else dk + dk_h
        dq = (jnp.concatenate(dq_t, axis=0).T.astype(BF).astype(F32) * SCALE).astype(BF)
        put(p * pair, pair, dq, dk.astype(BF), dv.astype(BF))


FC = 512
FWD = 1024
RC = 128
MC = 512


def ffn_fwd_kernel(
    mixed, normed, wo, we, wr, hb, bias, gains, shifts, cot,
    out, after_out, low_out, rstd_out, act_out, slope_out, gs2_out, gffn_out, sums,
):
    ff = we.shape[1]
    attn_sum = normed[...] + (dot(mixed[...], wo[...], NN) + bias[2:3])
    xh, rstd = norm_stats(attn_sum)
    after = xh * gains[1:2] + shifts[1:2]
    after_out[...] = after
    rstd_out[...] = rstd
    low = after.astype(BF)
    low_out[...] = low
    total = after + bias[3:4]
    for j in range(ff // FWD):
        cols = slice(j * FWD, (j + 1) * FWD)
        act, slope = gelu_parts(dot(low, we[:, cols], NN) + hb[:, cols])
        act = act.astype(BF)
        act_out[:, cols] = act
        slope_out[:, cols] = slope.astype(BF)
        total = total + dot(act, wr[cols, :], NN)
    xh, rstd = norm_stats(total)
    out[...] = (xh * gains[2:3] + shifts[2:3]).astype(BF)
    y = cot[...].astype(F32)
    gs2 = norm_back(y, xh, rstd, gains[2:3])
    gs2_out[...] = gs2
    gffn = gs2.astype(BF)
    gffn_out[...] = gffn
    part = jnp.concatenate([colsum(y * xh), colsum(y), colsum(gffn.astype(F32))], axis=0)

    @pl.when(pl.program_id(0) == 0)
    def _():
        sums[...] = part

    @pl.when(pl.program_id(0) != 0)
    def _():
        sums[...] = sums[...] + part


def ffn_fwd(mixed, normed, wo, we, wr, hb, bias, gains, shifts, cot, tile):
    tokens, width = mixed.shape
    ff = we.shape[1]
    rows = pl.BlockSpec((tile, width), lambda i: (i, 0))
    long = pl.BlockSpec((tile, ff), lambda i: (i, 0))
    shape = lambda dt, n=width: jax.ShapeDtypeStruct((tokens, n), dt)
    hb = hb.reshape(1, ff)
    return pl.pallas_call(
        ffn_fwd_kernel,
        grid=(tokens // tile,),
        in_specs=[rows, rows]
        + [full(a.shape) for a in (wo, we, wr, hb, bias, gains, shifts)]
        + [rows],
        out_specs=[rows, rows, rows, pl.BlockSpec((tile, 1), lambda i: (i, 0)), long, long, rows, rows]
        + [pl.BlockSpec((3, width), lambda i: (0, 0))],
        out_shape=[
            shape(BF), shape(F32), shape(BF), shape(F32, 1), shape(BF, ff), shape(BF, ff),
            shape(F32), shape(BF), jax.ShapeDtypeStruct((3, width), F32),
        ],
        compiler_params=params(),
        cost_estimate=cost(2 * tokens * width * (width + 2 * ff), 60 << 20, tokens * ff * 2),
        name="ffn_forward",
    )(mixed, normed, wo, we, wr, hb, bias, gains, shifts, cot)


def second_norm_back(gs1_out, after, rstd, gains, shifts, gattn_out, sums):
    tokens, width = after.shape

    def norm(i, carry):
        rows = pl.ds(pl.multiple_of(i * RC, RC), RC)
        total = gs1_out[rows, :]
        xh = (after[rows, :] - shifts[1:2]) * (1.0 / gains[1:2])
        gs1 = norm_back(total, xh, rstd[rows, :], gains[1:2])
        gs1_out[rows, :] = gs1
        gattn = gs1.astype(BF)
        gattn_out[rows, :] = gattn
        g, s, b = carry
        return g + colsum(total * xh), s + colsum(total), b + colsum(gattn.astype(F32))

    zero = jnp.zeros((1, width), F32)
    sums[...] = jnp.concatenate(lax.fori_loop(0, tokens // RC, norm, (zero, zero, zero)), axis=0)


def ffn_bwd_kernel(
    gffn, gs2, after, rstd, wo, gains, shifts, slope, wr, we,
    gh_out, gs1_out, gattn_out, gmixed_out, hsum, sums,
):
    step, last = pl.program_id(0), pl.num_programs(0) - 1
    tokens, width = gffn.shape

    @pl.when(step == 0)
    def _():
        gs1_out[...] = gs2[...]

    part = jnp.zeros((1, slope.shape[1]), F32)
    for m in range(0, tokens, MC):
        rows = slice(m, m + MC)
        gh = (dot(gffn[rows, :], wr[...], NT) * slope[rows, :].astype(F32)).astype(BF)
        gh_out[rows, :] = gh
        part = part + colsum(gh.astype(F32))
        gs1_out[rows, :] = gs1_out[rows, :] + dot(gh, we[...], NT)
    hsum[...] = part

    @pl.when(step == last)
    def _():
        second_norm_back(gs1_out, after, rstd, gains, shifts, gattn_out, sums)
        for m in range(0, tokens, MC):
            rows = slice(m, m + MC)
            gmixed_out[rows, :] = dot(gattn_out[rows, :], wo[...], NT).astype(BF)


def ffn_bwd(gffn, slope, gs2, after, rstd, wr, we, wo, gains, shifts):
    tokens, width = gffn.shape
    ff = we.shape[1]
    whole = full((tokens, width))
    long = pl.BlockSpec((tokens, FC), lambda s: (0, s))
    shape = lambda dt, n=width: jax.ShapeDtypeStruct((tokens, n), dt)
    return pl.pallas_call(
        ffn_bwd_kernel,
        grid=(ff // FC,),
        in_specs=[whole, whole, whole, full((tokens, 1))]
        + [full(a.shape) for a in (wo, gains, shifts)]
        + [
            long,
            pl.BlockSpec((FC, width), lambda s: (s, 0)),
            pl.BlockSpec((width, FC), lambda s: (0, s)),
        ],
        out_specs=[long, whole, whole, whole]
        + [pl.BlockSpec((1, FC), lambda s: (0, s)), full((3, width))],
        out_shape=[
            shape(BF, ff), shape(F32), shape(BF), shape(BF),
            jax.ShapeDtypeStruct((1, ff), F32), jax.ShapeDtypeStruct((3, width), F32),
        ],
        compiler_params=params(),
        cost_estimate=cost(2 * tokens * width * (width + 2 * ff), 60 << 20),
        name="ffn_backward",
    )(gffn, gs2, after, rstd, wo, gains, shifts, slope, wr, we)


FFN_PLAN = {
    4: [(0, 0)],
    8: [(1, 0), (1, 1)],
    10: [(2, 0), (1, 2)],
    11: [(2, 1), (1, 3)],
    12: [(3, 0)],
    13: [(2, 2)],
    14: [(3, 1)],
    15: [(2, 3)],
    16: [(3, 2)],
    17: [(3, 3)],
}
N_TOK, N_TAB = 8, 4


def block_of_step(s):
    s = jnp.minimum(s, N_TOK - 1)
    return 1 - s // 4, 1 - (s // 2) % 2, 1 - s % 2


def ffn_grads_kernel(
    gffn_in, gs2_in, after, rstd, low, mixed, wo, gains, shifts, act, slope, wr, we,
    gs1_out, gmixed_out, hsum, sums, ga, gb, reduce_out,
    gffn, gh, local, *scratch,
):
    step, last = pl.program_id(0), pl.num_programs(0) - 1
    tokens, width = after.shape
    summing = Summing(None, reduce_out, scratch)
    both = scratch[0]
    z = lax.axis_index("tab")
    first = pltpu.make_async_copy(gffn_in, gffn, local.at[0])
    later = pltpu.make_async_copy(gs2_in, gs1_out, local.at[1])

    @pl.when(step == 0)
    def _():
        first.start()
        later.start()
        meet(summing.devices())
        first.wait()

    @pl.when(step == N_TOK)
    def _():
        later.wait()

    summing.run(step, FFN_PLAN)

    @pl.when(step < N_TOK)
    def _():
        core, x, y = block_of_step(step)
        g = dot(gffn[...], act[...], TN).astype(BF)
        rows, half = both.shape[4:]
        for zc in range(N_TAB):
            i = (zc + N_TAB - 1 - z) % N_TAB
            for ch in range(2):
                piece = g[zc * rows : (zc + 1) * rows, ch * half : (ch + 1) * half]
                both[core, ch, i, (2 * x + y, 2 * y + x)[ch]] = piece

    @pl.when((step >= N_TOK) & (step < 2 * N_TOK))
    def _():
        part = jnp.zeros((1, slope.shape[1]), F32)
        for m in range(0, tokens, MC):
            rows = slice(m, m + MC)
            g = (dot(gffn[rows, :], wr[...], NT) * slope[rows, :].astype(F32)).astype(BF)
            gh[step - N_TOK, rows, :] = g
            part = part + colsum(g.astype(F32))
            gs1_out[rows, :] = gs1_out[rows, :] + dot(g, we[...], NT)
        hsum[...] = part

    @pl.when(step == 2 * N_TOK - 1)
    def _():
        second_norm_back(gs1_out, after, rstd, gains, shifts, gffn, sums)
        for m in range(0, tokens, MC):
            rows = slice(m, m + MC)
            gmixed_out[rows, :] = dot(gffn[rows, :], wo[...], NT).astype(BF)

    @pl.when(step >= 2 * N_TOK)
    def _():
        n = step - 2 * N_TOK
        quarter = width // N_TAB
        rows = width // N_TOK
        wide = gh.shape[2]
        for m in range(2):
            g = dot(low[...], gh[2 * n + m], TN).astype(BF)
            put_rows(g, ga, gb, slice(m * wide, (m + 1) * wide), rows)
        piece = gffn[:, pl.ds(pl.multiple_of(n * quarter, quarter), quarter)]
        g = dot(mixed[...], piece, TN).astype(BF)
        put_rows(g, ga, gb, slice(2 * wide, 2 * wide + quarter), rows)

    @pl.when(step == last)
    def _():
        summing.finish()


def ffn_grads(gffn, act, slope, gs2, after, low, rstd, mixed, wr, we, wo, gains, shifts):
    tokens, width = gffn.shape
    ff = we.shape[1]
    whole = full((tokens, width))
    anywhere = pl.BlockSpec(memory_space=pl.ANY)
    wide = ff // N_TOK
    half = width // (2 * N_TOK)
    out_wide = (ff + width) // N_TAB
    back = lambda s: jnp.clip(s - N_TOK, 0, N_TOK - 1)
    grad = lambda s: jnp.clip(s - 2 * N_TOK, 0, N_TAB - 1)

    def act_block(s):
        core, x, y = block_of_step(s)
        tok = lax.axis_index("tok")
        flip = lambda rel, mine: rel + mine - 2 * rel * mine
        return 0, 4 * flip(y, tok // 4) + 2 * flip(x, (tok // 2) % 2) + flip(core, tok % 2)

    rows, cols = width // N_TAB, wide // 2
    part = lambda *n: pltpu.VMEM((*n, rows, cols), BF)
    dma = pltpu.SemaphoreType.DMA
    shape = lambda dt: jax.ShapeDtypeStruct((tokens, width), dt)
    piece = pl.BlockSpec((2, 1, 4, half, out_wide), lambda s: (0, grad(s), 0, 0, 0))
    return pl.pallas_call(
        ffn_grads_kernel,
        grid=(2 * N_TOK + N_TAB,),
        in_specs=[anywhere, anywhere, whole, full((tokens, 1)), whole, whole]
        + [full(a.shape) for a in (wo, gains, shifts)]
        + [
            pl.BlockSpec((tokens, wide), act_block),
            pl.BlockSpec((tokens, wide), lambda s: (0, back(s))),
            pl.BlockSpec((wide, width), lambda s: (back(s), 0)),
            pl.BlockSpec((width, wide), lambda s: (0, back(s))),
        ],
        out_specs=[
            whole, whole, pl.BlockSpec((1, wide), lambda s: (0, back(s))), full((3, width)),
            piece, piece, full((2, rows, cols)),
        ],
        out_shape=[
            shape(F32), shape(BF),
            jax.ShapeDtypeStruct((1, ff), F32), jax.ShapeDtypeStruct((3, width), F32),
            jax.ShapeDtypeStruct((2, 4, 4, half, out_wide), BF),
            jax.ShapeDtypeStruct((2, 4, 4, half, out_wide), BF),
            jax.ShapeDtypeStruct((2, rows, cols), F32),
        ],
        scratch_shapes=[
            pltpu.VMEM((tokens, width), BF), pltpu.VMEM((N_TOK, tokens, wide), BF), dma((2,)),
            part(2, 2, 4, 4), part(2, 4, 4), part(2, 4, 2), part(2, 4), part(2, 3),
            dma((STAGES, 2, 4)), dma((STAGES, 2, 4)),
        ],
        compiler_params=pltpu.CompilerParams(
            vmem_limit_bytes=67043328, has_side_effects=True, collective_id=1
        ),
        cost_estimate=cost(2 * tokens * width * (2 * width + 4 * ff), 60 << 20),
        name="ffn_backward_grads",
    )(gffn, gs2, after, rstd, low, mixed, wo, gains, shifts, act, slope, wr, we)


BACK_PLAN = {
    0: [(0, 0)],
    1: [(1, 0)],
    2: [(1, 1)],
    3: [(2, 0), (1, 2)],
    5: [(2, 1), (1, 3)],
    6: [(3, 0)],
    8: [(2, 2)],
    9: [(3, 1)],
    11: [(2, 3)],
    12: [(3, 2)],
    13: [(3, 3)],
}


def back_kernel(*refs, pages, summed):
    q, k, v, mixed, go, lse, low, gs1, w, normed, rstd, ci, gains, shifts = refs[:14]
    refs = refs[14:]
    grads, refs = refs[: 2 * summed], refs[2 * summed :]
    out, cells, sums0, sums_qv = refs[:4]
    refs = refs[4:]
    if summed:
        ga, gb, summed_out, gj = refs[:4]
        summing = Summing(grads, summed_out, refs[4:])
    else:
        gj_out, gj = refs
    step = pl.program_id(0)
    width = gs1.shape[1]
    length = q.shape[0]
    groups = HEADS // HP
    wide = HP * HEAD_DIM
    n_attn = groups * pages
    n_joined = 4 if summed else 0

    if summed:

        @pl.when(step == 0)
        def _():
            meet(summing.devices())

        summing.run(step, BACK_PLAN)

    @pl.when(step < n_attn)
    def _():
        group, page = step // pages, step % pages
        rows = pl.ds(pl.multiple_of(page * length, length), length)

        def put(at, size, dq, dk, dv):
            cols = pl.ds(pl.multiple_of(group * wide + at, size), size)
            gj[0, rows, cols] = dq
            gj[1, rows, cols] = dk
            gj[2, rows, cols] = dv
            part = jnp.concatenate([colsum(dq.astype(F32)), colsum(dv.astype(F32))], axis=0)

            @pl.when(page == 0)
            def _():
                sums_qv[:, cols] = part

            @pl.when(page != 0)
            def _():
                sums_qv[:, cols] = sums_qv[:, cols] + part

        attn_back(q, k, v, mixed, go, lse, put)

    if summed:
        quarter = width // 4
        for n in range(n_joined):

            @pl.when(step == n_attn + n)
            def _(n=n):
                for m in range(3):
                    third, at = (3 * n + m) // 4, (3 * n + m) % 4
                    piece = gj[third, :, at * quarter : (at + 1) * quarter]
                    g = dot(low[...], piece, TN).astype(BF)
                    put_rows(g, ga, gb, slice(m * quarter, (m + 1) * quarter), width // 8)

    @pl.when(step >= n_attn + n_joined)
    def _():
        page = step - (n_attn + n_joined)
        rows = pl.ds(pl.multiple_of(page * length, length), length)
        total = gs1[...]
        for n in range(3):
            total = total + dot(gj[n, rows, :], w[:, n * width : (n + 1) * width], NT)
        xh = (normed[...] - shifts[0:1]) * (1.0 / gains[0:1])
        grad = norm_back(total, xh, rstd[...], gains[0:1])
        out[...] = grad
        number = lax.broadcasted_iota(jnp.int32, (CELLS, length), 0)
        pick = (number == ci[0]).astype(F32).astype(BF)
        cells[...] = dot(pick, grad.astype(BF), NN).astype(BF)
        part = jnp.concatenate([colsum(total * xh), colsum(total)], axis=0)

        @pl.when(page == 0)
        def _():
            sums0[...] = part

        @pl.when(page != 0)
        def _():
            sums0[...] = sums0[...] + part

    if summed:

        @pl.when(step == pl.num_programs(0) - 1)
        def _():
            summing.finish()
    else:
        gj_out[...] = gj[...]


def back(q, k, v, mixed, go, lse, low, gs1, w, normed, rstd, ci, gains, shifts, grads):
    tokens, width = q.shape
    pages, length = ci.shape
    groups = HEADS // HP
    wide = HP * HEAD_DIM
    summed = grads is not None
    n_attn = groups * pages
    before = n_attn + (4 if summed else 0)
    at = lambda s: jnp.minimum(s, n_attn - 1)
    page = lambda s: jnp.maximum(s - before, 0)
    block = lambda s: jnp.clip(s - n_attn, 0, 3)
    blk = pl.BlockSpec((length, wide), lambda s: (at(s) % pages, at(s) // pages))
    rows = pl.BlockSpec((length, width), lambda s: (page(s), 0))
    out_specs = [
        rows,
        pl.BlockSpec((CELLS, width), lambda s: (page(s), 0)),
        full((2, width)),
        full((2, width)),
    ]
    out_shape = [
        jax.ShapeDtypeStruct((tokens, width), F32),
        jax.ShapeDtypeStruct((pages * CELLS, width), BF),
        jax.ShapeDtypeStruct((2, width), F32),
        jax.ShapeDtypeStruct((2, width), F32),
    ]
    whole_gj = (3, tokens, width)
    more_in, more_out, more_shape, more_scratch, more = sum_specs(grads, 2)
    if summed:
        half = width // 16
        piece = pl.BlockSpec((2, 1, 4, half, 3 * width // 4), lambda s: (0, block(s), 0, 0, 0))
        out_specs += [piece, piece]
        out_shape += [jax.ShapeDtypeStruct((2, 4, 4, half, 3 * width // 4), BF)] * 2
    else:
        out_specs += [full(whole_gj)]
        out_shape += [jax.ShapeDtypeStruct(whole_gj, BF)]
    return pl.pallas_call(
        functools.partial(back_kernel, pages=pages, summed=summed),
        grid=(before + pages,),
        in_specs=[blk] * 5
        + [
            pl.BlockSpec((1, 1, HP, length), lambda s: (at(s) % pages, at(s) // pages, 0, 0)),
            full(low.shape),
            rows,
            full(w.shape),
            rows,
            pl.BlockSpec((length, 1), lambda s: (page(s), 0)),
            pl.BlockSpec((1, 1, length), lambda s: (page(s), 0, 0)),
            full(gains.shape),
            full(shifts.shape),
        ]
        + more_in,
        out_specs=out_specs + more_out,
        out_shape=out_shape + more_shape,
        scratch_shapes=[pltpu.VMEM(whole_gj, BF)] + more_scratch,
        compiler_params=params(**more),
        cost_estimate=cost(70e9, 40 << 20, pages * HEADS * length * length),
        name="attention_joined_embed_back",
    )(
        q, k, v, mixed, go, lse, low, gs1, w, normed, rstd, ci.reshape(pages, 1, length),
        gains, shifts, *(grads or ()),
    )


def table_kernel(tok, idx, g0, g1, g2, g3, out_a, out_b):
    rows = out_a.shape[1]
    count = idx.shape[2]
    half = out_a.shape[2]
    base = (pl.program_id(0) ^ tok[0]) * rows
    number = lax.broadcasted_iota(jnp.int32, (rows, count), 0) + base
    picks = []
    for s in range(4):
        first = (number == idx[s, 0:1, :]).astype(F32)
        second = (number == idx[s, 1:2, :]).astype(F32)
        picks.append((first + second).astype(BF))
    pick = jnp.concatenate(picks, axis=1)
    grads = jnp.concatenate([g0[...], g1[...], g2[...], g3[...]], axis=0)
    total = dot(pick, grads, NN).astype(BF)
    out_a[0] = total[:, :half]
    out_b[0] = total[:, half:]


def table_part(tok, idx, grads, blocks):
    groups, _, count = idx.shape
    width = grads[0].shape[1]
    rows = 1024 // blocks
    half = width // 2
    out = pl.BlockSpec((1, rows, half), lambda i, t: (i, 0, 0))
    return pl.pallas_call(
        table_kernel,
        grid_spec=pltpu.PrefetchScalarGridSpec(
            num_scalar_prefetch=1,
            grid=(blocks,),
            in_specs=[full(idx.shape)] + [full((count, width))] * groups,
            out_specs=[out, out],
        ),
        out_shape=[jax.ShapeDtypeStruct((blocks, rows, half), BF)] * 2,
        compiler_params=params(),
        cost_estimate=cost(2 * 1024 * groups * count * width, 4 << 20),
        name="table_grad",
    )(tok, idx, *grads)


BLOCK = 128


class TableSum:
    def __init__(self, scratch, done):
        self.part, self.r0, self.r1, self.r2, self.sent, self.got = scratch
        self.done = done
        tok = lax.axis_index("tok")
        core, x, y, _ = neighbours()
        self.c, cx, cy = tok % 2, (tok // 2) % 2, tok // 4
        self.core, self.first, self.second = core, (x, y), (y, x)
        self.f, self.g = (cx, cy), (cy, cx)

    def copy(self, stage, ch, u):
        c, f, g = self.c, self.f[ch], self.g[ch]
        part, done = self.part.at[ch, u], self.done.at[ch, u]
        src, dst, to = (
            (lambda: part.at[1 - c], self.r0.at[ch, u], self.core),
            (lambda: part.at[c, 1 - f], self.r1.at[ch, u], self.first[ch]),
            (lambda: part.at[c, f, 1 - g], self.r2.at[ch, u], self.second[ch]),
            (lambda: done.at[c, f, g], None, self.second[ch]),
            (lambda: done.at[c, f], None, self.first[ch]),
            (lambda: done.at[c], None, self.core),
        )[stage]
        src = src()
        return pltpu.make_async_remote_copy(
            src_ref=src, dst_ref=src if dst is None else dst,
            send_sem=self.sent.at[stage, ch, u], recv_sem=self.got.at[stage, ch, u],
            device_id=to, device_id_type=pl.DeviceIdType.MESH,
        )

    def store(self, u, ch, value):
        for b in range(8):
            c, x, y = split_rel(b)
            f, g = (x, y) if ch == 0 else (y, x)
            self.part[ch, u, c, f, g] = value[b * BLOCK : (b + 1) * BLOCK]
        self.copy(0, ch, u).start()

    def step(self, stage, u):
        for ch in range(2):
            c, f, g = self.c, self.f[ch], self.g[ch]
            self.copy(stage - 1, ch, u).wait_recv()
            if stage == 1:
                self.part[ch, u, c] = self.part[ch, u, c] + self.r0[ch, u]
            elif stage == 2:
                self.part[ch, u, c, f] = self.part[ch, u, c, f] + self.r1[ch, u]
            elif stage == 3:
                self.done[ch, u, c, f, g] = self.part[ch, u, c, f, g] + self.r2[ch, u]
            if stage < 6:
                self.copy(stage, ch, u).start()

    def finish(self):
        for stage in range(6):
            for ch in range(2):
                for u in range(2):
                    self.copy(stage, ch, u).wait_send()


def closing_kernel(
    cells, idx, small, ga, gb, done, joined, small_out,
    ring, total, ring_sent, ring_got, held, arrived, small_sent, small_got, *scratch,
):
    summing = Summing((ga, gb), joined, scratch[:8])
    table = TableSum(scratch[8:], done)
    core, x, y, peers = neighbours()
    z = lax.axis_index("tab")
    hops = [core, x, y, {"tab": z + 1 - 2 * (z % 2)}, {"tab": z + 2 - 4 * (z // 2)}]
    meet([core, x, y, *peers])
    count = cells.shape[0]
    half = cells.shape[1] // 2

    def pass_on(k, h):
        cols = pl.ds(h * half, half)
        src = cells.at[:, cols] if k == 0 else ring.at[k - 1, :, cols]
        return pltpu.make_async_remote_copy(
            src_ref=src, dst_ref=ring.at[k, :, cols],
            send_sem=ring_sent.at[k, h], recv_sem=ring_got.at[k, h],
            device_id=peers[0], device_id_type=pl.DeviceIdType.MESH,
        )

    def small_copy(n):
        return pltpu.make_async_remote_copy(
            src_ref=held.at[n], dst_ref=arrived.at[n],
            send_sem=small_sent.at[n], recv_sem=small_got.at[n],
            device_id=hops[n], device_id_type=pl.DeviceIdType.MESH,
        )

    def small_step(n):
        small_copy(n - 1).wait_recv()
        value = held[n - 1] + arrived[n - 1]
        if n < 5:
            held[n] = value
            small_copy(n).start()
        else:
            small_out[...] = value

    def relay(k, h):
        pass_on(k - 1, h).wait_recv()
        pass_on(k, h).start()

    def pick(s):
        number = lax.broadcasted_iota(jnp.int32, (total.shape[0], count), 0)
        first = (number == idx[s, 0:1, :]).astype(F32)
        second = (number == idx[s, 1:2, :]).astype(F32)
        return (first + second).astype(BF)

    def last_arrival(u):
        pass_on(2, u).wait_recv()
        for ch in range(2):
            cols = slice((2 * u + ch) * half // 2, (2 * u + ch + 1) * half // 2)
            value = total[:, cols] + dot(last, ring[2, :, cols], NN)
            table.store(u, ch, value.astype(BF))

    pass_on(0, 0).start()
    pass_on(0, 1).start()
    held[0] = small[...]
    small_copy(0).start()
    summing.start()
    total[...] = dot(pick(0), cells[...], NN)
    small_step(1)
    summing.step(1, 0)
    small_step(2)
    summing.step(1, 1)
    relay(1, 0)
    summing.step(2, 0)
    summing.step(1, 2)
    small_step(3)
    relay(1, 1)
    total[...] = total[...] + dot(pick(1), ring[0], NN)
    summing.step(2, 1)
    summing.step(1, 3)
    relay(2, 0)
    small_step(4)
    summing.step(2, 2)
    relay(2, 1)
    summing.step(3, 0)
    summing.step(3, 1)
    summing.step(2, 3)
    total[...] = total[...] + dot(pick(2), ring[1], NN)
    last = pick(3)
    last_arrival(0)
    table.step(1, 0)
    last_arrival(1)
    summing.step(3, 2)
    small_step(5)
    table.step(2, 0)
    table.step(1, 1)
    table.step(3, 0)
    table.step(2, 1)
    table.step(4, 0)
    table.step(3, 1)
    table.step(5, 0)
    table.step(4, 1)
    table.step(6, 0)
    table.step(5, 1)
    summing.step(3, 3)
    summing.finish()
    table.step(6, 1)
    table.finish()
    for k in range(3):
        for h in range(2):
            pass_on(k, h).wait_send()
    for n in range(5):
        small_copy(n).wait_send()


def closing(cells, idx, small, grads):
    count, width = cells.shape
    rows, cols = grads[0].shape[3:]
    wide = width // 4
    part = lambda *n: pltpu.VMEM((2, 2, *n, BLOCK, wide), BF)
    done = (2, 2, 2, 2, 2, BLOCK, wide)
    dma = pltpu.SemaphoreType.DMA
    return pl.pallas_call(
        closing_kernel,
        grid=(1,),
        in_specs=[full(cells.shape), full(idx.shape), full(small.shape)]
        + [pl.BlockSpec(memory_space=pl.ANY)] * 2,
        out_specs=[full(done), full((2, rows, cols)), full(small.shape)],
        out_shape=[
            jax.ShapeDtypeStruct(done, BF),
            jax.ShapeDtypeStruct((2, rows, cols), F32),
            jax.ShapeDtypeStruct(small.shape, F32),
        ],
        scratch_shapes=[
            pltpu.VMEM((3, count, width), BF), pltpu.VMEM((8 * BLOCK, width), F32),
            dma((3, 2)), dma((3, 2)),
            pltpu.VMEM((5, *small.shape), F32), pltpu.VMEM((5, *small.shape), F32), dma((5,)), dma((5,)),
        ]
        + sum_scratch(rows, cols)
        + [part(2, 2, 2), part(2, 2), part(2), part(), dma((6, 2, 2)), dma((6, 2, 2))],
        compiler_params=params(has_side_effects=True, collective_id=3),
        cost_estimate=cost(8 * count * width * 1024, 24 << 20),
        name="closing",
    )(cells, idx, small, *grads)


def table_out_kernel(a, b, out):
    wide = a.shape[6]
    for n, piece in enumerate((a, b)):
        for u in range(2):
            at = (2 * u + n) * wide
            out[:, 0, at : at + wide] = piece[0, u, 0, 0, 0].astype(F32)


def table_out(done, table_rows):
    wide = done.shape[6]
    block = (1, 2, 1, 1, 1, BLOCK, wide)
    first = lambda i: (0, 0, i % 2, (i // 2) % 2, i // 4, 0, 0)
    second = lambda i: (1, 0, i % 2, i // 4, (i // 2) % 2, 0, 0)
    out = pl.pallas_call(
        table_out_kernel,
        grid=(8,),
        in_specs=[pl.BlockSpec(block, first), pl.BlockSpec(block, second)],
        out_specs=pl.BlockSpec((BLOCK, 1, 4 * wide), lambda i: (i, 0, 0)),
        out_shape=jax.ShapeDtypeStruct((table_rows, 1, 4 * wide), F32),
        compiler_params=params(),
        cost_estimate=cost(0, 6 << 20),
        name="table_write",
    )(done, done)
    return out.transpose(1, 0, 2)


def flip_tok(value, bit, size):
    return lax.ppermute(value, "tok", [(i, i ^ bit) for i in range(size)])


def shift_tab(value, shift, size):
    return lax.ppermute(value, "tab", [(i, (i + shift) % size) for i in range(size)])


def small_sum(value, n_tok, n_tab):
    bit = 1
    while bit < n_tok:
        value = value + flip_tok(value, bit, n_tok)
        bit *= 2
    total = value
    for shift in range(1, n_tab):
        total = total + shift_tab(value, shift, n_tab)
    return total


def body(
    n_tok, n_tab,
    embedded, cell_index, cell_boxes, box_tables, joined_weight, output_weight,
    expand_weight, reduce_weight, hidden_bias, bias_rows, norm_gains, norm_shifts, cotangent,
):
    tokens, width = embedded.shape
    pages, length = cell_index.shape
    table_rows = box_tables.shape[1]
    ff = expand_weight.shape[1]
    tok = lax.axis_index("tok").astype(jnp.int32).reshape(1)
    z = lax.axis_index("tab")
    cubic = n_tok == 8 and n_tab == 4

    corners = cell_boxes[:, :, :CELLS]
    lo = lambda n: jnp.minimum(corners[:, n], corners[:, n + 2]).reshape(-1)
    hi = lambda n: jnp.maximum(corners[:, n], corners[:, n + 2]).reshape(-1)
    left, right, top, bottom = lo(0), hi(0), lo(1), hi(1)
    none = jnp.full_like(left, -1)
    index_table = jnp.stack(
        [
            jnp.stack([left, right]),
            jnp.stack([top, bottom]),
            jnp.stack([right - left, none]),
            jnp.stack([bottom - top, none]),
        ]
    )
    pick_table = lambda i: lax.dynamic_index_in_dim(index_table, i, 0, keepdims=False)
    group_index = jnp.stack(
        [pick_table(z)]
        + [shift_tab(pick_table((z + s) % n_tab), s, n_tab) for s in range(1, n_tab)]
    )
    padded = jnp.pad(box_tables[0], ((0, 1024 - table_rows), (0, 0)))
    found = lookup(group_index, padded)
    terms = [found[0]] + [shift_tab(found[s], n_tab - s, n_tab) for s in range(1, n_tab)]

    q, k, v, normed, normed_low, rstd0 = embed(
        embedded, cell_index, terms, joined_weight, norm_gains, norm_shifts, bias_rows
    )
    mixed, lse = attn_fwd(q, k, v, pages)
    layer_out, after, after_low, rstd1, act, slope, gs2, gffn, sums2 = ffn_fwd(
        mixed, normed, output_weight, expand_weight, reduce_weight, hidden_bias,
        bias_rows, norm_gains, norm_shifts, cotangent, min(256, tokens),
    )
    if cubic:
        gs1, gmixed, hidden_sum, sums1, *parts, reduce_sum = ffn_grads(
            gffn, act, slope, gs2, after, after_low, rstd1, mixed, reduce_weight, expand_weight,
            output_weight, norm_gains, norm_shifts,
        )
    else:
        parts = None
        gh, gs1, gattn, gmixed, hidden_sum, sums1 = ffn_bwd(
            gffn, slope, gs2, after, rstd1, reduce_weight, expand_weight, output_weight,
            norm_gains, norm_shifts,
        )
    embedded_grad, cell_grad, sums0, sums_qv, *more = back(
        q, k, v, mixed, gmixed, lse, normed_low, gs1, joined_weight, normed, rstd0, cell_index,
        norm_gains, norm_shifts, parts,
    )
    if cubic:
        parts, expand_sum = more[:2], more[2:]
    else:
        gj = more[0]

    small = jnp.concatenate(
        [
            sums0.reshape(-1), sums1.reshape(-1), sums2.reshape(-1),
            sums_qv.reshape(-1), hidden_sum.reshape(-1),
        ]
    ).reshape(-1, 128)
    if cubic:
        done, joined_sum, small = closing(cell_grad, group_index, small, parts)
        tables_grad = table_out(done, table_rows)
    else:
        cell_grads = [cell_grad] + [shift_tab(cell_grad, s, n_tab) for s in range(1, n_tab)]
        part_a, part_b = table_part(jnp.zeros_like(tok), group_index, cell_grads, 8)
        both = jnp.concatenate([part_a, part_b], axis=2).astype(F32)
        tables_grad = lax.psum(both.reshape(1, -1, width)[:, :table_rows], "tok")
        small = small_sum(small, n_tok, n_tab)
    small = small.reshape(-1)
    row = small.reshape(-1, width)
    gains_grad = jnp.stack([row[0], row[2], row[5]])
    shifts_grad = jnp.stack([row[1], row[3], row[6]])
    biases_grad = jnp.stack([row[8], row[9], row[4], row[7]])
    hidden_bias_grad = small[10 * width :]

    if cubic:
        reduce_grad = jnp.concatenate([reduce_sum[0], reduce_sum[1]], axis=1).T
        expand_sum = expand_sum[0].reshape(-1, expand_sum[0].shape[2])
        expand_grad = expand_sum[:, : ff // 4]
        output_grad = expand_sum[:, ff // 4 :]
        joined_grad = joined_sum.reshape(-1, joined_sum.shape[2])
    else:
        both = lambda a, b: jnp.einsum("ta,tb->ab", a, b, preferred_element_type=F32).astype(BF)

        def scattered(part):
            part = lax.psum_scatter(part, "tok", scatter_dimension=0, tiled=True)
            return lax.psum_scatter(part, "tab", scatter_dimension=1, tiled=True).astype(F32)

        reduce_grad = scattered(both(act, gffn))
        expand_grad = scattered(both(after_low, gh))
        output_grad = scattered(both(mixed, gattn))
        joined_grad = scattered(both(normed_low, jnp.concatenate([gj[0], gj[1], gj[2]], axis=1)))

    return (
        layer_out, embedded_grad, tables_grad, joined_grad, output_grad, expand_grad,
        reduce_grad, hidden_bias_grad, biases_grad, gains_grad, shifts_grad,
    )


def solution(mesh):
    rows = P(("tok", "tab"), None)
    return jax.shard_map(
        functools.partial(body, mesh.shape["tok"], mesh.shape["tab"]),
        mesh=mesh,
        in_specs=(
            rows, rows, P(("tok", "tab"), None, None), P("tab", None, None),
            P(), P(), P(), P(), P(), P(), P(), P(), rows,
        ),
        out_specs=(
            rows, rows, P("tab", None, None), P("tok", "tab"), P("tok", "tab"),
            P("tok", "tab"), P("tok", "tab"), P(), P(), P(), P(),
        ),
        check_vma=False,
    )
```

```python
import functools

import jax
import jax.numpy as jnp
from jax import lax
from jax.experimental import pallas as pl
from jax.experimental.pallas import tpu as pltpu
from jax.sharding import PartitionSpec as P

HEADS = 16
HEAD_DIM = 64
CELLS = 128
EPSILON = 1e-05
SCALE = HEAD_DIM ** (-0.5)
LOG2E = 1.4426950408889634
F32 = jnp.float32
BF = jnp.bfloat16
NN = ((1,), (0,))
NT = ((1,), (1,))
TN = ((0,), (0,))
ANY = pl.ANY

TAIL_P = 0.305
TAIL_C = (
    0.12164194255155772,
    0.12243138164026345,
    0.10365178645525906,
    0.12022714029486306,
    -0.03641303195181058,
    0.1839499605096701,
    -0.15192310059752684,
    0.03643391798251271,
)


def dot(a, b, dims):
    return lax.dot_general(a, b, (dims, ((), ())), preferred_element_type=F32)


def params(**kw):
    return pltpu.CompilerParams(vmem_limit_bytes=60 << 20, **kw)


def cost(flops, nbytes, trans=0):
    return pl.CostEstimate(
        flops=int(flops), bytes_accessed=int(nbytes), transcendentals=int(trans)
    )


def full(shape):
    zeros = (0,) * len(shape)
    return pl.BlockSpec(shape, lambda *_: zeros, pipeline_mode=pl.Buffered(1))


def gelu_parts(h):
    a = jnp.abs(h)
    t = 1.0 / (1.0 + TAIL_P * a)
    poly = jnp.full_like(t, TAIL_C[-1])
    for c in TAIL_C[-2::-1]:
        poly = poly * t + c
    e = jnp.exp2(h * h * (-0.5 * LOG2E))
    tail = poly * t * e
    phi_cdf = jnp.where(h > 0, 1.0 - tail, tail)
    act = h * phi_cdf
    slope = phi_cdf + h * e * 0.3989422804014327
    return act, slope


def norm_stats(v):
    mean = jnp.mean(v, axis=-1, keepdims=True)
    centred = v - mean
    var = jnp.mean(centred * centred, axis=-1, keepdims=True)
    rstd = lax.rsqrt(var + EPSILON)
    return centred * rstd, rstd


def norm_back(y, xh, rstd, gain):
    u = y * gain
    return (
        u - jnp.mean(u, axis=-1, keepdims=True) - xh * jnp.mean(u * xh, axis=-1, keepdims=True)
    ) * rstd


def colsum(v):
    return jnp.sum(v, axis=0, keepdims=True)


def lookup_kernel(idx, table, out):
    rows = table.shape[0]
    count = idx.shape[2]
    number = lax.broadcasted_iota(jnp.int32, (rows, count), 0)
    first = (number == idx[0, 0:1, :]).astype(F32)
    second = (number == idx[0, 1:2, :]).astype(F32)
    out[0] = dot((first + second).astype(BF), table[...], TN).astype(BF)


def lookup(idx, table):
    groups, _, count = idx.shape
    rows, width = table.shape
    return pl.pallas_call(
        lookup_kernel,
        grid=(groups,),
        in_specs=[
            pl.BlockSpec((1, 2, count), lambda i: (i, 0, 0)),
            full((rows, width)),
        ],
        out_specs=pl.BlockSpec((1, count, width), lambda i: (i, 0, 0)),
        out_shape=jax.ShapeDtypeStruct((groups, count, width), BF),
        compiler_params=params(),
        cost_estimate=cost(2 * groups * count * rows * width, 2 * groups * count * width),
        name="lookup",
    )(idx, table)


def embed_kernel(
    emb, ci, t0, t1, t2, t3, w, gains, shifts, bias, q, k, v, normed, low, rstd_out
):
    width = emb.shape[1]
    tokens = emb.shape[0]
    cells = jnp.concatenate([t0[...], t1[...], t2[...], t3[...]], axis=0)
    number = lax.broadcasted_iota(jnp.int32, (CELLS, tokens), 0)
    pick = (number == ci[0]).astype(F32).astype(BF)
    pick = jnp.concatenate([pick] * 4, axis=0)
    box = dot(pick, cells, TN)
    xh, rstd = norm_stats(emb[...].astype(F32) + box)
    y = xh * gains[0:1] + shifts[0:1]
    normed[...] = y
    rstd_out[...] = rstd
    y_low = y.astype(BF)
    low[...] = y_low
    q[...] = ((dot(y_low, w[:, :width], NN) + bias[0:1]) * SCALE).astype(BF)
    k[...] = dot(y_low, w[:, width : 2 * width], NN).astype(BF)
    v[...] = (dot(y_low, w[:, 2 * width :], NN) + bias[1:2]).astype(BF)


def embed(emb, ci, terms, w, gains, shifts, bias):
    tokens, width = emb.shape
    pages, length = ci.shape
    rows = pl.BlockSpec((length, width), lambda i: (i, 0))
    cell_rows = pl.BlockSpec((CELLS, width), lambda i: (i, 0))
    shape = lambda dt, n=width: jax.ShapeDtypeStruct((tokens, n), dt)
    return pl.pallas_call(
        embed_kernel,
        grid=(pages,),
        in_specs=[rows, pl.BlockSpec((1, 1, length), lambda i: (i, 0, 0))]
        + [cell_rows] * 4
        + [full(w.shape), full(gains.shape), full(shifts.shape), full(bias.shape)],
        out_specs=[rows] * 5 + [pl.BlockSpec((length, 1), lambda i: (i, 0))],
        out_shape=[shape(BF), shape(BF), shape(BF), shape(F32), shape(BF), shape(F32, 1)],
        compiler_params=params(),
        cost_estimate=cost(2 * tokens * width * 3 * width, 26 << 20),
        name="embed_joined",
    )(emb, ci.reshape(pages, 1, length), *terms, w, gains, shifts, bias)


STAGES = 4


def neighbours():
    tok, z = lax.axis_index("tok"), lax.axis_index("tab")
    core = {"tok": tok + 1 - 2 * (tok % 2)}
    x = {"tok": tok + 2 - 4 * ((tok // 2) % 2)}
    y = {"tok": tok + 4 - 8 * (tok // 4)}
    peers = [{"tab": (z + s) % 4} for s in range(1, 4)]
    return core, x, y, peers


def meet(devices):
    barrier = pltpu.get_barrier_semaphore()
    for d in devices:
        pl.semaphore_signal(barrier, inc=1, device_id=d, device_id_type=pl.DeviceIdType.MESH)
    pl.semaphore_wait(barrier, len(devices))


def sum_scratch(rows, cols):
    part = lambda *n: pltpu.VMEM((*n, rows, cols), BF)
    return [
        part(2, 4, 4), part(2, 4, 4), part(2, 4, 2), part(2, 4), part(2, 3),
        pltpu.SemaphoreType.DMA((2, 4)),
        pltpu.SemaphoreType.DMA((STAGES, 2, 4)),
        pltpu.SemaphoreType.DMA((STAGES, 2, 4)),
    ]


class Summing:
    def __init__(self, grads, out, scratch):
        self.grads, self.out = grads, out
        if grads is None:
            both, scratch = scratch[0], (scratch[0].at[0], *scratch[1:5], None, *scratch[5:])
            self.part = both.at[1]
        self.own, self.r0, self.r1, self.r2, self.r3, self.local, self.sent, self.got = scratch
        core, x, y, peers = neighbours()
        self.core, self.first, self.second, self.peers = core, (x, y), (y, x), peers
        self.z = lax.axis_index("tab")

    def devices(self):
        return [self.core, self.first[0], self.first[1], *self.peers]

    def copy(self, stage, ch, i):
        zc = (self.z + (i + 1)) % 4
        src, dst, to = (
            (
                lambda: self.part.at[ch, i] if self.grads is None else self.grads[ch].at[1, zc],
                self.r0.at[ch, i],
                self.core,
            ),
            (lambda: self.own.at[ch, i, pl.ds(2, 2)], self.r1.at[ch, i], self.first[ch]),
            (lambda: self.own.at[ch, i, 1], self.r2.at[ch, i], self.second[ch]),
            (lambda: self.own.at[ch, i, 0], self.r3.at[ch, min(i, 2)], self.peers[min(i, 2)]),
        )[stage]
        return pltpu.make_async_remote_copy(
            src_ref=src(), dst_ref=dst,
            send_sem=self.sent.at[stage, ch, i], recv_sem=self.got.at[stage, ch, i],
            device_id=to, device_id_type=pl.DeviceIdType.MESH,
        )

    def load(self, ch, i):
        zc = (self.z + (i + 1)) % 4
        return pltpu.make_async_copy(
            self.grads[ch].at[0, zc], self.own.at[ch, i], self.local.at[ch, i]
        )

    def start(self):
        for i in range(4):
            for ch in range(2):
                self.copy(0, ch, i).start()
                if self.grads is not None:
                    self.load(ch, i).start()

    def step(self, stage, i):
        for ch in range(2):
            self.copy(stage - 1, ch, i).wait_recv()
            if stage == 1:
                if self.grads is not None:
                    self.load(ch, i).wait()

                def add(j, _, ch=ch):
                    self.own[ch, i, j] = self.own[ch, i, j] + self.r0[ch, i, j]
                    return 0

                lax.fori_loop(0, 4, add, 0)
            elif stage == 2:

                def add(j, _, ch=ch):
                    self.own[ch, i, j] = self.own[ch, i, j] + self.r1[ch, i, j]
                    return 0

                lax.fori_loop(0, 2, add, 0)
            elif i < 3:
                self.own[ch, i, 0] = self.own[ch, i, 0] + self.r2[ch, i]
            if stage < 3 or i < 3:
                self.copy(stage, ch, i).start()

    def finish(self):
        for ch in range(2):
            total = self.own[ch, 3, 0].astype(F32) + self.r2[ch, 3].astype(F32)
            for i in range(3):
                self.copy(3, ch, i).wait_recv()
                total = total + self.r3[ch, i].astype(F32)
            self.out[ch] = total
        for stage in range(STAGES):
            for ch in range(2):
                for i in range(4 if stage < 3 else 3):
                    self.copy(stage, ch, i).wait_send()

    def run(self, step, plan):
        for at, events in plan.items():

            @pl.when(step == at)
            def _(events=events):
                for stage, i in events:
                    if stage == 0:
                        self.start()
                    elif stage == 4:
                        self.finish()
                    else:
                        self.step(stage, i)


def split_rel(r):
    return r & 1, (r >> 1) & 1, r >> 2


def rel_of(b):
    tok = lax.axis_index("tok")
    core, x, y = split_rel(b)
    flip = lambda static, mine: 1 - mine if static else mine
    return flip(core, tok % 2), flip(x, (tok // 2) % 2), flip(y, tok // 4)


def put_rows(g, ga, gb, cols, rows):
    half = rows // 2
    for b in range(8):
        core, x, y = rel_of(b)
        ga[core, 0, 2 * x + y, :, cols] = g[b * rows : b * rows + half]
        gb[core, 0, 2 * y + x, :, cols] = g[b * rows + half : (b + 1) * rows]


def sum_specs(grads, number):
    if grads is None:
        return [], [], [], [], {}
    rows, cols = grads[0].shape[3:]
    return (
        [pl.BlockSpec(memory_space=pl.ANY)] * 2,
        [full((2, rows, cols))],
        [jax.ShapeDtypeStruct((2, rows, cols), F32)],
        sum_scratch(rows, cols),
        {"has_side_effects": True, "collective_id": number},
    )


HP = 4


def head_masks(length, pair):
    lane = lax.broadcasted_iota(jnp.int32, (length, pair), 1)
    return lane < HEAD_DIM


def attn_fwd_kernel(q, k, v, mixed, lse):
    length = q.shape[0]
    pair = 2 * HEAD_DIM
    low_half = head_masks(length, pair)
    zero = jnp.zeros((length, pair), BF)
    for p in range(HP // 2):
        cols = slice(p * pair, (p + 1) * pair)
        qp, kp, vp = q[:, cols], k[:, cols], v[:, cols]
        vt = vp.T
        outs = []
        for h in range(2):
            km = jnp.where(low_half, kp, zero) if h == 0 else jnp.where(low_half, zero, kp)
            st = dot(km, qp, NT)
            top = jnp.max(st, axis=0, keepdims=True)
            raised = jnp.exp2((st - top) * LOG2E)
            total = jnp.sum(raised, axis=0, keepdims=True)
            lse[0, 0, 2 * p + h : 2 * p + h + 1, :] = top + jnp.log(total)
            ot = dot(vt[h * HEAD_DIM : (h + 1) * HEAD_DIM], raised.astype(BF), NN)
            outs.append(ot * (1.0 / total))
        mixed[:, cols] = jnp.concatenate(outs, axis=0).T.astype(BF)


def attn_fwd(q, k, v, pages):
    tokens, width = q.shape
    length = tokens // pages
    steps = HEADS // HP
    blk = pl.BlockSpec((length, HP * HEAD_DIM), lambda i, j: (i, j))
    return pl.pallas_call(
        attn_fwd_kernel,
        grid=(pages, steps),
        in_specs=[blk] * 3,
        out_specs=[blk, pl.BlockSpec((1, 1, HP, length), lambda i, j: (i, j, 0, 0))],
        out_shape=[
            jax.ShapeDtypeStruct((tokens, width), BF),
            jax.ShapeDtypeStruct((pages, steps, HP, length), F32),
        ],
        compiler_params=params(),
        cost_estimate=cost(14e9, 8 << 20, pages * HEADS * length * length),
        name="attention",
    )(q, k, v)


def attn_back(q, k, v, mixed, go, lse, put):
    length = q.shape[0]
    pair = 2 * HEAD_DIM
    low_half = head_masks(length, pair)
    zero = jnp.zeros((length, pair), BF)

    def pick(x, h):
        return jnp.where(low_half, x, zero) if h == 0 else jnp.where(low_half, zero, x)

    for p in range(HP // 2):
        cols = slice(p * pair, (p + 1) * pair)
        qp, kp, vp, op, gp = q[:, cols], k[:, cols], v[:, cols], mixed[:, cols], go[:, cols]
        kt = kp.T
        prod_t = (op.astype(F32) * gp.astype(F32)).T
        dq_t, dk, dv = [], None, None
        for h in range(2):
            st = dot(pick(kp, h), qp, NT)
            probs = jnp.exp2((st - lse[0, 0, 2 * p + h : 2 * p + h + 1, :]) * LOG2E)
            dv_h = dot(probs.astype(BF), pick(gp, h), NN)
            dpt = dot(pick(vp, h), gp, NT)
            delta = colsum(prod_t[h * HEAD_DIM : (h + 1) * HEAD_DIM])
            ds = (probs * (dpt - delta)).astype(BF)
            dk_h = dot(ds, pick(qp, h), NN)
            dq_t.append(dot(kt[h * HEAD_DIM : (h + 1) * HEAD_DIM], ds, NN))
            dv = dv_h if dv is None else dv + dv_h
            dk = dk_h if dk is None else dk + dk_h
        dq = (jnp.concatenate(dq_t, axis=0).T.astype(BF).astype(F32) * SCALE).astype(BF)
        put(p * pair, pair, dq, dk.astype(BF), dv.astype(BF))


FC = 512
FWD = 1024
RC = 128
MC = 512


def ffn_fwd_kernel(
    mixed, normed, wo, we, wr, hb, bias, gains, shifts, cot,
    out, after_out, low_out, rstd_out, act_out, slope_out, gs2_out, gffn_out, sums,
):
    ff = we.shape[1]
    attn_sum = normed[...] + (dot(mixed[...], wo[...], NN) + bias[2:3])
    xh, rstd = norm_stats(attn_sum)
    after = xh * gains[1:2] + shifts[1:2]
    after_out[...] = after
    rstd_out[...] = rstd
    low = after.astype(BF)
    low_out[...] = low
    total = after + bias[3:4]
    count = ff // FWD
    hidden = []
    for j in range(count + 1):
        if j < count:
            cols = slice(j * FWD, (j + 1) * FWD)
            hidden.append(dot(low, we[:, cols], NN) + hb[:, cols])
        if j > 0:
            cols = slice((j - 1) * FWD, j * FWD)
            act, slope = gelu_parts(hidden[j - 1])
            act = act.astype(BF)
            act_out[:, cols] = act
            slope_out[:, cols] = slope.astype(BF)
            total = total + dot(act, wr[cols, :], NN)
    xh, rstd = norm_stats(total)
    out[...] = (xh * gains[2:3] + shifts[2:3]).astype(BF)
    y = cot[...].astype(F32)
    gs2 = norm_back(y, xh, rstd, gains[2:3])
    gs2_out[...] = gs2
    gffn = gs2.astype(BF)
    gffn_out[...] = gffn
    part = jnp.concatenate([colsum(y * xh), colsum(y), colsum(gffn.astype(F32))], axis=0)

    @pl.when(pl.program_id(0) == 0)
    def _():
        sums[...] = part

    @pl.when(pl.program_id(0) != 0)
    def _():
        sums[...] = sums[...] + part


def ffn_fwd(mixed, normed, wo, we, wr, hb, bias, gains, shifts, cot, tile):
    tokens, width = mixed.shape
    ff = we.shape[1]
    rows = pl.BlockSpec((tile, width), lambda i: (i, 0))
    long = pl.BlockSpec((tile, ff), lambda i: (i, 0))
    shape = lambda dt, n=width: jax.ShapeDtypeStruct((tokens, n), dt)
    hb = hb.reshape(1, ff)
    return pl.pallas_call(
        ffn_fwd_kernel,
        grid=(tokens // tile,),
        in_specs=[rows, rows]
        + [full(a.shape) for a in (wo, we, wr, hb, bias, gains, shifts)]
        + [rows],
        out_specs=[rows, rows, rows, pl.BlockSpec((tile, 1), lambda i: (i, 0)), long, long, rows, rows]
        + [pl.BlockSpec((3, width), lambda i: (0, 0))],
        out_shape=[
            shape(BF), shape(F32), shape(BF), shape(F32, 1), shape(BF, ff), shape(BF, ff),
            shape(F32), shape(BF), jax.ShapeDtypeStruct((3, width), F32),
        ],
        compiler_params=params(),
        cost_estimate=cost(2 * tokens * width * (width + 2 * ff), 60 << 20, tokens * ff * 2),
        name="ffn_forward",
    )(mixed, normed, wo, we, wr, hb, bias, gains, shifts, cot)


def second_norm_back(gs1_out, after, rstd, gains, shifts, gattn_out, sums):
    tokens, width = after.shape

    def norm(i, carry):
        rows = pl.ds(pl.multiple_of(i * RC, RC), RC)
        total = gs1_out[rows, :]
        xh = (after[rows, :] - shifts[1:2]) * (1.0 / gains[1:2])
        gs1 = norm_back(total, xh, rstd[rows, :], gains[1:2])
        gs1_out[rows, :] = gs1
        gattn = gs1.astype(BF)
        gattn_out[rows, :] = gattn
        g, s, b = carry
        return g + colsum(total * xh), s + colsum(total), b + colsum(gattn.astype(F32))

    zero = jnp.zeros((1, width), F32)
    sums[...] = jnp.concatenate(lax.fori_loop(0, tokens // RC, norm, (zero, zero, zero)), axis=0)


def ffn_bwd_kernel(
    gffn, gs2, after, rstd, wo, gains, shifts, slope, wr, we,
    gh_out, gs1_out, gattn_out, gmixed_out, hsum, sums,
):
    step, last = pl.program_id(0), pl.num_programs(0) - 1
    tokens, width = gffn.shape

    @pl.when(step == 0)
    def _():
        gs1_out[...] = gs2[...]

    part = jnp.zeros((1, slope.shape[1]), F32)
    for m in range(0, tokens, MC):
        rows = slice(m, m + MC)
        gh = (dot(gffn[rows, :], wr[...], NT) * slope[rows, :].astype(F32)).astype(BF)
        gh_out[rows, :] = gh
        part = part + colsum(gh.astype(F32))
        gs1_out[rows, :] = gs1_out[rows, :] + dot(gh, we[...], NT)
    hsum[...] = part

    @pl.when(step == last)
    def _():
        second_norm_back(gs1_out, after, rstd, gains, shifts, gattn_out, sums)
        for m in range(0, tokens, MC):
            rows = slice(m, m + MC)
            gmixed_out[rows, :] = dot(gattn_out[rows, :], wo[...], NT).astype(BF)


def ffn_bwd(gffn, slope, gs2, after, rstd, wr, we, wo, gains, shifts):
    tokens, width = gffn.shape
    ff = we.shape[1]
    whole = full((tokens, width))
    long = pl.BlockSpec((tokens, FC), lambda s: (0, s))
    shape = lambda dt, n=width: jax.ShapeDtypeStruct((tokens, n), dt)
    return pl.pallas_call(
        ffn_bwd_kernel,
        grid=(ff // FC,),
        in_specs=[whole, whole, whole, full((tokens, 1))]
        + [full(a.shape) for a in (wo, gains, shifts)]
        + [
            long,
            pl.BlockSpec((FC, width), lambda s: (s, 0)),
            pl.BlockSpec((width, FC), lambda s: (0, s)),
        ],
        out_specs=[long, whole, whole, whole]
        + [pl.BlockSpec((1, FC), lambda s: (0, s)), full((3, width))],
        out_shape=[
            shape(BF, ff), shape(F32), shape(BF), shape(BF),
            jax.ShapeDtypeStruct((1, ff), F32), jax.ShapeDtypeStruct((3, width), F32),
        ],
        compiler_params=params(),
        cost_estimate=cost(2 * tokens * width * (width + 2 * ff), 60 << 20),
        name="ffn_backward",
    )(gffn, gs2, after, rstd, wo, gains, shifts, slope, wr, we)


FFN_PLAN = {
    4: [(0, 0)],
    8: [(1, 0), (1, 1)],
    10: [(2, 0), (1, 2)],
    12: [(2, 1), (1, 3)],
    13: [(3, 0)],
    14: [(2, 2)],
    15: [(3, 1)],
    16: [(2, 3)],
    17: [(3, 2)],
    18: [(3, 3)],
}
N_TOK, N_TAB = 8, 4


def block_of_step(s):
    s = jnp.minimum(s, N_TOK - 1)
    return 1 - s // 4, 1 - (s // 2) % 2, 1 - s % 2


def ffn_grads_kernel(
    gffn_in, gs2_in, after, rstd, low, mixed, wo, gains, shifts, act, slope, wr, we,
    gs1_out, gmixed_out, hsum, sums, ga, gb, reduce_out,
    gffn, gh, local, *scratch,
):
    step, last = pl.program_id(0), pl.num_programs(0) - 1
    tokens, width = after.shape
    summing = Summing(None, reduce_out, scratch)
    both = scratch[0]
    z = lax.axis_index("tab")
    first = pltpu.make_async_copy(gffn_in, gffn, local.at[0])
    later = pltpu.make_async_copy(gs2_in, gs1_out, local.at[1])

    @pl.when(step == 0)
    def _():
        first.start()
        later.start()
        meet(summing.devices())
        first.wait()

    @pl.when(step == N_TOK)
    def _():
        later.wait()

    summing.run(step, FFN_PLAN)

    @pl.when(step < N_TOK)
    def _():
        core, x, y = block_of_step(step)
        g = dot(gffn[...], act[...], TN).astype(BF)
        rows, half = both.shape[4:]
        for zc in range(N_TAB):
            i = (zc + N_TAB - 1 - z) % N_TAB
            for ch in range(2):
                piece = g[zc * rows : (zc + 1) * rows, ch * half : (ch + 1) * half]
                both[core, ch, i, (2 * x + y, 2 * y + x)[ch]] = piece

    @pl.when((step >= N_TOK) & (step < 2 * N_TOK))
    def _():
        part = jnp.zeros((1, slope.shape[1]), F32)
        for m in range(0, tokens, MC):
            rows = slice(m, m + MC)
            g = (dot(gffn[rows, :], wr[...], NT) * slope[rows, :].astype(F32)).astype(BF)
            gh[step - N_TOK, rows, :] = g
            part = part + colsum(g.astype(F32))
            gs1_out[rows, :] = gs1_out[rows, :] + dot(g, we[...], NT)
        hsum[...] = part

    @pl.when(step == 2 * N_TOK - 1)
    def _():
        second_norm_back(gs1_out, after, rstd, gains, shifts, gffn, sums)
        for m in range(0, tokens, MC):
            rows = slice(m, m + MC)
            gmixed_out[rows, :] = dot(gffn[rows, :], wo[...], NT).astype(BF)

    @pl.when(step >= 2 * N_TOK)
    def _():
        n = step - 2 * N_TOK
        quarter = width // N_TAB
        rows = width // N_TOK
        wide = gh.shape[2]
        for m in range(2):
            g = dot(low[...], gh[2 * n + m], TN).astype(BF)
            put_rows(g, ga, gb, slice(m * wide, (m + 1) * wide), rows)
        piece = gffn[:, pl.ds(pl.multiple_of(n * quarter, quarter), quarter)]
        g = dot(mixed[...], piece, TN).astype(BF)
        put_rows(g, ga, gb, slice(2 * wide, 2 * wide + quarter), rows)

    @pl.when(step == last)
    def _():
        summing.finish()


def ffn_grads(gffn, act, slope, gs2, after, low, rstd, mixed, wr, we, wo, gains, shifts):
    tokens, width = gffn.shape
    ff = we.shape[1]
    whole = full((tokens, width))
    anywhere = pl.BlockSpec(memory_space=pl.ANY)
    wide = ff // N_TOK
    half = width // (2 * N_TOK)
    out_wide = (ff + width) // N_TAB
    back = lambda s: jnp.clip(s - N_TOK, 0, N_TOK - 1)
    grad = lambda s: jnp.clip(s - 2 * N_TOK, 0, N_TAB - 1)

    def act_block(s):
        core, x, y = block_of_step(s)
        tok = lax.axis_index("tok")
        flip = lambda rel, mine: rel + mine - 2 * rel * mine
        return 0, 4 * flip(y, tok // 4) + 2 * flip(x, (tok // 2) % 2) + flip(core, tok % 2)

    rows, cols = width // N_TAB, wide // 2
    part = lambda *n: pltpu.VMEM((*n, rows, cols), BF)
    dma = pltpu.SemaphoreType.DMA
    shape = lambda dt: jax.ShapeDtypeStruct((tokens, width), dt)
    piece = pl.BlockSpec((2, 1, 4, half, out_wide), lambda s: (0, grad(s), 0, 0, 0))
    return pl.pallas_call(
        ffn_grads_kernel,
        grid=(2 * N_TOK + N_TAB,),
        in_specs=[anywhere, anywhere, whole, full((tokens, 1)), whole, whole]
        + [full(a.shape) for a in (wo, gains, shifts)]
        + [
            pl.BlockSpec((tokens, wide), act_block),
            pl.BlockSpec((tokens, wide), lambda s: (0, back(s))),
            pl.BlockSpec((wide, width), lambda s: (back(s), 0)),
            pl.BlockSpec((width, wide), lambda s: (0, back(s))),
        ],
        out_specs=[
            whole, whole, pl.BlockSpec((1, wide), lambda s: (0, back(s))), full((3, width)),
            piece, piece, full((2, rows, cols)),
        ],
        out_shape=[
            shape(F32), shape(BF),
            jax.ShapeDtypeStruct((1, ff), F32), jax.ShapeDtypeStruct((3, width), F32),
            jax.ShapeDtypeStruct((2, 4, 4, half, out_wide), BF),
            jax.ShapeDtypeStruct((2, 4, 4, half, out_wide), BF),
            jax.ShapeDtypeStruct((2, rows, cols), F32),
        ],
        scratch_shapes=[
            pltpu.VMEM((tokens, width), BF), pltpu.VMEM((N_TOK, tokens, wide), BF), dma((2,)),
            part(2, 2, 4, 4), part(2, 4, 4), part(2, 4, 2), part(2, 4), part(2, 3),
            dma((STAGES, 2, 4)), dma((STAGES, 2, 4)),
        ],
        compiler_params=pltpu.CompilerParams(
            vmem_limit_bytes=67043328, has_side_effects=True, collective_id=1
        ),
        cost_estimate=cost(2 * tokens * width * (2 * width + 4 * ff), 60 << 20),
        name="ffn_backward_grads",
    )(gffn, gs2, after, rstd, low, mixed, wo, gains, shifts, act, slope, wr, we)


BACK_PLAN = {
    0: [(0, 0)],
    1: [(1, 0)],
    2: [(1, 1)],
    3: [(2, 0), (1, 2)],
    5: [(2, 1), (1, 3)],
    6: [(3, 0)],
    8: [(2, 2)],
    9: [(3, 1)],
    11: [(2, 3)],
    12: [(3, 2)],
    13: [(3, 3)],
}


def back_kernel(*refs, pages, summed):
    q, k, v, mixed, go, lse, low, gs1, w, normed, rstd, ci, gains, shifts = refs[:14]
    refs = refs[14:]
    grads, refs = refs[: 2 * summed], refs[2 * summed :]
    out, cells, sums0, sums_qv = refs[:4]
    refs = refs[4:]
    if summed:
        ga, gb, summed_out, gj = refs[:4]
        summing = Summing(grads, summed_out, refs[4:])
    else:
        gj_out, gj = refs
    step = pl.program_id(0)
    width = gs1.shape[1]
    length = q.shape[0]
    groups = HEADS // HP
    wide = HP * HEAD_DIM
    n_attn = groups * pages
    n_joined = 4 if summed else 0

    if summed:

        @pl.when(step == 0)
        def _():
            meet(summing.devices())

        summing.run(step, BACK_PLAN)

    @pl.when(step < n_attn)
    def _():
        group, page = step // pages, step % pages
        rows = pl.ds(pl.multiple_of(page * length, length), length)

        def put(at, size, dq, dk, dv):
            cols = pl.ds(pl.multiple_of(group * wide + at, size), size)
            gj[0, rows, cols] = dq
            gj[1, rows, cols] = dk
            gj[2, rows, cols] = dv
            part = jnp.concatenate([colsum(dq.astype(F32)), colsum(dv.astype(F32))], axis=0)

            @pl.when(page == 0)
            def _():
                sums_qv[:, cols] = part

            @pl.when(page != 0)
            def _():
                sums_qv[:, cols] = sums_qv[:, cols] + part

        attn_back(q, k, v, mixed, go, lse, put)

    if summed:
        quarter = width // 4
        for n in range(n_joined):

            @pl.when(step == n_attn + n)
            def _(n=n):
                for m in range(3):
                    third, at = (3 * n + m) // 4, (3 * n + m) % 4
                    piece = gj[third, :, at * quarter : (at + 1) * quarter]
                    g = dot(low[...], piece, TN).astype(BF)
                    put_rows(g, ga, gb, slice(m * quarter, (m + 1) * quarter), width // 8)

    @pl.when(step >= n_attn + n_joined)
    def _():
        page = step - (n_attn + n_joined)
        rows = pl.ds(pl.multiple_of(page * length, length), length)
        total = gs1[...]
        for n in range(3):
            total = total + dot(gj[n, rows, :], w[:, n * width : (n + 1) * width], NT)
        xh = (normed[...] - shifts[0:1]) * (1.0 / gains[0:1])
        grad = norm_back(total, xh, rstd[...], gains[0:1])
        out[...] = grad
        number = lax.broadcasted_iota(jnp.int32, (CELLS, length), 0)
        pick = (number == ci[0]).astype(F32).astype(BF)
        cells[...] = dot(pick, grad.astype(BF), NN).astype(BF)
        part = jnp.concatenate([colsum(total * xh), colsum(total)], axis=0)

        @pl.when(page == 0)
        def _():
            sums0[...] = part

        @pl.when(page != 0)
        def _():
            sums0[...] = sums0[...] + part

    if summed:

        @pl.when(step == pl.num_programs(0) - 1)
        def _():
            summing.finish()
    else:
        gj_out[...] = gj[...]


def back(q, k, v, mixed, go, lse, low, gs1, w, normed, rstd, ci, gains, shifts, grads):
    tokens, width = q.shape
    pages, length = ci.shape
    groups = HEADS // HP
    wide = HP * HEAD_DIM
    summed = grads is not None
    n_attn = groups * pages
    before = n_attn + (4 if summed else 0)
    at = lambda s: jnp.minimum(s, n_attn - 1)
    page = lambda s: jnp.maximum(s - before, 0)
    block = lambda s: jnp.clip(s - n_attn, 0, 3)
    blk = pl.BlockSpec((length, wide), lambda s: (at(s) % pages, at(s) // pages))
    rows = pl.BlockSpec((length, width), lambda s: (page(s), 0))
    out_specs = [
        rows,
        pl.BlockSpec((CELLS, width), lambda s: (page(s), 0)),
        full((2, width)),
        full((2, width)),
    ]
    out_shape = [
        jax.ShapeDtypeStruct((tokens, width), F32),
        jax.ShapeDtypeStruct((pages * CELLS, width), BF),
        jax.ShapeDtypeStruct((2, width), F32),
        jax.ShapeDtypeStruct((2, width), F32),
    ]
    whole_gj = (3, tokens, width)
    more_in, more_out, more_shape, more_scratch, more = sum_specs(grads, 2)
    if summed:
        half = width // 16
        piece = pl.BlockSpec((2, 1, 4, half, 3 * width // 4), lambda s: (0, block(s), 0, 0, 0))
        out_specs += [piece, piece]
        out_shape += [jax.ShapeDtypeStruct((2, 4, 4, half, 3 * width // 4), BF)] * 2
    else:
        out_specs += [full(whole_gj)]
        out_shape += [jax.ShapeDtypeStruct(whole_gj, BF)]
    return pl.pallas_call(
        functools.partial(back_kernel, pages=pages, summed=summed),
        grid=(before + pages,),
        in_specs=[blk] * 5
        + [
            pl.BlockSpec((1, 1, HP, length), lambda s: (at(s) % pages, at(s) // pages, 0, 0)),
            full(low.shape),
            rows,
            full(w.shape),
            rows,
            pl.BlockSpec((length, 1), lambda s: (page(s), 0)),
            pl.BlockSpec((1, 1, length), lambda s: (page(s), 0, 0)),
            full(gains.shape),
            full(shifts.shape),
        ]
        + more_in,
        out_specs=out_specs + more_out,
        out_shape=out_shape + more_shape,
        scratch_shapes=[pltpu.VMEM(whole_gj, BF)] + more_scratch,
        compiler_params=params(**more),
        cost_estimate=cost(70e9, 40 << 20, pages * HEADS * length * length),
        name="attention_joined_embed_back",
    )(
        q, k, v, mixed, go, lse, low, gs1, w, normed, rstd, ci.reshape(pages, 1, length),
        gains, shifts, *(grads or ()),
    )


def table_kernel(tok, idx, g0, g1, g2, g3, out_a, out_b):
    rows = out_a.shape[1]
    count = idx.shape[2]
    half = out_a.shape[2]
    base = (pl.program_id(0) ^ tok[0]) * rows
    number = lax.broadcasted_iota(jnp.int32, (rows, count), 0) + base
    picks = []
    for s in range(4):
        first = (number == idx[s, 0:1, :]).astype(F32)
        second = (number == idx[s, 1:2, :]).astype(F32)
        picks.append((first + second).astype(BF))
    pick = jnp.concatenate(picks, axis=1)
    grads = jnp.concatenate([g0[...], g1[...], g2[...], g3[...]], axis=0)
    total = dot(pick, grads, NN).astype(BF)
    out_a[0] = total[:, :half]
    out_b[0] = total[:, half:]


def table_part(tok, idx, grads, blocks):
    groups, _, count = idx.shape
    width = grads[0].shape[1]
    rows = 1024 // blocks
    half = width // 2
    out = pl.BlockSpec((1, rows, half), lambda i, t: (i, 0, 0))
    return pl.pallas_call(
        table_kernel,
        grid_spec=pltpu.PrefetchScalarGridSpec(
            num_scalar_prefetch=1,
            grid=(blocks,),
            in_specs=[full(idx.shape)] + [full((count, width))] * groups,
            out_specs=[out, out],
        ),
        out_shape=[jax.ShapeDtypeStruct((blocks, rows, half), BF)] * 2,
        compiler_params=params(),
        cost_estimate=cost(2 * 1024 * groups * count * width, 4 << 20),
        name="table_grad",
    )(tok, idx, *grads)


BLOCK = 128


class TableSum:
    def __init__(self, scratch, done):
        self.part, self.r0, self.r1, self.r2, self.sent, self.got = scratch
        self.done = done
        tok = lax.axis_index("tok")
        core, x, y, _ = neighbours()
        self.c, cx, cy = tok % 2, (tok // 2) % 2, tok // 4
        self.core, self.first, self.second = core, (x, y), (y, x)
        self.f, self.g = (cx, cy), (cy, cx)

    def copy(self, stage, ch, u):
        c, f, g = self.c, self.f[ch], self.g[ch]
        part, done = self.part.at[ch, u], self.done.at[ch, u]
        src, dst, to = (
            (lambda: part.at[1 - c], self.r0.at[ch, u], self.core),
            (lambda: part.at[c, 1 - f], self.r1.at[ch, u], self.first[ch]),
            (lambda: part.at[c, f, 1 - g], self.r2.at[ch, u], self.second[ch]),
            (lambda: done.at[c, f, g], None, self.second[ch]),
            (lambda: done.at[c, f], None, self.first[ch]),
            (lambda: done.at[c], None, self.core),
        )[stage]
        src = src()
        return pltpu.make_async_remote_copy(
            src_ref=src, dst_ref=src if dst is None else dst,
            send_sem=self.sent.at[stage, ch, u], recv_sem=self.got.at[stage, ch, u],
            device_id=to, device_id_type=pl.DeviceIdType.MESH,
        )

    def store(self, u, ch, value):
        for b in range(8):
            c, x, y = split_rel(b)
            f, g = (x, y) if ch == 0 else (y, x)
            self.part[ch, u, c, f, g] = value[b * BLOCK : (b + 1) * BLOCK]
        self.copy(0, ch, u).start()

    def step(self, stage, u):
        for ch in range(2):
            c, f, g = self.c, self.f[ch], self.g[ch]
            self.copy(stage - 1, ch, u).wait_recv()
            if stage == 1:
                self.part[ch, u, c] = self.part[ch, u, c] + self.r0[ch, u]
            elif stage == 2:
                self.part[ch, u, c, f] = self.part[ch, u, c, f] + self.r1[ch, u]
            elif stage == 3:
                self.done[ch, u, c, f, g] = self.part[ch, u, c, f, g] + self.r2[ch, u]
            if stage < 6:
                self.copy(stage, ch, u).start()

    def finish(self):
        for stage in range(6):
            for ch in range(2):
                for u in range(2):
                    self.copy(stage, ch, u).wait_send()


def closing_kernel(
    cells, idx, sums0, sums1, sums2, sums_qv, hidden_sum, ga, gb, done, joined, small_out,
    ring, total, ring_sent, ring_got, held, arrived, small_sent, small_got, *scratch,
):
    summing = Summing((ga, gb), joined, scratch[:8])
    table = TableSum(scratch[8:], done)
    core, x, y, peers = neighbours()
    z = lax.axis_index("tab")
    hops = [core, x, y, {"tab": z + 1 - 2 * (z % 2)}, {"tab": z + 2 - 4 * (z // 2)}]
    meet([core, x, y, *peers])
    count = cells.shape[0]
    half = cells.shape[1] // 2

    def pass_on(k, h):
        cols = pl.ds(h * half, half)
        src = cells.at[:, cols] if k == 0 else ring.at[k - 1, :, cols]
        return pltpu.make_async_remote_copy(
            src_ref=src, dst_ref=ring.at[k, :, cols],
            send_sem=ring_sent.at[k, h], recv_sem=ring_got.at[k, h],
            device_id=peers[0], device_id_type=pl.DeviceIdType.MESH,
        )

    def small_copy(n):
        return pltpu.make_async_remote_copy(
            src_ref=held.at[n], dst_ref=arrived.at[n],
            send_sem=small_sent.at[n], recv_sem=small_got.at[n],
            device_id=hops[n], device_id_type=pl.DeviceIdType.MESH,
        )

    def small_step(n):
        small_copy(n - 1).wait_recv()
        value = held[n - 1] + arrived[n - 1]
        if n < 5:
            held[n] = value
            small_copy(n).start()
        else:
            small_out[...] = value

    def relay(k, h):
        pass_on(k - 1, h).wait_recv()
        pass_on(k, h).start()

    def pick(s):
        number = lax.broadcasted_iota(jnp.int32, (total.shape[0], count), 0)
        first = (number == idx[s, 0:1, :]).astype(F32)
        second = (number == idx[s, 1:2, :]).astype(F32)
        return (first + second).astype(BF)

    def last_arrival(u):
        pass_on(2, u).wait_recv()
        for ch in range(2):
            cols = slice((2 * u + ch) * half // 2, (2 * u + ch + 1) * half // 2)
            value = total[:, cols] + dot(last, ring[2, :, cols], NN)
            table.store(u, ch, value.astype(BF))

    pass_on(0, 0).start()
    pass_on(0, 1).start()
    at, width = 0, cells.shape[1]
    for part in (sums0, sums1, sums2, sums_qv):
        held[0, at : at + part.shape[0]] = part[...]
        at += part.shape[0]
    for n in range(hidden_sum.shape[1] // width):
        held[0, at + n : at + n + 1] = hidden_sum[:, n * width : (n + 1) * width]
    small_copy(0).start()
    summing.start()
    total[...] = dot(pick(0), cells[...], NN)
    small_step(1)
    summing.step(1, 0)
    small_step(2)
    summing.step(1, 1)
    relay(1, 0)
    summing.step(2, 0)
    summing.step(1, 2)
    small_step(3)
    relay(1, 1)
    total[...] = total[...] + dot(pick(1), ring[0], NN)
    summing.step(2, 1)
    summing.step(1, 3)
    relay(2, 0)
    small_step(4)
    summing.step(2, 2)
    relay(2, 1)
    summing.step(3, 0)
    summing.step(3, 1)
    summing.step(2, 3)
    total[...] = total[...] + dot(pick(2), ring[1], NN)
    last = pick(3)
    last_arrival(0)
    table.step(1, 0)
    last_arrival(1)
    summing.step(3, 2)
    small_step(5)
    table.step(2, 0)
    table.step(1, 1)
    table.step(3, 0)
    table.step(2, 1)
    table.step(4, 0)
    table.step(3, 1)
    table.step(5, 0)
    table.step(4, 1)
    table.step(6, 0)
    table.step(5, 1)
    summing.step(3, 3)
    summing.finish()
    table.step(6, 1)
    table.finish()
    for k in range(3):
        for h in range(2):
            pass_on(k, h).wait_send()
    for n in range(5):
        small_copy(n).wait_send()


def closing(cells, idx, sums, grads):
    count, width = cells.shape
    small = (sum(part.size for part in sums) // width, width)
    rows, cols = grads[0].shape[3:]
    wide = width // 4
    part = lambda *n: pltpu.VMEM((2, 2, *n, BLOCK, wide), BF)
    done = (2, 2, 2, 2, 2, BLOCK, wide)
    dma = pltpu.SemaphoreType.DMA
    return pl.pallas_call(
        closing_kernel,
        grid=(1,),
        in_specs=[full(cells.shape), full(idx.shape)]
        + [full(part.shape) for part in sums]
        + [pl.BlockSpec(memory_space=pl.ANY)] * 2,
        out_specs=[full(done), full((2, rows, cols)), full(small)],
        out_shape=[
            jax.ShapeDtypeStruct(done, BF),
            jax.ShapeDtypeStruct((2, rows, cols), F32),
            jax.ShapeDtypeStruct(small, F32),
        ],
        scratch_shapes=[
            pltpu.VMEM((3, count, width), BF), pltpu.VMEM((8 * BLOCK, width), F32),
            dma((3, 2)), dma((3, 2)),
            pltpu.VMEM((5, *small), F32), pltpu.VMEM((5, *small), F32), dma((5,)), dma((5,)),
        ]
        + sum_scratch(rows, cols)
        + [part(2, 2, 2), part(2, 2), part(2), part(), dma((6, 2, 2)), dma((6, 2, 2))],
        compiler_params=params(has_side_effects=True, collective_id=3),
        cost_estimate=cost(8 * count * width * 1024, 24 << 20),
        name="closing",
    )(cells, idx, *sums, *grads)


def write_kernel(
    a, b, embed, reduce_sum, expand_sum, joined_sum, small,
    table, embed_out, reduce_out, expand_out, output_out, joined_out,
    gains, shifts, biases, hidden_bias,
):
    wide = a.shape[6]
    lanes = table.shape[1]
    for n, piece in enumerate((a, b)):
        for u in range(2):
            value = piece[0, u, 0, 0, 0].astype(F32)
            for k in range(wide // lanes):
                row = ((2 * u + n) * wide) // lanes + k
                table[pl.ds(row, BLOCK, stride=4 * wide // lanes), :] = value[
                    :, k * lanes : (k + 1) * lanes
                ]
    embed_out[...] = embed[...]

    @pl.when(pl.program_id(0) == 0)
    def _():
        cols = reduce_sum.shape[2]
        rows = expand_sum.shape[1]
        wide = expand_out.shape[1]
        for n in range(2):
            reduce_out[n * cols : (n + 1) * cols, :] = reduce_sum[n].T
            expand_out[n * rows : (n + 1) * rows, :] = expand_sum[n, :, :wide]
            output_out[n * rows : (n + 1) * rows, :] = expand_sum[n, :, wide:]
            joined_out[n * rows : (n + 1) * rows, :] = joined_sum[n]
        for out, order in ((gains, (0, 2, 5)), (shifts, (1, 3, 6)), (biases, (8, 9, 4, 7))):
            for n, row in enumerate(order):
                out[n : n + 1, :] = small[row : row + 1, :]
        for n in range(hidden_bias.shape[0]):
            hidden_bias[n : n + 1, :] = small[10 + n : 11 + n, :]


def write(done, embed, reduce_sum, expand_sum, joined_sum, small, table_rows, ff):
    wide = done.shape[6]
    width = 4 * wide
    tokens = embed.shape[0]
    block = (1, 2, 1, 1, 1, BLOCK, wide)
    first = lambda i: (0, 0, i % 2, (i // 2) % 2, i // 4, 0, 0)
    second = lambda i: (1, 0, i % 2, i // 4, (i // 2) % 2, 0, 0)
    rows = 2 * expand_sum.shape[1]
    cols = ff // N_TAB
    f32 = lambda *n: jax.ShapeDtypeStruct(n, F32)
    shapes = [
        f32(2 * reduce_sum.shape[2], reduce_sum.shape[1]), f32(rows, cols),
        f32(rows, expand_sum.shape[2] - cols), f32(rows, joined_sum.shape[2]),
        f32(3, width), f32(3, width), f32(4, width), f32(ff // width, width),
    ]
    lanes = 128
    part = pl.BlockSpec((tokens // 8, width), lambda i: (i, 0))
    table, *rest = pl.pallas_call(
        write_kernel,
        grid=(8,),
        in_specs=[pl.BlockSpec(block, first), pl.BlockSpec(block, second), part]
        + [full(v.shape) for v in (reduce_sum, expand_sum, joined_sum, small)],
        out_specs=[pl.BlockSpec((BLOCK * width // lanes, lanes), lambda i: (i, 0)), part]
        + [full(v.shape) for v in shapes],
        out_shape=[f32(table_rows * width // lanes, lanes), f32(tokens, width)] + shapes,
        compiler_params=params(),
        cost_estimate=cost(0, 16 << 20),
        name="write",
    )(done, done, embed, reduce_sum, expand_sum, joined_sum, small)
    return table.reshape(1, table_rows, width), *rest


def flip_tok(value, bit, size):
    return lax.ppermute(value, "tok", [(i, i ^ bit) for i in range(size)])


def shift_tab(value, shift, size):
    return lax.ppermute(value, "tab", [(i, (i + shift) % size) for i in range(size)])


def small_sum(value, n_tok, n_tab):
    bit = 1
    while bit < n_tok:
        value = value + flip_tok(value, bit, n_tok)
        bit *= 2
    total = value
    for shift in range(1, n_tab):
        total = total + shift_tab(value, shift, n_tab)
    return total


def body(
    n_tok, n_tab,
    embedded, cell_index, cell_boxes, box_tables, joined_weight, output_weight,
    expand_weight, reduce_weight, hidden_bias, bias_rows, norm_gains, norm_shifts, cotangent,
):
    tokens, width = embedded.shape
    pages, length = cell_index.shape
    table_rows = box_tables.shape[1]
    ff = expand_weight.shape[1]
    tok = lax.axis_index("tok").astype(jnp.int32).reshape(1)
    z = lax.axis_index("tab")
    cubic = n_tok == 8 and n_tab == 4

    corners = cell_boxes[:, :, :CELLS]
    lo = lambda n: jnp.minimum(corners[:, n], corners[:, n + 2]).reshape(-1)
    hi = lambda n: jnp.maximum(corners[:, n], corners[:, n + 2]).reshape(-1)
    left, right, top, bottom = lo(0), hi(0), lo(1), hi(1)
    none = jnp.full_like(left, -1)
    index_table = jnp.stack(
        [
            jnp.stack([left, right]),
            jnp.stack([top, bottom]),
            jnp.stack([right - left, none]),
            jnp.stack([bottom - top, none]),
        ]
    )
    pick_table = lambda i: lax.dynamic_index_in_dim(index_table, i, 0, keepdims=False)
    group_index = jnp.stack(
        [pick_table(z)]
        + [shift_tab(pick_table((z + s) % n_tab), s, n_tab) for s in range(1, n_tab)]
    )
    padded = jnp.pad(box_tables[0], ((0, 1024 - table_rows), (0, 0)))
    found = lookup(group_index, padded)
    terms = [found[0]] + [shift_tab(found[s], n_tab - s, n_tab) for s in range(1, n_tab)]

    q, k, v, normed, normed_low, rstd0 = embed(
        embedded, cell_index, terms, joined_weight, norm_gains, norm_shifts, bias_rows
    )
    mixed, lse = attn_fwd(q, k, v, pages)
    layer_out, after, after_low, rstd1, act, slope, gs2, gffn, sums2 = ffn_fwd(
        mixed, normed, output_weight, expand_weight, reduce_weight, hidden_bias,
        bias_rows, norm_gains, norm_shifts, cotangent, min(256, tokens),
    )
    if cubic:
        gs1, gmixed, hidden_sum, sums1, *parts, reduce_sum = ffn_grads(
            gffn, act, slope, gs2, after, after_low, rstd1, mixed, reduce_weight, expand_weight,
            output_weight, norm_gains, norm_shifts,
        )
    else:
        parts = None
        gh, gs1, gattn, gmixed, hidden_sum, sums1 = ffn_bwd(
            gffn, slope, gs2, after, rstd1, reduce_weight, expand_weight, output_weight,
            norm_gains, norm_shifts,
        )
    embedded_grad, cell_grad, sums0, sums_qv, *more = back(
        q, k, v, mixed, gmixed, lse, normed_low, gs1, joined_weight, normed, rstd0, cell_index,
        norm_gains, norm_shifts, parts,
    )
    if cubic:
        parts, expand_sum = more[:2], more[2:]
    else:
        gj = more[0]

    sums = (sums0, sums1, sums2, sums_qv, hidden_sum)
    if cubic:
        done, joined_sum, small = closing(cell_grad, group_index, sums, parts)
        (
            tables_grad, embedded_grad, reduce_grad, expand_grad, output_grad, joined_grad,
            gains_grad, shifts_grad, biases_grad, hidden_bias_grad,
        ) = write(
            done, embedded_grad, reduce_sum, expand_sum[0], joined_sum, small, table_rows, ff
        )
        hidden_bias_grad = hidden_bias_grad.reshape(-1)
    else:
        cell_grads = [cell_grad] + [shift_tab(cell_grad, s, n_tab) for s in range(1, n_tab)]
        part_a, part_b = table_part(jnp.zeros_like(tok), group_index, cell_grads, 8)
        both = jnp.concatenate([part_a, part_b], axis=2).astype(F32)
        tables_grad = lax.psum(both.reshape(1, -1, width)[:, :table_rows], "tok")
        small = jnp.concatenate([part.reshape(-1) for part in sums]).reshape(-1, 128)
        small = small_sum(small, n_tok, n_tab).reshape(-1)
        row = small.reshape(-1, width)
        gains_grad = jnp.stack([row[0], row[2], row[5]])
        shifts_grad = jnp.stack([row[1], row[3], row[6]])
        biases_grad = jnp.stack([row[8], row[9], row[4], row[7]])
        hidden_bias_grad = small[10 * width :]
        both = lambda a, b: jnp.einsum("ta,tb->ab", a, b, preferred_element_type=F32).astype(BF)

        def scattered(part):
            part = lax.psum_scatter(part, "tok", scatter_dimension=0, tiled=True)
            return lax.psum_scatter(part, "tab", scatter_dimension=1, tiled=True).astype(F32)

        reduce_grad = scattered(both(act, gffn))
        expand_grad = scattered(both(after_low, gh))
        output_grad = scattered(both(mixed, gattn))
        joined_grad = scattered(both(normed_low, jnp.concatenate([gj[0], gj[1], gj[2]], axis=1)))

    return (
        layer_out, embedded_grad, tables_grad, joined_grad, output_grad, expand_grad,
        reduce_grad, hidden_bias_grad, biases_grad, gains_grad, shifts_grad,
    )


def solution(mesh):
    rows = P(("tok", "tab"), None)
    return jax.shard_map(
        functools.partial(body, mesh.shape["tok"], mesh.shape["tab"]),
        mesh=mesh,
        in_specs=(
            rows, rows, P(("tok", "tab"), None, None), P("tab", None, None),
            P(), P(), P(), P(), P(), P(), P(), P(), rows,
        ),
        out_specs=(
            rows, rows, P("tab", None, None), P("tok", "tab"), P("tok", "tab"),
            P("tok", "tab"), P("tok", "tab"), P(), P(), P(), P(),
        ),
        check_vma=False,
    )
```

```python
import functools

import jax
import jax.numpy as jnp
from jax import lax
from jax.experimental import pallas as pl
from jax.experimental.pallas import tpu as pltpu
from jax.sharding import PartitionSpec as P

HEADS = 16
HEAD_DIM = 64
CELLS = 128
EPSILON = 1e-05
SCALE = HEAD_DIM ** (-0.5)
LOG2E = 1.4426950408889634
F32 = jnp.float32
BF = jnp.bfloat16
NN = ((1,), (0,))
NT = ((1,), (1,))
TN = ((0,), (0,))
ANY = pl.ANY

TAIL_P = 0.305
TAIL_C = (
    0.12164194255155772,
    0.12243138164026345,
    0.10365178645525906,
    0.12022714029486306,
    -0.03641303195181058,
    0.1839499605096701,
    -0.15192310059752684,
    0.03643391798251271,
)


def dot(a, b, dims):
    return lax.dot_general(a, b, (dims, ((), ())), preferred_element_type=F32)


def params(**kw):
    return pltpu.CompilerParams(vmem_limit_bytes=60 << 20, **kw)


def cost(flops, nbytes, trans=0):
    return pl.CostEstimate(
        flops=int(flops), bytes_accessed=int(nbytes), transcendentals=int(trans)
    )


def full(shape):
    zeros = (0,) * len(shape)
    return pl.BlockSpec(shape, lambda *_: zeros, pipeline_mode=pl.Buffered(1))


def gelu_parts(h):
    a = jnp.abs(h)
    t = 1.0 / (1.0 + TAIL_P * a)
    poly = jnp.full_like(t, TAIL_C[-1])
    for c in TAIL_C[-2::-1]:
        poly = poly * t + c
    e = jnp.exp2(h * h * (-0.5 * LOG2E))
    tail = poly * t * e
    phi_cdf = jnp.where(h > 0, 1.0 - tail, tail)
    act = h * phi_cdf
    slope = phi_cdf + h * e * 0.3989422804014327
    return act, slope


def norm_stats(v):
    mean = jnp.mean(v, axis=-1, keepdims=True)
    centred = v - mean
    var = jnp.mean(centred * centred, axis=-1, keepdims=True)
    rstd = lax.rsqrt(var + EPSILON)
    return centred * rstd, rstd


def norm_back(y, xh, rstd, gain):
    u = y * gain
    return (
        u - jnp.mean(u, axis=-1, keepdims=True) - xh * jnp.mean(u * xh, axis=-1, keepdims=True)
    ) * rstd


def colsum(v):
    return jnp.sum(v, axis=0, keepdims=True)


def lookup_kernel(idx, table, out):
    rows = table.shape[0]
    count = idx.shape[2]
    number = lax.broadcasted_iota(jnp.int32, (rows, count), 0)
    first = (number == idx[0, 0:1, :]).astype(F32)
    second = (number == idx[0, 1:2, :]).astype(F32)
    out[0] = dot((first + second).astype(BF), table[...], TN).astype(BF)


def lookup(idx, table):
    groups, _, count = idx.shape
    rows, width = table.shape
    return pl.pallas_call(
        lookup_kernel,
        grid=(groups,),
        in_specs=[
            pl.BlockSpec((1, 2, count), lambda i: (i, 0, 0)),
            full((rows, width)),
        ],
        out_specs=pl.BlockSpec((1, count, width), lambda i: (i, 0, 0)),
        out_shape=jax.ShapeDtypeStruct((groups, count, width), BF),
        compiler_params=params(),
        cost_estimate=cost(2 * groups * count * rows * width, 2 * groups * count * width),
        name="lookup",
    )(idx, table)


def embed_kernel(
    emb, ci, terms, w, gains, shifts, bias, q, k, v, normed, low, rstd_out
):
    width = emb.shape[1]
    tokens = emb.shape[0]
    cells = terms[...].reshape(4 * CELLS, width)
    number = lax.broadcasted_iota(jnp.int32, (CELLS, tokens), 0)
    pick = (number == ci[0]).astype(F32).astype(BF)
    pick = jnp.concatenate([pick] * 4, axis=0)
    box = dot(pick, cells, TN)
    xh, rstd = norm_stats(emb[...].astype(F32) + box)
    y = xh * gains[0:1] + shifts[0:1]
    normed[...] = y
    rstd_out[...] = rstd
    y_low = y.astype(BF)
    low[...] = y_low
    q[...] = ((dot(y_low, w[:, :width], NN) + bias[0:1]) * SCALE).astype(BF)
    k[...] = dot(y_low, w[:, width : 2 * width], NN).astype(BF)
    v[...] = (dot(y_low, w[:, 2 * width :], NN) + bias[1:2]).astype(BF)


def embed(emb, ci, terms, w, gains, shifts, bias):
    tokens, width = emb.shape
    pages, length = ci.shape
    rows = pl.BlockSpec((length, width), lambda i: (i, 0))
    shape = lambda dt, n=width: jax.ShapeDtypeStruct((tokens, n), dt)
    return pl.pallas_call(
        embed_kernel,
        grid=(pages,),
        in_specs=[rows, pl.BlockSpec((1, 1, length), lambda i: (i, 0, 0))]
        + [pl.BlockSpec((4, CELLS, width), lambda i: (0, i, 0))]
        + [full(w.shape), full(gains.shape), full(shifts.shape), full(bias.shape)],
        out_specs=[rows] * 5 + [pl.BlockSpec((length, 1), lambda i: (i, 0))],
        out_shape=[shape(BF), shape(BF), shape(BF), shape(F32), shape(BF), shape(F32, 1)],
        compiler_params=params(),
        cost_estimate=cost(2 * tokens * width * 3 * width, 26 << 20),
        name="embed_joined",
    )(emb, ci.reshape(pages, 1, length), terms, w, gains, shifts, bias)


STAGES = 4


def neighbours():
    tok, z = lax.axis_index("tok"), lax.axis_index("tab")
    core = {"tok": tok + 1 - 2 * (tok % 2)}
    x = {"tok": tok + 2 - 4 * ((tok // 2) % 2)}
    y = {"tok": tok + 4 - 8 * (tok // 4)}
    peers = [{"tab": (z + s) % 4} for s in range(1, 4)]
    return core, x, y, peers


def meet(devices):
    barrier = pltpu.get_barrier_semaphore()
    for d in devices:
        pl.semaphore_signal(barrier, inc=1, device_id=d, device_id_type=pl.DeviceIdType.MESH)
    pl.semaphore_wait(barrier, len(devices))


def sum_scratch(rows, cols):
    part = lambda *n: pltpu.VMEM((*n, rows, cols), BF)
    return [
        part(2, 4, 4), part(2, 4, 4), part(2, 4, 2), part(2, 4), part(2, 3),
        pltpu.SemaphoreType.DMA((2, 4)),
        pltpu.SemaphoreType.DMA((STAGES, 2, 4)),
        pltpu.SemaphoreType.DMA((STAGES, 2, 4)),
    ]


class Summing:
    def __init__(self, grads, out, scratch):
        self.grads, self.out = grads, out
        if grads is None:
            both, scratch = scratch[0], (scratch[0].at[0], *scratch[1:5], None, *scratch[5:])
            self.part = both.at[1]
        self.own, self.r0, self.r1, self.r2, self.r3, self.local, self.sent, self.got = scratch
        core, x, y, peers = neighbours()
        self.core, self.first, self.second, self.peers = core, (x, y), (y, x), peers
        self.z = lax.axis_index("tab")

    def devices(self):
        return [self.core, self.first[0], self.first[1], *self.peers]

    def copy(self, stage, ch, i):
        zc = (self.z + (i + 1)) % 4
        src, dst, to = (
            (
                lambda: self.part.at[ch, i] if self.grads is None else self.grads[ch].at[1, zc],
                self.r0.at[ch, i],
                self.core,
            ),
            (lambda: self.own.at[ch, i, pl.ds(2, 2)], self.r1.at[ch, i], self.first[ch]),
            (lambda: self.own.at[ch, i, 1], self.r2.at[ch, i], self.second[ch]),
            (lambda: self.own.at[ch, i, 0], self.r3.at[ch, min(i, 2)], self.peers[min(i, 2)]),
        )[stage]
        return pltpu.make_async_remote_copy(
            src_ref=src(), dst_ref=dst,
            send_sem=self.sent.at[stage, ch, i], recv_sem=self.got.at[stage, ch, i],
            device_id=to, device_id_type=pl.DeviceIdType.MESH,
        )

    def load(self, ch, i):
        zc = (self.z + (i + 1)) % 4
        return pltpu.make_async_copy(
            self.grads[ch].at[0, zc], self.own.at[ch, i], self.local.at[ch, i]
        )

    def start(self):
        for i in range(4):
            for ch in range(2):
                self.copy(0, ch, i).start()
                if self.grads is not None:
                    self.load(ch, i).start()

    def step(self, stage, i):
        for ch in range(2):
            self.copy(stage - 1, ch, i).wait_recv()
            if stage == 1:
                if self.grads is not None:
                    self.load(ch, i).wait()

                def add(j, _, ch=ch):
                    self.own[ch, i, j] = self.own[ch, i, j] + self.r0[ch, i, j]
                    return 0

                lax.fori_loop(0, 4, add, 0)
            elif stage == 2:

                def add(j, _, ch=ch):
                    self.own[ch, i, j] = self.own[ch, i, j] + self.r1[ch, i, j]
                    return 0

                lax.fori_loop(0, 2, add, 0)
            elif i < 3:
                self.own[ch, i, 0] = self.own[ch, i, 0] + self.r2[ch, i]
            if stage < 3 or i < 3:
                self.copy(stage, ch, i).start()

    def finish(self):
        for ch in range(2):
            total = self.own[ch, 3, 0].astype(F32) + self.r2[ch, 3].astype(F32)
            for i in range(3):
                self.copy(3, ch, i).wait_recv()
                total = total + self.r3[ch, i].astype(F32)
            self.out[ch] = total
        for stage in range(STAGES):
            for ch in range(2):
                for i in range(4 if stage < 3 else 3):
                    self.copy(stage, ch, i).wait_send()

    def run(self, step, plan):
        for at, events in plan.items():

            @pl.when(step == at)
            def _(events=events):
                for stage, i in events:
                    if stage == 0:
                        self.start()
                    elif stage == 4:
                        self.finish()
                    else:
                        self.step(stage, i)


def split_rel(r):
    return r & 1, (r >> 1) & 1, r >> 2


def rel_of(b):
    tok = lax.axis_index("tok")
    core, x, y = split_rel(b)
    flip = lambda static, mine: 1 - mine if static else mine
    return flip(core, tok % 2), flip(x, (tok // 2) % 2), flip(y, tok // 4)


def put_rows(g, ga, gb, cols, rows):
    half = rows // 2
    for b in range(8):
        core, x, y = rel_of(b)
        ga[core, 0, 2 * x + y, :, cols] = g[b * rows : b * rows + half]
        gb[core, 0, 2 * y + x, :, cols] = g[b * rows + half : (b + 1) * rows]


def sum_specs(grads, number):
    if grads is None:
        return [], [], [], [], {}
    rows, cols = grads[0].shape[3:]
    return (
        [pl.BlockSpec(memory_space=pl.ANY)] * 2,
        [full((2, rows, cols))],
        [jax.ShapeDtypeStruct((2, rows, cols), F32)],
        sum_scratch(rows, cols),
        {"has_side_effects": True, "collective_id": number},
    )


BLOCK = 128


def spread_kernel(
    idx, table, found, group_idx,
    held, numbers, ring_sent, ring_got, plane_sent, plane_got, idx_sent, idx_got,
):
    tok, z = lax.axis_index("tok"), lax.axis_index("tab")
    core, x, y, peers = neighbours()
    c, cx, cy = tok % 2, (tok // 2) % 2, tok // 4
    first, second = (x, y), (y, x)
    f, g = (cx, cy), (cy, cx)
    meet([core, x, y, *peers])
    half = table.shape[1] // 2
    count = idx.shape[2]

    def ring(k, ch):
        if k == 0:
            start = pl.multiple_of(tok * BLOCK, BLOCK)
            src = table.at[pl.ds(start, BLOCK), pl.ds(ch * half, half)]
        else:
            src = held.at[k - 1, ch, c, g[ch], f[ch]]
        return pltpu.make_async_remote_copy(
            src_ref=src, dst_ref=held.at[k, ch, c, g[ch], f[ch]],
            send_sem=ring_sent.at[k, ch], recv_sem=ring_got.at[k, ch],
            device_id=peers[0], device_id_type=pl.DeviceIdType.MESH,
        )

    def plane(stage, k, ch):
        src, to = (
            (held.at[k, ch, c, g[ch], f[ch]], first[ch]),
            (held.at[k, ch, c, g[ch]], second[ch]),
            (held.at[k, ch, c], core),
        )[stage]
        return pltpu.make_async_remote_copy(
            src_ref=src, dst_ref=src,
            send_sem=plane_sent.at[stage, k, ch], recv_sem=plane_got.at[stage, k, ch],
            device_id=to, device_id_type=pl.DeviceIdType.MESH,
        )

    def number(s):
        return pltpu.make_async_remote_copy(
            src_ref=idx.at[(z + s) % 4], dst_ref=numbers.at[s - 1],
            send_sem=idx_sent.at[s - 1], recv_sem=idx_got.at[s - 1],
            device_id=peers[s - 1], device_id_type=pl.DeviceIdType.MESH,
        )

    def picks(owner):
        out = []
        for b in range(8):
            row = lax.broadcasted_iota(jnp.int32, (BLOCK, count), 0) + b * BLOCK
            one = (row == idx[owner, 0:1, :]).astype(F32)
            two = (row == idx[owner, 1:2, :]).astype(F32)
            out.append((one + two).astype(BF))
        return out

    def arrive(k):
        for ch in range(2):
            ring(k, ch).wait_recv()
            if k < 2:
                ring(k + 1, ch).start()
            plane(0, k, ch).start()

    def go_on(stage, k):
        for ch in range(2):
            plane(stage - 1, k, ch).wait_recv()
            plane(stage, k, ch).start()

    def look_up(k):
        rows = picks((z + 3 - k) % 4)
        for ch in range(2):
            plane(2, k, ch).wait_recv()
            order = [
                4 * a + 2 * b + n if ch == 0 else 4 * b + 2 * a + n
                for n in range(2)
                for a in range(2)
                for b in range(2)
            ]
            pick = jnp.concatenate([rows[b] for b in order], axis=0)
            data = held[k, ch].reshape(8 * BLOCK, half)
            found[k + 1, :, ch * half : (ch + 1) * half] = dot(pick, data, TN).astype(BF)

    for ch in range(2):
        ring(0, ch).start()
    for s in range(1, 4):
        number(s).start()
    found[0] = dot(jnp.concatenate(picks(z), axis=0), table[...], TN).astype(BF)
    arrive(0)
    go_on(1, 0)
    arrive(1)
    go_on(1, 1)
    go_on(2, 0)
    arrive(2)
    go_on(1, 2)
    group_idx[0] = idx[z]
    for s in range(1, 4):
        number(s).wait_recv()
        group_idx[s] = numbers[s - 1]
    look_up(0)
    go_on(2, 1)
    look_up(1)
    go_on(2, 2)
    look_up(2)
    for s in range(1, 4):
        number(s).wait_send()
    for k in range(3):
        for ch in range(2):
            ring(k, ch).wait_send()
            for stage in range(3):
                plane(stage, k, ch).wait_send()


def spread(idx, table):
    n_tab, _, count = idx.shape
    rows, width = table.shape
    dma = pltpu.SemaphoreType.DMA
    return pl.pallas_call(
        spread_kernel,
        grid=(1,),
        in_specs=[full(idx.shape), full(table.shape)],
        out_specs=[full((n_tab, count, width)), full(idx.shape)],
        out_shape=[
            jax.ShapeDtypeStruct((n_tab, count, width), BF),
            jax.ShapeDtypeStruct(idx.shape, jnp.int32),
        ],
        scratch_shapes=[
            pltpu.VMEM((3, 2, 2, 2, 2, BLOCK, width // 2), BF),
            pltpu.VMEM((3, 2, count), jnp.int32),
            dma((3, 2)), dma((3, 2)), dma((3, 3, 2)), dma((3, 3, 2)), dma((3,)), dma((3,)),
        ],
        compiler_params=params(has_side_effects=True, collective_id=4),
        cost_estimate=cost(8 * count * width * rows, 8 << 20),
        name="spread",
    )(idx, table)


HP = 4


def head_masks(length, pair):
    lane = lax.broadcasted_iota(jnp.int32, (length, pair), 1)
    return lane < HEAD_DIM


def attn_fwd_kernel(q, k, v, mixed, lse):
    length = q.shape[0]
    pair = 2 * HEAD_DIM
    low_half = head_masks(length, pair)
    zero = jnp.zeros((length, pair), BF)
    for p in range(HP // 2):
        cols = slice(p * pair, (p + 1) * pair)
        qp, kp, vp = q[:, cols], k[:, cols], v[:, cols]
        vt = vp.T
        outs = []
        for h in range(2):
            km = jnp.where(low_half, kp, zero) if h == 0 else jnp.where(low_half, zero, kp)
            st = dot(km, qp, NT)
            top = jnp.max(st, axis=0, keepdims=True)
            raised = jnp.exp2((st - top) * LOG2E)
            total = jnp.sum(raised, axis=0, keepdims=True)
            lse[0, 0, 2 * p + h : 2 * p + h + 1, :] = top + jnp.log(total)
            ot = dot(vt[h * HEAD_DIM : (h + 1) * HEAD_DIM], raised.astype(BF), NN)
            outs.append(ot * (1.0 / total))
        mixed[:, cols] = jnp.concatenate(outs, axis=0).T.astype(BF)


def attn_fwd(q, k, v, pages):
    tokens, width = q.shape
    length = tokens // pages
    steps = HEADS // HP
    blk = pl.BlockSpec((length, HP * HEAD_DIM), lambda i, j: (i, j))
    return pl.pallas_call(
        attn_fwd_kernel,
        grid=(pages, steps),
        in_specs=[blk] * 3,
        out_specs=[blk, pl.BlockSpec((1, 1, HP, length), lambda i, j: (i, j, 0, 0))],
        out_shape=[
            jax.ShapeDtypeStruct((tokens, width), BF),
            jax.ShapeDtypeStruct((pages, steps, HP, length), F32),
        ],
        compiler_params=params(),
        cost_estimate=cost(14e9, 8 << 20, pages * HEADS * length * length),
        name="attention",
    )(q, k, v)


def attn_back(q, k, v, mixed, go, lse, put):
    length = q.shape[0]
    pair = 2 * HEAD_DIM
    low_half = head_masks(length, pair)
    zero = jnp.zeros((length, pair), BF)

    def pick(x, h):
        return jnp.where(low_half, x, zero) if h == 0 else jnp.where(low_half, zero, x)

    for p in range(HP // 2):
        cols = slice(p * pair, (p + 1) * pair)
        qp, kp, vp, op, gp = q[:, cols], k[:, cols], v[:, cols], mixed[:, cols], go[:, cols]
        kt = kp.T
        prod_t = (op.astype(F32) * gp.astype(F32)).T
        dq_t, dk, dv = [], None, None
        for h in range(2):
            st = dot(pick(kp, h), qp, NT)
            probs = jnp.exp2((st - lse[0, 0, 2 * p + h : 2 * p + h + 1, :]) * LOG2E)
            dv_h = dot(probs.astype(BF), pick(gp, h), NN)
            dpt = dot(pick(vp, h), gp, NT)
            delta = colsum(prod_t[h * HEAD_DIM : (h + 1) * HEAD_DIM])
            ds = (probs * (dpt - delta)).astype(BF)
            dk_h = dot(ds, pick(qp, h), NN)
            dq_t.append(dot(kt[h * HEAD_DIM : (h + 1) * HEAD_DIM], ds, NN))
            dv = dv_h if dv is None else dv + dv_h
            dk = dk_h if dk is None else dk + dk_h
        dq = (jnp.concatenate(dq_t, axis=0).T.astype(BF).astype(F32) * SCALE).astype(BF)
        put(p * pair, pair, dq, dk.astype(BF), dv.astype(BF))


FC = 512
FWD = 1024
RC = 128
MC = 512


def ffn_fwd_kernel(
    mixed, normed, wo, we, wr, hb, bias, gains, shifts, cot,
    out, after_out, low_out, rstd_out, act_out, slope_out, gs2_out, gffn_out, sums,
):
    ff = we.shape[1]
    attn_sum = normed[...] + (dot(mixed[...], wo[...], NN) + bias[2:3])
    xh, rstd = norm_stats(attn_sum)
    after = xh * gains[1:2] + shifts[1:2]
    after_out[...] = after
    rstd_out[...] = rstd
    low = after.astype(BF)
    low_out[...] = low
    total = after + bias[3:4]
    count = ff // FWD
    hidden = []
    for j in range(count + 1):
        if j < count:
            cols = slice(j * FWD, (j + 1) * FWD)
            hidden.append(dot(low, we[:, cols], NN) + hb[:, cols])
        if j > 0:
            cols = slice((j - 1) * FWD, j * FWD)
            act, slope = gelu_parts(hidden[j - 1])
            act = act.astype(BF)
            act_out[:, cols] = act
            slope_out[:, cols] = slope.astype(BF)
            total = total + dot(act, wr[cols, :], NN)
    xh, rstd = norm_stats(total)
    out[...] = (xh * gains[2:3] + shifts[2:3]).astype(BF)
    y = cot[...].astype(F32)
    gs2 = norm_back(y, xh, rstd, gains[2:3])
    gs2_out[...] = gs2
    gffn = gs2.astype(BF)
    gffn_out[...] = gffn
    part = jnp.concatenate([colsum(y * xh), colsum(y), colsum(gffn.astype(F32))], axis=0)

    @pl.when(pl.program_id(0) == 0)
    def _():
        sums[...] = part

    @pl.when(pl.program_id(0) != 0)
    def _():
        sums[...] = sums[...] + part


def ffn_fwd(mixed, normed, wo, we, wr, hb, bias, gains, shifts, cot, tile):
    tokens, width = mixed.shape
    ff = we.shape[1]
    rows = pl.BlockSpec((tile, width), lambda i: (i, 0))
    long = pl.BlockSpec((tile, ff), lambda i: (i, 0))
    shape = lambda dt, n=width: jax.ShapeDtypeStruct((tokens, n), dt)
    hb = hb.reshape(1, ff)
    return pl.pallas_call(
        ffn_fwd_kernel,
        grid=(tokens // tile,),
        in_specs=[rows, rows]
        + [full(a.shape) for a in (wo, we, wr, hb, bias, gains, shifts)]
        + [rows],
        out_specs=[rows, rows, rows, pl.BlockSpec((tile, 1), lambda i: (i, 0)), long, long, rows, rows]
        + [pl.BlockSpec((3, width), lambda i: (0, 0))],
        out_shape=[
            shape(BF), shape(F32), shape(BF), shape(F32, 1), shape(BF, ff), shape(BF, ff),
            shape(F32), shape(BF), jax.ShapeDtypeStruct((3, width), F32),
        ],
        compiler_params=params(),
        cost_estimate=cost(2 * tokens * width * (width + 2 * ff), 60 << 20, tokens * ff * 2),
        name="ffn_forward",
    )(mixed, normed, wo, we, wr, hb, bias, gains, shifts, cot)


def second_norm_back(gs1_out, after, rstd, gains, shifts, gattn_out, sums):
    tokens, width = after.shape

    def norm(i, carry):
        rows = pl.ds(pl.multiple_of(i * RC, RC), RC)
        total = gs1_out[rows, :]
        xh = (after[rows, :] - shifts[1:2]) * (1.0 / gains[1:2])
        gs1 = norm_back(total, xh, rstd[rows, :], gains[1:2])
        gs1_out[rows, :] = gs1
        gattn = gs1.astype(BF)
        gattn_out[rows, :] = gattn
        g, s, b = carry
        return g + colsum(total * xh), s + colsum(total), b + colsum(gattn.astype(F32))

    zero = jnp.zeros((1, width), F32)
    sums[...] = jnp.concatenate(lax.fori_loop(0, tokens // RC, norm, (zero, zero, zero)), axis=0)


def ffn_bwd_kernel(
    gffn, gs2, after, rstd, wo, gains, shifts, slope, wr, we,
    gh_out, gs1_out, gattn_out, gmixed_out, hsum, sums,
):
    step, last = pl.program_id(0), pl.num_programs(0) - 1
    tokens, width = gffn.shape

    @pl.when(step == 0)
    def _():
        gs1_out[...] = gs2[...]

    part = jnp.zeros((1, slope.shape[1]), F32)
    for m in range(0, tokens, MC):
        rows = slice(m, m + MC)
        gh = (dot(gffn[rows, :], wr[...], NT) * slope[rows, :].astype(F32)).astype(BF)
        gh_out[rows, :] = gh
        part = part + colsum(gh.astype(F32))
        gs1_out[rows, :] = gs1_out[rows, :] + dot(gh, we[...], NT)
    hsum[...] = part

    @pl.when(step == last)
    def _():
        second_norm_back(gs1_out, after, rstd, gains, shifts, gattn_out, sums)
        for m in range(0, tokens, MC):
            rows = slice(m, m + MC)
            gmixed_out[rows, :] = dot(gattn_out[rows, :], wo[...], NT).astype(BF)


def ffn_bwd(gffn, slope, gs2, after, rstd, wr, we, wo, gains, shifts):
    tokens, width = gffn.shape
    ff = we.shape[1]
    whole = full((tokens, width))
    long = pl.BlockSpec((tokens, FC), lambda s: (0, s))
    shape = lambda dt, n=width: jax.ShapeDtypeStruct((tokens, n), dt)
    return pl.pallas_call(
        ffn_bwd_kernel,
        grid=(ff // FC,),
        in_specs=[whole, whole, whole, full((tokens, 1))]
        + [full(a.shape) for a in (wo, gains, shifts)]
        + [
            long,
            pl.BlockSpec((FC, width), lambda s: (s, 0)),
            pl.BlockSpec((width, FC), lambda s: (0, s)),
        ],
        out_specs=[long, whole, whole, whole]
        + [pl.BlockSpec((1, FC), lambda s: (0, s)), full((3, width))],
        out_shape=[
            shape(BF, ff), shape(F32), shape(BF), shape(BF),
            jax.ShapeDtypeStruct((1, ff), F32), jax.ShapeDtypeStruct((3, width), F32),
        ],
        compiler_params=params(),
        cost_estimate=cost(2 * tokens * width * (width + 2 * ff), 60 << 20),
        name="ffn_backward",
    )(gffn, gs2, after, rstd, wo, gains, shifts, slope, wr, we)


FFN_PLAN = {
    4: [(0, 0)],
    8: [(1, 0)],
    9: [(1, 1)],
    11: [(2, 0), (1, 2)],
    13: [(2, 1), (1, 3)],
    15: [(3, 0)],
    16: [(2, 2)],
    17: [(3, 1), (2, 3)],
    18: [(3, 2)],
    19: [(3, 3)],
}
N_TOK, N_TAB = 8, 4


def block_of_step(s):
    s = jnp.minimum(s, N_TOK - 1)
    return 1 - s // 4, 1 - (s // 2) % 2, 1 - s % 2


def ffn_grads_kernel(
    gffn_in, gs2_in, after, rstd, low, mixed, wo, gains, shifts, act, slope, wr, we,
    gs1_out, gmixed_out, hsum, sums, ga, gb, reduce_out,
    gffn, gh, local, *scratch,
):
    step, last = pl.program_id(0), pl.num_programs(0) - 1
    tokens, width = after.shape
    summing = Summing(None, reduce_out, scratch)
    both = scratch[0]
    z = lax.axis_index("tab")
    first = pltpu.make_async_copy(gffn_in, gffn, local.at[0])
    later = pltpu.make_async_copy(gs2_in, gs1_out, local.at[1])

    @pl.when(step == 0)
    def _():
        first.start()
        later.start()
        meet(summing.devices())
        first.wait()

    @pl.when(step == N_TOK)
    def _():
        later.wait()

    summing.run(step, FFN_PLAN)

    @pl.when(step < N_TOK)
    def _():
        core, x, y = block_of_step(step)
        g = dot(gffn[...], act[...], TN).astype(BF)
        rows, half = both.shape[4:]
        for zc in range(N_TAB):
            i = (zc + N_TAB - 1 - z) % N_TAB
            for ch in range(2):
                piece = g[zc * rows : (zc + 1) * rows, ch * half : (ch + 1) * half]
                both[core, ch, i, (2 * x + y, 2 * y + x)[ch]] = piece

    @pl.when((step >= N_TOK) & (step < 2 * N_TOK))
    def _():
        part = jnp.zeros((1, slope.shape[1]), F32)
        for m in range(0, tokens, MC):
            rows = slice(m, m + MC)
            g = (dot(gffn[rows, :], wr[...], NT) * slope[rows, :].astype(F32)).astype(BF)
            gh[step - N_TOK, rows, :] = g
            part = part + colsum(g.astype(F32))
            gs1_out[rows, :] = gs1_out[rows, :] + dot(g, we[...], NT)
        hsum[...] = part

    @pl.when(step == 2 * N_TOK - 1)
    def _():
        second_norm_back(gs1_out, after, rstd, gains, shifts, gffn, sums)
        for m in range(0, tokens, MC):
            rows = slice(m, m + MC)
            gmixed_out[rows, :] = dot(gffn[rows, :], wo[...], NT).astype(BF)

    @pl.when(step >= 2 * N_TOK)
    def _():
        n = step - 2 * N_TOK
        quarter = width // N_TAB
        rows = width // N_TOK
        wide = gh.shape[2]
        for m in range(2):
            g = dot(low[...], gh[2 * n + m], TN).astype(BF)
            put_rows(g, ga, gb, slice(m * wide, (m + 1) * wide), rows)
        piece = gffn[:, pl.ds(pl.multiple_of(n * quarter, quarter), quarter)]
        g = dot(mixed[...], piece, TN).astype(BF)
        put_rows(g, ga, gb, slice(2 * wide, 2 * wide + quarter), rows)

    @pl.when(step == last)
    def _():
        summing.finish()


def ffn_grads(gffn, act, slope, gs2, after, low, rstd, mixed, wr, we, wo, gains, shifts):
    tokens, width = gffn.shape
    ff = we.shape[1]
    whole = full((tokens, width))
    anywhere = pl.BlockSpec(memory_space=pl.ANY)
    wide = ff // N_TOK
    half = width // (2 * N_TOK)
    out_wide = (ff + width) // N_TAB
    back = lambda s: jnp.clip(s - N_TOK, 0, N_TOK - 1)
    grad = lambda s: jnp.clip(s - 2 * N_TOK, 0, N_TAB - 1)

    def act_block(s):
        core, x, y = block_of_step(s)
        tok = lax.axis_index("tok")
        flip = lambda rel, mine: rel + mine - 2 * rel * mine
        return 0, 4 * flip(y, tok // 4) + 2 * flip(x, (tok // 2) % 2) + flip(core, tok % 2)

    rows, cols = width // N_TAB, wide // 2
    part = lambda *n: pltpu.VMEM((*n, rows, cols), BF)
    dma = pltpu.SemaphoreType.DMA
    shape = lambda dt: jax.ShapeDtypeStruct((tokens, width), dt)
    piece = pl.BlockSpec((2, 1, 4, half, out_wide), lambda s: (0, grad(s), 0, 0, 0))
    return pl.pallas_call(
        ffn_grads_kernel,
        grid=(2 * N_TOK + N_TAB,),
        in_specs=[anywhere, anywhere, whole, full((tokens, 1)), whole, whole]
        + [full(a.shape) for a in (wo, gains, shifts)]
        + [
            pl.BlockSpec((tokens, wide), act_block),
            pl.BlockSpec((tokens, wide), lambda s: (0, back(s))),
            pl.BlockSpec((wide, width), lambda s: (back(s), 0)),
            pl.BlockSpec((width, wide), lambda s: (0, back(s))),
        ],
        out_specs=[
            whole, whole, pl.BlockSpec((1, wide), lambda s: (0, back(s))), full((3, width)),
            piece, piece, full((2, rows, cols)),
        ],
        out_shape=[
            shape(F32), shape(BF),
            jax.ShapeDtypeStruct((1, ff), F32), jax.ShapeDtypeStruct((3, width), F32),
            jax.ShapeDtypeStruct((2, 4, 4, half, out_wide), BF),
            jax.ShapeDtypeStruct((2, 4, 4, half, out_wide), BF),
            jax.ShapeDtypeStruct((2, rows, cols), F32),
        ],
        scratch_shapes=[
            pltpu.VMEM((tokens, width), BF), pltpu.VMEM((N_TOK, tokens, wide), BF), dma((2,)),
            part(2, 2, 4, 4), part(2, 4, 4), part(2, 4, 2), part(2, 4), part(2, 3),
            dma((STAGES, 2, 4)), dma((STAGES, 2, 4)),
        ],
        compiler_params=pltpu.CompilerParams(
            vmem_limit_bytes=67043328, has_side_effects=True, collective_id=1
        ),
        cost_estimate=cost(2 * tokens * width * (2 * width + 4 * ff), 60 << 20),
        name="ffn_backward_grads",
    )(gffn, gs2, after, rstd, low, mixed, wo, gains, shifts, act, slope, wr, we)


BACK_PLAN = {
    0: [(0, 0)],
    1: [(1, 0)],
    2: [(1, 1)],
    3: [(2, 0), (1, 2)],
    5: [(2, 1), (1, 3)],
    6: [(3, 0)],
    8: [(2, 2)],
    9: [(3, 1)],
    11: [(2, 3)],
    12: [(3, 2)],
    13: [(3, 3)],
}


def back_kernel(*refs, pages, summed):
    q, k, v, mixed, go, lse, low, gs1, w, normed, rstd, ci, gains, shifts = refs[:14]
    refs = refs[14:]
    grads, refs = refs[: 2 * summed], refs[2 * summed :]
    out, cells, sums0, sums_qv = refs[:4]
    refs = refs[4:]
    if summed:
        ga, gb, summed_out, gj = refs[:4]
        summing = Summing(grads, summed_out, refs[4:])
    else:
        gj_out, gj = refs
    step = pl.program_id(0)
    width = gs1.shape[1]
    length = q.shape[0]
    groups = HEADS // HP
    wide = HP * HEAD_DIM
    n_attn = groups * pages
    n_joined = 4 if summed else 0

    if summed:

        @pl.when(step == 0)
        def _():
            meet(summing.devices())

        summing.run(step, BACK_PLAN)

    @pl.when(step < n_attn)
    def _():
        group, page = step // pages, step % pages
        rows = pl.ds(pl.multiple_of(page * length, length), length)

        def put(at, size, dq, dk, dv):
            cols = pl.ds(pl.multiple_of(group * wide + at, size), size)
            gj[0, rows, cols] = dq
            gj[1, rows, cols] = dk
            gj[2, rows, cols] = dv
            part = jnp.concatenate([colsum(dq.astype(F32)), colsum(dv.astype(F32))], axis=0)

            @pl.when(page == 0)
            def _():
                sums_qv[:, cols] = part

            @pl.when(page != 0)
            def _():
                sums_qv[:, cols] = sums_qv[:, cols] + part

        attn_back(q, k, v, mixed, go, lse, put)

    if summed:
        quarter = width // 4
        for n in range(n_joined):

            @pl.when(step == n_attn + n)
            def _(n=n):
                for m in range(3):
                    third, at = (3 * n + m) // 4, (3 * n + m) % 4
                    piece = gj[third, :, at * quarter : (at + 1) * quarter]
                    g = dot(low[...], piece, TN).astype(BF)
                    put_rows(g, ga, gb, slice(m * quarter, (m + 1) * quarter), width // 8)

    @pl.when(step >= n_attn + n_joined)
    def _():
        page = step - (n_attn + n_joined)
        rows = pl.ds(pl.multiple_of(page * length, length), length)
        total = gs1[...]
        for n in range(3):
            total = total + dot(gj[n, rows, :], w[:, n * width : (n + 1) * width], NT)
        xh = (normed[...] - shifts[0:1]) * (1.0 / gains[0:1])
        grad = norm_back(total, xh, rstd[...], gains[0:1])
        out[...] = grad
        number = lax.broadcasted_iota(jnp.int32, (CELLS, length), 0)
        pick = (number == ci[0]).astype(F32).astype(BF)
        cells[...] = dot(pick, grad.astype(BF), NN).astype(BF)
        part = jnp.concatenate([colsum(total * xh), colsum(total)], axis=0)

        @pl.when(page == 0)
        def _():
            sums0[...] = part

        @pl.when(page != 0)
        def _():
            sums0[...] = sums0[...] + part

    if summed:

        @pl.when(step == pl.num_programs(0) - 1)
        def _():
            summing.finish()
    else:
        gj_out[...] = gj[...]


def back(q, k, v, mixed, go, lse, low, gs1, w, normed, rstd, ci, gains, shifts, grads):
    tokens, width = q.shape
    pages, length = ci.shape
    groups = HEADS // HP
    wide = HP * HEAD_DIM
    summed = grads is not None
    n_attn = groups * pages
    before = n_attn + (4 if summed else 0)
    at = lambda s: jnp.minimum(s, n_attn - 1)
    page = lambda s: jnp.maximum(s - before, 0)
    block = lambda s: jnp.clip(s - n_attn, 0, 3)
    blk = pl.BlockSpec((length, wide), lambda s: (at(s) % pages, at(s) // pages))
    rows = pl.BlockSpec((length, width), lambda s: (page(s), 0))
    out_specs = [
        rows,
        pl.BlockSpec((CELLS, width), lambda s: (page(s), 0)),
        full((2, width)),
        full((2, width)),
    ]
    out_shape = [
        jax.ShapeDtypeStruct((tokens, width), F32),
        jax.ShapeDtypeStruct((pages * CELLS, width), BF),
        jax.ShapeDtypeStruct((2, width), F32),
        jax.ShapeDtypeStruct((2, width), F32),
    ]
    whole_gj = (3, tokens, width)
    more_in, more_out, more_shape, more_scratch, more = sum_specs(grads, 2)
    if summed:
        half = width // 16
        piece = pl.BlockSpec((2, 1, 4, half, 3 * width // 4), lambda s: (0, block(s), 0, 0, 0))
        out_specs += [piece, piece]
        out_shape += [jax.ShapeDtypeStruct((2, 4, 4, half, 3 * width // 4), BF)] * 2
    else:
        out_specs += [full(whole_gj)]
        out_shape += [jax.ShapeDtypeStruct(whole_gj, BF)]
    return pl.pallas_call(
        functools.partial(back_kernel, pages=pages, summed=summed),
        grid=(before + pages,),
        in_specs=[blk] * 5
        + [
            pl.BlockSpec((1, 1, HP, length), lambda s: (at(s) % pages, at(s) // pages, 0, 0)),
            full(low.shape),
            rows,
            full(w.shape),
            rows,
            pl.BlockSpec((length, 1), lambda s: (page(s), 0)),
            pl.BlockSpec((1, 1, length), lambda s: (page(s), 0, 0)),
            full(gains.shape),
            full(shifts.shape),
        ]
        + more_in,
        out_specs=out_specs + more_out,
        out_shape=out_shape + more_shape,
        scratch_shapes=[pltpu.VMEM(whole_gj, BF)] + more_scratch,
        compiler_params=params(**more),
        cost_estimate=cost(70e9, 40 << 20, pages * HEADS * length * length),
        name="attention_joined_embed_back",
    )(
        q, k, v, mixed, go, lse, low, gs1, w, normed, rstd, ci.reshape(pages, 1, length),
        gains, shifts, *(grads or ()),
    )


def table_kernel(tok, idx, g0, g1, g2, g3, out_a, out_b):
    rows = out_a.shape[1]
    count = idx.shape[2]
    half = out_a.shape[2]
    base = (pl.program_id(0) ^ tok[0]) * rows
    number = lax.broadcasted_iota(jnp.int32, (rows, count), 0) + base
    picks = []
    for s in range(4):
        first = (number == idx[s, 0:1, :]).astype(F32)
        second = (number == idx[s, 1:2, :]).astype(F32)
        picks.append((first + second).astype(BF))
    pick = jnp.concatenate(picks, axis=1)
    grads = jnp.concatenate([g0[...], g1[...], g2[...], g3[...]], axis=0)
    total = dot(pick, grads, NN).astype(BF)
    out_a[0] = total[:, :half]
    out_b[0] = total[:, half:]


def table_part(tok, idx, grads, blocks):
    groups, _, count = idx.shape
    width = grads[0].shape[1]
    rows = 1024 // blocks
    half = width // 2
    out = pl.BlockSpec((1, rows, half), lambda i, t: (i, 0, 0))
    return pl.pallas_call(
        table_kernel,
        grid_spec=pltpu.PrefetchScalarGridSpec(
            num_scalar_prefetch=1,
            grid=(blocks,),
            in_specs=[full(idx.shape)] + [full((count, width))] * groups,
            out_specs=[out, out],
        ),
        out_shape=[jax.ShapeDtypeStruct((blocks, rows, half), BF)] * 2,
        compiler_params=params(),
        cost_estimate=cost(2 * 1024 * groups * count * width, 4 << 20),
        name="table_grad",
    )(tok, idx, *grads)


class TableSum:
    def __init__(self, scratch, done):
        self.part, self.r0, self.r1, self.r2, self.sent, self.got = scratch
        self.done = done
        tok = lax.axis_index("tok")
        core, x, y, _ = neighbours()
        self.c, cx, cy = tok % 2, (tok // 2) % 2, tok // 4
        self.core, self.first, self.second = core, (x, y), (y, x)
        self.f, self.g = (cx, cy), (cy, cx)

    def copy(self, stage, ch, u):
        c, f, g = self.c, self.f[ch], self.g[ch]
        part, done = self.part.at[ch, u], self.done.at[ch, u]
        src, dst, to = (
            (lambda: part.at[1 - c], self.r0.at[ch, u], self.core),
            (lambda: part.at[c, 1 - f], self.r1.at[ch, u], self.first[ch]),
            (lambda: part.at[c, f, 1 - g], self.r2.at[ch, u], self.second[ch]),
            (lambda: done.at[c, f, g], None, self.second[ch]),
            (lambda: done.at[c, f], None, self.first[ch]),
            (lambda: done.at[c], None, self.core),
        )[stage]
        src = src()
        return pltpu.make_async_remote_copy(
            src_ref=src, dst_ref=src if dst is None else dst,
            send_sem=self.sent.at[stage, ch, u], recv_sem=self.got.at[stage, ch, u],
            device_id=to, device_id_type=pl.DeviceIdType.MESH,
        )

    def store(self, u, ch, value):
        for b in range(8):
            c, x, y = split_rel(b)
            f, g = (x, y) if ch == 0 else (y, x)
            self.part[ch, u, c, f, g] = value[b * BLOCK : (b + 1) * BLOCK]
        self.copy(0, ch, u).start()

    def step(self, stage, u):
        for ch in range(2):
            c, f, g = self.c, self.f[ch], self.g[ch]
            self.copy(stage - 1, ch, u).wait_recv()
            if stage == 1:
                self.part[ch, u, c] = self.part[ch, u, c] + self.r0[ch, u]
            elif stage == 2:
                self.part[ch, u, c, f] = self.part[ch, u, c, f] + self.r1[ch, u]
            elif stage == 3:
                self.done[ch, u, c, f, g] = self.part[ch, u, c, f, g] + self.r2[ch, u]
            if stage < 6:
                self.copy(stage, ch, u).start()

    def finish(self):
        for stage in range(6):
            for ch in range(2):
                for u in range(2):
                    self.copy(stage, ch, u).wait_send()


def closing_kernel(
    cells, idx, sums0, sums1, sums2, sums_qv, hidden_sum, ga, gb, done, joined, small_out,
    ring, total, ring_sent, ring_got, held, arrived, small_sent, small_got, *scratch,
):
    summing = Summing((ga, gb), joined, scratch[:8])
    table = TableSum(scratch[8:], done)
    core, x, y, peers = neighbours()
    z = lax.axis_index("tab")
    hops = [core, x, y, {"tab": z + 1 - 2 * (z % 2)}, {"tab": z + 2 - 4 * (z // 2)}]
    meet([core, x, y, *peers])
    count = cells.shape[0]
    half = cells.shape[1] // 2

    def pass_on(k, h):
        cols = pl.ds(h * half, half)
        src = cells.at[:, cols] if k == 0 else ring.at[k - 1, :, cols]
        return pltpu.make_async_remote_copy(
            src_ref=src, dst_ref=ring.at[k, :, cols],
            send_sem=ring_sent.at[k, h], recv_sem=ring_got.at[k, h],
            device_id=peers[0], device_id_type=pl.DeviceIdType.MESH,
        )

    def small_copy(n):
        return pltpu.make_async_remote_copy(
            src_ref=held.at[n], dst_ref=arrived.at[n],
            send_sem=small_sent.at[n], recv_sem=small_got.at[n],
            device_id=hops[n], device_id_type=pl.DeviceIdType.MESH,
        )

    def small_step(n):
        small_copy(n - 1).wait_recv()
        value = held[n - 1] + arrived[n - 1]
        if n < 5:
            held[n] = value
            small_copy(n).start()
        else:
            small_out[...] = value

    def relay(k, h):
        pass_on(k - 1, h).wait_recv()
        pass_on(k, h).start()

    def pick(s):
        number = lax.broadcasted_iota(jnp.int32, (total.shape[0], count), 0)
        first = (number == idx[s, 0:1, :]).astype(F32)
        second = (number == idx[s, 1:2, :]).astype(F32)
        return (first + second).astype(BF)

    def last_arrival(u):
        pass_on(2, u).wait_recv()
        for ch in range(2):
            cols = slice((2 * u + ch) * half // 2, (2 * u + ch + 1) * half // 2)
            value = total[:, cols] + dot(last, ring[2, :, cols], NN)
            table.store(u, ch, value.astype(BF))

    pass_on(0, 0).start()
    pass_on(0, 1).start()
    at, width = 0, cells.shape[1]
    for part in (sums0, sums1, sums2, sums_qv):
        held[0, at : at + part.shape[0]] = part[...]
        at += part.shape[0]
    for n in range(hidden_sum.shape[1] // width):
        held[0, at + n : at + n + 1] = hidden_sum[:, n * width : (n + 1) * width]
    small_copy(0).start()
    summing.start()
    total[...] = dot(pick(0), cells[...], NN)
    small_step(1)
    summing.step(1, 0)
    small_step(2)
    summing.step(1, 1)
    relay(1, 0)
    summing.step(2, 0)
    summing.step(1, 2)
    small_step(3)
    relay(1, 1)
    total[...] = total[...] + dot(pick(1), ring[0], NN)
    summing.step(2, 1)
    summing.step(1, 3)
    relay(2, 0)
    small_step(4)
    summing.step(2, 2)
    relay(2, 1)
    summing.step(3, 0)
    summing.step(3, 1)
    summing.step(2, 3)
    total[...] = total[...] + dot(pick(2), ring[1], NN)
    last = pick(3)
    last_arrival(0)
    table.step(1, 0)
    last_arrival(1)
    summing.step(3, 2)
    small_step(5)
    table.step(2, 0)
    table.step(1, 1)
    table.step(3, 0)
    table.step(2, 1)
    table.step(4, 0)
    table.step(3, 1)
    table.step(5, 0)
    table.step(4, 1)
    table.step(6, 0)
    table.step(5, 1)
    summing.step(3, 3)
    summing.finish()
    table.step(6, 1)
    table.finish()
    for k in range(3):
        for h in range(2):
            pass_on(k, h).wait_send()
    for n in range(5):
        small_copy(n).wait_send()


def closing(cells, idx, sums, grads):
    count, width = cells.shape
    small = (sum(part.size for part in sums) // width, width)
    rows, cols = grads[0].shape[3:]
    wide = width // 4
    part = lambda *n: pltpu.VMEM((2, 2, *n, BLOCK, wide), BF)
    done = (2, 2, 2, 2, 2, BLOCK, wide)
    dma = pltpu.SemaphoreType.DMA
    return pl.pallas_call(
        closing_kernel,
        grid=(1,),
        in_specs=[full(cells.shape), full(idx.shape)]
        + [full(part.shape) for part in sums]
        + [pl.BlockSpec(memory_space=pl.ANY)] * 2,
        out_specs=[full(done), full((2, rows, cols)), full(small)],
        out_shape=[
            jax.ShapeDtypeStruct(done, BF),
            jax.ShapeDtypeStruct((2, rows, cols), F32),
            jax.ShapeDtypeStruct(small, F32),
        ],
        scratch_shapes=[
            pltpu.VMEM((3, count, width), BF), pltpu.VMEM((8 * BLOCK, width), F32),
            dma((3, 2)), dma((3, 2)),
            pltpu.VMEM((5, *small), F32), pltpu.VMEM((5, *small), F32), dma((5,)), dma((5,)),
        ]
        + sum_scratch(rows, cols)
        + [part(2, 2, 2), part(2, 2), part(2), part(), dma((6, 2, 2)), dma((6, 2, 2))],
        compiler_params=params(has_side_effects=True, collective_id=3),
        cost_estimate=cost(8 * count * width * 1024, 24 << 20),
        name="closing",
    )(cells, idx, *sums, *grads)


def write_kernel(
    a, b, embed, reduce_sum, expand_sum, joined_sum, small,
    table, embed_out, reduce_out, expand_out, output_out, joined_out,
    gains, shifts, biases, hidden_bias,
):
    wide = a.shape[6]
    lanes = table.shape[1]
    for n, piece in enumerate((a, b)):
        for u in range(2):
            value = piece[0, u, 0, 0, 0].astype(F32)
            for k in range(wide // lanes):
                row = ((2 * u + n) * wide) // lanes + k
                table[pl.ds(row, BLOCK, stride=4 * wide // lanes), :] = value[
                    :, k * lanes : (k + 1) * lanes
                ]
    embed_out[...] = embed[...]

    @pl.when(pl.program_id(0) == 0)
    def _():
        cols = reduce_sum.shape[2]
        rows = expand_sum.shape[1]
        wide = expand_out.shape[1]
        for n in range(2):
            reduce_out[n * cols : (n + 1) * cols, :] = reduce_sum[n].T
            expand_out[n * rows : (n + 1) * rows, :] = expand_sum[n, :, :wide]
            output_out[n * rows : (n + 1) * rows, :] = expand_sum[n, :, wide:]
            joined_out[n * rows : (n + 1) * rows, :] = joined_sum[n]
        for out, order in ((gains, (0, 2, 5)), (shifts, (1, 3, 6)), (biases, (8, 9, 4, 7))):
            for n, row in enumerate(order):
                out[n : n + 1, :] = small[row : row + 1, :]
        for n in range(hidden_bias.shape[0]):
            hidden_bias[n : n + 1, :] = small[10 + n : 11 + n, :]


def write(done, embed, reduce_sum, expand_sum, joined_sum, small, table_rows, ff):
    wide = done.shape[6]
    width = 4 * wide
    tokens = embed.shape[0]
    block = (1, 2, 1, 1, 1, BLOCK, wide)
    first = lambda i: (0, 0, i % 2, (i // 2) % 2, i // 4, 0, 0)
    second = lambda i: (1, 0, i % 2, i // 4, (i // 2) % 2, 0, 0)
    rows = 2 * expand_sum.shape[1]
    cols = ff // N_TAB
    f32 = lambda *n: jax.ShapeDtypeStruct(n, F32)
    shapes = [
        f32(2 * reduce_sum.shape[2], reduce_sum.shape[1]), f32(rows, cols),
        f32(rows, expand_sum.shape[2] - cols), f32(rows, joined_sum.shape[2]),
        f32(3, width), f32(3, width), f32(4, width), f32(ff // width, width),
    ]
    lanes = 128
    part = pl.BlockSpec((tokens // 8, width), lambda i: (i, 0))
    table, *rest = pl.pallas_call(
        write_kernel,
        grid=(8,),
        in_specs=[pl.BlockSpec(block, first), pl.BlockSpec(block, second), part]
        + [full(v.shape) for v in (reduce_sum, expand_sum, joined_sum, small)],
        out_specs=[pl.BlockSpec((BLOCK * width // lanes, lanes), lambda i: (i, 0)), part]
        + [full(v.shape) for v in shapes],
        out_shape=[f32(table_rows * width // lanes, lanes), f32(tokens, width)] + shapes,
        compiler_params=params(),
        cost_estimate=cost(0, 16 << 20),
        name="write",
    )(done, done, embed, reduce_sum, expand_sum, joined_sum, small)
    return table.reshape(1, table_rows, width), *rest


def flip_tok(value, bit, size):
    return lax.ppermute(value, "tok", [(i, i ^ bit) for i in range(size)])


def shift_tab(value, shift, size):
    return lax.ppermute(value, "tab", [(i, (i + shift) % size) for i in range(size)])


def small_sum(value, n_tok, n_tab):
    bit = 1
    while bit < n_tok:
        value = value + flip_tok(value, bit, n_tok)
        bit *= 2
    total = value
    for shift in range(1, n_tab):
        total = total + shift_tab(value, shift, n_tab)
    return total


def body(
    n_tok, n_tab,
    embedded, cell_index, cell_boxes, box_tables, joined_weight, output_weight,
    expand_weight, reduce_weight, hidden_bias, bias_rows, norm_gains, norm_shifts, cotangent,
):
    tokens, width = embedded.shape
    pages, length = cell_index.shape
    table_rows = box_tables.shape[1]
    ff = expand_weight.shape[1]
    tok = lax.axis_index("tok").astype(jnp.int32).reshape(1)
    z = lax.axis_index("tab")
    cubic = n_tok == 8 and n_tab == 4

    corners = cell_boxes[:, :, :CELLS]
    lo = lambda n: jnp.minimum(corners[:, n], corners[:, n + 2]).reshape(-1)
    hi = lambda n: jnp.maximum(corners[:, n], corners[:, n + 2]).reshape(-1)
    left, right, top, bottom = lo(0), hi(0), lo(1), hi(1)
    none = jnp.full_like(left, -1)
    index_table = jnp.stack(
        [
            jnp.stack([left, right]),
            jnp.stack([top, bottom]),
            jnp.stack([right - left, none]),
            jnp.stack([bottom - top, none]),
        ]
    )
    padded = jnp.pad(box_tables[0], ((0, 1024 - table_rows), (0, 0)))
    if cubic:
        terms, group_index = spread(index_table, padded)
    else:
        pick_table = lambda i: lax.dynamic_index_in_dim(index_table, i, 0, keepdims=False)
        group_index = jnp.stack(
            [pick_table(z)]
            + [shift_tab(pick_table((z + s) % n_tab), s, n_tab) for s in range(1, n_tab)]
        )
        found = lookup(group_index, padded)
        terms = jnp.stack(
            [found[0]] + [shift_tab(found[s], n_tab - s, n_tab) for s in range(1, n_tab)]
        )

    q, k, v, normed, normed_low, rstd0 = embed(
        embedded, cell_index, terms, joined_weight, norm_gains, norm_shifts, bias_rows
    )
    mixed, lse = attn_fwd(q, k, v, pages)
    layer_out, after, after_low, rstd1, act, slope, gs2, gffn, sums2 = ffn_fwd(
        mixed, normed, output_weight, expand_weight, reduce_weight, hidden_bias,
        bias_rows, norm_gains, norm_shifts, cotangent, min(256, tokens),
    )
    if cubic:
        gs1, gmixed, hidden_sum, sums1, *parts, reduce_sum = ffn_grads(
            gffn, act, slope, gs2, after, after_low, rstd1, mixed, reduce_weight, expand_weight,
            output_weight, norm_gains, norm_shifts,
        )
    else:
        parts = None
        gh, gs1, gattn, gmixed, hidden_sum, sums1 = ffn_bwd(
            gffn, slope, gs2, after, rstd1, reduce_weight, expand_weight, output_weight,
            norm_gains, norm_shifts,
        )
    embedded_grad, cell_grad, sums0, sums_qv, *more = back(
        q, k, v, mixed, gmixed, lse, normed_low, gs1, joined_weight, normed, rstd0, cell_index,
        norm_gains, norm_shifts, parts,
    )
    if cubic:
        parts, expand_sum = more[:2], more[2:]
    else:
        gj = more[0]

    sums = (sums0, sums1, sums2, sums_qv, hidden_sum)
    if cubic:
        done, joined_sum, small = closing(cell_grad, group_index, sums, parts)
        (
            tables_grad, embedded_grad, reduce_grad, expand_grad, output_grad, joined_grad,
            gains_grad, shifts_grad, biases_grad, hidden_bias_grad,
        ) = write(
            done, embedded_grad, reduce_sum, expand_sum[0], joined_sum, small, table_rows, ff
        )
        hidden_bias_grad = hidden_bias_grad.reshape(-1)
    else:
        cell_grads = [cell_grad] + [shift_tab(cell_grad, s, n_tab) for s in range(1, n_tab)]
        part_a, part_b = table_part(jnp.zeros_like(tok), group_index, cell_grads, 8)
        both = jnp.concatenate([part_a, part_b], axis=2).astype(F32)
        tables_grad = lax.psum(both.reshape(1, -1, width)[:, :table_rows], "tok")
        small = jnp.concatenate([part.reshape(-1) for part in sums]).reshape(-1, 128)
        small = small_sum(small, n_tok, n_tab).reshape(-1)
        row = small.reshape(-1, width)
        gains_grad = jnp.stack([row[0], row[2], row[5]])
        shifts_grad = jnp.stack([row[1], row[3], row[6]])
        biases_grad = jnp.stack([row[8], row[9], row[4], row[7]])
        hidden_bias_grad = small[10 * width :]
        both = lambda a, b: jnp.einsum("ta,tb->ab", a, b, preferred_element_type=F32).astype(BF)

        def scattered(part):
            part = lax.psum_scatter(part, "tok", scatter_dimension=0, tiled=True)
            return lax.psum_scatter(part, "tab", scatter_dimension=1, tiled=True).astype(F32)

        reduce_grad = scattered(both(act, gffn))
        expand_grad = scattered(both(after_low, gh))
        output_grad = scattered(both(mixed, gattn))
        joined_grad = scattered(both(normed_low, jnp.concatenate([gj[0], gj[1], gj[2]], axis=1)))

    return (
        layer_out, embedded_grad, tables_grad, joined_grad, output_grad, expand_grad,
        reduce_grad, hidden_bias_grad, biases_grad, gains_grad, shifts_grad,
    )


def solution(mesh):
    rows = P(("tok", "tab"), None)
    return jax.shard_map(
        functools.partial(body, mesh.shape["tok"], mesh.shape["tab"]),
        mesh=mesh,
        in_specs=(
            rows, rows, P(("tok", "tab"), None, None), P("tab", None, None),
            P(), P(), P(), P(), P(), P(), P(), P(), rows,
        ),
        out_specs=(
            rows, rows, P("tab", None, None), P("tok", "tab"), P("tok", "tab"),
            P("tok", "tab"), P("tok", "tab"), P(), P(), P(), P(),
        ),
        check_vma=False,
    )
```

```python
import functools

import jax
import jax.numpy as jnp
from jax import lax
from jax.experimental import pallas as pl
from jax.experimental.pallas import tpu as pltpu
from jax.sharding import PartitionSpec as P

HEADS = 16
HEAD_DIM = 64
CELLS = 128
EPSILON = 1e-05
SCALE = HEAD_DIM ** (-0.5)
LOG2E = 1.4426950408889634
F32 = jnp.float32
BF = jnp.bfloat16
NN = ((1,), (0,))
NT = ((1,), (1,))
TN = ((0,), (0,))
ANY = pl.ANY

TAIL_P = 0.305
TAIL_C = (
    0.12164194255155772,
    0.12243138164026345,
    0.10365178645525906,
    0.12022714029486306,
    -0.03641303195181058,
    0.1839499605096701,
    -0.15192310059752684,
    0.03643391798251271,
)


def dot(a, b, dims):
    return lax.dot_general(a, b, (dims, ((), ())), preferred_element_type=F32)


def params(**kw):
    return pltpu.CompilerParams(vmem_limit_bytes=60 << 20, **kw)


def cost(flops, nbytes, trans=0):
    return pl.CostEstimate(
        flops=int(flops), bytes_accessed=int(nbytes), transcendentals=int(trans)
    )


def full(shape):
    zeros = (0,) * len(shape)
    return pl.BlockSpec(shape, lambda *_: zeros, pipeline_mode=pl.Buffered(1))


def gelu_parts(h):
    a = jnp.abs(h)
    t = 1.0 / (1.0 + TAIL_P * a)
    poly = jnp.full_like(t, TAIL_C[-1])
    for c in TAIL_C[-2::-1]:
        poly = poly * t + c
    e = jnp.exp2(h * h * (-0.5 * LOG2E))
    tail = poly * t * e
    phi_cdf = jnp.where(h > 0, 1.0 - tail, tail)
    act = h * phi_cdf
    slope = phi_cdf + h * e * 0.3989422804014327
    return act, slope


def norm_stats(v):
    mean = jnp.mean(v, axis=-1, keepdims=True)
    centred = v - mean
    var = jnp.mean(centred * centred, axis=-1, keepdims=True)
    rstd = lax.rsqrt(var + EPSILON)
    return centred * rstd, rstd


def norm_back(y, xh, rstd, gain):
    u = y * gain
    return (
        u - jnp.mean(u, axis=-1, keepdims=True) - xh * jnp.mean(u * xh, axis=-1, keepdims=True)
    ) * rstd


def colsum(v):
    return jnp.sum(v, axis=0, keepdims=True)


def lookup_kernel(idx, table, out):
    rows = table.shape[0]
    count = idx.shape[2]
    number = lax.broadcasted_iota(jnp.int32, (rows, count), 0)
    first = (number == idx[0, 0:1, :]).astype(F32)
    second = (number == idx[0, 1:2, :]).astype(F32)
    out[0] = dot((first + second).astype(BF), table[...], TN).astype(BF)


def lookup(idx, table):
    groups, _, count = idx.shape
    rows, width = table.shape
    return pl.pallas_call(
        lookup_kernel,
        grid=(groups,),
        in_specs=[
            pl.BlockSpec((1, 2, count), lambda i: (i, 0, 0)),
            full((rows, width)),
        ],
        out_specs=pl.BlockSpec((1, count, width), lambda i: (i, 0, 0)),
        out_shape=jax.ShapeDtypeStruct((groups, count, width), BF),
        compiler_params=params(),
        cost_estimate=cost(2 * groups * count * rows * width, 2 * groups * count * width),
        name="lookup",
    )(idx, table)


def embed_kernel(
    emb, ci, terms, w, gains, shifts, bias, q, k, v, normed, low, rstd_out
):
    width = emb.shape[1]
    tokens = emb.shape[0]
    cells = terms[...].reshape(4 * CELLS, width)
    number = lax.broadcasted_iota(jnp.int32, (CELLS, tokens), 0)
    pick = (number == ci[0]).astype(F32).astype(BF)
    pick = jnp.concatenate([pick] * 4, axis=0)
    box = dot(pick, cells, TN)
    xh, rstd = norm_stats(emb[...].astype(F32) + box)
    y = xh * gains[0:1] + shifts[0:1]
    normed[...] = y
    rstd_out[...] = rstd
    y_low = y.astype(BF)
    low[...] = y_low
    q[...] = ((dot(y_low, w[:, :width], NN) + bias[0:1]) * SCALE).astype(BF)
    k[...] = dot(y_low, w[:, width : 2 * width], NN).astype(BF)
    v[...] = (dot(y_low, w[:, 2 * width :], NN) + bias[1:2]).astype(BF)


def embed(emb, ci, terms, w, gains, shifts, bias):
    tokens, width = emb.shape
    pages, length = ci.shape
    rows = pl.BlockSpec((length, width), lambda i: (i, 0))
    shape = lambda dt, n=width: jax.ShapeDtypeStruct((tokens, n), dt)
    return pl.pallas_call(
        embed_kernel,
        grid=(pages,),
        in_specs=[rows, pl.BlockSpec((1, 1, length), lambda i: (i, 0, 0))]
        + [pl.BlockSpec((4, CELLS, width), lambda i: (0, i, 0))]
        + [full(w.shape), full(gains.shape), full(shifts.shape), full(bias.shape)],
        out_specs=[rows] * 5 + [pl.BlockSpec((length, 1), lambda i: (i, 0))],
        out_shape=[shape(BF), shape(BF), shape(BF), shape(F32), shape(BF), shape(F32, 1)],
        compiler_params=params(),
        cost_estimate=cost(2 * tokens * width * 3 * width, 26 << 20),
        name="embed_joined",
    )(emb, ci.reshape(pages, 1, length), terms, w, gains, shifts, bias)


STAGES = 4


def neighbours():
    tok, z = lax.axis_index("tok"), lax.axis_index("tab")
    core = {"tok": tok + 1 - 2 * (tok % 2)}
    x = {"tok": tok + 2 - 4 * ((tok // 2) % 2)}
    y = {"tok": tok + 4 - 8 * (tok // 4)}
    peers = [{"tab": (z + s) % 4} for s in range(1, 4)]
    return core, x, y, peers


def meet(devices):
    barrier = pltpu.get_barrier_semaphore()
    for d in devices:
        pl.semaphore_signal(barrier, inc=1, device_id=d, device_id_type=pl.DeviceIdType.MESH)
    pl.semaphore_wait(barrier, len(devices))


def sum_scratch(rows, cols):
    part = lambda *n: pltpu.VMEM((*n, rows, cols), BF)
    return [
        part(2, 4, 4), part(2, 4, 4), part(2, 4, 2), part(2, 4), part(2, 3),
        pltpu.SemaphoreType.DMA((2, 4)),
        pltpu.SemaphoreType.DMA((STAGES, 2, 4)),
        pltpu.SemaphoreType.DMA((STAGES, 2, 4)),
    ]


class Summing:
    def __init__(self, grads, out, scratch):
        self.grads, self.out = grads, out
        if grads is None:
            both, scratch = scratch[0], (scratch[0].at[0], *scratch[1:5], None, *scratch[5:])
            self.part = both.at[1]
        self.own, self.r0, self.r1, self.r2, self.r3, self.local, self.sent, self.got = scratch
        core, x, y, peers = neighbours()
        self.core, self.first, self.second, self.peers = core, (x, y), (y, x), peers
        self.z = lax.axis_index("tab")

    def devices(self):
        return [self.core, self.first[0], self.first[1], *self.peers]

    def copy(self, stage, ch, i):
        zc = (self.z + (i + 1)) % 4
        src, dst, to = (
            (
                lambda: self.part.at[ch, i] if self.grads is None else self.grads[ch].at[1, zc],
                self.r0.at[ch, i],
                self.core,
            ),
            (lambda: self.own.at[ch, i, pl.ds(2, 2)], self.r1.at[ch, i], self.first[ch]),
            (lambda: self.own.at[ch, i, 1], self.r2.at[ch, i], self.second[ch]),
            (lambda: self.own.at[ch, i, 0], self.r3.at[ch, min(i, 2)], self.peers[min(i, 2)]),
        )[stage]
        return pltpu.make_async_remote_copy(
            src_ref=src(), dst_ref=dst,
            send_sem=self.sent.at[stage, ch, i], recv_sem=self.got.at[stage, ch, i],
            device_id=to, device_id_type=pl.DeviceIdType.MESH,
        )

    def load(self, ch, i):
        zc = (self.z + (i + 1)) % 4
        return pltpu.make_async_copy(
            self.grads[ch].at[0, zc], self.own.at[ch, i], self.local.at[ch, i]
        )

    def start(self):
        for i in range(4):
            for ch in range(2):
                self.copy(0, ch, i).start()
                if self.grads is not None:
                    self.load(ch, i).start()

    def step(self, stage, i):
        for ch in range(2):
            self.copy(stage - 1, ch, i).wait_recv()
            if stage == 1:
                if self.grads is not None:
                    self.load(ch, i).wait()

                def add(j, _, ch=ch):
                    self.own[ch, i, j] = self.own[ch, i, j] + self.r0[ch, i, j]
                    return 0

                lax.fori_loop(0, 4, add, 0)
            elif stage == 2:

                def add(j, _, ch=ch):
                    self.own[ch, i, j] = self.own[ch, i, j] + self.r1[ch, i, j]
                    return 0

                lax.fori_loop(0, 2, add, 0)
            elif i < 3:
                self.own[ch, i, 0] = self.own[ch, i, 0] + self.r2[ch, i]
            if stage < 3 or i < 3:
                self.copy(stage, ch, i).start()

    def finish(self):
        for ch in range(2):
            total = self.own[ch, 3, 0].astype(F32) + self.r2[ch, 3].astype(F32)
            for i in range(3):
                self.copy(3, ch, i).wait_recv()
                total = total + self.r3[ch, i].astype(F32)
            self.out[ch] = total
        for stage in range(STAGES):
            for ch in range(2):
                for i in range(4 if stage < 3 else 3):
                    self.copy(stage, ch, i).wait_send()

    def run(self, step, plan):
        for at, events in plan.items():

            @pl.when(step == at)
            def _(events=events):
                for stage, i in events:
                    if stage == 0:
                        self.start()
                    elif stage == 4:
                        self.finish()
                    else:
                        self.step(stage, i)


def split_rel(r):
    return r & 1, (r >> 1) & 1, r >> 2


def rel_of(b):
    tok = lax.axis_index("tok")
    core, x, y = split_rel(b)
    flip = lambda static, mine: 1 - mine if static else mine
    return flip(core, tok % 2), flip(x, (tok // 2) % 2), flip(y, tok // 4)


def put_rows(g, ga, gb, cols, rows):
    half = rows // 2
    for b in range(8):
        core, x, y = rel_of(b)
        ga[core, 0, 2 * x + y, :, cols] = g[b * rows : b * rows + half]
        gb[core, 0, 2 * y + x, :, cols] = g[b * rows + half : (b + 1) * rows]


def sum_specs(grads, number):
    if grads is None:
        return [], [], [], [], {}
    rows, cols = grads[0].shape[3:]
    return (
        [pl.BlockSpec(memory_space=pl.ANY)] * 2,
        [full((2, rows, cols))],
        [jax.ShapeDtypeStruct((2, rows, cols), F32)],
        sum_scratch(rows, cols),
        {"has_side_effects": True, "collective_id": number},
    )


BLOCK = 128


def spread_kernel(
    idx, table, found, group_idx,
    held, numbers, ring_sent, ring_got, plane_sent, plane_got, idx_sent, idx_got,
):
    tok, z = lax.axis_index("tok"), lax.axis_index("tab")
    core, x, y, peers = neighbours()
    c, cx, cy = tok % 2, (tok // 2) % 2, tok // 4
    first, second = (x, y), (y, x)
    f, g = (cx, cy), (cy, cx)
    meet([core, x, y, *peers])
    half = table.shape[1] // 2
    count = idx.shape[2]

    def ring(k, ch):
        if k == 0:
            start = pl.multiple_of(tok * BLOCK, BLOCK)
            src = table.at[pl.ds(start, BLOCK), pl.ds(ch * half, half)]
        else:
            src = held.at[k - 1, ch, c, g[ch], f[ch]]
        return pltpu.make_async_remote_copy(
            src_ref=src, dst_ref=held.at[k, ch, c, g[ch], f[ch]],
            send_sem=ring_sent.at[k, ch], recv_sem=ring_got.at[k, ch],
            device_id=peers[0], device_id_type=pl.DeviceIdType.MESH,
        )

    def plane(stage, k, ch):
        src, to = (
            (held.at[k, ch, c, g[ch], f[ch]], first[ch]),
            (held.at[k, ch, c, g[ch]], second[ch]),
            (held.at[k, ch, c], core),
        )[stage]
        return pltpu.make_async_remote_copy(
            src_ref=src, dst_ref=src,
            send_sem=plane_sent.at[stage, k, ch], recv_sem=plane_got.at[stage, k, ch],
            device_id=to, device_id_type=pl.DeviceIdType.MESH,
        )

    def number(s):
        return pltpu.make_async_remote_copy(
            src_ref=idx.at[(z + s) % 4], dst_ref=numbers.at[s - 1],
            send_sem=idx_sent.at[s - 1], recv_sem=idx_got.at[s - 1],
            device_id=peers[s - 1], device_id_type=pl.DeviceIdType.MESH,
        )

    def picks(owner):
        out = []
        for b in range(8):
            row = lax.broadcasted_iota(jnp.int32, (BLOCK, count), 0) + b * BLOCK
            one = (row == idx[owner, 0:1, :]).astype(F32)
            two = (row == idx[owner, 1:2, :]).astype(F32)
            out.append((one + two).astype(BF))
        return out

    def arrive(k):
        for ch in range(2):
            ring(k, ch).wait_recv()
            if k < 2:
                ring(k + 1, ch).start()
            plane(0, k, ch).start()

    def go_on(stage, k):
        for ch in range(2):
            plane(stage - 1, k, ch).wait_recv()
            plane(stage, k, ch).start()

    def look_up(k):
        rows = picks((z + 3 - k) % 4)
        for ch in range(2):
            plane(2, k, ch).wait_recv()
            order = [
                4 * a + 2 * b + n if ch == 0 else 4 * b + 2 * a + n
                for n in range(2)
                for a in range(2)
                for b in range(2)
            ]
            pick = jnp.concatenate([rows[b] for b in order], axis=0)
            data = held[k, ch].reshape(8 * BLOCK, half)
            found[k + 1, :, ch * half : (ch + 1) * half] = dot(pick, data, TN).astype(BF)

    for ch in range(2):
        ring(0, ch).start()
    for s in range(1, 4):
        number(s).start()
    found[0] = dot(jnp.concatenate(picks(z), axis=0), table[...], TN).astype(BF)
    arrive(0)
    go_on(1, 0)
    arrive(1)
    go_on(1, 1)
    go_on(2, 0)
    arrive(2)
    go_on(1, 2)
    group_idx[0] = idx[z]
    for s in range(1, 4):
        number(s).wait_recv()
        group_idx[s] = numbers[s - 1]

    def finish(k, _):
        look_up(k)

        @pl.when(k < 2)
        def _():
            go_on(2, k + 1)

        return 0

    lax.fori_loop(0, 3, finish, 0)
    for s in range(1, 4):
        number(s).wait_send()
    for k in range(3):
        for ch in range(2):
            ring(k, ch).wait_send()
            for stage in range(3):
                plane(stage, k, ch).wait_send()


def spread(idx, table):
    n_tab, _, count = idx.shape
    rows, width = table.shape
    dma = pltpu.SemaphoreType.DMA
    return pl.pallas_call(
        spread_kernel,
        grid=(1,),
        in_specs=[full(idx.shape), full(table.shape)],
        out_specs=[full((n_tab, count, width)), full(idx.shape)],
        out_shape=[
            jax.ShapeDtypeStruct((n_tab, count, width), BF),
            jax.ShapeDtypeStruct(idx.shape, jnp.int32),
        ],
        scratch_shapes=[
            pltpu.VMEM((3, 2, 2, 2, 2, BLOCK, width // 2), BF),
            pltpu.VMEM((3, 2, count), jnp.int32),
            dma((3, 2)), dma((3, 2)), dma((3, 3, 2)), dma((3, 3, 2)), dma((3,)), dma((3,)),
        ],
        compiler_params=params(has_side_effects=True, collective_id=4),
        cost_estimate=cost(8 * count * width * rows, 8 << 20),
        name="spread",
    )(idx, table)


HP = 4


def head_masks(length, pair):
    lane = lax.broadcasted_iota(jnp.int32, (length, pair), 1)
    return lane < HEAD_DIM


def attn_fwd_kernel(q, k, v, mixed, lse):
    length = q.shape[0]
    pair = 2 * HEAD_DIM
    low_half = head_masks(length, pair)
    zero = jnp.zeros((length, pair), BF)
    for p in range(HP // 2):
        cols = slice(p * pair, (p + 1) * pair)
        qp, kp, vp = q[:, cols], k[:, cols], v[:, cols]
        vt = vp.T
        outs = []
        for h in range(2):
            km = jnp.where(low_half, kp, zero) if h == 0 else jnp.where(low_half, zero, kp)
            st = dot(km, qp, NT)
            top = jnp.max(st, axis=0, keepdims=True)
            raised = jnp.exp2((st - top) * LOG2E)
            total = jnp.sum(raised, axis=0, keepdims=True)
            lse[0, 0, 2 * p + h : 2 * p + h + 1, :] = top + jnp.log(total)
            ot = dot(vt[h * HEAD_DIM : (h + 1) * HEAD_DIM], raised.astype(BF), NN)
            outs.append(ot * (1.0 / total))
        mixed[:, cols] = jnp.concatenate(outs, axis=0).T.astype(BF)


def attn_fwd(q, k, v, pages):
    tokens, width = q.shape
    length = tokens // pages
    steps = HEADS // HP
    blk = pl.BlockSpec((length, HP * HEAD_DIM), lambda i, j: (i, j))
    return pl.pallas_call(
        attn_fwd_kernel,
        grid=(pages, steps),
        in_specs=[blk] * 3,
        out_specs=[blk, pl.BlockSpec((1, 1, HP, length), lambda i, j: (i, j, 0, 0))],
        out_shape=[
            jax.ShapeDtypeStruct((tokens, width), BF),
            jax.ShapeDtypeStruct((pages, steps, HP, length), F32),
        ],
        compiler_params=params(),
        cost_estimate=cost(14e9, 8 << 20, pages * HEADS * length * length),
        name="attention",
    )(q, k, v)


def attn_back(q, k, v, mixed, go, lse, put):
    length = q.shape[0]
    pair = 2 * HEAD_DIM
    low_half = head_masks(length, pair)
    zero = jnp.zeros((length, pair), BF)

    def pick(x, h):
        return jnp.where(low_half, x, zero) if h == 0 else jnp.where(low_half, zero, x)

    for p in range(HP // 2):
        cols = slice(p * pair, (p + 1) * pair)
        qp, kp, vp, op, gp = q[:, cols], k[:, cols], v[:, cols], mixed[:, cols], go[:, cols]
        kt = kp.T
        prod_t = (op.astype(F32) * gp.astype(F32)).T
        dq_t, dk, dv = [], None, None
        for h in range(2):
            st = dot(pick(kp, h), qp, NT)
            probs = jnp.exp2((st - lse[0, 0, 2 * p + h : 2 * p + h + 1, :]) * LOG2E)
            dv_h = dot(probs.astype(BF), pick(gp, h), NN)
            dpt = dot(pick(vp, h), gp, NT)
            delta = colsum(prod_t[h * HEAD_DIM : (h + 1) * HEAD_DIM])
            ds = (probs * (dpt - delta)).astype(BF)
            dk_h = dot(ds, pick(qp, h), NN)
            dq_t.append(dot(kt[h * HEAD_DIM : (h + 1) * HEAD_DIM], ds, NN))
            dv = dv_h if dv is None else dv + dv_h
            dk = dk_h if dk is None else dk + dk_h
        dq = (jnp.concatenate(dq_t, axis=0).T.astype(BF).astype(F32) * SCALE).astype(BF)
        put(p * pair, pair, dq, dk.astype(BF), dv.astype(BF))


FC = 512
FWD = 1024
RC = 128
MC = 512


def ffn_fwd_kernel(
    mixed, normed, wo, we, wr, hb, bias, gains, shifts, cot,
    out, after_out, low_out, rstd_out, act_out, slope_out, gs2_out, gffn_out, sums,
):
    ff = we.shape[1]
    attn_sum = normed[...] + (dot(mixed[...], wo[...], NN) + bias[2:3])
    xh, rstd = norm_stats(attn_sum)
    after = xh * gains[1:2] + shifts[1:2]
    after_out[...] = after
    rstd_out[...] = rstd
    low = after.astype(BF)
    low_out[...] = low
    total = after + bias[3:4]
    count = ff // FWD
    hidden = []
    for j in range(count + 1):
        if j < count:
            cols = slice(j * FWD, (j + 1) * FWD)
            hidden.append(dot(low, we[:, cols], NN) + hb[:, cols])
        if j > 0:
            cols = slice((j - 1) * FWD, j * FWD)
            act, slope = gelu_parts(hidden[j - 1])
            act = act.astype(BF)
            act_out[:, cols] = act
            slope_out[:, cols] = slope.astype(BF)
            total = total + dot(act, wr[cols, :], NN)
    xh, rstd = norm_stats(total)
    out[...] = (xh * gains[2:3] + shifts[2:3]).astype(BF)
    y = cot[...].astype(F32)
    gs2 = norm_back(y, xh, rstd, gains[2:3])
    gs2_out[...] = gs2
    gffn = gs2.astype(BF)
    gffn_out[...] = gffn
    part = jnp.concatenate([colsum(y * xh), colsum(y), colsum(gffn.astype(F32))], axis=0)

    @pl.when(pl.program_id(0) == 0)
    def _():
        sums[...] = part

    @pl.when(pl.program_id(0) != 0)
    def _():
        sums[...] = sums[...] + part


def ffn_fwd(mixed, normed, wo, we, wr, hb, bias, gains, shifts, cot, tile):
    tokens, width = mixed.shape
    ff = we.shape[1]
    rows = pl.BlockSpec((tile, width), lambda i: (i, 0))
    long = pl.BlockSpec((tile, ff), lambda i: (i, 0))
    shape = lambda dt, n=width: jax.ShapeDtypeStruct((tokens, n), dt)
    hb = hb.reshape(1, ff)
    return pl.pallas_call(
        ffn_fwd_kernel,
        grid=(tokens // tile,),
        in_specs=[rows, rows]
        + [full(a.shape) for a in (wo, we, wr, hb, bias, gains, shifts)]
        + [rows],
        out_specs=[rows, rows, rows, pl.BlockSpec((tile, 1), lambda i: (i, 0)), long, long, rows, rows]
        + [pl.BlockSpec((3, width), lambda i: (0, 0))],
        out_shape=[
            shape(BF), shape(F32), shape(BF), shape(F32, 1), shape(BF, ff), shape(BF, ff),
            shape(F32), shape(BF), jax.ShapeDtypeStruct((3, width), F32),
        ],
        compiler_params=params(),
        cost_estimate=cost(2 * tokens * width * (width + 2 * ff), 60 << 20, tokens * ff * 2),
        name="ffn_forward",
    )(mixed, normed, wo, we, wr, hb, bias, gains, shifts, cot)


def second_norm_back(gs1_out, after, rstd, gains, shifts, gattn_out, sums):
    tokens, width = after.shape

    def norm(i, carry):
        rows = pl.ds(pl.multiple_of(i * RC, RC), RC)
        total = gs1_out[rows, :]
        xh = (after[rows, :] - shifts[1:2]) * (1.0 / gains[1:2])
        gs1 = norm_back(total, xh, rstd[rows, :], gains[1:2])
        gs1_out[rows, :] = gs1
        gattn = gs1.astype(BF)
        gattn_out[rows, :] = gattn
        g, s, b = carry
        return g + colsum(total * xh), s + colsum(total), b + colsum(gattn.astype(F32))

    zero = jnp.zeros((1, width), F32)
    sums[...] = jnp.concatenate(lax.fori_loop(0, tokens // RC, norm, (zero, zero, zero)), axis=0)


def ffn_bwd_kernel(
    gffn, gs2, after, rstd, wo, gains, shifts, slope, wr, we,
    gh_out, gs1_out, gattn_out, gmixed_out, hsum, sums,
):
    step, last = pl.program_id(0), pl.num_programs(0) - 1
    tokens, width = gffn.shape

    @pl.when(step == 0)
    def _():
        gs1_out[...] = gs2[...]

    part = jnp.zeros((1, slope.shape[1]), F32)
    for m in range(0, tokens, MC):
        rows = slice(m, m + MC)
        gh = (dot(gffn[rows, :], wr[...], NT) * slope[rows, :].astype(F32)).astype(BF)
        gh_out[rows, :] = gh
        part = part + colsum(gh.astype(F32))
        gs1_out[rows, :] = gs1_out[rows, :] + dot(gh, we[...], NT)
    hsum[...] = part

    @pl.when(step == last)
    def _():
        second_norm_back(gs1_out, after, rstd, gains, shifts, gattn_out, sums)
        for m in range(0, tokens, MC):
            rows = slice(m, m + MC)
            gmixed_out[rows, :] = dot(gattn_out[rows, :], wo[...], NT).astype(BF)


def ffn_bwd(gffn, slope, gs2, after, rstd, wr, we, wo, gains, shifts):
    tokens, width = gffn.shape
    ff = we.shape[1]
    whole = full((tokens, width))
    long = pl.BlockSpec((tokens, FC), lambda s: (0, s))
    shape = lambda dt, n=width: jax.ShapeDtypeStruct((tokens, n), dt)
    return pl.pallas_call(
        ffn_bwd_kernel,
        grid=(ff // FC,),
        in_specs=[whole, whole, whole, full((tokens, 1))]
        + [full(a.shape) for a in (wo, gains, shifts)]
        + [
            long,
            pl.BlockSpec((FC, width), lambda s: (s, 0)),
            pl.BlockSpec((width, FC), lambda s: (0, s)),
        ],
        out_specs=[long, whole, whole, whole]
        + [pl.BlockSpec((1, FC), lambda s: (0, s)), full((3, width))],
        out_shape=[
            shape(BF, ff), shape(F32), shape(BF), shape(BF),
            jax.ShapeDtypeStruct((1, ff), F32), jax.ShapeDtypeStruct((3, width), F32),
        ],
        compiler_params=params(),
        cost_estimate=cost(2 * tokens * width * (width + 2 * ff), 60 << 20),
        name="ffn_backward",
    )(gffn, gs2, after, rstd, wo, gains, shifts, slope, wr, we)


FFN_PLAN = {
    4: [(0, 0)],
    8: [(1, 0)],
    9: [(1, 1)],
    11: [(2, 0), (1, 2)],
    13: [(2, 1), (1, 3)],
    15: [(3, 0)],
    16: [(2, 2)],
    17: [(3, 1), (2, 3)],
    18: [(3, 2)],
    19: [(3, 3)],
}
N_TOK, N_TAB = 8, 4


def block_of_step(s):
    s = jnp.minimum(s, N_TOK - 1)
    return 1 - s // 4, 1 - (s // 2) % 2, 1 - s % 2


def ffn_grads_kernel(
    gffn_in, gs2_in, after, rstd, low, mixed, wo, gains, shifts, act, slope, wr, we,
    gs1_out, gmixed_out, hsum, sums, ga, gb, reduce_out,
    gffn, gh, local, *scratch,
):
    step, last = pl.program_id(0), pl.num_programs(0) - 1
    tokens, width = after.shape
    summing = Summing(None, reduce_out, scratch)
    both = scratch[0]
    z = lax.axis_index("tab")
    first = pltpu.make_async_copy(gffn_in, gffn, local.at[0])
    later = pltpu.make_async_copy(gs2_in, gs1_out, local.at[1])

    @pl.when(step == 0)
    def _():
        first.start()
        later.start()
        meet(summing.devices())
        first.wait()

    @pl.when(step == N_TOK)
    def _():
        later.wait()

    summing.run(step, FFN_PLAN)

    @pl.when(step < N_TOK)
    def _():
        core, x, y = block_of_step(step)
        g = dot(gffn[...], act[...], TN).astype(BF)
        rows, half = both.shape[4:]
        for zc in range(N_TAB):
            i = (zc + N_TAB - 1 - z) % N_TAB
            for ch in range(2):
                piece = g[zc * rows : (zc + 1) * rows, ch * half : (ch + 1) * half]
                both[core, ch, i, (2 * x + y, 2 * y + x)[ch]] = piece

    @pl.when((step >= N_TOK) & (step < 2 * N_TOK))
    def _():
        def block(m, part):
            rows = pl.ds(pl.multiple_of(m * MC, MC), MC)
            g = (dot(gffn[rows, :], wr[...], NT) * slope[rows, :].astype(F32)).astype(BF)
            gh[step - N_TOK, rows, :] = g
            gs1_out[rows, :] = gs1_out[rows, :] + dot(g, we[...], NT)
            return part + colsum(g.astype(F32))

        hsum[...] = lax.fori_loop(0, tokens // MC, block, jnp.zeros((1, slope.shape[1]), F32))

    @pl.when(step == 2 * N_TOK - 1)
    def _():
        second_norm_back(gs1_out, after, rstd, gains, shifts, gffn, sums)

        def block(m, _):
            rows = pl.ds(pl.multiple_of(m * MC, MC), MC)
            gmixed_out[rows, :] = dot(gffn[rows, :], wo[...], NT).astype(BF)
            return 0

        lax.fori_loop(0, tokens // MC, block, 0)

    @pl.when(step >= 2 * N_TOK)
    def _():
        n = step - 2 * N_TOK
        quarter = width // N_TAB
        rows = width // N_TOK
        wide = gh.shape[2]

        def block(m, _):
            g = dot(low[...], gh[2 * n + m], TN).astype(BF)
            put_rows(g, ga, gb, pl.ds(pl.multiple_of(m * wide, wide), wide), rows)
            return 0

        lax.fori_loop(0, 2, block, 0)
        piece = gffn[:, pl.ds(pl.multiple_of(n * quarter, quarter), quarter)]
        g = dot(mixed[...], piece, TN).astype(BF)
        put_rows(g, ga, gb, slice(2 * wide, 2 * wide + quarter), rows)

    @pl.when(step == last)
    def _():
        summing.finish()


def ffn_grads(gffn, act, slope, gs2, after, low, rstd, mixed, wr, we, wo, gains, shifts):
    tokens, width = gffn.shape
    ff = we.shape[1]
    whole = full((tokens, width))
    anywhere = pl.BlockSpec(memory_space=pl.ANY)
    wide = ff // N_TOK
    half = width // (2 * N_TOK)
    out_wide = (ff + width) // N_TAB
    back = lambda s: jnp.clip(s - N_TOK, 0, N_TOK - 1)
    grad = lambda s: jnp.clip(s - 2 * N_TOK, 0, N_TAB - 1)

    def act_block(s):
        core, x, y = block_of_step(s)
        tok = lax.axis_index("tok")
        flip = lambda rel, mine: rel + mine - 2 * rel * mine
        return 0, 4 * flip(y, tok // 4) + 2 * flip(x, (tok // 2) % 2) + flip(core, tok % 2)

    rows, cols = width // N_TAB, wide // 2
    part = lambda *n: pltpu.VMEM((*n, rows, cols), BF)
    dma = pltpu.SemaphoreType.DMA
    shape = lambda dt: jax.ShapeDtypeStruct((tokens, width), dt)
    piece = pl.BlockSpec((2, 1, 4, half, out_wide), lambda s: (0, grad(s), 0, 0, 0))
    return pl.pallas_call(
        ffn_grads_kernel,
        grid=(2 * N_TOK + N_TAB,),
        in_specs=[anywhere, anywhere, whole, full((tokens, 1)), whole, whole]
        + [full(a.shape) for a in (wo, gains, shifts)]
        + [
            pl.BlockSpec((tokens, wide), act_block),
            pl.BlockSpec((tokens, wide), lambda s: (0, back(s))),
            pl.BlockSpec((wide, width), lambda s: (back(s), 0)),
            pl.BlockSpec((width, wide), lambda s: (0, back(s))),
        ],
        out_specs=[
            whole, whole, pl.BlockSpec((1, wide), lambda s: (0, back(s))), full((3, width)),
            piece, piece, full((2, rows, cols)),
        ],
        out_shape=[
            shape(F32), shape(BF),
            jax.ShapeDtypeStruct((1, ff), F32), jax.ShapeDtypeStruct((3, width), F32),
            jax.ShapeDtypeStruct((2, 4, 4, half, out_wide), BF),
            jax.ShapeDtypeStruct((2, 4, 4, half, out_wide), BF),
            jax.ShapeDtypeStruct((2, rows, cols), F32),
        ],
        scratch_shapes=[
            pltpu.VMEM((tokens, width), BF), pltpu.VMEM((N_TOK, tokens, wide), BF), dma((2,)),
            part(2, 2, 4, 4), part(2, 4, 4), part(2, 4, 2), part(2, 4), part(2, 3),
            dma((STAGES, 2, 4)), dma((STAGES, 2, 4)),
        ],
        compiler_params=pltpu.CompilerParams(
            vmem_limit_bytes=67043328, has_side_effects=True, collective_id=1
        ),
        cost_estimate=cost(2 * tokens * width * (2 * width + 4 * ff), 60 << 20),
        name="ffn_backward_grads",
    )(gffn, gs2, after, rstd, low, mixed, wo, gains, shifts, act, slope, wr, we)


BACK_PLAN = {
    0: [(0, 0)],
    1: [(1, 0)],
    2: [(1, 1)],
    3: [(2, 0), (1, 2)],
    5: [(2, 1), (1, 3)],
    6: [(3, 0)],
    8: [(2, 2)],
    9: [(3, 1)],
    11: [(2, 3)],
    12: [(3, 2)],
    13: [(3, 3)],
}


def back_kernel(*refs, pages, summed):
    q, k, v, mixed, go, lse, low, gs1, w, normed, rstd, ci, gains, shifts = refs[:14]
    refs = refs[14:]
    grads, refs = refs[: 2 * summed], refs[2 * summed :]
    out, cells, sums0, sums_qv = refs[:4]
    refs = refs[4:]
    if summed:
        ga, gb, summed_out, gj = refs[:4]
        summing = Summing(grads, summed_out, refs[4:])
    else:
        gj_out, gj = refs
    step = pl.program_id(0)
    width = gs1.shape[1]
    length = q.shape[0]
    groups = HEADS // HP
    wide = HP * HEAD_DIM
    n_attn = groups * pages
    n_joined = 4 if summed else 0

    if summed:

        @pl.when(step == 0)
        def _():
            meet(summing.devices())

        summing.run(step, BACK_PLAN)

    @pl.when(step < n_attn)
    def _():
        group, page = step // pages, step % pages
        rows = pl.ds(pl.multiple_of(page * length, length), length)

        def put(at, size, dq, dk, dv):
            cols = pl.ds(pl.multiple_of(group * wide + at, size), size)
            gj[0, rows, cols] = dq
            gj[1, rows, cols] = dk
            gj[2, rows, cols] = dv
            part = jnp.concatenate([colsum(dq.astype(F32)), colsum(dv.astype(F32))], axis=0)

            @pl.when(page == 0)
            def _():
                sums_qv[:, cols] = part

            @pl.when(page != 0)
            def _():
                sums_qv[:, cols] = sums_qv[:, cols] + part

        attn_back(q, k, v, mixed, go, lse, put)

    if summed:
        quarter = width // 4

        @pl.when((step >= n_attn) & (step < n_attn + n_joined))
        def _():
            def block(m, _):
                unit = 3 * (step - n_attn) + m
                cols = pl.ds(pl.multiple_of((unit % 4) * quarter, quarter), quarter)
                g = dot(low[...], gj[unit // 4, :, cols], TN).astype(BF)
                at = pl.ds(pl.multiple_of(m * quarter, quarter), quarter)
                put_rows(g, ga, gb, at, width // 8)
                return 0

            lax.fori_loop(0, 3, block, 0)

    @pl.when(step >= n_attn + n_joined)
    def _():
        page = step - (n_attn + n_joined)
        rows = pl.ds(pl.multiple_of(page * length, length), length)
        total = gs1[...]
        for n in range(3):
            total = total + dot(gj[n, rows, :], w[:, n * width : (n + 1) * width], NT)
        xh = (normed[...] - shifts[0:1]) * (1.0 / gains[0:1])
        grad = norm_back(total, xh, rstd[...], gains[0:1])
        out[...] = grad
        number = lax.broadcasted_iota(jnp.int32, (CELLS, length), 0)
        pick = (number == ci[0]).astype(F32).astype(BF)
        cells[...] = dot(pick, grad.astype(BF), NN).astype(BF)
        part = jnp.concatenate([colsum(total * xh), colsum(total)], axis=0)

        @pl.when(page == 0)
        def _():
            sums0[...] = part

        @pl.when(page != 0)
        def _():
            sums0[...] = sums0[...] + part

    if summed:

        @pl.when(step == pl.num_programs(0) - 1)
        def _():
            summing.finish()
    else:
        gj_out[...] = gj[...]


def back(q, k, v, mixed, go, lse, low, gs1, w, normed, rstd, ci, gains, shifts, grads):
    tokens, width = q.shape
    pages, length = ci.shape
    groups = HEADS // HP
    wide = HP * HEAD_DIM
    summed = grads is not None
    n_attn = groups * pages
    before = n_attn + (4 if summed else 0)
    at = lambda s: jnp.minimum(s, n_attn - 1)
    page = lambda s: jnp.maximum(s - before, 0)
    block = lambda s: jnp.clip(s - n_attn, 0, 3)
    blk = pl.BlockSpec((length, wide), lambda s: (at(s) % pages, at(s) // pages))
    rows = pl.BlockSpec((length, width), lambda s: (page(s), 0))
    out_specs = [
        rows,
        pl.BlockSpec((CELLS, width), lambda s: (page(s), 0)),
        full((2, width)),
        full((2, width)),
    ]
    out_shape = [
        jax.ShapeDtypeStruct((tokens, width), F32),
        jax.ShapeDtypeStruct((pages * CELLS, width), BF),
        jax.ShapeDtypeStruct((2, width), F32),
        jax.ShapeDtypeStruct((2, width), F32),
    ]
    whole_gj = (3, tokens, width)
    more_in, more_out, more_shape, more_scratch, more = sum_specs(grads, 2)
    if summed:
        half = width // 16
        piece = pl.BlockSpec((2, 1, 4, half, 3 * width // 4), lambda s: (0, block(s), 0, 0, 0))
        out_specs += [piece, piece]
        out_shape += [jax.ShapeDtypeStruct((2, 4, 4, half, 3 * width // 4), BF)] * 2
    else:
        out_specs += [full(whole_gj)]
        out_shape += [jax.ShapeDtypeStruct(whole_gj, BF)]
    return pl.pallas_call(
        functools.partial(back_kernel, pages=pages, summed=summed),
        grid=(before + pages,),
        in_specs=[blk] * 5
        + [
            pl.BlockSpec((1, 1, HP, length), lambda s: (at(s) % pages, at(s) // pages, 0, 0)),
            full(low.shape),
            rows,
            full(w.shape),
            rows,
            pl.BlockSpec((length, 1), lambda s: (page(s), 0)),
            pl.BlockSpec((1, 1, length), lambda s: (page(s), 0, 0)),
            full(gains.shape),
            full(shifts.shape),
        ]
        + more_in,
        out_specs=out_specs + more_out,
        out_shape=out_shape + more_shape,
        scratch_shapes=[pltpu.VMEM(whole_gj, BF)] + more_scratch,
        compiler_params=params(**more),
        cost_estimate=cost(70e9, 40 << 20, pages * HEADS * length * length),
        name="attention_joined_embed_back",
    )(
        q, k, v, mixed, go, lse, low, gs1, w, normed, rstd, ci.reshape(pages, 1, length),
        gains, shifts, *(grads or ()),
    )


def table_kernel(tok, idx, g0, g1, g2, g3, out_a, out_b):
    rows = out_a.shape[1]
    count = idx.shape[2]
    half = out_a.shape[2]
    base = (pl.program_id(0) ^ tok[0]) * rows
    number = lax.broadcasted_iota(jnp.int32, (rows, count), 0) + base
    picks = []
    for s in range(4):
        first = (number == idx[s, 0:1, :]).astype(F32)
        second = (number == idx[s, 1:2, :]).astype(F32)
        picks.append((first + second).astype(BF))
    pick = jnp.concatenate(picks, axis=1)
    grads = jnp.concatenate([g0[...], g1[...], g2[...], g3[...]], axis=0)
    total = dot(pick, grads, NN).astype(BF)
    out_a[0] = total[:, :half]
    out_b[0] = total[:, half:]


def table_part(tok, idx, grads, blocks):
    groups, _, count = idx.shape
    width = grads[0].shape[1]
    rows = 1024 // blocks
    half = width // 2
    out = pl.BlockSpec((1, rows, half), lambda i, t: (i, 0, 0))
    return pl.pallas_call(
        table_kernel,
        grid_spec=pltpu.PrefetchScalarGridSpec(
            num_scalar_prefetch=1,
            grid=(blocks,),
            in_specs=[full(idx.shape)] + [full((count, width))] * groups,
            out_specs=[out, out],
        ),
        out_shape=[jax.ShapeDtypeStruct((blocks, rows, half), BF)] * 2,
        compiler_params=params(),
        cost_estimate=cost(2 * 1024 * groups * count * width, 4 << 20),
        name="table_grad",
    )(tok, idx, *grads)


class TableSum:
    def __init__(self, scratch, done):
        self.part, self.r0, self.r1, self.r2, self.sent, self.got = scratch
        self.done = done
        tok = lax.axis_index("tok")
        core, x, y, _ = neighbours()
        self.c, cx, cy = tok % 2, (tok // 2) % 2, tok // 4
        self.core, self.first, self.second = core, (x, y), (y, x)
        self.f, self.g = (cx, cy), (cy, cx)

    def copy(self, stage, ch, u):
        c, f, g = self.c, self.f[ch], self.g[ch]
        part, done = self.part.at[ch, u], self.done.at[ch, u]
        src, dst, to = (
            (lambda: part.at[1 - c], self.r0.at[ch, u], self.core),
            (lambda: part.at[c, 1 - f], self.r1.at[ch, u], self.first[ch]),
            (lambda: part.at[c, f, 1 - g], self.r2.at[ch, u], self.second[ch]),
            (lambda: done.at[c, f, g], None, self.second[ch]),
            (lambda: done.at[c, f], None, self.first[ch]),
            (lambda: done.at[c], None, self.core),
        )[stage]
        src = src()
        return pltpu.make_async_remote_copy(
            src_ref=src, dst_ref=src if dst is None else dst,
            send_sem=self.sent.at[stage, ch, u], recv_sem=self.got.at[stage, ch, u],
            device_id=to, device_id_type=pl.DeviceIdType.MESH,
        )

    def store(self, u, ch, value):
        for b in range(8):
            c, x, y = split_rel(b)
            f, g = (x, y) if ch == 0 else (y, x)
            self.part[ch, u, c, f, g] = value[b * BLOCK : (b + 1) * BLOCK]
        self.copy(0, ch, u).start()

    def step(self, stage, u):
        for ch in range(2):
            c, f, g = self.c, self.f[ch], self.g[ch]
            self.copy(stage - 1, ch, u).wait_recv()
            if stage == 1:
                self.part[ch, u, c] = self.part[ch, u, c] + self.r0[ch, u]
            elif stage == 2:
                self.part[ch, u, c, f] = self.part[ch, u, c, f] + self.r1[ch, u]
            elif stage == 3:
                self.done[ch, u, c, f, g] = self.part[ch, u, c, f, g] + self.r2[ch, u]
            if stage < 6:
                self.copy(stage, ch, u).start()

    def finish(self):
        for stage in range(6):
            for ch in range(2):
                for u in range(2):
                    self.copy(stage, ch, u).wait_send()


def closing_kernel(
    cells, idx, sums0, sums1, sums2, sums_qv, hidden_sum, ga, gb, done, joined, small_out,
    ring, total, ring_sent, ring_got, held, arrived, small_sent, small_got, *scratch,
):
    summing = Summing((ga, gb), joined, scratch[:8])
    table = TableSum(scratch[8:], done)
    core, x, y, peers = neighbours()
    z = lax.axis_index("tab")
    hops = [core, x, y, {"tab": z + 1 - 2 * (z % 2)}, {"tab": z + 2 - 4 * (z // 2)}]
    meet([core, x, y, *peers])
    count = cells.shape[0]
    half = cells.shape[1] // 2

    def pass_on(k, h):
        cols = pl.ds(h * half, half)
        src = cells.at[:, cols] if k == 0 else ring.at[k - 1, :, cols]
        return pltpu.make_async_remote_copy(
            src_ref=src, dst_ref=ring.at[k, :, cols],
            send_sem=ring_sent.at[k, h], recv_sem=ring_got.at[k, h],
            device_id=peers[0], device_id_type=pl.DeviceIdType.MESH,
        )

    def small_copy(n):
        return pltpu.make_async_remote_copy(
            src_ref=held.at[n], dst_ref=arrived.at[n],
            send_sem=small_sent.at[n], recv_sem=small_got.at[n],
            device_id=hops[n], device_id_type=pl.DeviceIdType.MESH,
        )

    def small_step(n):
        small_copy(n - 1).wait_recv()
        value = held[n - 1] + arrived[n - 1]
        if n < 5:
            held[n] = value
            small_copy(n).start()
        else:
            small_out[...] = value

    def relay(k, h):
        pass_on(k - 1, h).wait_recv()
        pass_on(k, h).start()

    def pick(s):
        number = lax.broadcasted_iota(jnp.int32, (total.shape[0], count), 0)
        first = (number == idx[s, 0:1, :]).astype(F32)
        second = (number == idx[s, 1:2, :]).astype(F32)
        return (first + second).astype(BF)

    def last_arrival(u):
        pass_on(2, u).wait_recv()
        for ch in range(2):
            cols = slice((2 * u + ch) * half // 2, (2 * u + ch + 1) * half // 2)
            value = total[:, cols] + dot(last, ring[2, :, cols], NN)
            table.store(u, ch, value.astype(BF))

    pass_on(0, 0).start()
    pass_on(0, 1).start()
    at, width = 0, cells.shape[1]
    for part in (sums0, sums1, sums2, sums_qv):
        held[0, at : at + part.shape[0]] = part[...]
        at += part.shape[0]
    for n in range(hidden_sum.shape[1] // width):
        held[0, at + n : at + n + 1] = hidden_sum[:, n * width : (n + 1) * width]
    small_copy(0).start()
    summing.start()
    total[...] = dot(pick(0), cells[...], NN)
    small_step(1)
    summing.step(1, 0)
    small_step(2)
    summing.step(1, 1)
    relay(1, 0)
    summing.step(2, 0)
    summing.step(1, 2)
    small_step(3)
    relay(1, 1)
    summing.step(2, 1)
    summing.step(1, 3)
    relay(2, 0)
    small_step(4)
    summing.step(2, 2)
    relay(2, 1)
    summing.step(3, 0)
    summing.step(3, 1)
    summing.step(2, 3)

    def add(k, _):
        total[...] = total[...] + dot(pick(k + 1), ring[k], NN)
        return 0

    lax.fori_loop(0, 2, add, 0)
    last = pick(3)
    last_arrival(0)
    table.step(1, 0)
    last_arrival(1)
    summing.step(3, 2)
    small_step(5)
    table.step(2, 0)
    table.step(1, 1)
    table.step(3, 0)
    table.step(2, 1)
    table.step(4, 0)
    table.step(3, 1)
    table.step(5, 0)
    table.step(4, 1)
    table.step(6, 0)
    table.step(5, 1)
    summing.step(3, 3)
    summing.finish()
    table.step(6, 1)
    table.finish()
    for k in range(3):
        for h in range(2):
            pass_on(k, h).wait_send()
    for n in range(5):
        small_copy(n).wait_send()


def closing(cells, idx, sums, grads):
    count, width = cells.shape
    small = (sum(part.size for part in sums) // width, width)
    rows, cols = grads[0].shape[3:]
    wide = width // 4
    part = lambda *n: pltpu.VMEM((2, 2, *n, BLOCK, wide), BF)
    done = (2, 2, 2, 2, 2, BLOCK, wide)
    dma = pltpu.SemaphoreType.DMA
    return pl.pallas_call(
        closing_kernel,
        grid=(1,),
        in_specs=[full(cells.shape), full(idx.shape)]
        + [full(part.shape) for part in sums]
        + [pl.BlockSpec(memory_space=pl.ANY)] * 2,
        out_specs=[full(done), full((2, rows, cols)), full(small)],
        out_shape=[
            jax.ShapeDtypeStruct(done, BF),
            jax.ShapeDtypeStruct((2, rows, cols), F32),
            jax.ShapeDtypeStruct(small, F32),
        ],
        scratch_shapes=[
            pltpu.VMEM((3, count, width), BF), pltpu.VMEM((8 * BLOCK, width), F32),
            dma((3, 2)), dma((3, 2)),
            pltpu.VMEM((5, *small), F32), pltpu.VMEM((5, *small), F32), dma((5,)), dma((5,)),
        ]
        + sum_scratch(rows, cols)
        + [part(2, 2, 2), part(2, 2), part(2), part(), dma((6, 2, 2)), dma((6, 2, 2))],
        compiler_params=params(has_side_effects=True, collective_id=3),
        cost_estimate=cost(8 * count * width * 1024, 24 << 20),
        name="closing",
    )(cells, idx, *sums, *grads)


def write_kernel(
    a, b, embed, reduce_sum, expand_sum, joined_sum, small,
    table, embed_out, reduce_out, expand_out, output_out, joined_out,
    gains, shifts, biases, hidden_bias,
):
    wide = a.shape[6]
    lanes = table.shape[1]
    for n, piece in enumerate((a, b)):
        for u in range(2):
            value = piece[0, u, 0, 0, 0].astype(F32)
            for k in range(wide // lanes):
                row = ((2 * u + n) * wide) // lanes + k
                table[pl.ds(row, BLOCK, stride=4 * wide // lanes), :] = value[
                    :, k * lanes : (k + 1) * lanes
                ]
    embed_out[...] = embed[...]

    @pl.when(pl.program_id(0) == 0)
    def _():
        cols = reduce_sum.shape[2]
        rows = expand_sum.shape[1]
        wide = expand_out.shape[1]
        for n in range(2):
            reduce_out[n * cols : (n + 1) * cols, :] = reduce_sum[n].T
            expand_out[n * rows : (n + 1) * rows, :] = expand_sum[n, :, :wide]
            output_out[n * rows : (n + 1) * rows, :] = expand_sum[n, :, wide:]
            joined_out[n * rows : (n + 1) * rows, :] = joined_sum[n]
        for out, order in ((gains, (0, 2, 5)), (shifts, (1, 3, 6)), (biases, (8, 9, 4, 7))):
            for n, row in enumerate(order):
                out[n : n + 1, :] = small[row : row + 1, :]
        for n in range(hidden_bias.shape[0]):
            hidden_bias[n : n + 1, :] = small[10 + n : 11 + n, :]


def write(done, embed, reduce_sum, expand_sum, joined_sum, small, table_rows, ff):
    wide = done.shape[6]
    width = 4 * wide
    tokens = embed.shape[0]
    block = (1, 2, 1, 1, 1, BLOCK, wide)
    first = lambda i: (0, 0, i % 2, (i // 2) % 2, i // 4, 0, 0)
    second = lambda i: (1, 0, i % 2, i // 4, (i // 2) % 2, 0, 0)
    rows = 2 * expand_sum.shape[1]
    cols = ff // N_TAB
    f32 = lambda *n: jax.ShapeDtypeStruct(n, F32)
    shapes = [
        f32(2 * reduce_sum.shape[2], reduce_sum.shape[1]), f32(rows, cols),
        f32(rows, expand_sum.shape[2] - cols), f32(rows, joined_sum.shape[2]),
        f32(3, width), f32(3, width), f32(4, width), f32(ff // width, width),
    ]
    lanes = 128
    part = pl.BlockSpec((tokens // 8, width), lambda i: (i, 0))
    table, *rest = pl.pallas_call(
        write_kernel,
        grid=(8,),
        in_specs=[pl.BlockSpec(block, first), pl.BlockSpec(block, second), part]
        + [full(v.shape) for v in (reduce_sum, expand_sum, joined_sum, small)],
        out_specs=[pl.BlockSpec((BLOCK * width // lanes, lanes), lambda i: (i, 0)), part]
        + [full(v.shape) for v in shapes],
        out_shape=[f32(table_rows * width // lanes, lanes), f32(tokens, width)] + shapes,
        compiler_params=params(),
        cost_estimate=cost(0, 16 << 20),
        name="write",
    )(done, done, embed, reduce_sum, expand_sum, joined_sum, small)
    return table.reshape(1, table_rows, width), *rest


def flip_tok(value, bit, size):
    return lax.ppermute(value, "tok", [(i, i ^ bit) for i in range(size)])


def shift_tab(value, shift, size):
    return lax.ppermute(value, "tab", [(i, (i + shift) % size) for i in range(size)])


def small_sum(value, n_tok, n_tab):
    bit = 1
    while bit < n_tok:
        value = value + flip_tok(value, bit, n_tok)
        bit *= 2
    total = value
    for shift in range(1, n_tab):
        total = total + shift_tab(value, shift, n_tab)
    return total


def body(
    n_tok, n_tab,
    embedded, cell_index, cell_boxes, box_tables, joined_weight, output_weight,
    expand_weight, reduce_weight, hidden_bias, bias_rows, norm_gains, norm_shifts, cotangent,
):
    tokens, width = embedded.shape
    pages, length = cell_index.shape
    table_rows = box_tables.shape[1]
    ff = expand_weight.shape[1]
    tok = lax.axis_index("tok").astype(jnp.int32).reshape(1)
    z = lax.axis_index("tab")
    cubic = n_tok == 8 and n_tab == 4

    corners = cell_boxes[:, :, :CELLS]
    lo = lambda n: jnp.minimum(corners[:, n], corners[:, n + 2]).reshape(-1)
    hi = lambda n: jnp.maximum(corners[:, n], corners[:, n + 2]).reshape(-1)
    left, right, top, bottom = lo(0), hi(0), lo(1), hi(1)
    none = jnp.full_like(left, -1)
    index_table = jnp.stack(
        [
            jnp.stack([left, right]),
            jnp.stack([top, bottom]),
            jnp.stack([right - left, none]),
            jnp.stack([bottom - top, none]),
        ]
    )
    padded = jnp.pad(box_tables[0], ((0, 1024 - table_rows), (0, 0)))
    if cubic:
        terms, group_index = spread(index_table, padded)
    else:
        pick_table = lambda i: lax.dynamic_index_in_dim(index_table, i, 0, keepdims=False)
        group_index = jnp.stack(
            [pick_table(z)]
            + [shift_tab(pick_table((z + s) % n_tab), s, n_tab) for s in range(1, n_tab)]
        )
        found = lookup(group_index, padded)
        terms = jnp.stack(
            [found[0]] + [shift_tab(found[s], n_tab - s, n_tab) for s in range(1, n_tab)]
        )

    q, k, v, normed, normed_low, rstd0 = embed(
        embedded, cell_index, terms, joined_weight, norm_gains, norm_shifts, bias_rows
    )
    mixed, lse = attn_fwd(q, k, v, pages)
    layer_out, after, after_low, rstd1, act, slope, gs2, gffn, sums2 = ffn_fwd(
        mixed, normed, output_weight, expand_weight, reduce_weight, hidden_bias,
        bias_rows, norm_gains, norm_shifts, cotangent, min(256, tokens),
    )
    if cubic:
        gs1, gmixed, hidden_sum, sums1, *parts, reduce_sum = ffn_grads(
            gffn, act, slope, gs2, after, after_low, rstd1, mixed, reduce_weight, expand_weight,
            output_weight, norm_gains, norm_shifts,
        )
    else:
        parts = None
        gh, gs1, gattn, gmixed, hidden_sum, sums1 = ffn_bwd(
            gffn, slope, gs2, after, rstd1, reduce_weight, expand_weight, output_weight,
            norm_gains, norm_shifts,
        )
    embedded_grad, cell_grad, sums0, sums_qv, *more = back(
        q, k, v, mixed, gmixed, lse, normed_low, gs1, joined_weight, normed, rstd0, cell_index,
        norm_gains, norm_shifts, parts,
    )
    if cubic:
        parts, expand_sum = more[:2], more[2:]
    else:
        gj = more[0]

    sums = (sums0, sums1, sums2, sums_qv, hidden_sum)
    if cubic:
        done, joined_sum, small = closing(cell_grad, group_index, sums, parts)
        (
            tables_grad, embedded_grad, reduce_grad, expand_grad, output_grad, joined_grad,
            gains_grad, shifts_grad, biases_grad, hidden_bias_grad,
        ) = write(
            done, embedded_grad, reduce_sum, expand_sum[0], joined_sum, small, table_rows, ff
        )
        hidden_bias_grad = hidden_bias_grad.reshape(-1)
    else:
        cell_grads = [cell_grad] + [shift_tab(cell_grad, s, n_tab) for s in range(1, n_tab)]
        part_a, part_b = table_part(jnp.zeros_like(tok), group_index, cell_grads, 8)
        both = jnp.concatenate([part_a, part_b], axis=2).astype(F32)
        tables_grad = lax.psum(both.reshape(1, -1, width)[:, :table_rows], "tok")
        small = jnp.concatenate([part.reshape(-1) for part in sums]).reshape(-1, 128)
        small = small_sum(small, n_tok, n_tab).reshape(-1)
        row = small.reshape(-1, width)
        gains_grad = jnp.stack([row[0], row[2], row[5]])
        shifts_grad = jnp.stack([row[1], row[3], row[6]])
        biases_grad = jnp.stack([row[8], row[9], row[4], row[7]])
        hidden_bias_grad = small[10 * width :]
        both = lambda a, b: jnp.einsum("ta,tb->ab", a, b, preferred_element_type=F32).astype(BF)

        def scattered(part):
            part = lax.psum_scatter(part, "tok", scatter_dimension=0, tiled=True)
            return lax.psum_scatter(part, "tab", scatter_dimension=1, tiled=True).astype(F32)

        reduce_grad = scattered(both(act, gffn))
        expand_grad = scattered(both(after_low, gh))
        output_grad = scattered(both(mixed, gattn))
        joined_grad = scattered(both(normed_low, jnp.concatenate([gj[0], gj[1], gj[2]], axis=1)))

    return (
        layer_out, embedded_grad, tables_grad, joined_grad, output_grad, expand_grad,
        reduce_grad, hidden_bias_grad, biases_grad, gains_grad, shifts_grad,
    )


def solution(mesh):
    rows = P(("tok", "tab"), None)
    return jax.shard_map(
        functools.partial(body, mesh.shape["tok"], mesh.shape["tab"]),
        mesh=mesh,
        in_specs=(
            rows, rows, P(("tok", "tab"), None, None), P("tab", None, None),
            P(), P(), P(), P(), P(), P(), P(), P(), rows,
        ),
        out_specs=(
            rows, rows, P("tab", None, None), P("tok", "tab"), P("tok", "tab"),
            P("tok", "tab"), P("tok", "tab"), P(), P(), P(), P(),
        ),
        check_vma=False,
    )
```

```python
import functools

import jax
import jax.numpy as jnp
from jax import lax
from jax.experimental import pallas as pl
from jax.experimental.pallas import tpu as pltpu
from jax.sharding import PartitionSpec as P

HEADS = 16
HEAD_DIM = 64
CELLS = 128
EPSILON = 1e-05
SCALE = HEAD_DIM ** (-0.5)
LOG2E = 1.4426950408889634
F32 = jnp.float32
BF = jnp.bfloat16
NN = ((1,), (0,))
NT = ((1,), (1,))
TN = ((0,), (0,))
ANY = pl.ANY

TAIL_P = 0.305
TAIL_C = (
    0.12164194255155772,
    0.12243138164026345,
    0.10365178645525906,
    0.12022714029486306,
    -0.03641303195181058,
    0.1839499605096701,
    -0.15192310059752684,
    0.03643391798251271,
)


def dot(a, b, dims):
    return lax.dot_general(a, b, (dims, ((), ())), preferred_element_type=F32)


def params(**kw):
    return pltpu.CompilerParams(vmem_limit_bytes=60 << 20, **kw)


def cost(flops, nbytes, trans=0):
    return pl.CostEstimate(
        flops=int(flops), bytes_accessed=int(nbytes), transcendentals=int(trans)
    )


def full(shape):
    zeros = (0,) * len(shape)
    return pl.BlockSpec(shape, lambda *_: zeros, pipeline_mode=pl.Buffered(1))


def gelu_parts(h):
    a = jnp.abs(h)
    t = 1.0 / (1.0 + TAIL_P * a)
    poly = jnp.full_like(t, TAIL_C[-1])
    for c in TAIL_C[-2::-1]:
        poly = poly * t + c
    e = jnp.exp2(h * h * (-0.5 * LOG2E))
    tail = poly * t * e
    phi_cdf = jnp.where(h > 0, 1.0 - tail, tail)
    act = h * phi_cdf
    slope = phi_cdf + h * e * 0.3989422804014327
    return act, slope


def norm_stats(v):
    mean = jnp.mean(v, axis=-1, keepdims=True)
    centred = v - mean
    var = jnp.mean(centred * centred, axis=-1, keepdims=True)
    rstd = lax.rsqrt(var + EPSILON)
    return centred * rstd, rstd


def norm_back(y, xh, rstd, gain):
    u = y * gain
    return (
        u - jnp.mean(u, axis=-1, keepdims=True) - xh * jnp.mean(u * xh, axis=-1, keepdims=True)
    ) * rstd


def colsum(v):
    return jnp.sum(v, axis=0, keepdims=True)


def lookup_kernel(idx, table, out):
    rows = table.shape[0]
    count = idx.shape[2]
    number = lax.broadcasted_iota(jnp.int32, (rows, count), 0)
    first = (number == idx[0, 0:1, :]).astype(F32)
    second = (number == idx[0, 1:2, :]).astype(F32)
    out[0] = dot((first + second).astype(BF), table[...], TN).astype(BF)


def lookup(idx, table):
    groups, _, count = idx.shape
    rows, width = table.shape
    return pl.pallas_call(
        lookup_kernel,
        grid=(groups,),
        in_specs=[
            pl.BlockSpec((1, 2, count), lambda i: (i, 0, 0)),
            full((rows, width)),
        ],
        out_specs=pl.BlockSpec((1, count, width), lambda i: (i, 0, 0)),
        out_shape=jax.ShapeDtypeStruct((groups, count, width), BF),
        compiler_params=params(),
        cost_estimate=cost(2 * groups * count * rows * width, 2 * groups * count * width),
        name="lookup",
    )(idx, table)


def embed_kernel(
    emb, ci, terms, w, gains, shifts, bias, q, k, v, normed, low, rstd_out
):
    width = emb.shape[1]
    tokens = emb.shape[0]
    cells = terms[...].reshape(4 * CELLS, width)
    number = lax.broadcasted_iota(jnp.int32, (CELLS, tokens), 0)
    pick = (number == ci[0]).astype(F32).astype(BF)
    pick = jnp.concatenate([pick] * 4, axis=0)
    box = dot(pick, cells, TN)
    xh, rstd = norm_stats(emb[...].astype(F32) + box)
    y = xh * gains[0:1] + shifts[0:1]
    normed[...] = y
    rstd_out[...] = rstd
    y_low = y.astype(BF)
    low[...] = y_low
    q[...] = ((dot(y_low, w[:, :width], NN) + bias[0:1]) * SCALE).astype(BF)
    k[...] = dot(y_low, w[:, width : 2 * width], NN).astype(BF)
    v[...] = (dot(y_low, w[:, 2 * width :], NN) + bias[1:2]).astype(BF)


def embed(emb, ci, terms, w, gains, shifts, bias):
    tokens, width = emb.shape
    pages, length = ci.shape
    rows = pl.BlockSpec((length, width), lambda i: (i, 0))
    shape = lambda dt, n=width: jax.ShapeDtypeStruct((tokens, n), dt)
    return pl.pallas_call(
        embed_kernel,
        grid=(pages,),
        in_specs=[rows, pl.BlockSpec((1, 1, length), lambda i: (i, 0, 0))]
        + [pl.BlockSpec((4, CELLS, width), lambda i: (0, i, 0))]
        + [full(w.shape), full(gains.shape), full(shifts.shape), full(bias.shape)],
        out_specs=[rows] * 5 + [pl.BlockSpec((length, 1), lambda i: (i, 0))],
        out_shape=[shape(BF), shape(BF), shape(BF), shape(F32), shape(BF), shape(F32, 1)],
        compiler_params=params(),
        cost_estimate=cost(2 * tokens * width * 3 * width, 26 << 20),
        name="embed_joined",
    )(emb, ci.reshape(pages, 1, length), terms, w, gains, shifts, bias)


STAGES = 4


def neighbours():
    tok, z = lax.axis_index("tok"), lax.axis_index("tab")
    core = {"tok": tok + 1 - 2 * (tok % 2)}
    x = {"tok": tok + 2 - 4 * ((tok // 2) % 2)}
    y = {"tok": tok + 4 - 8 * (tok // 4)}
    peers = [{"tab": (z + s) % 4} for s in range(1, 4)]
    return core, x, y, peers


def meet(devices):
    barrier = pltpu.get_barrier_semaphore()
    for d in devices:
        pl.semaphore_signal(barrier, inc=1, device_id=d, device_id_type=pl.DeviceIdType.MESH)
    pl.semaphore_wait(barrier, len(devices))


def sum_scratch(rows, cols):
    part = lambda *n: pltpu.VMEM((*n, rows, cols), BF)
    return [
        part(2, 4, 4), part(2, 4, 4), part(2, 4, 2), part(2, 4), part(2, 3),
        pltpu.SemaphoreType.DMA((2, 4)),
        pltpu.SemaphoreType.DMA((STAGES, 2, 4)),
        pltpu.SemaphoreType.DMA((STAGES, 2, 4)),
    ]


class Summing:
    def __init__(self, grads, out, scratch):
        self.grads, self.out = grads, out
        if grads is None:
            both, scratch = scratch[0], (scratch[0].at[0], *scratch[1:5], None, *scratch[5:])
            self.part = both.at[1]
        self.own, self.r0, self.r1, self.r2, self.r3, self.local, self.sent, self.got = scratch
        core, x, y, peers = neighbours()
        self.core, self.first, self.second, self.peers = core, (x, y), (y, x), peers
        self.z = lax.axis_index("tab")

    def devices(self):
        return [self.core, self.first[0], self.first[1], *self.peers]

    def copy(self, stage, ch, i):
        zc = (self.z + (i + 1)) % 4
        src, dst, to = (
            (
                lambda: self.part.at[ch, i] if self.grads is None else self.grads[ch].at[1, zc],
                self.r0.at[ch, i],
                self.core,
            ),
            (lambda: self.own.at[ch, i, pl.ds(2, 2)], self.r1.at[ch, i], self.first[ch]),
            (lambda: self.own.at[ch, i, 1], self.r2.at[ch, i], self.second[ch]),
            (lambda: self.own.at[ch, i, 0], self.r3.at[ch, min(i, 2)], self.peers[min(i, 2)]),
        )[stage]
        return pltpu.make_async_remote_copy(
            src_ref=src(), dst_ref=dst,
            send_sem=self.sent.at[stage, ch, i], recv_sem=self.got.at[stage, ch, i],
            device_id=to, device_id_type=pl.DeviceIdType.MESH,
        )

    def load(self, ch, i):
        zc = (self.z + (i + 1)) % 4
        return pltpu.make_async_copy(
            self.grads[ch].at[0, zc], self.own.at[ch, i], self.local.at[ch, i]
        )

    def start(self):
        for i in range(4):
            for ch in range(2):
                self.copy(0, ch, i).start()
                if self.grads is not None:
                    self.load(ch, i).start()

    def step(self, stage, i):
        for ch in range(2):
            self.copy(stage - 1, ch, i).wait_recv()
            if stage == 1:
                if self.grads is not None:
                    self.load(ch, i).wait()

                def add(j, _, ch=ch):
                    self.own[ch, i, j] = self.own[ch, i, j] + self.r0[ch, i, j]
                    return 0

                lax.fori_loop(0, 4, add, 0)
            elif stage == 2:

                def add(j, _, ch=ch):
                    self.own[ch, i, j] = self.own[ch, i, j] + self.r1[ch, i, j]
                    return 0

                lax.fori_loop(0, 2, add, 0)
            elif i < 3:
                self.own[ch, i, 0] = self.own[ch, i, 0] + self.r2[ch, i]
            if stage < 3 or i < 3:
                self.copy(stage, ch, i).start()

    def finish(self):
        for ch in range(2):
            total = self.own[ch, 3, 0].astype(F32) + self.r2[ch, 3].astype(F32)
            for i in range(3):
                self.copy(3, ch, i).wait_recv()
                total = total + self.r3[ch, i].astype(F32)
            self.out[ch] = total
        for stage in range(STAGES):
            for ch in range(2):
                for i in range(4 if stage < 3 else 3):
                    self.copy(stage, ch, i).wait_send()

    def run(self, step, plan):
        for at, events in plan.items():

            @pl.when(step == at)
            def _(events=events):
                for stage, i in events:
                    if stage == 0:
                        self.start()
                    elif stage == 4:
                        self.finish()
                    else:
                        self.step(stage, i)


def split_rel(r):
    return r & 1, (r >> 1) & 1, r >> 2


def rel_of(b):
    tok = lax.axis_index("tok")
    core, x, y = split_rel(b)
    flip = lambda static, mine: 1 - mine if static else mine
    return flip(core, tok % 2), flip(x, (tok // 2) % 2), flip(y, tok // 4)


def put_rows(g, ga, gb, cols, rows):
    half = rows // 2
    for b in range(8):
        core, x, y = rel_of(b)
        ga[core, 0, 2 * x + y, :, cols] = g[b * rows : b * rows + half]
        gb[core, 0, 2 * y + x, :, cols] = g[b * rows + half : (b + 1) * rows]


def sum_specs(grads, number):
    if grads is None:
        return [], [], [], [], {}
    rows, cols = grads[0].shape[3:]
    return (
        [pl.BlockSpec(memory_space=pl.ANY)] * 2,
        [full((2, rows, cols))],
        [jax.ShapeDtypeStruct((2, rows, cols), F32)],
        sum_scratch(rows, cols),
        {"has_side_effects": True, "collective_id": number},
    )


BLOCK = 128


def spread_kernel(
    idx, table, found, group_idx,
    held, numbers, ring_sent, ring_got, plane_sent, plane_got, idx_sent, idx_got,
):
    tok, z = lax.axis_index("tok"), lax.axis_index("tab")
    core, x, y, peers = neighbours()
    c, cx, cy = tok % 2, (tok // 2) % 2, tok // 4
    first, second = (x, y), (y, x)
    f, g = (cx, cy), (cy, cx)
    meet([core, x, y, *peers])
    half = table.shape[1] // 2
    count = idx.shape[2]

    def ring(k, ch):
        if k == 0:
            start = pl.multiple_of(tok * BLOCK, BLOCK)
            src = table.at[pl.ds(start, BLOCK), pl.ds(ch * half, half)]
        else:
            src = held.at[k - 1, ch, c, g[ch], f[ch]]
        return pltpu.make_async_remote_copy(
            src_ref=src, dst_ref=held.at[k, ch, c, g[ch], f[ch]],
            send_sem=ring_sent.at[k, ch], recv_sem=ring_got.at[k, ch],
            device_id=peers[0], device_id_type=pl.DeviceIdType.MESH,
        )

    def plane(stage, k, ch):
        src, to = (
            (held.at[k, ch, c, g[ch], f[ch]], first[ch]),
            (held.at[k, ch, c, g[ch]], second[ch]),
            (held.at[k, ch, c], core),
        )[stage]
        return pltpu.make_async_remote_copy(
            src_ref=src, dst_ref=src,
            send_sem=plane_sent.at[stage, k, ch], recv_sem=plane_got.at[stage, k, ch],
            device_id=to, device_id_type=pl.DeviceIdType.MESH,
        )

    def number(s):
        return pltpu.make_async_remote_copy(
            src_ref=idx.at[(z + s) % 4], dst_ref=numbers.at[s - 1],
            send_sem=idx_sent.at[s - 1], recv_sem=idx_got.at[s - 1],
            device_id=peers[s - 1], device_id_type=pl.DeviceIdType.MESH,
        )

    def picks(owner):
        out = []
        for b in range(8):
            row = lax.broadcasted_iota(jnp.int32, (BLOCK, count), 0) + b * BLOCK
            one = (row == idx[owner, 0:1, :]).astype(F32)
            two = (row == idx[owner, 1:2, :]).astype(F32)
            out.append((one + two).astype(BF))
        return out

    def arrive(k):
        for ch in range(2):
            ring(k, ch).wait_recv()
            if k < 2:
                ring(k + 1, ch).start()
            plane(0, k, ch).start()

    def go_on(stage, k):
        for ch in range(2):
            plane(stage - 1, k, ch).wait_recv()
            plane(stage, k, ch).start()

    def look_up(k):
        rows = picks((z + 3 - k) % 4)
        for ch in range(2):
            plane(2, k, ch).wait_recv()
            order = [
                4 * a + 2 * b + n if ch == 0 else 4 * b + 2 * a + n
                for n in range(2)
                for a in range(2)
                for b in range(2)
            ]
            pick = jnp.concatenate([rows[b] for b in order], axis=0)
            data = held[k, ch].reshape(8 * BLOCK, half)
            found[k + 1, :, ch * half : (ch + 1) * half] = dot(pick, data, TN).astype(BF)

    for ch in range(2):
        ring(0, ch).start()
    for s in range(1, 4):
        number(s).start()
    found[0] = dot(jnp.concatenate(picks(z), axis=0), table[...], TN).astype(BF)
    arrive(0)
    go_on(1, 0)
    arrive(1)
    go_on(1, 1)
    go_on(2, 0)
    arrive(2)
    go_on(1, 2)
    group_idx[0] = idx[z]
    for s in range(1, 4):
        number(s).wait_recv()
        group_idx[s] = numbers[s - 1]

    def finish(k, _):
        look_up(k)

        @pl.when(k < 2)
        def _():
            go_on(2, k + 1)

        return 0

    lax.fori_loop(0, 3, finish, 0)
    for s in range(1, 4):
        number(s).wait_send()
    for k in range(3):
        for ch in range(2):
            ring(k, ch).wait_send()
            for stage in range(3):
                plane(stage, k, ch).wait_send()


def spread(idx, table):
    n_tab, _, count = idx.shape
    rows, width = table.shape
    dma = pltpu.SemaphoreType.DMA
    return pl.pallas_call(
        spread_kernel,
        grid=(1,),
        in_specs=[full(idx.shape), full(table.shape)],
        out_specs=[full((n_tab, count, width)), full(idx.shape)],
        out_shape=[
            jax.ShapeDtypeStruct((n_tab, count, width), BF),
            jax.ShapeDtypeStruct(idx.shape, jnp.int32),
        ],
        scratch_shapes=[
            pltpu.VMEM((3, 2, 2, 2, 2, BLOCK, width // 2), BF),
            pltpu.VMEM((3, 2, count), jnp.int32),
            dma((3, 2)), dma((3, 2)), dma((3, 3, 2)), dma((3, 3, 2)), dma((3,)), dma((3,)),
        ],
        compiler_params=params(has_side_effects=True, collective_id=4),
        cost_estimate=cost(8 * count * width * rows, 8 << 20),
        name="spread",
    )(idx, table)


HP = 4


def head_masks(length, pair):
    lane = lax.broadcasted_iota(jnp.int32, (length, pair), 1)
    return lane < HEAD_DIM


def attn_fwd_kernel(q, k, v, mixed, lse):
    length = q.shape[0]
    pair = 2 * HEAD_DIM
    low_half = head_masks(length, pair)
    zero = jnp.zeros((length, pair), BF)
    for p in range(HP // 2):
        cols = slice(p * pair, (p + 1) * pair)
        qp, kp, vp = q[:, cols], k[:, cols], v[:, cols]
        vt = vp.T
        outs = []
        for h in range(2):
            km = jnp.where(low_half, kp, zero) if h == 0 else jnp.where(low_half, zero, kp)
            st = dot(km, qp, NT)
            top = jnp.max(st, axis=0, keepdims=True)
            raised = jnp.exp2((st - top) * LOG2E)
            total = jnp.sum(raised, axis=0, keepdims=True)
            lse[0, 0, 2 * p + h : 2 * p + h + 1, :] = top + jnp.log(total)
            ot = dot(vt[h * HEAD_DIM : (h + 1) * HEAD_DIM], raised.astype(BF), NN)
            outs.append(ot * (1.0 / total))
        mixed[:, cols] = jnp.concatenate(outs, axis=0).T.astype(BF)


def attn_fwd(q, k, v, pages):
    tokens, width = q.shape
    length = tokens // pages
    steps = HEADS // HP
    blk = pl.BlockSpec((length, HP * HEAD_DIM), lambda i, j: (i, j))
    return pl.pallas_call(
        attn_fwd_kernel,
        grid=(pages, steps),
        in_specs=[blk] * 3,
        out_specs=[blk, pl.BlockSpec((1, 1, HP, length), lambda i, j: (i, j, 0, 0))],
        out_shape=[
            jax.ShapeDtypeStruct((tokens, width), BF),
            jax.ShapeDtypeStruct((pages, steps, HP, length), F32),
        ],
        compiler_params=params(),
        cost_estimate=cost(14e9, 8 << 20, pages * HEADS * length * length),
        name="attention",
    )(q, k, v)


def attn_back(q, k, v, mixed, go, lse, put):
    length = q.shape[0]
    pair = 2 * HEAD_DIM
    low_half = head_masks(length, pair)
    zero = jnp.zeros((length, pair), BF)

    def pick(x, h):
        return jnp.where(low_half, x, zero) if h == 0 else jnp.where(low_half, zero, x)

    def pair_of_heads(p, _):
        cols = pl.ds(pl.multiple_of(p * pair, pair), pair)
        qp, kp, vp, op, gp = q[:, cols], k[:, cols], v[:, cols], mixed[:, cols], go[:, cols]
        kt = kp.T
        prod_t = (op.astype(F32) * gp.astype(F32)).T
        dq_t, dk, dv = [], None, None
        for h in range(2):
            st = dot(pick(kp, h), qp, NT)
            probs = jnp.exp2((st - lse[0, 0, pl.ds(2 * p + h, 1), :]) * LOG2E)
            dv_h = dot(probs.astype(BF), pick(gp, h), NN)
            dpt = dot(pick(vp, h), gp, NT)
            delta = colsum(prod_t[h * HEAD_DIM : (h + 1) * HEAD_DIM])
            ds = (probs * (dpt - delta)).astype(BF)
            dk_h = dot(ds, pick(qp, h), NN)
            dq_t.append(dot(kt[h * HEAD_DIM : (h + 1) * HEAD_DIM], ds, NN))
            dv = dv_h if dv is None else dv + dv_h
            dk = dk_h if dk is None else dk + dk_h
        dq = (jnp.concatenate(dq_t, axis=0).T.astype(BF).astype(F32) * SCALE).astype(BF)
        put(p * pair, pair, dq, dk.astype(BF), dv.astype(BF))
        return 0

    lax.fori_loop(0, HP // 2, pair_of_heads, 0)


FC = 512
FWD = 1024
RC = 128
MC = 512


def ffn_fwd_kernel(
    mixed, normed, wo, we, wr, hb, bias, gains, shifts, cot,
    out, after_out, low_out, rstd_out, act_out, slope_out, gs2_out, gffn_out, sums,
):
    ff = we.shape[1]
    attn_sum = normed[...] + (dot(mixed[...], wo[...], NN) + bias[2:3])
    xh, rstd = norm_stats(attn_sum)
    after = xh * gains[1:2] + shifts[1:2]
    after_out[...] = after
    rstd_out[...] = rstd
    low = after.astype(BF)
    low_out[...] = low
    total = after + bias[3:4]
    count = ff // FWD
    hidden = []
    for j in range(count + 1):
        if j < count:
            cols = slice(j * FWD, (j + 1) * FWD)
            hidden.append(dot(low, we[:, cols], NN) + hb[:, cols])
        if j > 0:
            cols = slice((j - 1) * FWD, j * FWD)
            act, slope = gelu_parts(hidden[j - 1])
            act = act.astype(BF)
            act_out[:, cols] = act
            slope_out[:, cols] = slope.astype(BF)
            total = total + dot(act, wr[cols, :], NN)
    xh, rstd = norm_stats(total)
    out[...] = (xh * gains[2:3] + shifts[2:3]).astype(BF)
    y = cot[...].astype(F32)
    gs2 = norm_back(y, xh, rstd, gains[2:3])
    gs2_out[...] = gs2
    gffn = gs2.astype(BF)
    gffn_out[...] = gffn
    part = jnp.concatenate([colsum(y * xh), colsum(y), colsum(gffn.astype(F32))], axis=0)

    @pl.when(pl.program_id(0) == 0)
    def _():
        sums[...] = part

    @pl.when(pl.program_id(0) != 0)
    def _():
        sums[...] = sums[...] + part


def ffn_fwd(mixed, normed, wo, we, wr, hb, bias, gains, shifts, cot, tile):
    tokens, width = mixed.shape
    ff = we.shape[1]
    rows = pl.BlockSpec((tile, width), lambda i: (i, 0))
    long = pl.BlockSpec((tile, ff), lambda i: (i, 0))
    shape = lambda dt, n=width: jax.ShapeDtypeStruct((tokens, n), dt)
    hb = hb.reshape(1, ff)
    return pl.pallas_call(
        ffn_fwd_kernel,
        grid=(tokens // tile,),
        in_specs=[rows, rows]
        + [full(a.shape) for a in (wo, we, wr, hb, bias, gains, shifts)]
        + [rows],
        out_specs=[rows, rows, rows, pl.BlockSpec((tile, 1), lambda i: (i, 0)), long, long, rows, rows]
        + [pl.BlockSpec((3, width), lambda i: (0, 0))],
        out_shape=[
            shape(BF), shape(F32), shape(BF), shape(F32, 1), shape(BF, ff), shape(BF, ff),
            shape(F32), shape(BF), jax.ShapeDtypeStruct((3, width), F32),
        ],
        compiler_params=params(),
        cost_estimate=cost(2 * tokens * width * (width + 2 * ff), 60 << 20, tokens * ff * 2),
        name="ffn_forward",
    )(mixed, normed, wo, we, wr, hb, bias, gains, shifts, cot)


def second_norm_back(gs1_out, after, rstd, gains, shifts, gattn_out, sums):
    tokens, width = after.shape

    def norm(i, carry):
        rows = pl.ds(pl.multiple_of(i * RC, RC), RC)
        total = gs1_out[rows, :]
        xh = (after[rows, :] - shifts[1:2]) * (1.0 / gains[1:2])
        gs1 = norm_back(total, xh, rstd[rows, :], gains[1:2])
        gs1_out[rows, :] = gs1
        gattn = gs1.astype(BF)
        gattn_out[rows, :] = gattn
        g, s, b = carry
        return g + colsum(total * xh), s + colsum(total), b + colsum(gattn.astype(F32))

    zero = jnp.zeros((1, width), F32)
    sums[...] = jnp.concatenate(lax.fori_loop(0, tokens // RC, norm, (zero, zero, zero)), axis=0)


def ffn_bwd_kernel(
    gffn, gs2, after, rstd, wo, gains, shifts, slope, wr, we,
    gh_out, gs1_out, gattn_out, gmixed_out, hsum, sums,
):
    step, last = pl.program_id(0), pl.num_programs(0) - 1
    tokens, width = gffn.shape

    @pl.when(step == 0)
    def _():
        gs1_out[...] = gs2[...]

    part = jnp.zeros((1, slope.shape[1]), F32)
    for m in range(0, tokens, MC):
        rows = slice(m, m + MC)
        gh = (dot(gffn[rows, :], wr[...], NT) * slope[rows, :].astype(F32)).astype(BF)
        gh_out[rows, :] = gh
        part = part + colsum(gh.astype(F32))
        gs1_out[rows, :] = gs1_out[rows, :] + dot(gh, we[...], NT)
    hsum[...] = part

    @pl.when(step == last)
    def _():
        second_norm_back(gs1_out, after, rstd, gains, shifts, gattn_out, sums)
        for m in range(0, tokens, MC):
            rows = slice(m, m + MC)
            gmixed_out[rows, :] = dot(gattn_out[rows, :], wo[...], NT).astype(BF)


def ffn_bwd(gffn, slope, gs2, after, rstd, wr, we, wo, gains, shifts):
    tokens, width = gffn.shape
    ff = we.shape[1]
    whole = full((tokens, width))
    long = pl.BlockSpec((tokens, FC), lambda s: (0, s))
    shape = lambda dt, n=width: jax.ShapeDtypeStruct((tokens, n), dt)
    return pl.pallas_call(
        ffn_bwd_kernel,
        grid=(ff // FC,),
        in_specs=[whole, whole, whole, full((tokens, 1))]
        + [full(a.shape) for a in (wo, gains, shifts)]
        + [
            long,
            pl.BlockSpec((FC, width), lambda s: (s, 0)),
            pl.BlockSpec((width, FC), lambda s: (0, s)),
        ],
        out_specs=[long, whole, whole, whole]
        + [pl.BlockSpec((1, FC), lambda s: (0, s)), full((3, width))],
        out_shape=[
            shape(BF, ff), shape(F32), shape(BF), shape(BF),
            jax.ShapeDtypeStruct((1, ff), F32), jax.ShapeDtypeStruct((3, width), F32),
        ],
        compiler_params=params(),
        cost_estimate=cost(2 * tokens * width * (width + 2 * ff), 60 << 20),
        name="ffn_backward",
    )(gffn, gs2, after, rstd, wo, gains, shifts, slope, wr, we)


FFN_PLAN = {
    4: [(0, 0)],
    8: [(1, 0)],
    9: [(1, 1)],
    11: [(2, 0), (1, 2)],
    13: [(2, 1), (1, 3)],
    15: [(3, 0)],
    16: [(2, 2)],
    17: [(3, 1), (2, 3)],
    18: [(3, 2)],
    19: [(3, 3)],
}
N_TOK, N_TAB = 8, 4


def block_of_step(s):
    s = jnp.minimum(s, N_TOK - 1)
    return 1 - s // 4, 1 - (s // 2) % 2, 1 - s % 2


def ffn_grads_kernel(
    gffn_in, gs2_in, after, rstd, low, mixed, wo, gains, shifts, act, slope, wr, we,
    gs1_out, gmixed_out, hsum, sums, ga, gb, reduce_out,
    gffn, gh, local, *scratch,
):
    step, last = pl.program_id(0), pl.num_programs(0) - 1
    tokens, width = after.shape
    summing = Summing(None, reduce_out, scratch)
    both = scratch[0]
    z = lax.axis_index("tab")
    first = pltpu.make_async_copy(gffn_in, gffn, local.at[0])
    later = pltpu.make_async_copy(gs2_in, gs1_out, local.at[1])

    @pl.when(step == 0)
    def _():
        first.start()
        later.start()
        meet(summing.devices())
        first.wait()

    @pl.when(step == N_TOK)
    def _():
        later.wait()

    summing.run(step, FFN_PLAN)

    @pl.when(step < N_TOK)
    def _():
        core, x, y = block_of_step(step)
        g = dot(gffn[...], act[...], TN).astype(BF)
        rows, half = both.shape[4:]
        for zc in range(N_TAB):
            i = (zc + N_TAB - 1 - z) % N_TAB
            for ch in range(2):
                piece = g[zc * rows : (zc + 1) * rows, ch * half : (ch + 1) * half]
                both[core, ch, i, (2 * x + y, 2 * y + x)[ch]] = piece

    @pl.when((step >= N_TOK) & (step < 2 * N_TOK))
    def _():
        part = jnp.zeros((1, slope.shape[1]), F32)
        for m in range(0, tokens, MC):
            rows = slice(m, m + MC)
            g = (dot(gffn[rows, :], wr[...], NT) * slope[rows, :].astype(F32)).astype(BF)
            gh[step - N_TOK, rows, :] = g
            part = part + colsum(g.astype(F32))
            gs1_out[rows, :] = gs1_out[rows, :] + dot(g, we[...], NT)
        hsum[...] = part

    @pl.when(step == 2 * N_TOK - 1)
    def _():
        second_norm_back(gs1_out, after, rstd, gains, shifts, gffn, sums)

        def block(m, _):
            rows = pl.ds(pl.multiple_of(m * MC, MC), MC)
            gmixed_out[rows, :] = dot(gffn[rows, :], wo[...], NT).astype(BF)
            return 0

        lax.fori_loop(0, tokens // MC, block, 0)

    @pl.when(step >= 2 * N_TOK)
    def _():
        n = step - 2 * N_TOK
        quarter = width // N_TAB
        rows = width // N_TOK
        wide = gh.shape[2]

        def block(m, _):
            g = dot(low[...], gh[2 * n + m], TN).astype(BF)
            put_rows(g, ga, gb, pl.ds(pl.multiple_of(m * wide, wide), wide), rows)
            return 0

        lax.fori_loop(0, 2, block, 0)
        piece = gffn[:, pl.ds(pl.multiple_of(n * quarter, quarter), quarter)]
        g = dot(mixed[...], piece, TN).astype(BF)
        put_rows(g, ga, gb, slice(2 * wide, 2 * wide + quarter), rows)

    @pl.when(step == last)
    def _():
        summing.finish()


def ffn_grads(gffn, act, slope, gs2, after, low, rstd, mixed, wr, we, wo, gains, shifts):
    tokens, width = gffn.shape
    ff = we.shape[1]
    whole = full((tokens, width))
    anywhere = pl.BlockSpec(memory_space=pl.ANY)
    wide = ff // N_TOK
    half = width // (2 * N_TOK)
    out_wide = (ff + width) // N_TAB
    back = lambda s: jnp.clip(s - N_TOK, 0, N_TOK - 1)
    grad = lambda s: jnp.clip(s - 2 * N_TOK, 0, N_TAB - 1)

    def act_block(s):
        core, x, y = block_of_step(s)
        tok = lax.axis_index("tok")
        flip = lambda rel, mine: rel + mine - 2 * rel * mine
        return 0, 4 * flip(y, tok // 4) + 2 * flip(x, (tok // 2) % 2) + flip(core, tok % 2)

    rows, cols = width // N_TAB, wide // 2
    part = lambda *n: pltpu.VMEM((*n, rows, cols), BF)
    dma = pltpu.SemaphoreType.DMA
    shape = lambda dt: jax.ShapeDtypeStruct((tokens, width), dt)
    piece = pl.BlockSpec((2, 1, 4, half, out_wide), lambda s: (0, grad(s), 0, 0, 0))
    return pl.pallas_call(
        ffn_grads_kernel,
        grid=(2 * N_TOK + N_TAB,),
        in_specs=[anywhere, anywhere, whole, full((tokens, 1)), whole, whole]
        + [full(a.shape) for a in (wo, gains, shifts)]
        + [
            pl.BlockSpec((tokens, wide), act_block),
            pl.BlockSpec((tokens, wide), lambda s: (0, back(s))),
            pl.BlockSpec((wide, width), lambda s: (back(s), 0)),
            pl.BlockSpec((width, wide), lambda s: (0, back(s))),
        ],
        out_specs=[
            whole, whole, pl.BlockSpec((1, wide), lambda s: (0, back(s))), full((3, width)),
            piece, piece, full((2, rows, cols)),
        ],
        out_shape=[
            shape(F32), shape(BF),
            jax.ShapeDtypeStruct((1, ff), F32), jax.ShapeDtypeStruct((3, width), F32),
            jax.ShapeDtypeStruct((2, 4, 4, half, out_wide), BF),
            jax.ShapeDtypeStruct((2, 4, 4, half, out_wide), BF),
            jax.ShapeDtypeStruct((2, rows, cols), F32),
        ],
        scratch_shapes=[
            pltpu.VMEM((tokens, width), BF), pltpu.VMEM((N_TOK, tokens, wide), BF), dma((2,)),
            part(2, 2, 4, 4), part(2, 4, 4), part(2, 4, 2), part(2, 4), part(2, 3),
            dma((STAGES, 2, 4)), dma((STAGES, 2, 4)),
        ],
        compiler_params=pltpu.CompilerParams(
            vmem_limit_bytes=67043328, has_side_effects=True, collective_id=1
        ),
        cost_estimate=cost(2 * tokens * width * (2 * width + 4 * ff), 60 << 20),
        name="ffn_backward_grads",
    )(gffn, gs2, after, rstd, low, mixed, wo, gains, shifts, act, slope, wr, we)


BACK_PLAN = {
    0: [(0, 0)],
    1: [(1, 0)],
    2: [(1, 1)],
    3: [(2, 0), (1, 2)],
    5: [(2, 1), (1, 3)],
    6: [(3, 0)],
    8: [(2, 2)],
    9: [(3, 1)],
    11: [(2, 3)],
    12: [(3, 2)],
    13: [(3, 3)],
}


def back_kernel(*refs, pages, summed):
    q, k, v, mixed, go, lse, low, gs1, w, normed, rstd, ci, gains, shifts = refs[:14]
    refs = refs[14:]
    grads, refs = refs[: 2 * summed], refs[2 * summed :]
    out, cells, sums0, sums_qv = refs[:4]
    refs = refs[4:]
    if summed:
        ga, gb, summed_out, gj = refs[:4]
        summing = Summing(grads, summed_out, refs[4:])
    else:
        gj_out, gj = refs
    step = pl.program_id(0)
    width = gs1.shape[1]
    length = q.shape[0]
    groups = HEADS // HP
    wide = HP * HEAD_DIM
    n_attn = groups * pages
    n_joined = 4 if summed else 0

    if summed:

        @pl.when(step == 0)
        def _():
            meet(summing.devices())

        summing.run(step, BACK_PLAN)

    @pl.when(step < n_attn)
    def _():
        group, page = step // pages, step % pages
        rows = pl.ds(pl.multiple_of(page * length, length), length)

        def put(at, size, dq, dk, dv):
            cols = pl.ds(pl.multiple_of(group * wide + at, size), size)
            gj[0, rows, cols] = dq
            gj[1, rows, cols] = dk
            gj[2, rows, cols] = dv
            part = jnp.concatenate([colsum(dq.astype(F32)), colsum(dv.astype(F32))], axis=0)

            @pl.when(page == 0)
            def _():
                sums_qv[:, cols] = part

            @pl.when(page != 0)
            def _():
                sums_qv[:, cols] = sums_qv[:, cols] + part

        attn_back(q, k, v, mixed, go, lse, put)

    if summed:
        quarter = width // 4

        @pl.when((step >= n_attn) & (step < n_attn + n_joined))
        def _():
            def block(m, _):
                unit = 3 * (step - n_attn) + m
                cols = pl.ds(pl.multiple_of((unit % 4) * quarter, quarter), quarter)
                g = dot(low[...], gj[unit // 4, :, cols], TN).astype(BF)
                at = pl.ds(pl.multiple_of(m * quarter, quarter), quarter)
                put_rows(g, ga, gb, at, width // 8)
                return 0

            lax.fori_loop(0, 3, block, 0)

    @pl.when(step >= n_attn + n_joined)
    def _():
        page = step - (n_attn + n_joined)
        rows = pl.ds(pl.multiple_of(page * length, length), length)
        total = gs1[...]
        for n in range(3):
            total = total + dot(gj[n, rows, :], w[:, n * width : (n + 1) * width], NT)
        xh = (normed[...] - shifts[0:1]) * (1.0 / gains[0:1])
        grad = norm_back(total, xh, rstd[...], gains[0:1])
        out[...] = grad
        number = lax.broadcasted_iota(jnp.int32, (CELLS, length), 0)
        pick = (number == ci[0]).astype(F32).astype(BF)
        cells[...] = dot(pick, grad.astype(BF), NN).astype(BF)
        part = jnp.concatenate([colsum(total * xh), colsum(total)], axis=0)

        @pl.when(page == 0)
        def _():
            sums0[...] = part

        @pl.when(page != 0)
        def _():
            sums0[...] = sums0[...] + part

    if summed:

        @pl.when(step == pl.num_programs(0) - 1)
        def _():
            summing.finish()
    else:
        gj_out[...] = gj[...]


def back(q, k, v, mixed, go, lse, low, gs1, w, normed, rstd, ci, gains, shifts, grads):
    tokens, width = q.shape
    pages, length = ci.shape
    groups = HEADS // HP
    wide = HP * HEAD_DIM
    summed = grads is not None
    n_attn = groups * pages
    before = n_attn + (4 if summed else 0)
    at = lambda s: jnp.minimum(s, n_attn - 1)
    page = lambda s: jnp.maximum(s - before, 0)
    block = lambda s: jnp.clip(s - n_attn, 0, 3)
    blk = pl.BlockSpec((length, wide), lambda s: (at(s) % pages, at(s) // pages))
    rows = pl.BlockSpec((length, width), lambda s: (page(s), 0))
    out_specs = [
        rows,
        pl.BlockSpec((CELLS, width), lambda s: (page(s), 0)),
        full((2, width)),
        full((2, width)),
    ]
    out_shape = [
        jax.ShapeDtypeStruct((tokens, width), F32),
        jax.ShapeDtypeStruct((pages * CELLS, width), BF),
        jax.ShapeDtypeStruct((2, width), F32),
        jax.ShapeDtypeStruct((2, width), F32),
    ]
    whole_gj = (3, tokens, width)
    more_in, more_out, more_shape, more_scratch, more = sum_specs(grads, 2)
    if summed:
        half = width // 16
        piece = pl.BlockSpec((2, 1, 4, half, 3 * width // 4), lambda s: (0, block(s), 0, 0, 0))
        out_specs += [piece, piece]
        out_shape += [jax.ShapeDtypeStruct((2, 4, 4, half, 3 * width // 4), BF)] * 2
    else:
        out_specs += [full(whole_gj)]
        out_shape += [jax.ShapeDtypeStruct(whole_gj, BF)]
    return pl.pallas_call(
        functools.partial(back_kernel, pages=pages, summed=summed),
        grid=(before + pages,),
        in_specs=[blk] * 5
        + [
            pl.BlockSpec((1, 1, HP, length), lambda s: (at(s) % pages, at(s) // pages, 0, 0)),
            full(low.shape),
            rows,
            full(w.shape),
            rows,
            pl.BlockSpec((length, 1), lambda s: (page(s), 0)),
            pl.BlockSpec((1, 1, length), lambda s: (page(s), 0, 0)),
            full(gains.shape),
            full(shifts.shape),
        ]
        + more_in,
        out_specs=out_specs + more_out,
        out_shape=out_shape + more_shape,
        scratch_shapes=[pltpu.VMEM(whole_gj, BF)] + more_scratch,
        compiler_params=params(**more),
        cost_estimate=cost(70e9, 40 << 20, pages * HEADS * length * length),
        name="attention_joined_embed_back",
    )(
        q, k, v, mixed, go, lse, low, gs1, w, normed, rstd, ci.reshape(pages, 1, length),
        gains, shifts, *(grads or ()),
    )


def table_kernel(tok, idx, g0, g1, g2, g3, out_a, out_b):
    rows = out_a.shape[1]
    count = idx.shape[2]
    half = out_a.shape[2]
    base = (pl.program_id(0) ^ tok[0]) * rows
    number = lax.broadcasted_iota(jnp.int32, (rows, count), 0) + base
    picks = []
    for s in range(4):
        first = (number == idx[s, 0:1, :]).astype(F32)
        second = (number == idx[s, 1:2, :]).astype(F32)
        picks.append((first + second).astype(BF))
    pick = jnp.concatenate(picks, axis=1)
    grads = jnp.concatenate([g0[...], g1[...], g2[...], g3[...]], axis=0)
    total = dot(pick, grads, NN).astype(BF)
    out_a[0] = total[:, :half]
    out_b[0] = total[:, half:]


def table_part(tok, idx, grads, blocks):
    groups, _, count = idx.shape
    width = grads[0].shape[1]
    rows = 1024 // blocks
    half = width // 2
    out = pl.BlockSpec((1, rows, half), lambda i, t: (i, 0, 0))
    return pl.pallas_call(
        table_kernel,
        grid_spec=pltpu.PrefetchScalarGridSpec(
            num_scalar_prefetch=1,
            grid=(blocks,),
            in_specs=[full(idx.shape)] + [full((count, width))] * groups,
            out_specs=[out, out],
        ),
        out_shape=[jax.ShapeDtypeStruct((blocks, rows, half), BF)] * 2,
        compiler_params=params(),
        cost_estimate=cost(2 * 1024 * groups * count * width, 4 << 20),
        name="table_grad",
    )(tok, idx, *grads)


class TableSum:
    def __init__(self, scratch, done):
        self.part, self.r0, self.r1, self.r2, self.sent, self.got = scratch
        self.done = done
        tok = lax.axis_index("tok")
        core, x, y, _ = neighbours()
        self.c, cx, cy = tok % 2, (tok // 2) % 2, tok // 4
        self.core, self.first, self.second = core, (x, y), (y, x)
        self.f, self.g = (cx, cy), (cy, cx)

    def copy(self, stage, ch, u):
        c, f, g = self.c, self.f[ch], self.g[ch]
        part, done = self.part.at[ch, u], self.done.at[ch, u]
        src, dst, to = (
            (lambda: part.at[1 - c], self.r0.at[ch, u], self.core),
            (lambda: part.at[c, 1 - f], self.r1.at[ch, u], self.first[ch]),
            (lambda: part.at[c, f, 1 - g], self.r2.at[ch, u], self.second[ch]),
            (lambda: done.at[c, f, g], None, self.second[ch]),
            (lambda: done.at[c, f], None, self.first[ch]),
            (lambda: done.at[c], None, self.core),
        )[stage]
        src = src()
        return pltpu.make_async_remote_copy(
            src_ref=src, dst_ref=src if dst is None else dst,
            send_sem=self.sent.at[stage, ch, u], recv_sem=self.got.at[stage, ch, u],
            device_id=to, device_id_type=pl.DeviceIdType.MESH,
        )

    def store(self, u, ch, value):
        for b in range(8):
            c, x, y = split_rel(b)
            f, g = (x, y) if ch == 0 else (y, x)
            self.part[ch, u, c, f, g] = value[b * BLOCK : (b + 1) * BLOCK]
        self.copy(0, ch, u).start()

    def step(self, stage, u):
        for ch in range(2):
            c, f, g = self.c, self.f[ch], self.g[ch]
            self.copy(stage - 1, ch, u).wait_recv()
            if stage == 1:
                self.part[ch, u, c] = self.part[ch, u, c] + self.r0[ch, u]
            elif stage == 2:
                self.part[ch, u, c, f] = self.part[ch, u, c, f] + self.r1[ch, u]
            elif stage == 3:
                self.done[ch, u, c, f, g] = self.part[ch, u, c, f, g] + self.r2[ch, u]
            if stage < 6:
                self.copy(stage, ch, u).start()

    def finish(self):
        for stage in range(6):
            for ch in range(2):
                for u in range(2):
                    self.copy(stage, ch, u).wait_send()


def closing_kernel(
    cells, idx, sums0, sums1, sums2, sums_qv, hidden_sum, ga, gb, done, joined, small_out,
    ring, total, ring_sent, ring_got, held, arrived, small_sent, small_got, *scratch,
):
    summing = Summing((ga, gb), joined, scratch[:8])
    table = TableSum(scratch[8:], done)
    core, x, y, peers = neighbours()
    z = lax.axis_index("tab")
    hops = [core, x, y, {"tab": z + 1 - 2 * (z % 2)}, {"tab": z + 2 - 4 * (z // 2)}]
    meet([core, x, y, *peers])
    count = cells.shape[0]
    half = cells.shape[1] // 2

    def pass_on(k, h):
        cols = pl.ds(h * half, half)
        src = cells.at[:, cols] if k == 0 else ring.at[k - 1, :, cols]
        return pltpu.make_async_remote_copy(
            src_ref=src, dst_ref=ring.at[k, :, cols],
            send_sem=ring_sent.at[k, h], recv_sem=ring_got.at[k, h],
            device_id=peers[0], device_id_type=pl.DeviceIdType.MESH,
        )

    def small_copy(n):
        return pltpu.make_async_remote_copy(
            src_ref=held.at[n], dst_ref=arrived.at[n],
            send_sem=small_sent.at[n], recv_sem=small_got.at[n],
            device_id=hops[n], device_id_type=pl.DeviceIdType.MESH,
        )

    def small_step(n):
        small_copy(n - 1).wait_recv()
        value = held[n - 1] + arrived[n - 1]
        if n < 5:
            held[n] = value
            small_copy(n).start()
        else:
            small_out[...] = value

    def relay(k, h):
        pass_on(k - 1, h).wait_recv()
        pass_on(k, h).start()

    def pick(s):
        number = lax.broadcasted_iota(jnp.int32, (total.shape[0], count), 0)
        first = (number == idx[s, 0:1, :]).astype(F32)
        second = (number == idx[s, 1:2, :]).astype(F32)
        return (first + second).astype(BF)

    def last_arrival(u):
        pass_on(2, u).wait_recv()
        for ch in range(2):
            cols = slice((2 * u + ch) * half // 2, (2 * u + ch + 1) * half // 2)
            value = total[:, cols] + dot(last, ring[2, :, cols], NN)
            table.store(u, ch, value.astype(BF))

    pass_on(0, 0).start()
    pass_on(0, 1).start()
    at, width = 0, cells.shape[1]
    for part in (sums0, sums1, sums2, sums_qv):
        held[0, at : at + part.shape[0]] = part[...]
        at += part.shape[0]
    for n in range(hidden_sum.shape[1] // width):
        held[0, at + n : at + n + 1] = hidden_sum[:, n * width : (n + 1) * width]
    small_copy(0).start()
    summing.start()
    total[...] = dot(pick(0), cells[...], NN)
    small_step(1)
    summing.step(1, 0)
    small_step(2)
    summing.step(1, 1)
    relay(1, 0)
    summing.step(2, 0)
    summing.step(1, 2)
    small_step(3)
    relay(1, 1)
    summing.step(2, 1)
    summing.step(1, 3)
    relay(2, 0)
    small_step(4)
    summing.step(2, 2)
    relay(2, 1)
    summing.step(3, 0)
    summing.step(3, 1)
    summing.step(2, 3)

    def add(k, _):
        total[...] = total[...] + dot(pick(k + 1), ring[k], NN)
        return 0

    lax.fori_loop(0, 2, add, 0)
    last = pick(3)
    last_arrival(0)
    table.step(1, 0)
    last_arrival(1)
    summing.step(3, 2)
    small_step(5)
    table.step(2, 0)
    table.step(1, 1)
    table.step(3, 0)
    table.step(2, 1)
    table.step(4, 0)
    table.step(3, 1)
    table.step(5, 0)
    table.step(4, 1)
    table.step(6, 0)
    table.step(5, 1)
    summing.step(3, 3)
    summing.finish()
    table.step(6, 1)
    table.finish()
    for k in range(3):
        for h in range(2):
            pass_on(k, h).wait_send()
    for n in range(5):
        small_copy(n).wait_send()


def closing(cells, idx, sums, grads):
    count, width = cells.shape
    small = (sum(part.size for part in sums) // width, width)
    rows, cols = grads[0].shape[3:]
    wide = width // 4
    part = lambda *n: pltpu.VMEM((2, 2, *n, BLOCK, wide), BF)
    done = (2, 2, 2, 2, 2, BLOCK, wide)
    dma = pltpu.SemaphoreType.DMA
    return pl.pallas_call(
        closing_kernel,
        grid=(1,),
        in_specs=[full(cells.shape), full(idx.shape)]
        + [full(part.shape) for part in sums]
        + [pl.BlockSpec(memory_space=pl.ANY)] * 2,
        out_specs=[full(done), full((2, rows, cols)), full(small)],
        out_shape=[
            jax.ShapeDtypeStruct(done, BF),
            jax.ShapeDtypeStruct((2, rows, cols), F32),
            jax.ShapeDtypeStruct(small, F32),
        ],
        scratch_shapes=[
            pltpu.VMEM((3, count, width), BF), pltpu.VMEM((8 * BLOCK, width), F32),
            dma((3, 2)), dma((3, 2)),
            pltpu.VMEM((5, *small), F32), pltpu.VMEM((5, *small), F32), dma((5,)), dma((5,)),
        ]
        + sum_scratch(rows, cols)
        + [part(2, 2, 2), part(2, 2), part(2), part(), dma((6, 2, 2)), dma((6, 2, 2))],
        compiler_params=params(has_side_effects=True, collective_id=3),
        cost_estimate=cost(8 * count * width * 1024, 24 << 20),
        name="closing",
    )(cells, idx, *sums, *grads)


def write_kernel(
    a, b, embed, reduce_sum, expand_sum, joined_sum, small,
    table, embed_out, reduce_out, expand_out, output_out, joined_out,
    gains, shifts, biases, hidden_bias,
):
    wide = a.shape[6]
    lanes = table.shape[1]
    for n, piece in enumerate((a, b)):
        for u in range(2):
            for c in range(2):
                value = piece[0, u, c, 0, 0].astype(F32)
                for k in range(wide // lanes):
                    row = c * BLOCK * (4 * wide // lanes) + ((2 * u + n) * wide) // lanes + k
                    table[pl.ds(row, BLOCK, stride=4 * wide // lanes), :] = value[
                        :, k * lanes : (k + 1) * lanes
                    ]
    embed_out[...] = embed[...]

    @pl.when(pl.program_id(0) == 0)
    def _():
        cols = reduce_sum.shape[2]
        rows = expand_sum.shape[1]
        wide = expand_out.shape[1]
        for n in range(2):
            reduce_out[n * cols : (n + 1) * cols, :] = reduce_sum[n].T
            expand_out[n * rows : (n + 1) * rows, :] = expand_sum[n, :, :wide]
            output_out[n * rows : (n + 1) * rows, :] = expand_sum[n, :, wide:]
            joined_out[n * rows : (n + 1) * rows, :] = joined_sum[n]
        for out, order in ((gains, (0, 2, 5)), (shifts, (1, 3, 6)), (biases, (8, 9, 4, 7))):
            for n, row in enumerate(order):
                out[n : n + 1, :] = small[row : row + 1, :]
        for n in range(hidden_bias.shape[0]):
            hidden_bias[n : n + 1, :] = small[10 + n : 11 + n, :]


def write(done, embed, reduce_sum, expand_sum, joined_sum, small, table_rows, ff):
    wide = done.shape[6]
    width = 4 * wide
    tokens = embed.shape[0]
    block = (1, 2, 2, 1, 1, BLOCK, wide)
    first = lambda i: (0, 0, 0, i % 2, i // 2, 0, 0)
    second = lambda i: (1, 0, 0, i // 2, i % 2, 0, 0)
    rows = 2 * expand_sum.shape[1]
    cols = ff // N_TAB
    f32 = lambda *n: jax.ShapeDtypeStruct(n, F32)
    shapes = [
        f32(2 * reduce_sum.shape[2], reduce_sum.shape[1]), f32(rows, cols),
        f32(rows, expand_sum.shape[2] - cols), f32(rows, joined_sum.shape[2]),
        f32(3, width), f32(3, width), f32(4, width), f32(ff // width, width),
    ]
    lanes = 128
    part = pl.BlockSpec((tokens // 4, width), lambda i: (i, 0))
    table, *rest = pl.pallas_call(
        write_kernel,
        grid=(4,),
        in_specs=[pl.BlockSpec(block, first), pl.BlockSpec(block, second), part]
        + [full(v.shape) for v in (reduce_sum, expand_sum, joined_sum, small)],
        out_specs=[pl.BlockSpec((2 * BLOCK * width // lanes, lanes), lambda i: (i, 0)), part]
        + [full(v.shape) for v in shapes],
        out_shape=[f32(table_rows * width // lanes, lanes), f32(tokens, width)] + shapes,
        compiler_params=params(),
        cost_estimate=cost(0, 16 << 20),
        name="write",
    )(done, done, embed, reduce_sum, expand_sum, joined_sum, small)
    return table.reshape(1, table_rows, width), *rest


def flip_tok(value, bit, size):
    return lax.ppermute(value, "tok", [(i, i ^ bit) for i in range(size)])


def shift_tab(value, shift, size):
    return lax.ppermute(value, "tab", [(i, (i + shift) % size) for i in range(size)])


def small_sum(value, n_tok, n_tab):
    bit = 1
    while bit < n_tok:
        value = value + flip_tok(value, bit, n_tok)
        bit *= 2
    total = value
    for shift in range(1, n_tab):
        total = total + shift_tab(value, shift, n_tab)
    return total


def body(
    n_tok, n_tab,
    embedded, cell_index, cell_boxes, box_tables, joined_weight, output_weight,
    expand_weight, reduce_weight, hidden_bias, bias_rows, norm_gains, norm_shifts, cotangent,
):
    tokens, width = embedded.shape
    pages, length = cell_index.shape
    table_rows = box_tables.shape[1]
    ff = expand_weight.shape[1]
    tok = lax.axis_index("tok").astype(jnp.int32).reshape(1)
    z = lax.axis_index("tab")
    cubic = n_tok == 8 and n_tab == 4

    corners = cell_boxes[:, :, :CELLS]
    lo = lambda n: jnp.minimum(corners[:, n], corners[:, n + 2]).reshape(-1)
    hi = lambda n: jnp.maximum(corners[:, n], corners[:, n + 2]).reshape(-1)
    left, right, top, bottom = lo(0), hi(0), lo(1), hi(1)
    none = jnp.full_like(left, -1)
    index_table = jnp.stack(
        [
            jnp.stack([left, right]),
            jnp.stack([top, bottom]),
            jnp.stack([right - left, none]),
            jnp.stack([bottom - top, none]),
        ]
    )
    padded = jnp.pad(box_tables[0], ((0, 1024 - table_rows), (0, 0)))
    if cubic:
        terms, group_index = spread(index_table, padded)
    else:
        pick_table = lambda i: lax.dynamic_index_in_dim(index_table, i, 0, keepdims=False)
        group_index = jnp.stack(
            [pick_table(z)]
            + [shift_tab(pick_table((z + s) % n_tab), s, n_tab) for s in range(1, n_tab)]
        )
        found = lookup(group_index, padded)
        terms = jnp.stack(
            [found[0]] + [shift_tab(found[s], n_tab - s, n_tab) for s in range(1, n_tab)]
        )

    q, k, v, normed, normed_low, rstd0 = embed(
        embedded, cell_index, terms, joined_weight, norm_gains, norm_shifts, bias_rows
    )
    mixed, lse = attn_fwd(q, k, v, pages)
    layer_out, after, after_low, rstd1, act, slope, gs2, gffn, sums2 = ffn_fwd(
        mixed, normed, output_weight, expand_weight, reduce_weight, hidden_bias,
        bias_rows, norm_gains, norm_shifts, cotangent, min(256, tokens),
    )
    if cubic:
        gs1, gmixed, hidden_sum, sums1, *parts, reduce_sum = ffn_grads(
            gffn, act, slope, gs2, after, after_low, rstd1, mixed, reduce_weight, expand_weight,
            output_weight, norm_gains, norm_shifts,
        )
    else:
        parts = None
        gh, gs1, gattn, gmixed, hidden_sum, sums1 = ffn_bwd(
            gffn, slope, gs2, after, rstd1, reduce_weight, expand_weight, output_weight,
            norm_gains, norm_shifts,
        )
    embedded_grad, cell_grad, sums0, sums_qv, *more = back(
        q, k, v, mixed, gmixed, lse, normed_low, gs1, joined_weight, normed, rstd0, cell_index,
        norm_gains, norm_shifts, parts,
    )
    if cubic:
        parts, expand_sum = more[:2], more[2:]
    else:
        gj = more[0]

    sums = (sums0, sums1, sums2, sums_qv, hidden_sum)
    if cubic:
        done, joined_sum, small = closing(cell_grad, group_index, sums, parts)
        (
            tables_grad, embedded_grad, reduce_grad, expand_grad, output_grad, joined_grad,
            gains_grad, shifts_grad, biases_grad, hidden_bias_grad,
        ) = write(
            done, embedded_grad, reduce_sum, expand_sum[0], joined_sum, small, table_rows, ff
        )
        hidden_bias_grad = hidden_bias_grad.reshape(-1)
    else:
        cell_grads = [cell_grad] + [shift_tab(cell_grad, s, n_tab) for s in range(1, n_tab)]
        part_a, part_b = table_part(jnp.zeros_like(tok), group_index, cell_grads, 8)
        both = jnp.concatenate([part_a, part_b], axis=2).astype(F32)
        tables_grad = lax.psum(both.reshape(1, -1, width)[:, :table_rows], "tok")
        small = jnp.concatenate([part.reshape(-1) for part in sums]).reshape(-1, 128)
        small = small_sum(small, n_tok, n_tab).reshape(-1)
        row = small.reshape(-1, width)
        gains_grad = jnp.stack([row[0], row[2], row[5]])
        shifts_grad = jnp.stack([row[1], row[3], row[6]])
        biases_grad = jnp.stack([row[8], row[9], row[4], row[7]])
        hidden_bias_grad = small[10 * width :]
        both = lambda a, b: jnp.einsum("ta,tb->ab", a, b, preferred_element_type=F32).astype(BF)

        def scattered(part):
            part = lax.psum_scatter(part, "tok", scatter_dimension=0, tiled=True)
            return lax.psum_scatter(part, "tab", scatter_dimension=1, tiled=True).astype(F32)

        reduce_grad = scattered(both(act, gffn))
        expand_grad = scattered(both(after_low, gh))
        output_grad = scattered(both(mixed, gattn))
        joined_grad = scattered(both(normed_low, jnp.concatenate([gj[0], gj[1], gj[2]], axis=1)))

    return (
        layer_out, embedded_grad, tables_grad, joined_grad, output_grad, expand_grad,
        reduce_grad, hidden_bias_grad, biases_grad, gains_grad, shifts_grad,
    )


def solution(mesh):
    rows = P(("tok", "tab"), None)
    return jax.shard_map(
        functools.partial(body, mesh.shape["tok"], mesh.shape["tab"]),
        mesh=mesh,
        in_specs=(
            rows, rows, P(("tok", "tab"), None, None), P("tab", None, None),
            P(), P(), P(), P(), P(), P(), P(), P(), rows,
        ),
        out_specs=(
            rows, rows, P("tab", None, None), P("tok", "tab"), P("tok", "tab"),
            P("tok", "tab"), P("tok", "tab"), P(), P(), P(), P(),
        ),
        check_vma=False,
    )
```

```python
import functools

import jax
import jax.numpy as jnp
from jax import lax
from jax.experimental import pallas as pl
from jax.experimental.pallas import tpu as pltpu
from jax.sharding import PartitionSpec as P

HEADS = 16
HEAD_DIM = 64
CELLS = 128
EPSILON = 1e-05
SCALE = HEAD_DIM ** (-0.5)
LOG2E = 1.4426950408889634
F32 = jnp.float32
BF = jnp.bfloat16
NN = ((1,), (0,))
NT = ((1,), (1,))
TN = ((0,), (0,))
ANY = pl.ANY

TAIL_P = 0.305
TAIL_C = (
    0.12164194255155772,
    0.12243138164026345,
    0.10365178645525906,
    0.12022714029486306,
    -0.03641303195181058,
    0.1839499605096701,
    -0.15192310059752684,
    0.03643391798251271,
)


def dot(a, b, dims):
    return lax.dot_general(a, b, (dims, ((), ())), preferred_element_type=F32)


def params(**kw):
    return pltpu.CompilerParams(vmem_limit_bytes=60 << 20, **kw)


def cost(flops, nbytes, trans=0):
    return pl.CostEstimate(
        flops=int(flops), bytes_accessed=int(nbytes), transcendentals=int(trans)
    )


def full(shape):
    zeros = (0,) * len(shape)
    return pl.BlockSpec(shape, lambda *_: zeros, pipeline_mode=pl.Buffered(1))


def gelu_parts(h):
    a = jnp.abs(h)
    t = 1.0 / (1.0 + TAIL_P * a)
    poly = jnp.full_like(t, TAIL_C[-1])
    for c in TAIL_C[-2::-1]:
        poly = poly * t + c
    e = jnp.exp2(h * h * (-0.5 * LOG2E))
    tail = poly * t * e
    phi_cdf = jnp.where(h > 0, 1.0 - tail, tail)
    act = h * phi_cdf
    slope = phi_cdf + h * e * 0.3989422804014327
    return act, slope


def norm_stats(v):
    mean = jnp.mean(v, axis=-1, keepdims=True)
    centred = v - mean
    var = jnp.mean(centred * centred, axis=-1, keepdims=True)
    rstd = lax.rsqrt(var + EPSILON)
    return centred * rstd, rstd


def norm_back(y, xh, rstd, gain):
    u = y * gain
    return (
        u - jnp.mean(u, axis=-1, keepdims=True) - xh * jnp.mean(u * xh, axis=-1, keepdims=True)
    ) * rstd


def colsum(v):
    return jnp.sum(v, axis=0, keepdims=True)


def lookup_kernel(idx, table, out):
    rows = table.shape[0]
    count = idx.shape[2]
    number = lax.broadcasted_iota(jnp.int32, (rows, count), 0)
    first = (number == idx[0, 0:1, :]).astype(F32)
    second = (number == idx[0, 1:2, :]).astype(F32)
    out[0] = dot((first + second).astype(BF), table[...], TN).astype(BF)


def lookup(idx, table):
    groups, _, count = idx.shape
    rows, width = table.shape
    return pl.pallas_call(
        lookup_kernel,
        grid=(groups,),
        in_specs=[
            pl.BlockSpec((1, 2, count), lambda i: (i, 0, 0)),
            full((rows, width)),
        ],
        out_specs=pl.BlockSpec((1, count, width), lambda i: (i, 0, 0)),
        out_shape=jax.ShapeDtypeStruct((groups, count, width), BF),
        compiler_params=params(),
        cost_estimate=cost(2 * groups * count * rows * width, 2 * groups * count * width),
        name="lookup",
    )(idx, table)


def embed_kernel(
    emb, ci, terms, w, gains, shifts, bias, q, k, v, normed, low, rstd_out
):
    width = emb.shape[1]
    tokens = emb.shape[0]
    cells = terms[...].reshape(4 * CELLS, width)
    number = lax.broadcasted_iota(jnp.int32, (CELLS, tokens), 0)
    pick = (number == ci[0]).astype(F32).astype(BF)
    pick = jnp.concatenate([pick] * 4, axis=0)
    box = dot(pick, cells, TN)
    xh, rstd = norm_stats(emb[...].astype(F32) + box)
    y = xh * gains[0:1] + shifts[0:1]
    normed[...] = y
    rstd_out[...] = rstd
    y_low = y.astype(BF)
    low[...] = y_low
    q[...] = ((dot(y_low, w[:, :width], NN) + bias[0:1]) * SCALE).astype(BF)
    k[...] = dot(y_low, w[:, width : 2 * width], NN).astype(BF)
    v[...] = (dot(y_low, w[:, 2 * width :], NN) + bias[1:2]).astype(BF)


def embed(emb, ci, terms, w, gains, shifts, bias):
    tokens, width = emb.shape
    pages, length = ci.shape
    rows = pl.BlockSpec((length, width), lambda i: (i, 0))
    shape = lambda dt, n=width: jax.ShapeDtypeStruct((tokens, n), dt)
    return pl.pallas_call(
        embed_kernel,
        grid=(pages,),
        in_specs=[rows, pl.BlockSpec((1, 1, length), lambda i: (i, 0, 0))]
        + [pl.BlockSpec((4, CELLS, width), lambda i: (0, i, 0))]
        + [full(w.shape), full(gains.shape), full(shifts.shape), full(bias.shape)],
        out_specs=[rows] * 5 + [pl.BlockSpec((length, 1), lambda i: (i, 0))],
        out_shape=[shape(BF), shape(BF), shape(BF), shape(F32), shape(BF), shape(F32, 1)],
        compiler_params=params(),
        cost_estimate=cost(2 * tokens * width * 3 * width, 26 << 20),
        name="embed_joined",
    )(emb, ci.reshape(pages, 1, length), terms, w, gains, shifts, bias)


STAGES = 4


def neighbours():
    tok, z = lax.axis_index("tok"), lax.axis_index("tab")
    core = {"tok": tok + 1 - 2 * (tok % 2)}
    x = {"tok": tok + 2 - 4 * ((tok // 2) % 2)}
    y = {"tok": tok + 4 - 8 * (tok // 4)}
    peers = [{"tab": (z + s) % 4} for s in range(1, 4)]
    return core, x, y, peers


def meet(devices):
    barrier = pltpu.get_barrier_semaphore()
    for d in devices:
        pl.semaphore_signal(barrier, inc=1, device_id=d, device_id_type=pl.DeviceIdType.MESH)
    pl.semaphore_wait(barrier, len(devices))


def sum_scratch(rows, cols):
    part = lambda *n: pltpu.VMEM((*n, rows, cols), BF)
    return [
        part(2, 4, 4), part(2, 4, 4), part(2, 4, 2), part(2, 4), part(2, 3),
        pltpu.SemaphoreType.DMA((2, 4)),
        pltpu.SemaphoreType.DMA((STAGES, 2, 4)),
        pltpu.SemaphoreType.DMA((STAGES, 2, 4)),
    ]


class Summing:
    def __init__(self, grads, out, scratch):
        self.grads, self.out = grads, out
        if grads is None:
            both, scratch = scratch[0], (scratch[0].at[0], *scratch[1:5], None, *scratch[5:])
            self.part = both.at[1]
        self.own, self.r0, self.r1, self.r2, self.r3, self.local, self.sent, self.got = scratch
        core, x, y, peers = neighbours()
        self.core, self.first, self.second, self.peers = core, (x, y), (y, x), peers
        self.z = lax.axis_index("tab")

    def devices(self):
        return [self.core, self.first[0], self.first[1], *self.peers]

    def copy(self, stage, ch, i):
        zc = (self.z + (i + 1)) % 4
        src, dst, to = (
            (
                lambda: self.part.at[ch, i] if self.grads is None else self.grads[ch].at[1, zc],
                self.r0.at[ch, i],
                self.core,
            ),
            (lambda: self.own.at[ch, i, pl.ds(2, 2)], self.r1.at[ch, i], self.first[ch]),
            (lambda: self.own.at[ch, i, 1], self.r2.at[ch, i], self.second[ch]),
            (lambda: self.own.at[ch, i, 0], self.r3.at[ch, min(i, 2)], self.peers[min(i, 2)]),
        )[stage]
        return pltpu.make_async_remote_copy(
            src_ref=src(), dst_ref=dst,
            send_sem=self.sent.at[stage, ch, i], recv_sem=self.got.at[stage, ch, i],
            device_id=to, device_id_type=pl.DeviceIdType.MESH,
        )

    def load(self, ch, i):
        zc = (self.z + (i + 1)) % 4
        return pltpu.make_async_copy(
            self.grads[ch].at[0, zc], self.own.at[ch, i], self.local.at[ch, i]
        )

    def start(self):
        for i in range(4):
            for ch in range(2):
                self.copy(0, ch, i).start()
                if self.grads is not None:
                    self.load(ch, i).start()

    def step(self, stage, i):
        for ch in range(2):
            self.copy(stage - 1, ch, i).wait_recv()
            if stage == 1:
                if self.grads is not None:
                    self.load(ch, i).wait()

                def add(j, _, ch=ch):
                    self.own[ch, i, j] = self.own[ch, i, j] + self.r0[ch, i, j]
                    return 0

                lax.fori_loop(0, 4, add, 0)
            elif stage == 2:

                def add(j, _, ch=ch):
                    self.own[ch, i, j] = self.own[ch, i, j] + self.r1[ch, i, j]
                    return 0

                lax.fori_loop(0, 2, add, 0)
            elif i < 3:
                self.own[ch, i, 0] = self.own[ch, i, 0] + self.r2[ch, i]
            if stage < 3 or i < 3:
                self.copy(stage, ch, i).start()

    def finish(self):
        for ch in range(2):
            total = self.own[ch, 3, 0].astype(F32) + self.r2[ch, 3].astype(F32)
            for i in range(3):
                self.copy(3, ch, i).wait_recv()
                total = total + self.r3[ch, i].astype(F32)
            self.out[ch] = total
        for stage in range(STAGES):
            for ch in range(2):
                for i in range(4 if stage < 3 else 3):
                    self.copy(stage, ch, i).wait_send()

    def run(self, step, plan):
        for at, events in plan.items():

            @pl.when(step == at)
            def _(events=events):
                for stage, i in events:
                    if stage == 0:
                        self.start()
                    elif stage == 4:
                        self.finish()
                    else:
                        self.step(stage, i)


def split_rel(r):
    return r & 1, (r >> 1) & 1, r >> 2


def rel_of(b):
    tok = lax.axis_index("tok")
    core, x, y = split_rel(b)
    flip = lambda static, mine: 1 - mine if static else mine
    return flip(core, tok % 2), flip(x, (tok // 2) % 2), flip(y, tok // 4)


def put_rows(g, ga, gb, cols, rows):
    half = rows // 2
    for b in range(8):
        core, x, y = rel_of(b)
        ga[core, 0, 2 * x + y, :, cols] = g[b * rows : b * rows + half]
        gb[core, 0, 2 * y + x, :, cols] = g[b * rows + half : (b + 1) * rows]


def sum_specs(grads, number):
    if grads is None:
        return [], [], [], [], {}
    rows, cols = grads[0].shape[3:]
    return (
        [pl.BlockSpec(memory_space=pl.ANY)] * 2,
        [full((2, rows, cols))],
        [jax.ShapeDtypeStruct((2, rows, cols), F32)],
        sum_scratch(rows, cols),
        {"has_side_effects": True, "collective_id": number},
    )


BLOCK = 128


def spread_kernel(
    idx, table, found, group_idx,
    held, numbers, ring_sent, ring_got, plane_sent, plane_got, idx_sent, idx_got,
):
    tok, z = lax.axis_index("tok"), lax.axis_index("tab")
    core, x, y, peers = neighbours()
    c, cx, cy = tok % 2, (tok // 2) % 2, tok // 4
    first, second = (x, y), (y, x)
    f, g = (cx, cy), (cy, cx)
    meet([core, x, y, *peers])
    half = table.shape[1] // 2
    count = idx.shape[2]

    def ring(k, ch):
        if k == 0:
            start = pl.multiple_of(tok * BLOCK, BLOCK)
            src = table.at[pl.ds(start, BLOCK), pl.ds(ch * half, half)]
        else:
            src = held.at[k - 1, ch, c, g[ch], f[ch]]
        return pltpu.make_async_remote_copy(
            src_ref=src, dst_ref=held.at[k, ch, c, g[ch], f[ch]],
            send_sem=ring_sent.at[k, ch], recv_sem=ring_got.at[k, ch],
            device_id=peers[0], device_id_type=pl.DeviceIdType.MESH,
        )

    def plane(stage, k, ch):
        src, to = (
            (held.at[k, ch, c, g[ch], f[ch]], first[ch]),
            (held.at[k, ch, c, g[ch]], second[ch]),
            (held.at[k, ch, c], core),
        )[stage]
        return pltpu.make_async_remote_copy(
            src_ref=src, dst_ref=src,
            send_sem=plane_sent.at[stage, k, ch], recv_sem=plane_got.at[stage, k, ch],
            device_id=to, device_id_type=pl.DeviceIdType.MESH,
        )

    def number(s):
        return pltpu.make_async_remote_copy(
            src_ref=idx.at[(z + s) % 4], dst_ref=numbers.at[s - 1],
            send_sem=idx_sent.at[s - 1], recv_sem=idx_got.at[s - 1],
            device_id=peers[s - 1], device_id_type=pl.DeviceIdType.MESH,
        )

    def picks(owner):
        out = []
        for b in range(8):
            row = lax.broadcasted_iota(jnp.int32, (BLOCK, count), 0) + b * BLOCK
            one = (row == idx[owner, 0:1, :]).astype(F32)
            two = (row == idx[owner, 1:2, :]).astype(F32)
            out.append((one + two).astype(BF))
        return out

    def arrive(k):
        for ch in range(2):
            ring(k, ch).wait_recv()
            if k < 2:
                ring(k + 1, ch).start()
            plane(0, k, ch).start()

    def go_on(stage, k):
        for ch in range(2):
            plane(stage - 1, k, ch).wait_recv()
            plane(stage, k, ch).start()

    def look_up(k):
        rows = picks((z + 3 - k) % 4)
        for ch in range(2):
            plane(2, k, ch).wait_recv()
            order = [
                4 * a + 2 * b + n if ch == 0 else 4 * b + 2 * a + n
                for n in range(2)
                for a in range(2)
                for b in range(2)
            ]
            pick = jnp.concatenate([rows[b] for b in order], axis=0)
            data = held[k, ch].reshape(8 * BLOCK, half)
            found[k + 1, :, ch * half : (ch + 1) * half] = dot(pick, data, TN).astype(BF)

    for ch in range(2):
        ring(0, ch).start()
    for s in range(1, 4):
        number(s).start()
    found[0] = dot(jnp.concatenate(picks(z), axis=0), table[...], TN).astype(BF)
    arrive(0)
    go_on(1, 0)
    arrive(1)
    go_on(1, 1)
    go_on(2, 0)
    arrive(2)
    go_on(1, 2)
    group_idx[0] = idx[z]
    for s in range(1, 4):
        number(s).wait_recv()
        group_idx[s] = numbers[s - 1]

    def finish(k, _):
        look_up(k)

        @pl.when(k < 2)
        def _():
            go_on(2, k + 1)

        return 0

    lax.fori_loop(0, 3, finish, 0)
    for s in range(1, 4):
        number(s).wait_send()
    for k in range(3):
        for ch in range(2):
            ring(k, ch).wait_send()
            for stage in range(3):
                plane(stage, k, ch).wait_send()


def spread(idx, table):
    n_tab, _, count = idx.shape
    rows, width = table.shape
    dma = pltpu.SemaphoreType.DMA
    return pl.pallas_call(
        spread_kernel,
        grid=(1,),
        in_specs=[full(idx.shape), full(table.shape)],
        out_specs=[full((n_tab, count, width)), full(idx.shape)],
        out_shape=[
            jax.ShapeDtypeStruct((n_tab, count, width), BF),
            jax.ShapeDtypeStruct(idx.shape, jnp.int32),
        ],
        scratch_shapes=[
            pltpu.VMEM((3, 2, 2, 2, 2, BLOCK, width // 2), BF),
            pltpu.VMEM((3, 2, count), jnp.int32),
            dma((3, 2)), dma((3, 2)), dma((3, 3, 2)), dma((3, 3, 2)), dma((3,)), dma((3,)),
        ],
        compiler_params=params(has_side_effects=True, collective_id=4),
        cost_estimate=cost(8 * count * width * rows, 8 << 20),
        name="spread",
    )(idx, table)


HP = 4


def head_masks(length, pair):
    lane = lax.broadcasted_iota(jnp.int32, (length, pair), 1)
    return lane < HEAD_DIM


def attn_fwd_kernel(q, k, v, mixed, lse):
    length = q.shape[0]
    pair = 2 * HEAD_DIM
    low_half = head_masks(length, pair)
    zero = jnp.zeros((length, pair), BF)
    for p in range(HP // 2):
        cols = slice(p * pair, (p + 1) * pair)
        qp, kp, vp = q[:, cols], k[:, cols], v[:, cols]
        vt = vp.T
        outs = []
        for h in range(2):
            km = jnp.where(low_half, kp, zero) if h == 0 else jnp.where(low_half, zero, kp)
            st = dot(km, qp, NT)
            top = jnp.max(st, axis=0, keepdims=True)
            raised = jnp.exp2((st - top) * LOG2E)
            total = jnp.sum(raised, axis=0, keepdims=True)
            lse[0, 0, 2 * p + h : 2 * p + h + 1, :] = top + jnp.log(total)
            ot = dot(vt[h * HEAD_DIM : (h + 1) * HEAD_DIM], raised.astype(BF), NN)
            outs.append(ot * (1.0 / total))
        mixed[:, cols] = jnp.concatenate(outs, axis=0).T.astype(BF)


def attn_fwd(q, k, v, pages):
    tokens, width = q.shape
    length = tokens // pages
    steps = HEADS // HP
    blk = pl.BlockSpec((length, HP * HEAD_DIM), lambda i, j: (i, j))
    return pl.pallas_call(
        attn_fwd_kernel,
        grid=(pages, steps),
        in_specs=[blk] * 3,
        out_specs=[blk, pl.BlockSpec((1, 1, HP, length), lambda i, j: (i, j, 0, 0))],
        out_shape=[
            jax.ShapeDtypeStruct((tokens, width), BF),
            jax.ShapeDtypeStruct((pages, steps, HP, length), F32),
        ],
        compiler_params=params(),
        cost_estimate=cost(14e9, 8 << 20, pages * HEADS * length * length),
        name="attention",
    )(q, k, v)


def attn_back(q, k, v, mixed, go, lse, put):
    length = q.shape[0]
    pair = 2 * HEAD_DIM
    low_half = head_masks(length, pair)
    zero = jnp.zeros((length, pair), BF)

    def pick(x, h):
        return jnp.where(low_half, x, zero) if h == 0 else jnp.where(low_half, zero, x)

    def pair_of_heads(p, _):
        cols = pl.ds(pl.multiple_of(p * pair, pair), pair)
        qp, kp, vp, op, gp = q[:, cols], k[:, cols], v[:, cols], mixed[:, cols], go[:, cols]
        kt = kp.T
        prod_t = (op.astype(F32) * gp.astype(F32)).T
        dq_t, dk, dv = [], None, None
        for h in range(2):
            st = dot(pick(kp, h), qp, NT)
            probs = jnp.exp2((st - lse[0, 0, pl.ds(2 * p + h, 1), :]) * LOG2E)
            dv_h = dot(probs.astype(BF), pick(gp, h), NN)
            dpt = dot(pick(vp, h), gp, NT)
            delta = colsum(prod_t[h * HEAD_DIM : (h + 1) * HEAD_DIM])
            ds = (probs * (dpt - delta)).astype(BF)
            dk_h = dot(ds, pick(qp, h), NN)
            dq_t.append(dot(kt[h * HEAD_DIM : (h + 1) * HEAD_DIM], ds, NN))
            dv = dv_h if dv is None else dv + dv_h
            dk = dk_h if dk is None else dk + dk_h
        dq = (jnp.concatenate(dq_t, axis=0).T.astype(BF).astype(F32) * SCALE).astype(BF)
        put(p * pair, pair, dq, dk.astype(BF), dv.astype(BF))
        return 0

    lax.fori_loop(0, HP // 2, pair_of_heads, 0)


FC = 512
FWD = 1024
RC = 128
MC = 512


def ffn_fwd_kernel(
    mixed, normed, wo, we, wr, hb, bias, gains, shifts, cot,
    out, after_out, low_out, rstd_out, act_out, slope_out, gs2_out, gffn_out, sums,
):
    ff = we.shape[1]
    attn_sum = normed[...] + (dot(mixed[...], wo[...], NN) + bias[2:3])
    xh, rstd = norm_stats(attn_sum)
    after = xh * gains[1:2] + shifts[1:2]
    after_out[...] = after
    rstd_out[...] = rstd
    low = after.astype(BF)
    low_out[...] = low
    total = after + bias[3:4]
    count = ff // FWD
    hidden = []
    for j in range(count + 1):
        if j < count:
            cols = slice(j * FWD, (j + 1) * FWD)
            hidden.append(dot(low, we[:, cols], NN) + hb[:, cols])
        if j > 0:
            cols = slice((j - 1) * FWD, j * FWD)
            act, slope = gelu_parts(hidden[j - 1])
            act = act.astype(BF)
            act_out[:, cols] = act
            slope_out[:, cols] = slope.astype(BF)
            total = total + dot(act, wr[cols, :], NN)
    xh, rstd = norm_stats(total)
    out[...] = (xh * gains[2:3] + shifts[2:3]).astype(BF)
    y = cot[...].astype(F32)
    gs2 = norm_back(y, xh, rstd, gains[2:3])
    gs2_out[...] = gs2
    gffn = gs2.astype(BF)
    gffn_out[...] = gffn
    part = jnp.concatenate([colsum(y * xh), colsum(y), colsum(gffn.astype(F32))], axis=0)

    @pl.when(pl.program_id(0) == 0)
    def _():
        sums[...] = part

    @pl.when(pl.program_id(0) != 0)
    def _():
        sums[...] = sums[...] + part


def ffn_fwd(mixed, normed, wo, we, wr, hb, bias, gains, shifts, cot, tile):
    tokens, width = mixed.shape
    ff = we.shape[1]
    rows = pl.BlockSpec((tile, width), lambda i: (i, 0))
    long = pl.BlockSpec((tile, ff), lambda i: (i, 0))
    shape = lambda dt, n=width: jax.ShapeDtypeStruct((tokens, n), dt)
    hb = hb.reshape(1, ff)
    return pl.pallas_call(
        ffn_fwd_kernel,
        grid=(tokens // tile,),
        in_specs=[rows, rows]
        + [full(a.shape) for a in (wo, we, wr, hb, bias, gains, shifts)]
        + [rows],
        out_specs=[rows, rows, rows, pl.BlockSpec((tile, 1), lambda i: (i, 0)), long, long, rows, rows]
        + [pl.BlockSpec((3, width), lambda i: (0, 0))],
        out_shape=[
            shape(BF), shape(F32), shape(BF), shape(F32, 1), shape(BF, ff), shape(BF, ff),
            shape(F32), shape(BF), jax.ShapeDtypeStruct((3, width), F32),
        ],
        compiler_params=params(),
        cost_estimate=cost(2 * tokens * width * (width + 2 * ff), 60 << 20, tokens * ff * 2),
        name="ffn_forward",
    )(mixed, normed, wo, we, wr, hb, bias, gains, shifts, cot)


def second_norm_back(gs1_out, after, rstd, gains, shifts, gattn_out, sums):
    tokens, width = after.shape

    def norm(i, carry):
        rows = pl.ds(pl.multiple_of(i * RC, RC), RC)
        total = gs1_out[rows, :]
        xh = (after[rows, :] - shifts[1:2]) * (1.0 / gains[1:2])
        gs1 = norm_back(total, xh, rstd[rows, :], gains[1:2])
        gs1_out[rows, :] = gs1
        gattn = gs1.astype(BF)
        gattn_out[rows, :] = gattn
        g, s, b = carry
        return g + colsum(total * xh), s + colsum(total), b + colsum(gattn.astype(F32))

    zero = jnp.zeros((1, width), F32)
    sums[...] = jnp.concatenate(lax.fori_loop(0, tokens // RC, norm, (zero, zero, zero)), axis=0)


def ffn_bwd_kernel(
    gffn, gs2, after, rstd, wo, gains, shifts, slope, wr, we,
    gh_out, gs1_out, gattn_out, gmixed_out, hsum, sums,
):
    step, last = pl.program_id(0), pl.num_programs(0) - 1
    tokens, width = gffn.shape

    @pl.when(step == 0)
    def _():
        gs1_out[...] = gs2[...]

    part = jnp.zeros((1, slope.shape[1]), F32)
    for m in range(0, tokens, MC):
        rows = slice(m, m + MC)
        gh = (dot(gffn[rows, :], wr[...], NT) * slope[rows, :].astype(F32)).astype(BF)
        gh_out[rows, :] = gh
        part = part + colsum(gh.astype(F32))
        gs1_out[rows, :] = gs1_out[rows, :] + dot(gh, we[...], NT)
    hsum[...] = part

    @pl.when(step == last)
    def _():
        second_norm_back(gs1_out, after, rstd, gains, shifts, gattn_out, sums)
        for m in range(0, tokens, MC):
            rows = slice(m, m + MC)
            gmixed_out[rows, :] = dot(gattn_out[rows, :], wo[...], NT).astype(BF)


def ffn_bwd(gffn, slope, gs2, after, rstd, wr, we, wo, gains, shifts):
    tokens, width = gffn.shape
    ff = we.shape[1]
    whole = full((tokens, width))
    long = pl.BlockSpec((tokens, FC), lambda s: (0, s))
    shape = lambda dt, n=width: jax.ShapeDtypeStruct((tokens, n), dt)
    return pl.pallas_call(
        ffn_bwd_kernel,
        grid=(ff // FC,),
        in_specs=[whole, whole, whole, full((tokens, 1))]
        + [full(a.shape) for a in (wo, gains, shifts)]
        + [
            long,
            pl.BlockSpec((FC, width), lambda s: (s, 0)),
            pl.BlockSpec((width, FC), lambda s: (0, s)),
        ],
        out_specs=[long, whole, whole, whole]
        + [pl.BlockSpec((1, FC), lambda s: (0, s)), full((3, width))],
        out_shape=[
            shape(BF, ff), shape(F32), shape(BF), shape(BF),
            jax.ShapeDtypeStruct((1, ff), F32), jax.ShapeDtypeStruct((3, width), F32),
        ],
        compiler_params=params(),
        cost_estimate=cost(2 * tokens * width * (width + 2 * ff), 60 << 20),
        name="ffn_backward",
    )(gffn, gs2, after, rstd, wo, gains, shifts, slope, wr, we)


FFN_PLAN = {
    4: [(0, 0)],
    8: [(1, 0)],
    9: [(1, 1)],
    11: [(2, 0), (1, 2)],
    13: [(2, 1), (1, 3)],
    15: [(3, 0)],
    16: [(2, 2)],
    17: [(3, 1), (2, 3)],
    18: [(3, 2)],
    19: [(3, 3)],
}
N_TOK, N_TAB = 8, 4


def block_of_step(s):
    s = jnp.minimum(s, N_TOK - 1)
    return 1 - s // 4, 1 - (s // 2) % 2, 1 - s % 2


def ffn_grads_kernel(
    gffn_in, gs2_in, after_in, rstd, low_in, mixed_in, wo_in, gains, shifts, act, slope, wr, we,
    gs1_out, gmixed_out, hsum, sums, ga, gb, reduce_out,
    gffn, gh, after, low, mixed, wo, local, *scratch,
):
    step, last = pl.program_id(0), pl.num_programs(0) - 1
    tokens, width = after.shape
    summing = Summing(None, reduce_out, scratch)
    both = scratch[0]
    z = lax.axis_index("tab")
    first = pltpu.make_async_copy(gffn_in, gffn, local.at[0])
    later = [
        pltpu.make_async_copy(src, dst, local.at[1 + n])
        for n, (src, dst) in enumerate(
            ((gs2_in, gs1_out), (after_in, after), (wo_in, wo), (low_in, low), (mixed_in, mixed))
        )
    ]

    @pl.when(step == 0)
    def _():
        first.start()
        for copy in later:
            copy.start()
        meet(summing.devices())
        first.wait()

    @pl.when(step == N_TOK)
    def _():
        for copy in later:
            copy.wait()

    summing.run(step, FFN_PLAN)

    @pl.when(step < N_TOK)
    def _():
        core, x, y = block_of_step(step)
        g = dot(gffn[...], act[...], TN).astype(BF)
        rows, half = both.shape[4:]
        for zc in range(N_TAB):
            i = (zc + N_TAB - 1 - z) % N_TAB
            for ch in range(2):
                piece = g[zc * rows : (zc + 1) * rows, ch * half : (ch + 1) * half]
                both[core, ch, i, (2 * x + y, 2 * y + x)[ch]] = piece

    @pl.when((step >= N_TOK) & (step < 2 * N_TOK))
    def _():
        part = jnp.zeros((1, slope.shape[1]), F32)
        for m in range(0, tokens, MC):
            rows = slice(m, m + MC)
            g = (dot(gffn[rows, :], wr[...], NT) * slope[rows, :].astype(F32)).astype(BF)
            gh[step - N_TOK, rows, :] = g
            part = part + colsum(g.astype(F32))
            gs1_out[rows, :] = gs1_out[rows, :] + dot(g, we[...], NT)
        hsum[...] = part

    @pl.when(step == 2 * N_TOK - 1)
    def _():
        second_norm_back(gs1_out, after, rstd, gains, shifts, gffn, sums)

        def block(m, _):
            rows = pl.ds(pl.multiple_of(m * MC, MC), MC)
            gmixed_out[rows, :] = dot(gffn[rows, :], wo[...], NT).astype(BF)
            return 0

        lax.fori_loop(0, tokens // MC, block, 0)

    @pl.when(step >= 2 * N_TOK)
    def _():
        n = step - 2 * N_TOK
        quarter = width // N_TAB
        rows = width // N_TOK
        wide = gh.shape[2]

        def block(m, _):
            g = dot(low[...], gh[2 * n + m], TN).astype(BF)
            put_rows(g, ga, gb, pl.ds(pl.multiple_of(m * wide, wide), wide), rows)
            return 0

        lax.fori_loop(0, 2, block, 0)
        piece = gffn[:, pl.ds(pl.multiple_of(n * quarter, quarter), quarter)]
        g = dot(mixed[...], piece, TN).astype(BF)
        put_rows(g, ga, gb, slice(2 * wide, 2 * wide + quarter), rows)

    @pl.when(step == last)
    def _():
        summing.finish()


def ffn_grads(gffn, act, slope, gs2, after, low, rstd, mixed, wr, we, wo, gains, shifts):
    tokens, width = gffn.shape
    ff = we.shape[1]
    whole = full((tokens, width))
    anywhere = pl.BlockSpec(memory_space=pl.ANY)
    wide = ff // N_TOK
    half = width // (2 * N_TOK)
    out_wide = (ff + width) // N_TAB
    back = lambda s: jnp.clip(s - N_TOK, 0, N_TOK - 1)
    grad = lambda s: jnp.clip(s - 2 * N_TOK, 0, N_TAB - 1)

    def act_block(s):
        core, x, y = block_of_step(s)
        tok = lax.axis_index("tok")
        flip = lambda rel, mine: rel + mine - 2 * rel * mine
        return 0, 4 * flip(y, tok // 4) + 2 * flip(x, (tok // 2) % 2) + flip(core, tok % 2)

    rows, cols = width // N_TAB, wide // 2
    part = lambda *n: pltpu.VMEM((*n, rows, cols), BF)
    dma = pltpu.SemaphoreType.DMA
    shape = lambda dt: jax.ShapeDtypeStruct((tokens, width), dt)
    piece = pl.BlockSpec((2, 1, 4, half, out_wide), lambda s: (0, grad(s), 0, 0, 0))
    return pl.pallas_call(
        ffn_grads_kernel,
        grid=(2 * N_TOK + N_TAB,),
        in_specs=[anywhere, anywhere, anywhere, full((tokens, 1)), anywhere, anywhere, anywhere]
        + [full(a.shape) for a in (gains, shifts)]
        + [
            pl.BlockSpec((tokens, wide), act_block),
            pl.BlockSpec((tokens, wide), lambda s: (0, back(s))),
            pl.BlockSpec((wide, width), lambda s: (back(s), 0)),
            pl.BlockSpec((width, wide), lambda s: (0, back(s))),
        ],
        out_specs=[
            whole, whole, pl.BlockSpec((1, wide), lambda s: (0, back(s))), full((3, width)),
            piece, piece, full((2, rows, cols)),
        ],
        out_shape=[
            shape(F32), shape(BF),
            jax.ShapeDtypeStruct((1, ff), F32), jax.ShapeDtypeStruct((3, width), F32),
            jax.ShapeDtypeStruct((2, 4, 4, half, out_wide), BF),
            jax.ShapeDtypeStruct((2, 4, 4, half, out_wide), BF),
            jax.ShapeDtypeStruct((2, rows, cols), F32),
        ],
        scratch_shapes=[
            pltpu.VMEM((tokens, width), BF), pltpu.VMEM((N_TOK, tokens, wide), BF),
            pltpu.VMEM((tokens, width), F32), pltpu.VMEM((tokens, width), BF),
            pltpu.VMEM((tokens, width), BF), pltpu.VMEM(wo.shape, BF), dma((6,)),
            part(2, 2, 4, 4), part(2, 4, 4), part(2, 4, 2), part(2, 4), part(2, 3),
            dma((STAGES, 2, 4)), dma((STAGES, 2, 4)),
        ],
        compiler_params=pltpu.CompilerParams(
            vmem_limit_bytes=67043328, has_side_effects=True, collective_id=1
        ),
        cost_estimate=cost(2 * tokens * width * (2 * width + 4 * ff), 60 << 20),
        name="ffn_backward_grads",
    )(gffn, gs2, after, rstd, low, mixed, wo, gains, shifts, act, slope, wr, we)


BACK_PLAN = {
    0: [(0, 0)],
    1: [(1, 0)],
    2: [(1, 1)],
    3: [(2, 0), (1, 2)],
    5: [(2, 1), (1, 3)],
    6: [(3, 0)],
    8: [(2, 2)],
    9: [(3, 1)],
    11: [(2, 3)],
    12: [(3, 2)],
    13: [(3, 3)],
}


def back_kernel(*refs, pages, summed):
    q, k, v, mixed, go, lse, low_in, gs1, w_in, normed, rstd, ci, gains, shifts = refs[:14]
    refs = refs[14:]
    grads, refs = refs[: 2 * summed], refs[2 * summed :]
    out, cells, sums0, sums_qv = refs[:4]
    refs = refs[4:]
    if summed:
        ga, gb, summed_out, gj, low, w, local = refs[:7]
        summing = Summing(grads, summed_out, refs[7:])
    else:
        gj_out, gj, low, w, local = refs
    step = pl.program_id(0)
    width = gs1.shape[1]
    length = q.shape[0]
    groups = HEADS // HP
    wide = HP * HEAD_DIM
    n_attn = groups * pages
    n_joined = 4 if summed else 0
    loads = [
        pltpu.make_async_copy(low_in, low, local.at[0]),
        pltpu.make_async_copy(w_in, w, local.at[1]),
    ]

    @pl.when(step == 0)
    def _():
        for copy in loads:
            copy.start()

    @pl.when(step == n_attn)
    def _():
        for copy in loads:
            copy.wait()

    if summed:

        @pl.when(step == 0)
        def _():
            meet(summing.devices())

        summing.run(step, BACK_PLAN)

    @pl.when(step < n_attn)
    def _():
        group, page = step // pages, step % pages
        rows = pl.ds(pl.multiple_of(page * length, length), length)

        def put(at, size, dq, dk, dv):
            cols = pl.ds(pl.multiple_of(group * wide + at, size), size)
            gj[0, rows, cols] = dq
            gj[1, rows, cols] = dk
            gj[2, rows, cols] = dv
            part = jnp.concatenate([colsum(dq.astype(F32)), colsum(dv.astype(F32))], axis=0)

            @pl.when(page == 0)
            def _():
                sums_qv[:, cols] = part

            @pl.when(page != 0)
            def _():
                sums_qv[:, cols] = sums_qv[:, cols] + part

        attn_back(q, k, v, mixed, go, lse, put)

    if summed:
        quarter = width // 4

        @pl.when((step >= n_attn) & (step < n_attn + n_joined))
        def _():
            def block(m, _):
                unit = 3 * (step - n_attn) + m
                cols = pl.ds(pl.multiple_of((unit % 4) * quarter, quarter), quarter)
                g = dot(low[...], gj[unit // 4, :, cols], TN).astype(BF)
                at = pl.ds(pl.multiple_of(m * quarter, quarter), quarter)
                put_rows(g, ga, gb, at, width // 8)
                return 0

            lax.fori_loop(0, 3, block, 0)

    @pl.when(step >= n_attn + n_joined)
    def _():
        page = step - (n_attn + n_joined)
        rows = pl.ds(pl.multiple_of(page * length, length), length)
        total = gs1[...]
        for n in range(3):
            total = total + dot(gj[n, rows, :], w[:, n * width : (n + 1) * width], NT)
        xh = (normed[...] - shifts[0:1]) * (1.0 / gains[0:1])
        grad = norm_back(total, xh, rstd[...], gains[0:1])
        out[...] = grad
        number = lax.broadcasted_iota(jnp.int32, (CELLS, length), 0)
        pick = (number == ci[0]).astype(F32).astype(BF)
        cells[...] = dot(pick, grad.astype(BF), NN).astype(BF)
        part = jnp.concatenate([colsum(total * xh), colsum(total)], axis=0)

        @pl.when(page == 0)
        def _():
            sums0[...] = part

        @pl.when(page != 0)
        def _():
            sums0[...] = sums0[...] + part

    if summed:

        @pl.when(step == pl.num_programs(0) - 1)
        def _():
            summing.finish()
    else:
        gj_out[...] = gj[...]


def back(q, k, v, mixed, go, lse, low, gs1, w, normed, rstd, ci, gains, shifts, grads):
    tokens, width = q.shape
    pages, length = ci.shape
    groups = HEADS // HP
    wide = HP * HEAD_DIM
    summed = grads is not None
    n_attn = groups * pages
    before = n_attn + (4 if summed else 0)
    at = lambda s: jnp.minimum(s, n_attn - 1)
    page = lambda s: jnp.maximum(s - before, 0)
    block = lambda s: jnp.clip(s - n_attn, 0, 3)
    blk = pl.BlockSpec((length, wide), lambda s: (at(s) % pages, at(s) // pages))
    rows = pl.BlockSpec((length, width), lambda s: (page(s), 0))
    out_specs = [
        rows,
        pl.BlockSpec((CELLS, width), lambda s: (page(s), 0)),
        full((2, width)),
        full((2, width)),
    ]
    out_shape = [
        jax.ShapeDtypeStruct((tokens, width), F32),
        jax.ShapeDtypeStruct((pages * CELLS, width), BF),
        jax.ShapeDtypeStruct((2, width), F32),
        jax.ShapeDtypeStruct((2, width), F32),
    ]
    whole_gj = (3, tokens, width)
    more_in, more_out, more_shape, more_scratch, more = sum_specs(grads, 2)
    if summed:
        half = width // 16
        piece = pl.BlockSpec((2, 1, 4, half, 3 * width // 4), lambda s: (0, block(s), 0, 0, 0))
        out_specs += [piece, piece]
        out_shape += [jax.ShapeDtypeStruct((2, 4, 4, half, 3 * width // 4), BF)] * 2
    else:
        out_specs += [full(whole_gj)]
        out_shape += [jax.ShapeDtypeStruct(whole_gj, BF)]
    return pl.pallas_call(
        functools.partial(back_kernel, pages=pages, summed=summed),
        grid=(before + pages,),
        in_specs=[blk] * 5
        + [
            pl.BlockSpec((1, 1, HP, length), lambda s: (at(s) % pages, at(s) // pages, 0, 0)),
            pl.BlockSpec(memory_space=pl.ANY),
            rows,
            pl.BlockSpec(memory_space=pl.ANY),
            rows,
            pl.BlockSpec((length, 1), lambda s: (page(s), 0)),
            pl.BlockSpec((1, 1, length), lambda s: (page(s), 0, 0)),
            full(gains.shape),
            full(shifts.shape),
        ]
        + more_in,
        out_specs=out_specs + more_out,
        out_shape=out_shape + more_shape,
        scratch_shapes=[
            pltpu.VMEM(whole_gj, BF), pltpu.VMEM(low.shape, BF), pltpu.VMEM(w.shape, BF),
            pltpu.SemaphoreType.DMA((2,)),
        ]
        + more_scratch,
        compiler_params=params(**more),
        cost_estimate=cost(70e9, 40 << 20, pages * HEADS * length * length),
        name="attention_joined_embed_back",
    )(
        q, k, v, mixed, go, lse, low, gs1, w, normed, rstd, ci.reshape(pages, 1, length),
        gains, shifts, *(grads or ()),
    )


def table_kernel(tok, idx, g0, g1, g2, g3, out_a, out_b):
    rows = out_a.shape[1]
    count = idx.shape[2]
    half = out_a.shape[2]
    base = (pl.program_id(0) ^ tok[0]) * rows
    number = lax.broadcasted_iota(jnp.int32, (rows, count), 0) + base
    picks = []
    for s in range(4):
        first = (number == idx[s, 0:1, :]).astype(F32)
        second = (number == idx[s, 1:2, :]).astype(F32)
        picks.append((first + second).astype(BF))
    pick = jnp.concatenate(picks, axis=1)
    grads = jnp.concatenate([g0[...], g1[...], g2[...], g3[...]], axis=0)
    total = dot(pick, grads, NN).astype(BF)
    out_a[0] = total[:, :half]
    out_b[0] = total[:, half:]


def table_part(tok, idx, grads, blocks):
    groups, _, count = idx.shape
    width = grads[0].shape[1]
    rows = 1024 // blocks
    half = width // 2
    out = pl.BlockSpec((1, rows, half), lambda i, t: (i, 0, 0))
    return pl.pallas_call(
        table_kernel,
        grid_spec=pltpu.PrefetchScalarGridSpec(
            num_scalar_prefetch=1,
            grid=(blocks,),
            in_specs=[full(idx.shape)] + [full((count, width))] * groups,
            out_specs=[out, out],
        ),
        out_shape=[jax.ShapeDtypeStruct((blocks, rows, half), BF)] * 2,
        compiler_params=params(),
        cost_estimate=cost(2 * 1024 * groups * count * width, 4 << 20),
        name="table_grad",
    )(tok, idx, *grads)


class TableSum:
    def __init__(self, scratch, done):
        self.part, self.r0, self.r1, self.r2, self.sent, self.got = scratch
        self.done = done
        tok = lax.axis_index("tok")
        core, x, y, _ = neighbours()
        self.c, cx, cy = tok % 2, (tok // 2) % 2, tok // 4
        self.core, self.first, self.second = core, (x, y), (y, x)
        self.f, self.g = (cx, cy), (cy, cx)

    def copy(self, stage, ch, u):
        c, f, g = self.c, self.f[ch], self.g[ch]
        part, done = self.part.at[ch, u], self.done.at[ch, u]
        src, dst, to = (
            (lambda: part.at[1 - c], self.r0.at[ch, u], self.core),
            (lambda: part.at[c, 1 - f], self.r1.at[ch, u], self.first[ch]),
            (lambda: part.at[c, f, 1 - g], self.r2.at[ch, u], self.second[ch]),
            (lambda: done.at[c, f, g], None, self.second[ch]),
            (lambda: done.at[c, f], None, self.first[ch]),
            (lambda: done.at[c], None, self.core),
        )[stage]
        src = src()
        return pltpu.make_async_remote_copy(
            src_ref=src, dst_ref=src if dst is None else dst,
            send_sem=self.sent.at[stage, ch, u], recv_sem=self.got.at[stage, ch, u],
            device_id=to, device_id_type=pl.DeviceIdType.MESH,
        )

    def store(self, u, ch, value):
        for b in range(8):
            c, x, y = split_rel(b)
            f, g = (x, y) if ch == 0 else (y, x)
            self.part[ch, u, c, f, g] = value[b * BLOCK : (b + 1) * BLOCK]
        self.copy(0, ch, u).start()

    def step(self, stage, u):
        for ch in range(2):
            c, f, g = self.c, self.f[ch], self.g[ch]
            self.copy(stage - 1, ch, u).wait_recv()
            if stage == 1:
                self.part[ch, u, c] = self.part[ch, u, c] + self.r0[ch, u]
            elif stage == 2:
                self.part[ch, u, c, f] = self.part[ch, u, c, f] + self.r1[ch, u]
            elif stage == 3:
                self.done[ch, u, c, f, g] = self.part[ch, u, c, f, g] + self.r2[ch, u]
            if stage < 6:
                self.copy(stage, ch, u).start()

    def finish(self):
        for stage in range(6):
            for ch in range(2):
                for u in range(2):
                    self.copy(stage, ch, u).wait_send()


def closing_kernel(
    cells, idx, sums0, sums1, sums2, sums_qv, hidden_sum, ga, gb, done, joined, small_out,
    ring, total, ring_sent, ring_got, held, arrived, small_sent, small_got, *scratch,
):
    summing = Summing((ga, gb), joined, scratch[:8])
    table = TableSum(scratch[8:], done)
    core, x, y, peers = neighbours()
    z = lax.axis_index("tab")
    hops = [core, x, y, {"tab": z + 1 - 2 * (z % 2)}, {"tab": z + 2 - 4 * (z // 2)}]
    meet([core, x, y, *peers])
    count = cells.shape[0]
    half = cells.shape[1] // 2

    def pass_on(k, h):
        cols = pl.ds(h * half, half)
        src = cells.at[:, cols] if k == 0 else ring.at[k - 1, :, cols]
        return pltpu.make_async_remote_copy(
            src_ref=src, dst_ref=ring.at[k, :, cols],
            send_sem=ring_sent.at[k, h], recv_sem=ring_got.at[k, h],
            device_id=peers[0], device_id_type=pl.DeviceIdType.MESH,
        )

    def small_copy(n):
        return pltpu.make_async_remote_copy(
            src_ref=held.at[n], dst_ref=arrived.at[n],
            send_sem=small_sent.at[n], recv_sem=small_got.at[n],
            device_id=hops[n], device_id_type=pl.DeviceIdType.MESH,
        )

    def small_step(n):
        small_copy(n - 1).wait_recv()
        value = held[n - 1] + arrived[n - 1]
        if n < 5:
            held[n] = value
            small_copy(n).start()
        else:
            small_out[...] = value

    def relay(k, h):
        pass_on(k - 1, h).wait_recv()
        pass_on(k, h).start()

    def pick(s):
        number = lax.broadcasted_iota(jnp.int32, (total.shape[0], count), 0)
        first = (number == idx[s, 0:1, :]).astype(F32)
        second = (number == idx[s, 1:2, :]).astype(F32)
        return (first + second).astype(BF)

    def last_arrival(u):
        pass_on(2, u).wait_recv()
        for ch in range(2):
            cols = slice((2 * u + ch) * half // 2, (2 * u + ch + 1) * half // 2)
            value = total[:, cols] + dot(last, ring[2, :, cols], NN)
            table.store(u, ch, value.astype(BF))

    pass_on(0, 0).start()
    pass_on(0, 1).start()
    at, width = 0, cells.shape[1]
    for part in (sums0, sums1, sums2, sums_qv):
        held[0, at : at + part.shape[0]] = part[...]
        at += part.shape[0]
    for n in range(hidden_sum.shape[1] // width):
        held[0, at + n : at + n + 1] = hidden_sum[:, n * width : (n + 1) * width]
    small_copy(0).start()
    summing.start()
    total[...] = dot(pick(0), cells[...], NN)
    small_step(1)
    summing.step(1, 0)
    small_step(2)
    summing.step(1, 1)
    relay(1, 0)
    summing.step(2, 0)
    summing.step(1, 2)
    small_step(3)
    relay(1, 1)
    summing.step(2, 1)
    summing.step(1, 3)
    relay(2, 0)
    small_step(4)
    summing.step(2, 2)
    relay(2, 1)
    summing.step(3, 0)
    summing.step(3, 1)
    summing.step(2, 3)

    def add(k, _):
        total[...] = total[...] + dot(pick(k + 1), ring[k], NN)
        return 0

    lax.fori_loop(0, 2, add, 0)
    last = pick(3)
    last_arrival(0)
    table.step(1, 0)
    last_arrival(1)
    summing.step(3, 2)
    small_step(5)
    table.step(2, 0)
    table.step(1, 1)
    table.step(3, 0)
    table.step(2, 1)
    table.step(4, 0)
    table.step(3, 1)
    table.step(5, 0)
    table.step(4, 1)
    table.step(6, 0)
    table.step(5, 1)
    summing.step(3, 3)
    summing.finish()
    table.step(6, 1)
    table.finish()
    for k in range(3):
        for h in range(2):
            pass_on(k, h).wait_send()
    for n in range(5):
        small_copy(n).wait_send()


def closing(cells, idx, sums, grads):
    count, width = cells.shape
    small = (sum(part.size for part in sums) // width, width)
    rows, cols = grads[0].shape[3:]
    wide = width // 4
    part = lambda *n: pltpu.VMEM((2, 2, *n, BLOCK, wide), BF)
    done = (2, 2, 2, 2, 2, BLOCK, wide)
    dma = pltpu.SemaphoreType.DMA
    return pl.pallas_call(
        closing_kernel,
        grid=(1,),
        in_specs=[full(cells.shape), full(idx.shape)]
        + [full(part.shape) for part in sums]
        + [pl.BlockSpec(memory_space=pl.ANY)] * 2,
        out_specs=[full(done), full((2, rows, cols)), full(small)],
        out_shape=[
            jax.ShapeDtypeStruct(done, BF),
            jax.ShapeDtypeStruct((2, rows, cols), F32),
            jax.ShapeDtypeStruct(small, F32),
        ],
        scratch_shapes=[
            pltpu.VMEM((3, count, width), BF), pltpu.VMEM((8 * BLOCK, width), F32),
            dma((3, 2)), dma((3, 2)),
            pltpu.VMEM((5, *small), F32), pltpu.VMEM((5, *small), F32), dma((5,)), dma((5,)),
        ]
        + sum_scratch(rows, cols)
        + [part(2, 2, 2), part(2, 2), part(2), part(), dma((6, 2, 2)), dma((6, 2, 2))],
        compiler_params=params(has_side_effects=True, collective_id=3),
        cost_estimate=cost(8 * count * width * 1024, 24 << 20),
        name="closing",
    )(cells, idx, *sums, *grads)


def write_kernel(
    a, b, embed, reduce_sum, expand_sum, joined_sum, small,
    table, embed_out, reduce_out, expand_out, output_out, joined_out,
    gains, shifts, biases, hidden_bias,
):
    wide = a.shape[6]
    lanes = table.shape[1]
    for n, piece in enumerate((a, b)):
        for u in range(2):
            for c in range(2):
                value = piece[0, u, c, 0, 0].astype(F32)
                for k in range(wide // lanes):
                    row = c * BLOCK * (4 * wide // lanes) + ((2 * u + n) * wide) // lanes + k
                    table[pl.ds(row, BLOCK, stride=4 * wide // lanes), :] = value[
                        :, k * lanes : (k + 1) * lanes
                    ]
    embed_out[...] = embed[...]

    @pl.when(pl.program_id(0) == 0)
    def _():
        cols = reduce_sum.shape[2]
        rows = expand_sum.shape[1]
        wide = expand_out.shape[1]
        for n in range(2):
            reduce_out[n * cols : (n + 1) * cols, :] = reduce_sum[n].T
            expand_out[n * rows : (n + 1) * rows, :] = expand_sum[n, :, :wide]
            output_out[n * rows : (n + 1) * rows, :] = expand_sum[n, :, wide:]
            joined_out[n * rows : (n + 1) * rows, :] = joined_sum[n]
        for out, order in ((gains, (0, 2, 5)), (shifts, (1, 3, 6)), (biases, (8, 9, 4, 7))):
            for n, row in enumerate(order):
                out[n : n + 1, :] = small[row : row + 1, :]
        for n in range(hidden_bias.shape[0]):
            hidden_bias[n : n + 1, :] = small[10 + n : 11 + n, :]


def write(done, embed, reduce_sum, expand_sum, joined_sum, small, table_rows, ff):
    wide = done.shape[6]
    width = 4 * wide
    tokens = embed.shape[0]
    block = (1, 2, 2, 1, 1, BLOCK, wide)
    first = lambda i: (0, 0, 0, i % 2, i // 2, 0, 0)
    second = lambda i: (1, 0, 0, i // 2, i % 2, 0, 0)
    rows = 2 * expand_sum.shape[1]
    cols = ff // N_TAB
    f32 = lambda *n: jax.ShapeDtypeStruct(n, F32)
    shapes = [
        f32(2 * reduce_sum.shape[2], reduce_sum.shape[1]), f32(rows, cols),
        f32(rows, expand_sum.shape[2] - cols), f32(rows, joined_sum.shape[2]),
        f32(3, width), f32(3, width), f32(4, width), f32(ff // width, width),
    ]
    lanes = 128
    part = pl.BlockSpec((tokens // 4, width), lambda i: (i, 0))
    table, *rest = pl.pallas_call(
        write_kernel,
        grid=(4,),
        in_specs=[pl.BlockSpec(block, first), pl.BlockSpec(block, second), part]
        + [full(v.shape) for v in (reduce_sum, expand_sum, joined_sum, small)],
        out_specs=[pl.BlockSpec((2 * BLOCK * width // lanes, lanes), lambda i: (i, 0)), part]
        + [full(v.shape) for v in shapes],
        out_shape=[f32(table_rows * width // lanes, lanes), f32(tokens, width)] + shapes,
        compiler_params=params(),
        cost_estimate=cost(0, 16 << 20),
        name="write",
    )(done, done, embed, reduce_sum, expand_sum, joined_sum, small)
    return table.reshape(1, table_rows, width), *rest


def flip_tok(value, bit, size):
    return lax.ppermute(value, "tok", [(i, i ^ bit) for i in range(size)])


def shift_tab(value, shift, size):
    return lax.ppermute(value, "tab", [(i, (i + shift) % size) for i in range(size)])


def small_sum(value, n_tok, n_tab):
    bit = 1
    while bit < n_tok:
        value = value + flip_tok(value, bit, n_tok)
        bit *= 2
    total = value
    for shift in range(1, n_tab):
        total = total + shift_tab(value, shift, n_tab)
    return total


def body(
    n_tok, n_tab,
    embedded, cell_index, cell_boxes, box_tables, joined_weight, output_weight,
    expand_weight, reduce_weight, hidden_bias, bias_rows, norm_gains, norm_shifts, cotangent,
):
    tokens, width = embedded.shape
    pages, length = cell_index.shape
    table_rows = box_tables.shape[1]
    ff = expand_weight.shape[1]
    tok = lax.axis_index("tok").astype(jnp.int32).reshape(1)
    z = lax.axis_index("tab")
    cubic = n_tok == 8 and n_tab == 4

    corners = cell_boxes[:, :, :CELLS]
    lo = lambda n: jnp.minimum(corners[:, n], corners[:, n + 2]).reshape(-1)
    hi = lambda n: jnp.maximum(corners[:, n], corners[:, n + 2]).reshape(-1)
    left, right, top, bottom = lo(0), hi(0), lo(1), hi(1)
    none = jnp.full_like(left, -1)
    index_table = jnp.stack(
        [
            jnp.stack([left, right]),
            jnp.stack([top, bottom]),
            jnp.stack([right - left, none]),
            jnp.stack([bottom - top, none]),
        ]
    )
    padded = jnp.pad(box_tables[0], ((0, 1024 - table_rows), (0, 0)))
    if cubic:
        terms, group_index = spread(index_table, padded)
    else:
        pick_table = lambda i: lax.dynamic_index_in_dim(index_table, i, 0, keepdims=False)
        group_index = jnp.stack(
            [pick_table(z)]
            + [shift_tab(pick_table((z + s) % n_tab), s, n_tab) for s in range(1, n_tab)]
        )
        found = lookup(group_index, padded)
        terms = jnp.stack(
            [found[0]] + [shift_tab(found[s], n_tab - s, n_tab) for s in range(1, n_tab)]
        )

    q, k, v, normed, normed_low, rstd0 = embed(
        embedded, cell_index, terms, joined_weight, norm_gains, norm_shifts, bias_rows
    )
    mixed, lse = attn_fwd(q, k, v, pages)
    layer_out, after, after_low, rstd1, act, slope, gs2, gffn, sums2 = ffn_fwd(
        mixed, normed, output_weight, expand_weight, reduce_weight, hidden_bias,
        bias_rows, norm_gains, norm_shifts, cotangent, min(256, tokens),
    )
    if cubic:
        gs1, gmixed, hidden_sum, sums1, *parts, reduce_sum = ffn_grads(
            gffn, act, slope, gs2, after, after_low, rstd1, mixed, reduce_weight, expand_weight,
            output_weight, norm_gains, norm_shifts,
        )
    else:
        parts = None
        gh, gs1, gattn, gmixed, hidden_sum, sums1 = ffn_bwd(
            gffn, slope, gs2, after, rstd1, reduce_weight, expand_weight, output_weight,
            norm_gains, norm_shifts,
        )
    embedded_grad, cell_grad, sums0, sums_qv, *more = back(
        q, k, v, mixed, gmixed, lse, normed_low, gs1, joined_weight, normed, rstd0, cell_index,
        norm_gains, norm_shifts, parts,
    )
    if cubic:
        parts, expand_sum = more[:2], more[2:]
    else:
        gj = more[0]

    sums = (sums0, sums1, sums2, sums_qv, hidden_sum)
    if cubic:
        done, joined_sum, small = closing(cell_grad, group_index, sums, parts)
        (
            tables_grad, embedded_grad, reduce_grad, expand_grad, output_grad, joined_grad,
            gains_grad, shifts_grad, biases_grad, hidden_bias_grad,
        ) = write(
            done, embedded_grad, reduce_sum, expand_sum[0], joined_sum, small, table_rows, ff
        )
        hidden_bias_grad = hidden_bias_grad.reshape(-1)
    else:
        cell_grads = [cell_grad] + [shift_tab(cell_grad, s, n_tab) for s in range(1, n_tab)]
        part_a, part_b = table_part(jnp.zeros_like(tok), group_index, cell_grads, 8)
        both = jnp.concatenate([part_a, part_b], axis=2).astype(F32)
        tables_grad = lax.psum(both.reshape(1, -1, width)[:, :table_rows], "tok")
        small = jnp.concatenate([part.reshape(-1) for part in sums]).reshape(-1, 128)
        small = small_sum(small, n_tok, n_tab).reshape(-1)
        row = small.reshape(-1, width)
        gains_grad = jnp.stack([row[0], row[2], row[5]])
        shifts_grad = jnp.stack([row[1], row[3], row[6]])
        biases_grad = jnp.stack([row[8], row[9], row[4], row[7]])
        hidden_bias_grad = small[10 * width :]
        both = lambda a, b: jnp.einsum("ta,tb->ab", a, b, preferred_element_type=F32).astype(BF)

        def scattered(part):
            part = lax.psum_scatter(part, "tok", scatter_dimension=0, tiled=True)
            return lax.psum_scatter(part, "tab", scatter_dimension=1, tiled=True).astype(F32)

        reduce_grad = scattered(both(act, gffn))
        expand_grad = scattered(both(after_low, gh))
        output_grad = scattered(both(mixed, gattn))
        joined_grad = scattered(both(normed_low, jnp.concatenate([gj[0], gj[1], gj[2]], axis=1)))

    return (
        layer_out, embedded_grad, tables_grad, joined_grad, output_grad, expand_grad,
        reduce_grad, hidden_bias_grad, biases_grad, gains_grad, shifts_grad,
    )


def solution(mesh):
    rows = P(("tok", "tab"), None)
    return jax.shard_map(
        functools.partial(body, mesh.shape["tok"], mesh.shape["tab"]),
        mesh=mesh,
        in_specs=(
            rows, rows, P(("tok", "tab"), None, None), P("tab", None, None),
            P(), P(), P(), P(), P(), P(), P(), P(), rows,
        ),
        out_specs=(
            rows, rows, P("tab", None, None), P("tok", "tab"), P("tok", "tab"),
            P("tok", "tab"), P("tok", "tab"), P(), P(), P(), P(),
        ),
        check_vma=False,
    )
```

```python
import functools

import jax
import jax.numpy as jnp
from jax import lax
from jax.experimental import pallas as pl
from jax.experimental.pallas import tpu as pltpu
from jax.sharding import PartitionSpec as P

HEADS = 16
HEAD_DIM = 64
CELLS = 128
EPSILON = 1e-05
SCALE = HEAD_DIM ** (-0.5)
LOG2E = 1.4426950408889634
F32 = jnp.float32
BF = jnp.bfloat16
NN = ((1,), (0,))
NT = ((1,), (1,))
TN = ((0,), (0,))
ANY = pl.ANY

TAIL_P = 0.305
TAIL_C = (
    0.12164194255155772,
    0.12243138164026345,
    0.10365178645525906,
    0.12022714029486306,
    -0.03641303195181058,
    0.1839499605096701,
    -0.15192310059752684,
    0.03643391798251271,
)


def dot(a, b, dims):
    return lax.dot_general(a, b, (dims, ((), ())), preferred_element_type=F32)


def params(**kw):
    return pltpu.CompilerParams(vmem_limit_bytes=60 << 20, **kw)


def cost(flops, nbytes, trans=0):
    return pl.CostEstimate(
        flops=int(flops), bytes_accessed=int(nbytes), transcendentals=int(trans)
    )


def full(shape):
    zeros = (0,) * len(shape)
    return pl.BlockSpec(shape, lambda *_: zeros, pipeline_mode=pl.Buffered(1))


def gelu_parts(h):
    a = jnp.abs(h)
    t = 1.0 / (1.0 + TAIL_P * a)
    poly = jnp.full_like(t, TAIL_C[-1])
    for c in TAIL_C[-2::-1]:
        poly = poly * t + c
    e = jnp.exp2(h * h * (-0.5 * LOG2E))
    tail = poly * t * e
    phi_cdf = jnp.where(h > 0, 1.0 - tail, tail)
    act = h * phi_cdf
    slope = phi_cdf + h * e * 0.3989422804014327
    return act, slope


def norm_stats(v):
    mean = jnp.mean(v, axis=-1, keepdims=True)
    centred = v - mean
    var = jnp.mean(centred * centred, axis=-1, keepdims=True)
    rstd = lax.rsqrt(var + EPSILON)
    return centred * rstd, rstd


def norm_back(y, xh, rstd, gain):
    u = y * gain
    return (
        u - jnp.mean(u, axis=-1, keepdims=True) - xh * jnp.mean(u * xh, axis=-1, keepdims=True)
    ) * rstd


def colsum(v):
    return jnp.sum(v, axis=0, keepdims=True)


def lookup_kernel(idx, table, out):
    rows = table.shape[0]
    count = idx.shape[2]
    number = lax.broadcasted_iota(jnp.int32, (rows, count), 0)
    first = (number == idx[0, 0:1, :]).astype(F32)
    second = (number == idx[0, 1:2, :]).astype(F32)
    out[0] = dot((first + second).astype(BF), table[...], TN).astype(BF)


def lookup(idx, table):
    groups, _, count = idx.shape
    rows, width = table.shape
    return pl.pallas_call(
        lookup_kernel,
        grid=(groups,),
        in_specs=[
            pl.BlockSpec((1, 2, count), lambda i: (i, 0, 0)),
            full((rows, width)),
        ],
        out_specs=pl.BlockSpec((1, count, width), lambda i: (i, 0, 0)),
        out_shape=jax.ShapeDtypeStruct((groups, count, width), BF),
        compiler_params=params(),
        cost_estimate=cost(2 * groups * count * rows * width, 2 * groups * count * width),
        name="lookup",
    )(idx, table)


def embed_kernel(
    emb, ci, terms, w, gains, shifts, bias, q, k, v, normed, low, rstd_out
):
    width = emb.shape[1]
    tokens = emb.shape[0]
    cells = terms[...].reshape(4 * CELLS, width)
    number = lax.broadcasted_iota(jnp.int32, (CELLS, tokens), 0)
    pick = (number == ci[0]).astype(F32).astype(BF)
    pick = jnp.concatenate([pick] * 4, axis=0)
    box = dot(pick, cells, TN)
    xh, rstd = norm_stats(emb[...].astype(F32) + box)
    y = xh * gains[0:1] + shifts[0:1]
    normed[...] = y
    rstd_out[...] = rstd
    y_low = y.astype(BF)
    low[...] = y_low
    q[...] = ((dot(y_low, w[:, :width], NN) + bias[0:1]) * SCALE).astype(BF)
    k[...] = dot(y_low, w[:, width : 2 * width], NN).astype(BF)
    v[...] = (dot(y_low, w[:, 2 * width :], NN) + bias[1:2]).astype(BF)


def embed(emb, ci, terms, w, gains, shifts, bias):
    tokens, width = emb.shape
    pages, length = ci.shape
    rows = pl.BlockSpec((length, width), lambda i: (i, 0))
    shape = lambda dt, n=width: jax.ShapeDtypeStruct((tokens, n), dt)
    return pl.pallas_call(
        embed_kernel,
        grid=(pages,),
        in_specs=[rows, pl.BlockSpec((1, 1, length), lambda i: (i, 0, 0))]
        + [pl.BlockSpec((4, CELLS, width), lambda i: (0, i, 0))]
        + [full(w.shape), full(gains.shape), full(shifts.shape), full(bias.shape)],
        out_specs=[rows] * 5 + [pl.BlockSpec((length, 1), lambda i: (i, 0))],
        out_shape=[shape(BF), shape(BF), shape(BF), shape(F32), shape(BF), shape(F32, 1)],
        compiler_params=params(),
        cost_estimate=cost(2 * tokens * width * 3 * width, 26 << 20),
        name="embed_joined",
    )(emb, ci.reshape(pages, 1, length), terms, w, gains, shifts, bias)


STAGES = 4


def neighbours():
    tok, z = lax.axis_index("tok"), lax.axis_index("tab")
    core = {"tok": tok + 1 - 2 * (tok % 2)}
    x = {"tok": tok + 2 - 4 * ((tok // 2) % 2)}
    y = {"tok": tok + 4 - 8 * (tok // 4)}
    peers = [{"tab": (z + s) % 4} for s in range(1, 4)]
    return core, x, y, peers


def meet(devices):
    barrier = pltpu.get_barrier_semaphore()
    for d in devices:
        pl.semaphore_signal(barrier, inc=1, device_id=d, device_id_type=pl.DeviceIdType.MESH)
    pl.semaphore_wait(barrier, len(devices))


def sum_scratch(rows, cols):
    part = lambda *n: pltpu.VMEM((*n, rows, cols), BF)
    return [
        part(2, 4, 4), part(2, 4, 4), part(2, 4, 2), part(2, 4), part(2, 3),
        pltpu.SemaphoreType.DMA((2, 4)),
        pltpu.SemaphoreType.DMA((STAGES, 2, 4)),
        pltpu.SemaphoreType.DMA((STAGES, 2, 4)),
    ]


class Summing:
    def __init__(self, grads, out, scratch):
        self.grads, self.out = grads, out
        if grads is None:
            both, scratch = scratch[0], (scratch[0].at[0], *scratch[1:5], None, *scratch[5:])
            self.part = both.at[1]
        self.own, self.r0, self.r1, self.r2, self.r3, self.local, self.sent, self.got = scratch
        core, x, y, peers = neighbours()
        self.core, self.first, self.second, self.peers = core, (x, y), (y, x), peers
        self.z = lax.axis_index("tab")

    def devices(self):
        return [self.core, self.first[0], self.first[1], *self.peers]

    def copy(self, stage, ch, i):
        zc = (self.z + (i + 1)) % 4
        src, dst, to = (
            (
                lambda: self.part.at[ch, i] if self.grads is None else self.grads[ch].at[1, zc],
                self.r0.at[ch, i],
                self.core,
            ),
            (lambda: self.own.at[ch, i, pl.ds(2, 2)], self.r1.at[ch, i], self.first[ch]),
            (lambda: self.own.at[ch, i, 1], self.r2.at[ch, i], self.second[ch]),
            (lambda: self.own.at[ch, i, 0], self.r3.at[ch, min(i, 2)], self.peers[min(i, 2)]),
        )[stage]
        return pltpu.make_async_remote_copy(
            src_ref=src(), dst_ref=dst,
            send_sem=self.sent.at[stage, ch, i], recv_sem=self.got.at[stage, ch, i],
            device_id=to, device_id_type=pl.DeviceIdType.MESH,
        )

    def load(self, ch, i):
        zc = (self.z + (i + 1)) % 4
        return pltpu.make_async_copy(
            self.grads[ch].at[0, zc], self.own.at[ch, i], self.local.at[ch, i]
        )

    def start(self):
        for i in range(4):
            for ch in range(2):
                self.copy(0, ch, i).start()
                if self.grads is not None:
                    self.load(ch, i).start()

    def step(self, stage, i):
        for ch in range(2):
            self.copy(stage - 1, ch, i).wait_recv()
            if stage == 1:
                if self.grads is not None:
                    self.load(ch, i).wait()

                def add(j, _, ch=ch):
                    self.own[ch, i, j] = self.own[ch, i, j] + self.r0[ch, i, j]
                    return 0

                lax.fori_loop(0, 4, add, 0)
            elif stage == 2:

                def add(j, _, ch=ch):
                    self.own[ch, i, j] = self.own[ch, i, j] + self.r1[ch, i, j]
                    return 0

                lax.fori_loop(0, 2, add, 0)
            elif i < 3:
                self.own[ch, i, 0] = self.own[ch, i, 0] + self.r2[ch, i]
            if stage < 3 or i < 3:
                self.copy(stage, ch, i).start()

    def finish(self):
        for ch in range(2):
            total = self.own[ch, 3, 0].astype(F32) + self.r2[ch, 3].astype(F32)
            for i in range(3):
                self.copy(3, ch, i).wait_recv()
                total = total + self.r3[ch, i].astype(F32)
            self.out[ch] = total
        for stage in range(STAGES):
            for ch in range(2):
                for i in range(4 if stage < 3 else 3):
                    self.copy(stage, ch, i).wait_send()

    def run(self, step, plan):
        for at, events in plan.items():

            @pl.when(step == at)
            def _(events=events):
                for stage, i in events:
                    if stage == 0:
                        self.start()
                    elif stage == 4:
                        self.finish()
                    else:
                        self.step(stage, i)


def split_rel(r):
    return r & 1, (r >> 1) & 1, r >> 2


def rel_of(b):
    tok = lax.axis_index("tok")
    core, x, y = split_rel(b)
    flip = lambda static, mine: 1 - mine if static else mine
    return flip(core, tok % 2), flip(x, (tok // 2) % 2), flip(y, tok // 4)


def put_rows(g, ga, gb, cols, rows):
    half = rows // 2
    for b in range(8):
        core, x, y = rel_of(b)
        ga[core, 0, 2 * x + y, :, cols] = g[b * rows : b * rows + half]
        gb[core, 0, 2 * y + x, :, cols] = g[b * rows + half : (b + 1) * rows]


def sum_specs(grads, number):
    if grads is None:
        return [], [], [], [], {}
    rows, cols = grads[0].shape[3:]
    return (
        [pl.BlockSpec(memory_space=pl.ANY)] * 2,
        [full((2, rows, cols))],
        [jax.ShapeDtypeStruct((2, rows, cols), F32)],
        sum_scratch(rows, cols),
        {"has_side_effects": True, "collective_id": number},
    )


BLOCK = 128


def spread_kernel(
    idx, table, found, group_idx,
    held, numbers, ring_sent, ring_got, plane_sent, plane_got, idx_sent, idx_got,
):
    tok, z = lax.axis_index("tok"), lax.axis_index("tab")
    core, x, y, peers = neighbours()
    c, cx, cy = tok % 2, (tok // 2) % 2, tok // 4
    first, second = (x, y), (y, x)
    f, g = (cx, cy), (cy, cx)
    meet([core, x, y, *peers])
    half = table.shape[1] // 2
    count = idx.shape[2]

    def ring(k, ch):
        if k == 0:
            start = pl.multiple_of(tok * BLOCK, BLOCK)
            src = table.at[pl.ds(start, BLOCK), pl.ds(ch * half, half)]
        else:
            src = held.at[k - 1, ch, c, g[ch], f[ch]]
        return pltpu.make_async_remote_copy(
            src_ref=src, dst_ref=held.at[k, ch, c, g[ch], f[ch]],
            send_sem=ring_sent.at[k, ch], recv_sem=ring_got.at[k, ch],
            device_id=peers[0], device_id_type=pl.DeviceIdType.MESH,
        )

    def plane(stage, k, ch):
        src, to = (
            (held.at[k, ch, c, g[ch], f[ch]], first[ch]),
            (held.at[k, ch, c, g[ch]], second[ch]),
            (held.at[k, ch, c], core),
        )[stage]
        return pltpu.make_async_remote_copy(
            src_ref=src, dst_ref=src,
            send_sem=plane_sent.at[stage, k, ch], recv_sem=plane_got.at[stage, k, ch],
            device_id=to, device_id_type=pl.DeviceIdType.MESH,
        )

    def number(s):
        return pltpu.make_async_remote_copy(
            src_ref=idx.at[(z + s) % 4], dst_ref=numbers.at[s - 1],
            send_sem=idx_sent.at[s - 1], recv_sem=idx_got.at[s - 1],
            device_id=peers[s - 1], device_id_type=pl.DeviceIdType.MESH,
        )

    def picks(owner):
        out = []
        for b in range(8):
            row = lax.broadcasted_iota(jnp.int32, (BLOCK, count), 0) + b * BLOCK
            one = (row == idx[owner, 0:1, :]).astype(F32)
            two = (row == idx[owner, 1:2, :]).astype(F32)
            out.append((one + two).astype(BF))
        return out

    def arrive(k):
        for ch in range(2):
            ring(k, ch).wait_recv()
            if k < 2:
                ring(k + 1, ch).start()
            plane(0, k, ch).start()

    def go_on(stage, k):
        for ch in range(2):
            plane(stage - 1, k, ch).wait_recv()
            plane(stage, k, ch).start()

    def look_up(k):
        rows = picks((z + 3 - k) % 4)
        for ch in range(2):
            plane(2, k, ch).wait_recv()
            order = [
                4 * a + 2 * b + n if ch == 0 else 4 * b + 2 * a + n
                for n in range(2)
                for a in range(2)
                for b in range(2)
            ]
            pick = jnp.concatenate([rows[b] for b in order], axis=0)
            data = held[k, ch].reshape(8 * BLOCK, half)
            found[k + 1, :, ch * half : (ch + 1) * half] = dot(pick, data, TN).astype(BF)

    for ch in range(2):
        ring(0, ch).start()
    for s in range(1, 4):
        number(s).start()
    found[0] = dot(jnp.concatenate(picks(z), axis=0), table[...], TN).astype(BF)
    arrive(0)
    go_on(1, 0)
    arrive(1)
    go_on(1, 1)
    go_on(2, 0)
    arrive(2)
    go_on(1, 2)
    group_idx[0] = idx[z]
    for s in range(1, 4):
        number(s).wait_recv()
        group_idx[s] = numbers[s - 1]

    def finish(k, _):
        look_up(k)

        @pl.when(k < 2)
        def _():
            go_on(2, k + 1)

        return 0

    lax.fori_loop(0, 3, finish, 0)
    for s in range(1, 4):
        number(s).wait_send()
    for k in range(3):
        for ch in range(2):
            ring(k, ch).wait_send()
            for stage in range(3):
                plane(stage, k, ch).wait_send()


def spread(idx, table):
    n_tab, _, count = idx.shape
    rows, width = table.shape
    dma = pltpu.SemaphoreType.DMA
    return pl.pallas_call(
        spread_kernel,
        grid=(1,),
        in_specs=[full(idx.shape), full(table.shape)],
        out_specs=[full((n_tab, count, width)), full(idx.shape)],
        out_shape=[
            jax.ShapeDtypeStruct((n_tab, count, width), BF),
            jax.ShapeDtypeStruct(idx.shape, jnp.int32),
        ],
        scratch_shapes=[
            pltpu.VMEM((3, 2, 2, 2, 2, BLOCK, width // 2), BF),
            pltpu.VMEM((3, 2, count), jnp.int32),
            dma((3, 2)), dma((3, 2)), dma((3, 3, 2)), dma((3, 3, 2)), dma((3,)), dma((3,)),
        ],
        compiler_params=params(has_side_effects=True, collective_id=4),
        cost_estimate=cost(8 * count * width * rows, 8 << 20),
        name="spread",
    )(idx, table)


HP = 4


def head_masks(length, pair):
    lane = lax.broadcasted_iota(jnp.int32, (length, pair), 1)
    return lane < HEAD_DIM


def attn_fwd_kernel(q, k, v, mixed, lse):
    length = q.shape[0]
    pair = 2 * HEAD_DIM
    low_half = head_masks(length, pair)
    zero = jnp.zeros((length, pair), BF)
    for p in range(HP // 2):
        cols = slice(p * pair, (p + 1) * pair)
        qp, kp, vp = q[:, cols], k[:, cols], v[:, cols]
        vt = vp.T
        outs = []
        for h in range(2):
            km = jnp.where(low_half, kp, zero) if h == 0 else jnp.where(low_half, zero, kp)
            st = dot(km, qp, NT)
            top = jnp.max(st, axis=0, keepdims=True)
            raised = jnp.exp2((st - top) * LOG2E)
            total = jnp.sum(raised, axis=0, keepdims=True)
            lse[0, 0, 2 * p + h : 2 * p + h + 1, :] = top + jnp.log(total)
            ot = dot(vt[h * HEAD_DIM : (h + 1) * HEAD_DIM], raised.astype(BF), NN)
            outs.append(ot * (1.0 / total))
        mixed[:, cols] = jnp.concatenate(outs, axis=0).T.astype(BF)


def attn_fwd(q, k, v, pages):
    tokens, width = q.shape
    length = tokens // pages
    steps = HEADS // HP
    blk = pl.BlockSpec((length, HP * HEAD_DIM), lambda i, j: (i, j))
    return pl.pallas_call(
        attn_fwd_kernel,
        grid=(pages, steps),
        in_specs=[blk] * 3,
        out_specs=[blk, pl.BlockSpec((1, 1, HP, length), lambda i, j: (i, j, 0, 0))],
        out_shape=[
            jax.ShapeDtypeStruct((tokens, width), BF),
            jax.ShapeDtypeStruct((pages, steps, HP, length), F32),
        ],
        compiler_params=params(),
        cost_estimate=cost(14e9, 8 << 20, pages * HEADS * length * length),
        name="attention",
    )(q, k, v)


def attn_back(q, k, v, mixed, go, lse, put):
    length = q.shape[0]
    pair = 2 * HEAD_DIM
    low_half = head_masks(length, pair)
    zero = jnp.zeros((length, pair), BF)

    def pick(x, h):
        return jnp.where(low_half, x, zero) if h == 0 else jnp.where(low_half, zero, x)

    def pair_of_heads(p, _):
        cols = pl.ds(pl.multiple_of(p * pair, pair), pair)
        qp, kp, vp, op, gp = q[:, cols], k[:, cols], v[:, cols], mixed[:, cols], go[:, cols]
        kt = kp.T
        prod_t = (op.astype(F32) * gp.astype(F32)).T
        dq_t, dk, dv = [], None, None
        for h in range(2):
            st = dot(pick(kp, h), qp, NT)
            probs = jnp.exp2((st - lse[0, 0, pl.ds(2 * p + h, 1), :]) * LOG2E)
            dv_h = dot(probs.astype(BF), pick(gp, h), NN)
            dpt = dot(pick(vp, h), gp, NT)
            delta = colsum(prod_t[h * HEAD_DIM : (h + 1) * HEAD_DIM])
            ds = (probs * (dpt - delta)).astype(BF)
            dk_h = dot(ds, pick(qp, h), NN)
            dq_t.append(dot(kt[h * HEAD_DIM : (h + 1) * HEAD_DIM], ds, NN))
            dv = dv_h if dv is None else dv + dv_h
            dk = dk_h if dk is None else dk + dk_h
        dq = (jnp.concatenate(dq_t, axis=0).T.astype(BF).astype(F32) * SCALE).astype(BF)
        put(p * pair, pair, dq, dk.astype(BF), dv.astype(BF))
        return 0

    lax.fori_loop(0, HP // 2, pair_of_heads, 0)


FC = 512
FWD = 1024
RC = 128
MC = 512


def ffn_fwd_kernel(
    mixed, normed, wo, we_in, wr_in, hb, bias, gains, shifts, cot,
    out, after_out, low_out, rstd_out, act_out, slope_out, gs2_out, gffn_out, sums,
    we, wr, local,
):
    loads = [
        pltpu.make_async_copy(we_in, we, local.at[0]),
        pltpu.make_async_copy(wr_in, wr, local.at[1]),
    ]

    @pl.when(pl.program_id(0) == 0)
    def _():
        for copy in loads:
            copy.start()

    ff = we.shape[1]
    attn_sum = normed[...] + (dot(mixed[...], wo[...], NN) + bias[2:3])
    xh, rstd = norm_stats(attn_sum)
    after = xh * gains[1:2] + shifts[1:2]
    after_out[...] = after
    rstd_out[...] = rstd
    low = after.astype(BF)
    low_out[...] = low
    total = after + bias[3:4]

    @pl.when(pl.program_id(0) == 0)
    def _():
        for copy in loads:
            copy.wait()

    count = ff // FWD
    hidden = []
    for j in range(count + 1):
        if j < count:
            cols = slice(j * FWD, (j + 1) * FWD)
            hidden.append(dot(low, we[:, cols], NN) + hb[:, cols])
        if j > 0:
            cols = slice((j - 1) * FWD, j * FWD)
            act, slope = gelu_parts(hidden[j - 1])
            act = act.astype(BF)
            act_out[:, cols] = act
            slope_out[:, cols] = slope.astype(BF)
            total = total + dot(act, wr[cols, :], NN)
    xh, rstd = norm_stats(total)
    out[...] = (xh * gains[2:3] + shifts[2:3]).astype(BF)
    y = cot[...].astype(F32)
    gs2 = norm_back(y, xh, rstd, gains[2:3])
    gs2_out[...] = gs2
    gffn = gs2.astype(BF)
    gffn_out[...] = gffn
    part = jnp.concatenate([colsum(y * xh), colsum(y), colsum(gffn.astype(F32))], axis=0)

    @pl.when(pl.program_id(0) == 0)
    def _():
        sums[...] = part

    @pl.when(pl.program_id(0) != 0)
    def _():
        sums[...] = sums[...] + part


def ffn_fwd(mixed, normed, wo, we, wr, hb, bias, gains, shifts, cot, tile):
    tokens, width = mixed.shape
    ff = we.shape[1]
    rows = pl.BlockSpec((tile, width), lambda i: (i, 0))
    long = pl.BlockSpec((tile, ff), lambda i: (i, 0))
    shape = lambda dt, n=width: jax.ShapeDtypeStruct((tokens, n), dt)
    hb = hb.reshape(1, ff)
    return pl.pallas_call(
        ffn_fwd_kernel,
        grid=(tokens // tile,),
        in_specs=[rows, rows]
        + [full(wo.shape)]
        + [pl.BlockSpec(memory_space=pl.ANY)] * 2
        + [full(a.shape) for a in (hb, bias, gains, shifts)]
        + [rows],
        out_specs=[rows, rows, rows, pl.BlockSpec((tile, 1), lambda i: (i, 0)), long, long, rows, rows]
        + [pl.BlockSpec((3, width), lambda i: (0, 0))],
        out_shape=[
            shape(BF), shape(F32), shape(BF), shape(F32, 1), shape(BF, ff), shape(BF, ff),
            shape(F32), shape(BF), jax.ShapeDtypeStruct((3, width), F32),
        ],
        scratch_shapes=[
            pltpu.VMEM(we.shape, BF), pltpu.VMEM(wr.shape, BF), pltpu.SemaphoreType.DMA((2,)),
        ],
        compiler_params=params(),
        cost_estimate=cost(2 * tokens * width * (width + 2 * ff), 60 << 20, tokens * ff * 2),
        name="ffn_forward",
    )(mixed, normed, wo, we, wr, hb, bias, gains, shifts, cot)


def second_norm_back(gs1_out, after, rstd, gains, shifts, gattn_out, sums):
    tokens, width = after.shape

    def norm(i, carry):
        rows = pl.ds(pl.multiple_of(i * RC, RC), RC)
        total = gs1_out[rows, :]
        xh = (after[rows, :] - shifts[1:2]) * (1.0 / gains[1:2])
        gs1 = norm_back(total, xh, rstd[rows, :], gains[1:2])
        gs1_out[rows, :] = gs1
        gattn = gs1.astype(BF)
        gattn_out[rows, :] = gattn
        g, s, b = carry
        return g + colsum(total * xh), s + colsum(total), b + colsum(gattn.astype(F32))

    zero = jnp.zeros((1, width), F32)
    sums[...] = jnp.concatenate(lax.fori_loop(0, tokens // RC, norm, (zero, zero, zero)), axis=0)


def ffn_bwd_kernel(
    gffn, gs2, after, rstd, wo, gains, shifts, slope, wr, we,
    gh_out, gs1_out, gattn_out, gmixed_out, hsum, sums,
):
    step, last = pl.program_id(0), pl.num_programs(0) - 1
    tokens, width = gffn.shape

    @pl.when(step == 0)
    def _():
        gs1_out[...] = gs2[...]

    part = jnp.zeros((1, slope.shape[1]), F32)
    for m in range(0, tokens, MC):
        rows = slice(m, m + MC)
        gh = (dot(gffn[rows, :], wr[...], NT) * slope[rows, :].astype(F32)).astype(BF)
        gh_out[rows, :] = gh
        part = part + colsum(gh.astype(F32))
        gs1_out[rows, :] = gs1_out[rows, :] + dot(gh, we[...], NT)
    hsum[...] = part

    @pl.when(step == last)
    def _():
        second_norm_back(gs1_out, after, rstd, gains, shifts, gattn_out, sums)
        for m in range(0, tokens, MC):
            rows = slice(m, m + MC)
            gmixed_out[rows, :] = dot(gattn_out[rows, :], wo[...], NT).astype(BF)


def ffn_bwd(gffn, slope, gs2, after, rstd, wr, we, wo, gains, shifts):
    tokens, width = gffn.shape
    ff = we.shape[1]
    whole = full((tokens, width))
    long = pl.BlockSpec((tokens, FC), lambda s: (0, s))
    shape = lambda dt, n=width: jax.ShapeDtypeStruct((tokens, n), dt)
    return pl.pallas_call(
        ffn_bwd_kernel,
        grid=(ff // FC,),
        in_specs=[whole, whole, whole, full((tokens, 1))]
        + [full(a.shape) for a in (wo, gains, shifts)]
        + [
            long,
            pl.BlockSpec((FC, width), lambda s: (s, 0)),
            pl.BlockSpec((width, FC), lambda s: (0, s)),
        ],
        out_specs=[long, whole, whole, whole]
        + [pl.BlockSpec((1, FC), lambda s: (0, s)), full((3, width))],
        out_shape=[
            shape(BF, ff), shape(F32), shape(BF), shape(BF),
            jax.ShapeDtypeStruct((1, ff), F32), jax.ShapeDtypeStruct((3, width), F32),
        ],
        compiler_params=params(),
        cost_estimate=cost(2 * tokens * width * (width + 2 * ff), 60 << 20),
        name="ffn_backward",
    )(gffn, gs2, after, rstd, wo, gains, shifts, slope, wr, we)


FFN_PLAN = {
    4: [(0, 0)],
    8: [(1, 0)],
    9: [(1, 1)],
    11: [(2, 0), (1, 2)],
    13: [(2, 1), (1, 3)],
    15: [(3, 0)],
    16: [(2, 2)],
    17: [(3, 1), (2, 3)],
    18: [(3, 2)],
    19: [(3, 3)],
}
N_TOK, N_TAB = 8, 4


def block_of_step(s):
    s = jnp.minimum(s, N_TOK - 1)
    return 1 - s // 4, 1 - (s // 2) % 2, 1 - s % 2


def ffn_grads_kernel(
    gffn_in, gs2_in, after_in, rstd, low_in, mixed_in, wo_in, gains, shifts, act, slope, wr, we,
    gs1_out, gmixed_out, hsum, sums, ga, gb, reduce_out,
    gffn, gh, after, low, mixed, wo, local, *scratch,
):
    step, last = pl.program_id(0), pl.num_programs(0) - 1
    tokens, width = after.shape
    summing = Summing(None, reduce_out, scratch)
    both = scratch[0]
    z = lax.axis_index("tab")
    first = pltpu.make_async_copy(gffn_in, gffn, local.at[0])
    later = [
        pltpu.make_async_copy(src, dst, local.at[1 + n])
        for n, (src, dst) in enumerate(
            ((gs2_in, gs1_out), (after_in, after), (wo_in, wo), (low_in, low), (mixed_in, mixed))
        )
    ]

    @pl.when(step == 0)
    def _():
        first.start()
        for copy in later:
            copy.start()
        meet(summing.devices())
        first.wait()

    @pl.when(step == N_TOK)
    def _():
        for copy in later:
            copy.wait()

    summing.run(step, FFN_PLAN)

    @pl.when(step < N_TOK)
    def _():
        core, x, y = block_of_step(step)
        g = dot(gffn[...], act[...], TN).astype(BF)
        rows, half = both.shape[4:]
        for zc in range(N_TAB):
            i = (zc + N_TAB - 1 - z) % N_TAB
            for ch in range(2):
                piece = g[zc * rows : (zc + 1) * rows, ch * half : (ch + 1) * half]
                both[core, ch, i, (2 * x + y, 2 * y + x)[ch]] = piece

    @pl.when((step >= N_TOK) & (step < 2 * N_TOK))
    def _():
        part = jnp.zeros((1, slope.shape[1]), F32)
        for m in range(0, tokens, MC):
            rows = slice(m, m + MC)
            g = (dot(gffn[rows, :], wr[...], NT) * slope[rows, :].astype(F32)).astype(BF)
            gh[step - N_TOK, rows, :] = g
            part = part + colsum(g.astype(F32))
            gs1_out[rows, :] = gs1_out[rows, :] + dot(g, we[...], NT)
        hsum[...] = part

    @pl.when(step == 2 * N_TOK - 1)
    def _():
        second_norm_back(gs1_out, after, rstd, gains, shifts, gffn, sums)

        def block(m, _):
            rows = pl.ds(pl.multiple_of(m * MC, MC), MC)
            gmixed_out[rows, :] = dot(gffn[rows, :], wo[...], NT).astype(BF)
            return 0

        lax.fori_loop(0, tokens // MC, block, 0)

    @pl.when(step >= 2 * N_TOK)
    def _():
        n = step - 2 * N_TOK
        quarter = width // N_TAB
        rows = width // N_TOK
        wide = gh.shape[2]

        def block(m, _):
            g = dot(low[...], gh[2 * n + m], TN).astype(BF)
            put_rows(g, ga, gb, pl.ds(pl.multiple_of(m * wide, wide), wide), rows)
            return 0

        lax.fori_loop(0, 2, block, 0)
        piece = gffn[:, pl.ds(pl.multiple_of(n * quarter, quarter), quarter)]
        g = dot(mixed[...], piece, TN).astype(BF)
        put_rows(g, ga, gb, slice(2 * wide, 2 * wide + quarter), rows)

    @pl.when(step == last)
    def _():
        summing.finish()


def ffn_grads(gffn, act, slope, gs2, after, low, rstd, mixed, wr, we, wo, gains, shifts):
    tokens, width = gffn.shape
    ff = we.shape[1]
    whole = full((tokens, width))
    anywhere = pl.BlockSpec(memory_space=pl.ANY)
    wide = ff // N_TOK
    half = width // (2 * N_TOK)
    out_wide = (ff + width) // N_TAB
    back = lambda s: jnp.clip(s - N_TOK, 0, N_TOK - 1)
    grad = lambda s: jnp.clip(s - 2 * N_TOK, 0, N_TAB - 1)

    def act_block(s):
        core, x, y = block_of_step(s)
        tok = lax.axis_index("tok")
        flip = lambda rel, mine: rel + mine - 2 * rel * mine
        return 0, 4 * flip(y, tok // 4) + 2 * flip(x, (tok // 2) % 2) + flip(core, tok % 2)

    rows, cols = width // N_TAB, wide // 2
    part = lambda *n: pltpu.VMEM((*n, rows, cols), BF)
    dma = pltpu.SemaphoreType.DMA
    shape = lambda dt: jax.ShapeDtypeStruct((tokens, width), dt)
    piece = pl.BlockSpec((2, 1, 4, half, out_wide), lambda s: (0, grad(s), 0, 0, 0))
    return pl.pallas_call(
        ffn_grads_kernel,
        grid=(2 * N_TOK + N_TAB,),
        in_specs=[anywhere, anywhere, anywhere, full((tokens, 1)), anywhere, anywhere, anywhere]
        + [full(a.shape) for a in (gains, shifts)]
        + [
            pl.BlockSpec((tokens, wide), act_block),
            pl.BlockSpec((tokens, wide), lambda s: (0, back(s))),
            pl.BlockSpec((wide, width), lambda s: (back(s), 0)),
            pl.BlockSpec((width, wide), lambda s: (0, back(s))),
        ],
        out_specs=[
            whole, whole, pl.BlockSpec((1, wide), lambda s: (0, back(s))), full((3, width)),
            piece, piece, full((2, rows, cols)),
        ],
        out_shape=[
            shape(F32), shape(BF),
            jax.ShapeDtypeStruct((1, ff), F32), jax.ShapeDtypeStruct((3, width), F32),
            jax.ShapeDtypeStruct((2, 4, 4, half, out_wide), BF),
            jax.ShapeDtypeStruct((2, 4, 4, half, out_wide), BF),
            jax.ShapeDtypeStruct((2, rows, cols), F32),
        ],
        scratch_shapes=[
            pltpu.VMEM((tokens, width), BF), pltpu.VMEM((N_TOK, tokens, wide), BF),
            pltpu.VMEM((tokens, width), F32), pltpu.VMEM((tokens, width), BF),
            pltpu.VMEM((tokens, width), BF), pltpu.VMEM(wo.shape, BF), dma((6,)),
            part(2, 2, 4, 4), part(2, 4, 4), part(2, 4, 2), part(2, 4), part(2, 3),
            dma((STAGES, 2, 4)), dma((STAGES, 2, 4)),
        ],
        compiler_params=pltpu.CompilerParams(
            vmem_limit_bytes=67043328, has_side_effects=True, collective_id=1
        ),
        cost_estimate=cost(2 * tokens * width * (2 * width + 4 * ff), 60 << 20),
        name="ffn_backward_grads",
    )(gffn, gs2, after, rstd, low, mixed, wo, gains, shifts, act, slope, wr, we)


BACK_PLAN = {
    0: [(0, 0)],
    1: [(1, 0)],
    2: [(1, 1)],
    3: [(2, 0), (1, 2)],
    5: [(2, 1), (1, 3)],
    6: [(3, 0)],
    8: [(2, 2)],
    9: [(3, 1)],
    11: [(2, 3)],
    12: [(3, 2)],
    13: [(3, 3)],
}


def back_kernel(*refs, pages, summed):
    q, k, v, mixed, go, lse, low_in, gs1, w_in, normed, rstd, ci, gains, shifts = refs[:14]
    refs = refs[14:]
    grads, refs = refs[: 2 * summed], refs[2 * summed :]
    out, cells, sums0, sums_qv = refs[:4]
    refs = refs[4:]
    if summed:
        ga, gb, summed_out, gj, low, w, local = refs[:7]
        summing = Summing(grads, summed_out, refs[7:])
    else:
        gj_out, gj, low, w, local = refs
    step = pl.program_id(0)
    width = gs1.shape[1]
    length = q.shape[0]
    groups = HEADS // HP
    wide = HP * HEAD_DIM
    n_attn = groups * pages
    n_joined = 4 if summed else 0
    loads = [
        pltpu.make_async_copy(low_in, low, local.at[0]),
        pltpu.make_async_copy(w_in, w, local.at[1]),
    ]

    @pl.when(step == 0)
    def _():
        for copy in loads:
            copy.start()

    @pl.when(step == n_attn)
    def _():
        for copy in loads:
            copy.wait()

    if summed:

        @pl.when(step == 0)
        def _():
            meet(summing.devices())

        summing.run(step, BACK_PLAN)

    @pl.when(step < n_attn)
    def _():
        group, page = step // pages, step % pages
        rows = pl.ds(pl.multiple_of(page * length, length), length)

        def put(at, size, dq, dk, dv):
            cols = pl.ds(pl.multiple_of(group * wide + at, size), size)
            gj[0, rows, cols] = dq
            gj[1, rows, cols] = dk
            gj[2, rows, cols] = dv
            part = jnp.concatenate([colsum(dq.astype(F32)), colsum(dv.astype(F32))], axis=0)

            @pl.when(page == 0)
            def _():
                sums_qv[:, cols] = part

            @pl.when(page != 0)
            def _():
                sums_qv[:, cols] = sums_qv[:, cols] + part

        attn_back(q, k, v, mixed, go, lse, put)

    if summed:
        quarter = width // 4

        @pl.when((step >= n_attn) & (step < n_attn + n_joined))
        def _():
            def block(m, _):
                unit = 3 * (step - n_attn) + m
                cols = pl.ds(pl.multiple_of((unit % 4) * quarter, quarter), quarter)
                g = dot(low[...], gj[unit // 4, :, cols], TN).astype(BF)
                at = pl.ds(pl.multiple_of(m * quarter, quarter), quarter)
                put_rows(g, ga, gb, at, width // 8)
                return 0

            lax.fori_loop(0, 3, block, 0)

    @pl.when(step >= n_attn + n_joined)
    def _():
        page = step - (n_attn + n_joined)
        rows = pl.ds(pl.multiple_of(page * length, length), length)
        total = gs1[...]
        for n in range(3):
            total = total + dot(gj[n, rows, :], w[:, n * width : (n + 1) * width], NT)
        xh = (normed[...] - shifts[0:1]) * (1.0 / gains[0:1])
        grad = norm_back(total, xh, rstd[...], gains[0:1])
        out[...] = grad
        number = lax.broadcasted_iota(jnp.int32, (CELLS, length), 0)
        pick = (number == ci[0]).astype(F32).astype(BF)
        cells[...] = dot(pick, grad.astype(BF), NN).astype(BF)
        part = jnp.concatenate([colsum(total * xh), colsum(total)], axis=0)

        @pl.when(page == 0)
        def _():
            sums0[...] = part

        @pl.when(page != 0)
        def _():
            sums0[...] = sums0[...] + part

    if summed:

        @pl.when(step == pl.num_programs(0) - 1)
        def _():
            summing.finish()
    else:
        gj_out[...] = gj[...]


def back(q, k, v, mixed, go, lse, low, gs1, w, normed, rstd, ci, gains, shifts, grads):
    tokens, width = q.shape
    pages, length = ci.shape
    groups = HEADS // HP
    wide = HP * HEAD_DIM
    summed = grads is not None
    n_attn = groups * pages
    before = n_attn + (4 if summed else 0)
    at = lambda s: jnp.minimum(s, n_attn - 1)
    page = lambda s: jnp.maximum(s - before, 0)
    block = lambda s: jnp.clip(s - n_attn, 0, 3)
    blk = pl.BlockSpec((length, wide), lambda s: (at(s) % pages, at(s) // pages))
    rows = pl.BlockSpec((length, width), lambda s: (page(s), 0))
    out_specs = [
        rows,
        pl.BlockSpec((CELLS, width), lambda s: (page(s), 0)),
        full((2, width)),
        full((2, width)),
    ]
    out_shape = [
        jax.ShapeDtypeStruct((tokens, width), F32),
        jax.ShapeDtypeStruct((pages * CELLS, width), BF),
        jax.ShapeDtypeStruct((2, width), F32),
        jax.ShapeDtypeStruct((2, width), F32),
    ]
    whole_gj = (3, tokens, width)
    more_in, more_out, more_shape, more_scratch, more = sum_specs(grads, 2)
    if summed:
        half = width // 16
        piece = pl.BlockSpec((2, 1, 4, half, 3 * width // 4), lambda s: (0, block(s), 0, 0, 0))
        out_specs += [piece, piece]
        out_shape += [jax.ShapeDtypeStruct((2, 4, 4, half, 3 * width // 4), BF)] * 2
    else:
        out_specs += [full(whole_gj)]
        out_shape += [jax.ShapeDtypeStruct(whole_gj, BF)]
    return pl.pallas_call(
        functools.partial(back_kernel, pages=pages, summed=summed),
        grid=(before + pages,),
        in_specs=[blk] * 5
        + [
            pl.BlockSpec((1, 1, HP, length), lambda s: (at(s) % pages, at(s) // pages, 0, 0)),
            pl.BlockSpec(memory_space=pl.ANY),
            rows,
            pl.BlockSpec(memory_space=pl.ANY),
            rows,
            pl.BlockSpec((length, 1), lambda s: (page(s), 0)),
            pl.BlockSpec((1, 1, length), lambda s: (page(s), 0, 0)),
            full(gains.shape),
            full(shifts.shape),
        ]
        + more_in,
        out_specs=out_specs + more_out,
        out_shape=out_shape + more_shape,
        scratch_shapes=[
            pltpu.VMEM(whole_gj, BF), pltpu.VMEM(low.shape, BF), pltpu.VMEM(w.shape, BF),
            pltpu.SemaphoreType.DMA((2,)),
        ]
        + more_scratch,
        compiler_params=params(**more),
        cost_estimate=cost(70e9, 40 << 20, pages * HEADS * length * length),
        name="attention_joined_embed_back",
    )(
        q, k, v, mixed, go, lse, low, gs1, w, normed, rstd, ci.reshape(pages, 1, length),
        gains, shifts, *(grads or ()),
    )


def table_kernel(tok, idx, g0, g1, g2, g3, out_a, out_b):
    rows = out_a.shape[1]
    count = idx.shape[2]
    half = out_a.shape[2]
    base = (pl.program_id(0) ^ tok[0]) * rows
    number = lax.broadcasted_iota(jnp.int32, (rows, count), 0) + base
    picks = []
    for s in range(4):
        first = (number == idx[s, 0:1, :]).astype(F32)
        second = (number == idx[s, 1:2, :]).astype(F32)
        picks.append((first + second).astype(BF))
    pick = jnp.concatenate(picks, axis=1)
    grads = jnp.concatenate([g0[...], g1[...], g2[...], g3[...]], axis=0)
    total = dot(pick, grads, NN).astype(BF)
    out_a[0] = total[:, :half]
    out_b[0] = total[:, half:]


def table_part(tok, idx, grads, blocks):
    groups, _, count = idx.shape
    width = grads[0].shape[1]
    rows = 1024 // blocks
    half = width // 2
    out = pl.BlockSpec((1, rows, half), lambda i, t: (i, 0, 0))
    return pl.pallas_call(
        table_kernel,
        grid_spec=pltpu.PrefetchScalarGridSpec(
            num_scalar_prefetch=1,
            grid=(blocks,),
            in_specs=[full(idx.shape)] + [full((count, width))] * groups,
            out_specs=[out, out],
        ),
        out_shape=[jax.ShapeDtypeStruct((blocks, rows, half), BF)] * 2,
        compiler_params=params(),
        cost_estimate=cost(2 * 1024 * groups * count * width, 4 << 20),
        name="table_grad",
    )(tok, idx, *grads)


class TableSum:
    def __init__(self, scratch, done):
        self.part, self.r0, self.r1, self.r2, self.sent, self.got = scratch
        self.done = done
        tok = lax.axis_index("tok")
        core, x, y, _ = neighbours()
        self.c, cx, cy = tok % 2, (tok // 2) % 2, tok // 4
        self.core, self.first, self.second = core, (x, y), (y, x)
        self.f, self.g = (cx, cy), (cy, cx)

    def copy(self, stage, ch, u):
        c, f, g = self.c, self.f[ch], self.g[ch]
        part, done = self.part.at[ch, u], self.done.at[ch, u]
        src, dst, to = (
            (lambda: part.at[1 - c], self.r0.at[ch, u], self.core),
            (lambda: part.at[c, 1 - f], self.r1.at[ch, u], self.first[ch]),
            (lambda: part.at[c, f, 1 - g], self.r2.at[ch, u], self.second[ch]),
            (lambda: done.at[c, f, g], None, self.second[ch]),
            (lambda: done.at[c, f], None, self.first[ch]),
            (lambda: done.at[c], None, self.core),
        )[stage]
        src = src()
        return pltpu.make_async_remote_copy(
            src_ref=src, dst_ref=src if dst is None else dst,
            send_sem=self.sent.at[stage, ch, u], recv_sem=self.got.at[stage, ch, u],
            device_id=to, device_id_type=pl.DeviceIdType.MESH,
        )

    def store(self, u, ch, value):
        for b in range(8):
            c, x, y = split_rel(b)
            f, g = (x, y) if ch == 0 else (y, x)
            self.part[ch, u, c, f, g] = value[b * BLOCK : (b + 1) * BLOCK]
        self.copy(0, ch, u).start()

    def step(self, stage, u):
        for ch in range(2):
            c, f, g = self.c, self.f[ch], self.g[ch]
            self.copy(stage - 1, ch, u).wait_recv()
            if stage == 1:
                self.part[ch, u, c] = self.part[ch, u, c] + self.r0[ch, u]
            elif stage == 2:
                self.part[ch, u, c, f] = self.part[ch, u, c, f] + self.r1[ch, u]
            elif stage == 3:
                self.done[ch, u, c, f, g] = self.part[ch, u, c, f, g] + self.r2[ch, u]
            if stage < 6:
                self.copy(stage, ch, u).start()

    def finish(self):
        for stage in range(6):
            for ch in range(2):
                for u in range(2):
                    self.copy(stage, ch, u).wait_send()


def closing_kernel(
    cells, idx, sums0, sums1, sums2, sums_qv, hidden_sum, ga, gb, done, joined, small_out,
    ring, total, ring_sent, ring_got, held, arrived, small_sent, small_got, *scratch,
):
    summing = Summing((ga, gb), joined, scratch[:8])
    table = TableSum(scratch[8:], done)
    core, x, y, peers = neighbours()
    z = lax.axis_index("tab")
    hops = [core, x, y, {"tab": z + 1 - 2 * (z % 2)}, {"tab": z + 2 - 4 * (z // 2)}]
    meet([core, x, y, *peers])
    count = cells.shape[0]
    half = cells.shape[1] // 2

    def pass_on(k, h):
        cols = pl.ds(h * half, half)
        src = cells.at[:, cols] if k == 0 else ring.at[k - 1, :, cols]
        return pltpu.make_async_remote_copy(
            src_ref=src, dst_ref=ring.at[k, :, cols],
            send_sem=ring_sent.at[k, h], recv_sem=ring_got.at[k, h],
            device_id=peers[0], device_id_type=pl.DeviceIdType.MESH,
        )

    def small_copy(n):
        return pltpu.make_async_remote_copy(
            src_ref=held.at[n], dst_ref=arrived.at[n],
            send_sem=small_sent.at[n], recv_sem=small_got.at[n],
            device_id=hops[n], device_id_type=pl.DeviceIdType.MESH,
        )

    def small_step(n):
        small_copy(n - 1).wait_recv()
        value = held[n - 1] + arrived[n - 1]
        if n < 5:
            held[n] = value
            small_copy(n).start()
        else:
            small_out[...] = value

    def relay(k, h):
        pass_on(k - 1, h).wait_recv()
        pass_on(k, h).start()

    def pick(s):
        number = lax.broadcasted_iota(jnp.int32, (total.shape[0], count), 0)
        first = (number == idx[s, 0:1, :]).astype(F32)
        second = (number == idx[s, 1:2, :]).astype(F32)
        return (first + second).astype(BF)

    def last_arrival(u):
        pass_on(2, u).wait_recv()
        for ch in range(2):
            cols = slice((2 * u + ch) * half // 2, (2 * u + ch + 1) * half // 2)
            value = total[:, cols] + dot(last, ring[2, :, cols], NN)
            table.store(u, ch, value.astype(BF))

    pass_on(0, 0).start()
    pass_on(0, 1).start()
    at, width = 0, cells.shape[1]
    for part in (sums0, sums1, sums2, sums_qv):
        held[0, at : at + part.shape[0]] = part[...]
        at += part.shape[0]
    for n in range(hidden_sum.shape[1] // width):
        held[0, at + n : at + n + 1] = hidden_sum[:, n * width : (n + 1) * width]
    small_copy(0).start()
    summing.start()
    total[...] = dot(pick(0), cells[...], NN)
    small_step(1)
    summing.step(1, 0)
    small_step(2)
    summing.step(1, 1)
    relay(1, 0)
    summing.step(2, 0)
    summing.step(1, 2)
    small_step(3)
    relay(1, 1)
    summing.step(2, 1)
    summing.step(1, 3)
    relay(2, 0)
    small_step(4)
    summing.step(2, 2)
    relay(2, 1)
    summing.step(3, 0)
    summing.step(3, 1)
    summing.step(2, 3)

    def add(k, _):
        total[...] = total[...] + dot(pick(k + 1), ring[k], NN)
        return 0

    lax.fori_loop(0, 2, add, 0)
    last = pick(3)
    last_arrival(0)
    table.step(1, 0)
    last_arrival(1)
    summing.step(3, 2)
    small_step(5)
    table.step(2, 0)
    table.step(1, 1)
    table.step(3, 0)
    table.step(2, 1)
    table.step(4, 0)
    table.step(3, 1)
    table.step(5, 0)
    table.step(4, 1)
    table.step(6, 0)
    table.step(5, 1)
    summing.step(3, 3)
    summing.finish()
    table.step(6, 1)
    table.finish()
    for k in range(3):
        for h in range(2):
            pass_on(k, h).wait_send()
    for n in range(5):
        small_copy(n).wait_send()


def closing(cells, idx, sums, grads):
    count, width = cells.shape
    small = (sum(part.size for part in sums) // width, width)
    rows, cols = grads[0].shape[3:]
    wide = width // 4
    part = lambda *n: pltpu.VMEM((2, 2, *n, BLOCK, wide), BF)
    done = (2, 2, 2, 2, 2, BLOCK, wide)
    dma = pltpu.SemaphoreType.DMA
    return pl.pallas_call(
        closing_kernel,
        grid=(1,),
        in_specs=[full(cells.shape), full(idx.shape)]
        + [full(part.shape) for part in sums]
        + [pl.BlockSpec(memory_space=pl.ANY)] * 2,
        out_specs=[full(done), full((2, rows, cols)), full(small)],
        out_shape=[
            jax.ShapeDtypeStruct(done, BF),
            jax.ShapeDtypeStruct((2, rows, cols), F32),
            jax.ShapeDtypeStruct(small, F32),
        ],
        scratch_shapes=[
            pltpu.VMEM((3, count, width), BF), pltpu.VMEM((8 * BLOCK, width), F32),
            dma((3, 2)), dma((3, 2)),
            pltpu.VMEM((5, *small), F32), pltpu.VMEM((5, *small), F32), dma((5,)), dma((5,)),
        ]
        + sum_scratch(rows, cols)
        + [part(2, 2, 2), part(2, 2), part(2), part(), dma((6, 2, 2)), dma((6, 2, 2))],
        compiler_params=params(has_side_effects=True, collective_id=3),
        cost_estimate=cost(8 * count * width * 1024, 24 << 20),
        name="closing",
    )(cells, idx, *sums, *grads)


def write_kernel(
    a, b, embed, reduce_sum, expand_sum, joined_sum, small,
    table, embed_out, reduce_out, expand_out, output_out, joined_out,
    gains, shifts, biases, hidden_bias,
):
    wide = a.shape[6]
    lanes = table.shape[1]
    for n, piece in enumerate((a, b)):
        for u in range(2):
            for c in range(2):
                value = piece[0, u, c, 0, 0].astype(F32)
                for k in range(wide // lanes):
                    row = c * BLOCK * (4 * wide // lanes) + ((2 * u + n) * wide) // lanes + k
                    table[pl.ds(row, BLOCK, stride=4 * wide // lanes), :] = value[
                        :, k * lanes : (k + 1) * lanes
                    ]
    embed_out[...] = embed[...]

    @pl.when(pl.program_id(0) == 0)
    def _():
        cols = reduce_sum.shape[2]
        rows = expand_sum.shape[1]
        wide = expand_out.shape[1]
        for n in range(2):
            reduce_out[n * cols : (n + 1) * cols, :] = reduce_sum[n].T
            expand_out[n * rows : (n + 1) * rows, :] = expand_sum[n, :, :wide]
            output_out[n * rows : (n + 1) * rows, :] = expand_sum[n, :, wide:]
            joined_out[n * rows : (n + 1) * rows, :] = joined_sum[n]
        for out, order in ((gains, (0, 2, 5)), (shifts, (1, 3, 6)), (biases, (8, 9, 4, 7))):
            for n, row in enumerate(order):
                out[n : n + 1, :] = small[row : row + 1, :]
        for n in range(hidden_bias.shape[0]):
            hidden_bias[n : n + 1, :] = small[10 + n : 11 + n, :]


def write(done, embed, reduce_sum, expand_sum, joined_sum, small, table_rows, ff):
    wide = done.shape[6]
    width = 4 * wide
    tokens = embed.shape[0]
    block = (1, 2, 2, 1, 1, BLOCK, wide)
    first = lambda i: (0, 0, 0, i % 2, i // 2, 0, 0)
    second = lambda i: (1, 0, 0, i // 2, i % 2, 0, 0)
    rows = 2 * expand_sum.shape[1]
    cols = ff // N_TAB
    f32 = lambda *n: jax.ShapeDtypeStruct(n, F32)
    shapes = [
        f32(2 * reduce_sum.shape[2], reduce_sum.shape[1]), f32(rows, cols),
        f32(rows, expand_sum.shape[2] - cols), f32(rows, joined_sum.shape[2]),
        f32(3, width), f32(3, width), f32(4, width), f32(ff // width, width),
    ]
    lanes = 128
    part = pl.BlockSpec((tokens // 4, width), lambda i: (i, 0))
    table, *rest = pl.pallas_call(
        write_kernel,
        grid=(4,),
        in_specs=[pl.BlockSpec(block, first), pl.BlockSpec(block, second), part]
        + [full(v.shape) for v in (reduce_sum, expand_sum, joined_sum, small)],
        out_specs=[pl.BlockSpec((2 * BLOCK * width // lanes, lanes), lambda i: (i, 0)), part]
        + [full(v.shape) for v in shapes],
        out_shape=[f32(table_rows * width // lanes, lanes), f32(tokens, width)] + shapes,
        compiler_params=params(),
        cost_estimate=cost(0, 16 << 20),
        name="write",
    )(done, done, embed, reduce_sum, expand_sum, joined_sum, small)
    return table.reshape(1, table_rows, width), *rest


def flip_tok(value, bit, size):
    return lax.ppermute(value, "tok", [(i, i ^ bit) for i in range(size)])


def shift_tab(value, shift, size):
    return lax.ppermute(value, "tab", [(i, (i + shift) % size) for i in range(size)])


def small_sum(value, n_tok, n_tab):
    bit = 1
    while bit < n_tok:
        value = value + flip_tok(value, bit, n_tok)
        bit *= 2
    total = value
    for shift in range(1, n_tab):
        total = total + shift_tab(value, shift, n_tab)
    return total


def body(
    n_tok, n_tab,
    embedded, cell_index, cell_boxes, box_tables, joined_weight, output_weight,
    expand_weight, reduce_weight, hidden_bias, bias_rows, norm_gains, norm_shifts, cotangent,
):
    tokens, width = embedded.shape
    pages, length = cell_index.shape
    table_rows = box_tables.shape[1]
    ff = expand_weight.shape[1]
    tok = lax.axis_index("tok").astype(jnp.int32).reshape(1)
    z = lax.axis_index("tab")
    cubic = n_tok == 8 and n_tab == 4

    corners = cell_boxes[:, :, :CELLS]
    lo = lambda n: jnp.minimum(corners[:, n], corners[:, n + 2]).reshape(-1)
    hi = lambda n: jnp.maximum(corners[:, n], corners[:, n + 2]).reshape(-1)
    left, right, top, bottom = lo(0), hi(0), lo(1), hi(1)
    none = jnp.full_like(left, -1)
    index_table = jnp.stack(
        [
            jnp.stack([left, right]),
            jnp.stack([top, bottom]),
            jnp.stack([right - left, none]),
            jnp.stack([bottom - top, none]),
        ]
    )
    padded = jnp.pad(box_tables[0], ((0, 1024 - table_rows), (0, 0)))
    if cubic:
        terms, group_index = spread(index_table, padded)
    else:
        pick_table = lambda i: lax.dynamic_index_in_dim(index_table, i, 0, keepdims=False)
        group_index = jnp.stack(
            [pick_table(z)]
            + [shift_tab(pick_table((z + s) % n_tab), s, n_tab) for s in range(1, n_tab)]
        )
        found = lookup(group_index, padded)
        terms = jnp.stack(
            [found[0]] + [shift_tab(found[s], n_tab - s, n_tab) for s in range(1, n_tab)]
        )

    q, k, v, normed, normed_low, rstd0 = embed(
        embedded, cell_index, terms, joined_weight, norm_gains, norm_shifts, bias_rows
    )
    mixed, lse = attn_fwd(q, k, v, pages)
    layer_out, after, after_low, rstd1, act, slope, gs2, gffn, sums2 = ffn_fwd(
        mixed, normed, output_weight, expand_weight, reduce_weight, hidden_bias,
        bias_rows, norm_gains, norm_shifts, cotangent, min(256, tokens),
    )
    if cubic:
        gs1, gmixed, hidden_sum, sums1, *parts, reduce_sum = ffn_grads(
            gffn, act, slope, gs2, after, after_low, rstd1, mixed, reduce_weight, expand_weight,
            output_weight, norm_gains, norm_shifts,
        )
    else:
        parts = None
        gh, gs1, gattn, gmixed, hidden_sum, sums1 = ffn_bwd(
            gffn, slope, gs2, after, rstd1, reduce_weight, expand_weight, output_weight,
            norm_gains, norm_shifts,
        )
    embedded_grad, cell_grad, sums0, sums_qv, *more = back(
        q, k, v, mixed, gmixed, lse, normed_low, gs1, joined_weight, normed, rstd0, cell_index,
        norm_gains, norm_shifts, parts,
    )
    if cubic:
        parts, expand_sum = more[:2], more[2:]
    else:
        gj = more[0]

    sums = (sums0, sums1, sums2, sums_qv, hidden_sum)
    if cubic:
        done, joined_sum, small = closing(cell_grad, group_index, sums, parts)
        (
            tables_grad, embedded_grad, reduce_grad, expand_grad, output_grad, joined_grad,
            gains_grad, shifts_grad, biases_grad, hidden_bias_grad,
        ) = write(
            done, embedded_grad, reduce_sum, expand_sum[0], joined_sum, small, table_rows, ff
        )
        hidden_bias_grad = hidden_bias_grad.reshape(-1)
    else:
        cell_grads = [cell_grad] + [shift_tab(cell_grad, s, n_tab) for s in range(1, n_tab)]
        part_a, part_b = table_part(jnp.zeros_like(tok), group_index, cell_grads, 8)
        both = jnp.concatenate([part_a, part_b], axis=2).astype(F32)
        tables_grad = lax.psum(both.reshape(1, -1, width)[:, :table_rows], "tok")
        small = jnp.concatenate([part.reshape(-1) for part in sums]).reshape(-1, 128)
        small = small_sum(small, n_tok, n_tab).reshape(-1)
        row = small.reshape(-1, width)
        gains_grad = jnp.stack([row[0], row[2], row[5]])
        shifts_grad = jnp.stack([row[1], row[3], row[6]])
        biases_grad = jnp.stack([row[8], row[9], row[4], row[7]])
        hidden_bias_grad = small[10 * width :]
        both = lambda a, b: jnp.einsum("ta,tb->ab", a, b, preferred_element_type=F32).astype(BF)

        def scattered(part):
            part = lax.psum_scatter(part, "tok", scatter_dimension=0, tiled=True)
            return lax.psum_scatter(part, "tab", scatter_dimension=1, tiled=True).astype(F32)

        reduce_grad = scattered(both(act, gffn))
        expand_grad = scattered(both(after_low, gh))
        output_grad = scattered(both(mixed, gattn))
        joined_grad = scattered(both(normed_low, jnp.concatenate([gj[0], gj[1], gj[2]], axis=1)))

    return (
        layer_out, embedded_grad, tables_grad, joined_grad, output_grad, expand_grad,
        reduce_grad, hidden_bias_grad, biases_grad, gains_grad, shifts_grad,
    )


def solution(mesh):
    rows = P(("tok", "tab"), None)
    return jax.shard_map(
        functools.partial(body, mesh.shape["tok"], mesh.shape["tab"]),
        mesh=mesh,
        in_specs=(
            rows, rows, P(("tok", "tab"), None, None), P("tab", None, None),
            P(), P(), P(), P(), P(), P(), P(), P(), rows,
        ),
        out_specs=(
            rows, rows, P("tab", None, None), P("tok", "tab"), P("tok", "tab"),
            P("tok", "tab"), P("tok", "tab"), P(), P(), P(), P(),
        ),
        check_vma=False,
    )
```
